32 devices in a mesh: dp: 8 (over y, x, core), mod: 4 (over z).
Axes of the slice: x: 2, y: 2, z: 4, core: 2. Of those that a mesh axis runs over, the one named last changes fastest.
Arguments:
- tokens: bfloat16 [8192, 1152], P(('dp', 'mod')), may hold values from -6 to 6
- conditions: bfloat16 [128, 1152], P(('dp', 'mod')), may hold values from -6 to 6
- image_lengths: int32 [32, 4], P(('dp', 'mod')), may hold values from 0 to 256, as said below
- cotangent: bfloat16 [8192, 1152], P(('dp', 'mod')), may hold values from -6 to 6
- project_weight: float32 [1152, 3456], P('dp'), may hold values from -0.1875 to 0.1875
- project_moment: float32 [1152, 3456], P('dp'), may hold values from -0.00012207031 to 0.00012207031
- project_square: float32 [1152, 3456], P('dp'), may hold values from 2.0917e-11 to 3.34672e-10
- output_weight: float32 [1152, 1152], P('dp'), may hold values from -1.5 to 1.5
- output_moment: float32 [1152, 1152], P('dp'), may hold values from -0.00012207031 to 0.00012207031
- output_square: float32 [1152, 1152], P('dp'), may hold values from 5.8567604e-12 to 2.3427042e-11
- expand_weight: float32 [1152, 4608], P('dp'), may hold values from -0.1875 to 0.1875
- expand_moment: float32 [1152, 4608], P('dp'), may hold values from -0.00012207031 to 0.00012207031
- expand_square: float32 [1152, 4608], P('dp'), may hold values from 2.3008702e-12 to 9.203481e-12
- shrink_weight: float32 [4608, 1152], P('dp'), may hold values from -0.09375 to 0.09375
- shrink_moment: float32 [4608, 1152], P('dp'), may hold values from -0.00012207031 to 0.00012207031
- shrink_square: float32 [4608, 1152], P('dp'), may hold values from 8.3668e-12 to 3.34672e-11
- modulate_weight: float32 [1152, 6912], P('dp', 'mod'), may hold values from -0.1875 to 0.1875
- modulate_moment: float32 [1152, 6912], P('dp', 'mod'), may hold values from -0.00012207031 to 0.00012207031
- modulate_square: float32 [1152, 6912], P('dp', 'mod'), may hold values from 2.0917e-11 to 3.34672e-10
- bias_vector: float32 [16128], P('dp'), may hold values from -1.75 to 1.75
- bias_moment: float32 [16128], P('dp'), may hold values from -0.00012207031 to 0.00012207031
- bias_square: float32 [16128], P('dp'), may hold values from 2.0917e-11 to 3.34672e-10
Outputs:
- block_output: bfloat16 [8192, 1152], P(('dp', 'mod'))
- token_grads: float32 [8192, 1152], P(('dp', 'mod'))
- condition_grads: float32 [128, 1152], P(('dp', 'mod'))
- global_norm: float32 [], replicated
- next_project: float32 [1152, 3456], P('dp')
- first_project: float32 [1152, 3456], P('dp')
- second_project: float32 [1152, 3456], P('dp')
- next_output: float32 [1152, 1152], P('dp')
- first_output: float32 [1152, 1152], P('dp')
- second_output: float32 [1152, 1152], P('dp')
- next_expand: float32 [1152, 4608], P('dp')
- first_expand: float32 [1152, 4608], P('dp')
- second_expand: float32 [1152, 4608], P('dp')
- next_shrink: float32 [4608, 1152], P('dp')
- first_shrink: float32 [4608, 1152], P('dp')
- second_shrink: float32 [4608, 1152], P('dp')
- next_modulate: float32 [1152, 6912], P('dp', 'mod')
- first_modulate: float32 [1152, 6912], P('dp', 'mod')
- second_modulate: float32 [1152, 6912], P('dp', 'mod')
- next_biases: float32 [16128], P('dp')
- first_biases: float32 [16128], P('dp')
- second_biases: float32 [16128], P('dp')
The draws below stay inside these ranges and needn't reach their ends.
Inputs may be any that keep to these rules, and one draw needn't show every extreme that they name: `image_lengths`: each packed row lists, from its first slot, zero to 1 images of 256 tokens, then images of 64 tokens, then zeros; every row holds at least one image; the images lie end to end from the row's first token, their lengths sum to at most 256, and the rest of the row is padding.
All inputs are finite; a program needn't handle non-finite values.
Results may differ from the reference program's by a relative error of at most 0.025.
The reference program's roundings to bfloat16 on the way count: a program that leaves them out, or rounds other values in their place, can miss the bound.
Values may be sent and summed in bfloat16 or wider, within the bound.
A program may use at most 256 MiB of HBM per device.

```python
import math
import jax
import jax.numpy as jnp
from jax import lax

D = 1152
HEADS = 16
HEAD_DIM = 72
FF = 4608
ROW = 256
BIG_IMG = 256
SMALL_IMG = 64
STEP = 10
IMG_ROW = 4
ROWS = 32
TOKENS = 8192
SAMPLES = 128


def draw_image_lengths(key, part):
    first_key, second_key = jax.random.split(jax.random.fold_in(key, 17))
    row_index = jnp.arange(ROWS, dtype=jnp.int32)[:, None]
    large_count = jax.random.randint(first_key, (ROWS, 1), 0, ROW // BIG_IMG + 1, dtype=jnp.int32)
    large_count = jnp.where(row_index == 0, jnp.maximum(large_count, 1), large_count)
    room = (ROW - large_count * BIG_IMG) // SMALL_IMG
    small_pick = jax.random.randint(second_key, (ROWS, 1), 0, IMG_ROW + 1, dtype=jnp.int32)
    small_count = room - jnp.remainder(small_pick, room // 2 + 1)
    slots = jnp.arange(IMG_ROW, dtype=jnp.int32)[None, :]
    lengths = jnp.where(slots < large_count, BIG_IMG, jnp.where(slots < large_count + small_count, SMALL_IMG, 0))
    return lengths.astype(jnp.int32)


def levels(key, extent, shards, smallest, high):
    factor_of = 1.0
    for axis_at, parts in shards:
        draws = jax.random.uniform(jax.random.fold_in(jax.random.fold_in(key, 6), axis_at), (parts,), jnp.float32, smallest / len(shards), high / len(shards))
        factor_of = factor_of * jnp.repeat(jnp.exp(draws), extent[axis_at] // parts).reshape((-1,) + (1,) * (len(extent) - 1 - axis_at))
    return factor_of


def bell_draw(key, extent, scale, bound, pieces=(), kind=jnp.bfloat16):
    level = levels(key, extent, pieces, -0.22, 0.18) if pieces else 1.0
    values = jax.random.normal(key, extent, jnp.float32) * scale * level
    return jnp.minimum(jnp.maximum(values, -bound), bound).astype(kind)


def setup_inputs(seed: int = 0) -> dict:
    streams_of = jax.random.split(jax.random.key(seed), 23)
    return {
        "tokens": bell_draw(streams_of[0], (TOKENS, D), 1.0, 6.0, ((0, 32),)),
        "conditions": bell_draw(streams_of[1], (SAMPLES, D), 1.0, 6.0, ((0, 32),)),
        "image_lengths": draw_image_lengths(jax.random.fold_in(streams_of[22], 71), 0),
        "cotangent": bell_draw(streams_of[3], (TOKENS, D), 1.0, 6.0, ((0, 32),)),
        "project_weight": bell_draw(streams_of[4], (D, 3 * D), D ** -0.5, 0.1875, ((0, 8),), jnp.float32),
        "project_moment": bell_draw(streams_of[5], (D, 3 * D), (0.11 / (10*D*D + 2*D*FF + 10*D + FF) ** 0.5), 0.00012207031, ((0, 8),), jnp.float32),
        "project_square": jnp.clip(jnp.exp(math.log(3.346720123253988e-10) - 2.7725887 * jax.random.uniform(streams_of[6], (D, 3 * D), jnp.float32) ** levels(streams_of[6], (D, 3 * D), ((0, 8),), -0.2, 0.2)), 2.0917000770337424e-11, 3.346720123253988e-10),
        "output_weight": bell_draw(streams_of[7], (D, D), (D // 64) ** -0.5, 1.5, ((0, 8),), jnp.float32),
        "output_moment": bell_draw(streams_of[8], (D, D), (0.11 / (10*D*D + 2*D*FF + 10*D + FF) ** 0.5), 0.00012207031, ((0, 8),), jnp.float32),
        "output_square": jnp.clip(jnp.exp(math.log(2.3427041556667305e-11) - 1.3862944 * jax.random.uniform(streams_of[9], (D, D), jnp.float32) ** levels(streams_of[9], (D, D), ((0, 8),), -0.2, 0.2)), 5.856760389166826e-12, 2.3427041556667305e-11),
        "expand_weight": bell_draw(streams_of[10], (D, FF), D ** -0.5, 0.1875, ((0, 8),), jnp.float32),
        "expand_moment": bell_draw(streams_of[11], (D, FF), (0.11 / (10*D*D + 2*D*FF + 10*D + FF) ** 0.5), 0.00012207031, ((0, 8),), jnp.float32),
        "expand_square": jnp.clip(jnp.exp(math.log(9.20348085936551e-12) - 1.3862944 * jax.random.uniform(streams_of[12], (D, FF), jnp.float32) ** levels(streams_of[12], (D, FF), ((0, 8),), -0.2, 0.2)), 2.3008702148413773e-12, 9.20348085936551e-12),
        "shrink_weight": bell_draw(streams_of[13], (FF, D), FF ** -0.5, 0.09375, ((0, 8),), jnp.float32),
        "shrink_moment": bell_draw(streams_of[14], (FF, D), (0.11 / (10*D*D + 2*D*FF + 10*D + FF) ** 0.5), 0.00012207031, ((0, 8),), jnp.float32),
        "shrink_square": jnp.clip(jnp.exp(math.log(3.346720123253988e-11) - 1.3862944 * jax.random.uniform(streams_of[15], (FF, D), jnp.float32) ** levels(streams_of[15], (FF, D), ((0, 8),), -0.2, 0.2)), 8.36680030813497e-12, 3.346720123253988e-11),
        "modulate_weight": bell_draw(streams_of[16], (D, 6 * D), D ** -0.5, 0.1875, ((0, 8), (1, 4)), jnp.float32),
        "modulate_moment": bell_draw(streams_of[17], (D, 6 * D), (0.11 / (10*D*D + 2*D*FF + 10*D + FF) ** 0.5), 0.00012207031, ((0, 8), (1, 4)), jnp.float32),
        "modulate_square": jnp.clip(jnp.exp(math.log(3.346720123253988e-10) - 2.7725887 * jax.random.uniform(streams_of[18], (D, 6 * D), jnp.float32) ** levels(streams_of[18], (D, 6 * D), ((0, 8), (1, 4)), -0.2, 0.2)), 2.0917000770337424e-11, 3.346720123253988e-10),
        "bias_vector": bell_draw(streams_of[19], (10 * D + FF,), 0.3, 1.75, ((0, 8),), jnp.float32),
        "bias_moment": bell_draw(streams_of[20], (10 * D + FF,), (0.11 / (10*D*D + 2*D*FF + 10*D + FF) ** 0.5), 0.00012207031, ((0, 8),), jnp.float32),
        "bias_square": jnp.clip(jnp.exp(math.log(3.346720123253988e-10) - 2.7725887 * jax.random.uniform(streams_of[21], (10 * D + FF,), jnp.float32) ** levels(streams_of[21], (10 * D + FF,), ((0, 8),), -0.2, 0.2)), 2.0917000770337424e-11, 3.346720123253988e-10),
    }


@jax.custom_vjp
def low(v):
    return lax.optimization_barrier(v.astype(jnp.bfloat16)).astype(jnp.float32)

@jax.custom_vjp
def low_back(v):
    return v

def low_keep(v):
    return (low(v), None)

def low_pass(kept, grad):
    return (grad,)

def back_keep(v):
    return (v, None)

def back_low(kept, grad):
    return (low(grad),)
low.defvjp(low_keep, low_pass)
low_back.defvjp(back_keep, back_low)
beta_first = 0.9
beta_second = 0.999
weight_decay = 0.01
adam_epsilon = 1e-08
tanh_scale = 0.7978845608028654
cubic_term = 0.044715

def rounded_both(values):
    return low_back(low(values))

def product(left, right):
    return jnp.dot(left, right, precision=lax.Precision.HIGHEST, preferred_element_type=jnp.float32)

def normalize(values):
    center = values - lax.optimization_barrier(jnp.mean(values, axis=-1, keepdims=True))
    spread = lax.optimization_barrier(jnp.mean(center * center, axis=-1, keepdims=True))
    return center * lax.rsqrt(spread + 1e-06)

def gelu_tanh(values):
    return 0.5 * values * (1.0 + jnp.tanh(tanh_scale * (values + cubic_term * values * values * values)))

def slot_numbers(row_lengths):
    ends = jnp.cumsum(row_lengths, dtype=jnp.int32)
    positions = jnp.arange(ROW, dtype=jnp.int32)
    return lax.optimization_barrier(jnp.sum((positions[:, None] >= ends[None, :]).astype(jnp.int32), axis=1, dtype=jnp.int32))

def row_forward(params, row_tokens, row_mod, row_lengths):
    project, output, expand, shrink, bias_query, bias_value, bias_output, bias_expand, bias_shrink = params
    slots = slot_numbers(row_lengths)
    onehot = (slots[:, None] == jnp.arange(IMG_ROW, dtype=jnp.int32)[None, :]).astype(jnp.float32)
    per_token = product(onehot, row_mod)
    shift_attend = per_token[:, 0:D]
    scale_attend = per_token[:, D:2 * D]
    gate_attend = per_token[:, 2 * D:3 * D]
    shift_feed = per_token[:, 3 * D:4 * D]
    scale_feed = per_token[:, 4 * D:5 * D]
    gate_feed = per_token[:, 5 * D:6 * D]
    normed_attend = normalize(row_tokens)
    attend_in = low(normed_attend * (1.0 + scale_attend) + shift_attend)
    projected = product(attend_in, project)
    query = rounded_both(projected[:, 0:D] + bias_query).reshape(ROW, HEADS, HEAD_DIM)
    keys = rounded_both(projected[:, D:2 * D]).reshape(ROW, HEADS, HEAD_DIM)
    values = rounded_both(projected[:, 2 * D:3 * D] + bias_value).reshape(ROW, HEADS, HEAD_DIM)
    raw = jnp.einsum('qhd,khd->hqk', query, keys, precision=lax.Precision.HIGHEST) * HEAD_DIM ** (-0.5)
    same_image = slots[:, None] == slots[None, :]
    scores = jnp.where(same_image[None], low_back(raw), -1e+30)
    row_top = lax.optimization_barrier(jnp.max(scores, axis=-1, keepdims=True))
    exponent = jnp.exp(scores - row_top)
    probs = exponent / lax.optimization_barrier(jnp.sum(exponent, axis=-1, keepdims=True))
    mixed = jnp.einsum('hqk,khd->qhd', low(probs), values, precision=lax.Precision.HIGHEST).reshape(ROW, D)
    attend_out = low_back(product(rounded_both(mixed), output) + bias_output)
    resid = row_tokens + gate_attend * attend_out
    normed_feed = normalize(resid)
    feed_in = low(normed_feed * (1.0 + scale_feed) + shift_feed)
    hidden_pre = low_back(product(feed_in, expand) + bias_expand)
    hidden = low(gelu_tanh(hidden_pre))
    feed_out = low_back(product(hidden, shrink) + bias_shrink)
    return resid + gate_feed * feed_out

def forward(token_values, condition_values, project, output, expand, shrink, modulate, biases, lengths):
    rounded = low(biases)
    bias_query = rounded[0:D]
    bias_value = rounded[D:2 * D]
    bias_output = rounded[2 * D:3 * D]
    bias_expand = rounded[3 * D:3 * D + FF]
    bias_shrink = rounded[3 * D + FF:4 * D + FF]
    bias_modulate = rounded[4 * D + FF:10 * D + FF]
    modulation = rounded_both(product(low(jax.nn.silu(condition_values)), low(modulate)) + bias_modulate)
    params = (low(project), low(output), low(expand), low(shrink), bias_query, bias_value, bias_output, bias_expand, bias_shrink)

    def one_row(carry, inputs):
        row_tokens, row_mod, row_lengths = inputs
        return (carry, row_forward(params, row_tokens, row_mod, row_lengths))
    token_rows = token_values.reshape(ROWS, ROW, D)
    mod_rows = modulation.reshape(ROWS, IMG_ROW, 6 * D)
    carry_out, outputs = lax.scan(jax.checkpoint(one_row), jnp.zeros((), jnp.float32), (token_rows, mod_rows, lengths))
    return outputs.reshape(TOKENS, D)

def adam_update(weight, moment, square, grad, rate):
    first = beta_first * moment + (1.0 - beta_first) * grad
    second = beta_second * square + (1.0 - beta_second) * grad * grad
    step_size = first / (1.0 - beta_first ** STEP)
    divisor = jnp.sqrt(second / (1.0 - beta_second ** STEP)) + adam_epsilon
    return (weight - rate * (step_size / divisor + weight_decay * weight), first, second)

def reference(tokens, conditions, image_lengths, cotangent, project_weight, project_moment, project_square, output_weight, output_moment, output_square, expand_weight, expand_moment, expand_square, shrink_weight, shrink_moment, shrink_square, modulate_weight, modulate_moment, modulate_square, bias_vector, bias_moment, bias_square):

    def run(token_values, condition_values, project, output, expand, shrink, modulate, biases):
        return forward(token_values, condition_values, project, output, expand, shrink, modulate, biases, image_lengths)
    result, pullback = jax.vjp(run, tokens.astype(jnp.float32), conditions.astype(jnp.float32), project_weight, output_weight, expand_weight, shrink_weight, modulate_weight, bias_vector)
    grads = pullback(cotangent.astype(jnp.float32))
    token_grads = grads[0]
    condition_grads = grads[1]
    weight_grads = grads[2:]
    square_total = jnp.zeros((), jnp.float32)
    for grad in weight_grads:
        square_total = square_total + jnp.sum(grad * grad)
    global_norm = jnp.sqrt(square_total)
    clip_factor = jnp.minimum(1.0, 1.0 / (global_norm + 1e-06))
    rates = (D ** (-0.5), (D // 64) ** (-0.5), D ** (-0.5), FF ** (-0.5), D ** (-0.5), 0.3)
    states = ((project_weight, project_moment, project_square), (output_weight, output_moment, output_square), (expand_weight, expand_moment, expand_square), (shrink_weight, shrink_moment, shrink_square), (modulate_weight, modulate_moment, modulate_square), (bias_vector, bias_moment, bias_square))
    updated = []
    for state, grad, rate in zip(states, weight_grads, rates):
        updated.append(adam_update(state[0], state[1], state[2], grad * clip_factor, rate))
    return (result.astype(jnp.bfloat16), token_grads, condition_grads, global_norm, updated[0][0], updated[0][1], updated[0][2], updated[1][0], updated[1][1], updated[1][2], updated[2][0], updated[2][1], updated[2][2], updated[3][0], updated[3][1], updated[3][2], updated[4][0], updated[4][1], updated[4][2], updated[5][0], updated[5][1], updated[5][2])
```

```python
import functools

import jax
import jax.numpy as jnp
from jax import lax
from jax.experimental import pallas as pl
from jax.experimental.pallas import tpu as pltpu
from jax.sharding import PartitionSpec as P

D = 1152
HEADS = 16
HEAD_DIM = 72
FF = 4608
ROW = 256
STEP = 10
IMG_ROW = 4


beta_first = 0.9
beta_second = 0.999
weight_decay = 0.01
adam_epsilon = 1e-08
tanh_scale = 0.7978845608028654
cubic_term = 0.044715


def contract(left, right, left_axis, right_axis):
    return lax.dot_general(
        left, right, (((left_axis,), (right_axis,)), ((), ())), preferred_element_type=jnp.float32
    )


def normalize_rows(values):
    center = values - jnp.mean(values, axis=-1, keepdims=True)
    inverse = lax.rsqrt(jnp.mean(center * center, axis=-1, keepdims=True) + 1e-06)
    return (center * inverse, inverse)


def normalize_back(grad_normed, normed, inverse):
    centered = grad_normed - jnp.mean(grad_normed, axis=-1, keepdims=True)
    return (centered - normed * jnp.mean(grad_normed * normed, axis=-1, keepdims=True)) * inverse


def adam_update(weight, moment, square, grad, rate):
    first = beta_first * moment + (1.0 - beta_first) * grad
    second = beta_second * square + (1.0 - beta_second) * grad * grad
    step_size = first / (1.0 - beta_first**STEP)
    divisor = jnp.sqrt(second / (1.0 - beta_second**STEP)) + adam_epsilon
    return (weight - rate * (step_size / divisor + weight_decay * weight), first, second)


def merge_heads(stacked):
    return stacked.transpose(1, 0, 2).reshape(stacked.shape[1], stacked.shape[0] * stacked.shape[2])


MESH = pl.DeviceIdType.MESH
GROUP = 8
DEPTH = 4
VMEM_BYTES = 60 << 20
low_type = jnp.bfloat16
full_type = jnp.float32


def vmem():
    return pl.BlockSpec(memory_space=pltpu.VMEM)


def anywhere():
    return pl.BlockSpec(memory_space=pl.ANY)


def plane_places():
    place = lax.axis_index("dp")
    layer = lax.axis_index("mod")
    twin = place + 1 - 2 * lax.rem(place, 2)
    side = 2 - 4 * lax.rem(lax.div(place, 2), 2)
    across = place + side
    along = place + 4 - 8 * lax.div(place, 4)
    corner = along + side
    return place, layer, twin, across, along, corner


def twin_of(place):
    return place + 1 - 2 * lax.rem(place, 2)


def send(source, target, send_sem, recv_sem, place, layer):
    copy = pltpu.make_async_remote_copy(
        src_ref=source,
        dst_ref=target,
        send_sem=send_sem,
        recv_sem=recv_sem,
        device_id=(place, layer),
        device_id_type=MESH,
    )
    copy.start()
    return copy


def greet(peers):
    barrier = pltpu.get_barrier_semaphore()
    for peer in peers:
        pl.semaphore_signal(barrier, inc=1, device_id=peer, device_id_type=MESH)
    pl.semaphore_wait(barrier, len(peers))


class Gather:
    def __init__(self, own, slots, sends, recvs, rows, cut):
        self.own, self.slots, self.sends, self.recvs = own, slots, sends, recvs
        self.first, self.second = pl.ds(0, cut), pl.ds(cut, rows - cut)
        self.place, self.layer, self.twin, self.across, self.along, self.corner = plane_places()
        self.copies = {}

    def push(self, index, source, slot, part, peer):
        target = self.slots.at[slot] if part is None else self.slots.at[slot, part]
        if source is None:
            source = target
        self.copies[index] = send(
            source, target, self.sends.at[index], self.recvs.at[index], peer, self.layer
        )

    def start_twin(self):
        self.push(2, self.own, self.place, None, self.twin)

    def start_links(self):
        self.push(0, self.own, self.place, None, self.across)
        self.push(1, self.own, self.place, None, self.along)

    def forward_near(self):
        self.copies[0].wait_recv()
        self.push(3, None, self.across, self.first, self.along)
        self.push(5, None, self.across, None, self.twin)
        self.copies[1].wait_recv()
        self.push(4, None, self.along, self.second, self.across)
        self.push(6, None, self.along, None, self.twin)

    def forward_far(self):
        self.copies[3].wait_recv()
        self.push(7, None, self.corner, self.first, self.twin)
        self.copies[4].wait_recv()
        self.push(8, None, self.corner, self.second, self.twin)

    def arrived(self, *indices):
        for index in indices:
            self.copies[index].wait_recv()

    def finish_sends(self):
        for index in range(9):
            self.copies[index].wait_send()


class Scatter:
    def __init__(self, parts, from_twin, half_across, half_along, whole_across, whole_along, sends, recvs, rows, cut):
        self.parts, self.from_twin = parts, from_twin
        self.half_across, self.half_along = half_across, half_along
        self.whole_across, self.whole_along = whole_across, whole_along
        self.sends, self.recvs = sends, recvs
        self.first, self.second = pl.ds(0, cut), pl.ds(cut, rows - cut)
        self.place, self.layer, self.twin, self.across, self.along, self.corner = plane_places()
        self.copies = {}

    def push(self, index, source, target, peer):
        self.copies[index] = send(
            source, target, self.sends.at[index], self.recvs.at[index], peer, self.layer
        )

    def start_twin(self):
        for index, slot in ((3, self.corner), (1, self.across), (2, self.along), (0, self.place)):
            self.push(index, self.parts.at[twin_of(slot)], self.from_twin.at[index], self.twin)

    def add(self, slot, part, other):
        total = self.parts[slot, part].astype(full_type) + other.astype(full_type)
        self.parts[slot, part] = total.astype(self.parts.dtype)

    def start_links(self):
        whole = slice(None)
        self.copies[3].wait_recv()
        self.add(self.corner, whole, self.from_twin[3])
        self.push(4, self.parts.at[self.corner, self.first], self.half_across, self.across)
        self.push(5, self.parts.at[self.corner, self.second], self.half_along, self.along)
        self.copies[1].wait_recv()
        self.add(self.across, whole, self.from_twin[1])
        self.push(6, self.parts.at[self.across, self.first], self.whole_across.at[self.first], self.across)
        self.copies[2].wait_recv()
        self.add(self.along, whole, self.from_twin[2])
        self.push(7, self.parts.at[self.along, self.second], self.whole_along.at[self.second], self.along)

    def forward(self):
        self.copies[5].wait_recv()
        self.add(self.across, self.second, self.half_along[...])
        self.push(8, self.parts.at[self.across, self.second], self.whole_across.at[self.second], self.across)
        self.copies[4].wait_recv()
        self.add(self.along, self.first, self.half_across[...])
        self.push(9, self.parts.at[self.along, self.first], self.whole_along.at[self.first], self.along)

    def finish(self):
        self.copies[0].wait_recv()
        for index in (6, 8, 7, 9):
            self.copies[index].wait_recv()
        total = (
            self.parts[self.place].astype(full_type)
            + self.from_twin[0].astype(full_type)
            + (self.whole_across[...].astype(full_type) + self.whole_along[...].astype(full_type))
        )
        for index in range(10):
            self.copies[index].wait_send()
        return total


def scatter_scratch(rows, cut, columns):
    return [
        pltpu.VMEM((4, rows, columns), low_type),
        pltpu.VMEM((cut, columns), low_type),
        pltpu.VMEM((rows - cut, columns), low_type),
        pltpu.VMEM((rows, columns), low_type),
        pltpu.VMEM((rows, columns), low_type),
        pltpu.SemaphoreType.DMA((10,)),
        pltpu.SemaphoreType.DMA((10,)),
    ]


def iota(shape, axis):
    return lax.broadcasted_iota(jnp.int32, shape, axis)


def sample_picker():
    row, column = iota((128, 256), 0), iota((128, 256), 1)
    wanted = ((row >> 2) & 3) * 64 + (row >> 4) * 8 + (row & 3)
    return (column == wanted).astype(full_type).astype(low_type)


def slot_spreader():
    row, column = iota((32, 16), 0), iota((32, 16), 1)
    return jnp.where(((row & 7) < 4) & (column == (row >> 3) * 4 + (row & 7)), 1.0, 0.0).astype(low_type)


def start_kernel(
    conditions,
    project,
    output,
    expand,
    modulate,
    bias_piece,
    bias_own,
    project_out,
    output_out,
    expand_out,
    mod_out,
    active_out,
    bias_out,
    own_project,
    own_output,
    own_expand,
    cond_send,
    cond_plane,
    cond_all,
    part_send,
    part_recv,
    mod_send,
    mod_recv,
    bias_recv,
    small_send,
    small_recv,
    project_sends,
    project_recvs,
    output_sends,
    output_recvs,
    expand_sends,
    expand_recvs,
    local_sems,
):
    place, layer, *_ = plane_places()
    plane = [lax.rem(place + step, GROUP) for step in range(1, GROUP)]
    column = [lax.rem(layer + step, DEPTH) for step in range(1, DEPTH)]
    cut_columns = expand.shape[1] // GROUP
    cut_rows = project.shape[0]

    values = conditions[...].astype(full_type)
    active = (values * jax.nn.sigmoid(values)).astype(low_type).astype(full_type)
    cond_send[...] = jnp.zeros_like(cond_send)
    for step in range(GROUP):
        cond_send[step, 0:IMG_ROW, :] = active[:, step * cut_rows : (step + 1) * cut_rows]
    bias_recv[place] = bias_own[...].astype(low_type).astype(full_type)
    own_project[...] = project[...].astype(low_type)
    own_output[...] = output[...].astype(low_type)
    for step in range(GROUP):
        own_expand[step] = expand[:, step * cut_columns : (step + 1) * cut_columns].astype(low_type)

    greet([(peer, layer) for peer in plane] + [(place, peer) for peer in column])

    small = []
    for step, peer in enumerate(plane):
        small.append(
            send(cond_send.at[peer], cond_plane.at[place], small_send.at[step], small_recv.at[step], peer, layer)
        )
    project_gather = Gather(own_project, project_out, project_sends, project_recvs, cut_rows, 80)
    output_gather = Gather(own_output, output_out, output_sends, output_recvs, cut_rows, 64)
    project_gather.start_links()
    project_gather.start_twin()
    output_gather.start_twin()
    locals_ = [
        pltpu.make_async_copy(own_project, project_out.at[place], local_sems.at[0]),
        pltpu.make_async_copy(own_output, output_out.at[place], local_sems.at[1]),
        pltpu.make_async_copy(own_expand.at[place], expand_out.at[place], local_sems.at[2]),
    ]
    for copy in locals_:
        copy.start()

    cond_plane[place] = cond_send[place]
    for copy in small:
        copy.wait_recv()
    waits = list(small)
    small = []
    for step, peer in enumerate(column):
        small.append(
            send(cond_plane, cond_all.at[layer], small_send.at[7 + step], small_recv.at[7 + step], place, peer)
        )
    cond_all[layer] = cond_plane[...]
    for copy in small:
        copy.wait_recv()
    waits += small
    padded = cond_all[...].reshape(DEPTH * GROUP * 8, cut_rows).astype(low_type)
    picked = contract(sample_picker(), padded, 1, 0).astype(low_type)
    active_out[...] = picked
    partial = contract(picked, modulate[...].astype(low_type), 1, 0)
    partial = partial + bias_piece[...].astype(low_type).astype(full_type)
    part_send[...] = partial.reshape(part_send.shape)
    small = []
    for step, peer in enumerate(plane):
        small.append(
            send(part_send.at[peer], part_recv.at[place], small_send.at[10 + step], small_recv.at[10 + step], peer, layer)
        )
        small.append(
            send(bias_recv.at[place], bias_recv.at[place], small_send.at[20 + step], small_recv.at[20 + step], peer, layer)
        )
    part_recv[place] = part_send[place]
    for copy in small:
        copy.wait_recv()
    waits += small
    total = part_recv[0]
    for step in range(1, GROUP):
        total = total + part_recv[step]
    spread = contract(slot_spreader(), total.astype(low_type), 1, 0)
    mod_send[...] = spread.reshape(mod_send.shape)
    small = []
    for step, peer in enumerate(column):
        small.append(
            send(mod_send.at[peer], mod_recv.at[layer], small_send.at[17 + step], small_recv.at[17 + step], place, peer)
        )
    mod_recv[layer] = mod_send[layer]

    project_gather.forward_near()
    output_gather.start_links()
    exchange = []
    for step, peer in enumerate(plane):
        exchange.append(
            send(own_expand.at[peer], expand_out.at[place], expand_sends.at[step], expand_recvs.at[step], peer, layer)
        )
    for copy in small:
        copy.wait_recv()
    waits += small
    mod_out[...] = mod_recv[...]
    bias_out[...] = bias_recv[...]
    project_gather.forward_far()
    output_gather.forward_near()
    output_gather.forward_far()
    for gather in (project_gather, output_gather):
        gather.arrived(2, 5, 6, 7, 8)
        gather.finish_sends()
    for copy in exchange:
        copy.wait()
    for copy in waits:
        copy.wait_send()
    for copy in locals_:
        copy.wait()


def start_call(conditions, project, output, expand, modulate, bias_piece, bias_own):
    rows = project.shape[0]
    hidden = expand.shape[1] // GROUP
    columns = modulate.shape[1]
    shape = jax.ShapeDtypeStruct
    dma = pltpu.SemaphoreType.DMA
    return pl.pallas_call(
        start_kernel,
        out_shape=(
            shape((GROUP, rows, project.shape[1]), low_type),
            shape((GROUP, rows, output.shape[1]), low_type),
            shape((GROUP, rows, hidden), low_type),
            shape((DEPTH, 8, columns), full_type),
            shape((128, rows), low_type),
            shape((GROUP,) + bias_own.shape, full_type),
        ),
        in_specs=[vmem()] * 7,
        out_specs=(anywhere(), anywhere(), anywhere(), vmem(), vmem(), vmem()),
        scratch_shapes=[
            pltpu.VMEM(project.shape, low_type),
            pltpu.VMEM(output.shape, low_type),
            pltpu.VMEM((GROUP, rows, hidden), low_type),
            pltpu.VMEM((GROUP, 8, rows), full_type),
            pltpu.VMEM((GROUP, 8, rows), full_type),
            pltpu.VMEM((DEPTH, GROUP, 8, rows), full_type),
            pltpu.VMEM((GROUP, 16, columns), full_type),
            pltpu.VMEM((GROUP, 16, columns), full_type),
            pltpu.VMEM((DEPTH, 8, columns), full_type),
            pltpu.VMEM((DEPTH, 8, columns), full_type),
            pltpu.VMEM((GROUP,) + bias_own.shape, full_type),
            dma((27,)),
            dma((27,)),
            dma((9,)),
            dma((9,)),
            dma((9,)),
            dma((9,)),
            dma((7,)),
            dma((7,)),
            dma((3,)),
        ],
        compiler_params=pltpu.CompilerParams(
            collective_id=0, has_side_effects=True, vmem_limit_bytes=VMEM_BYTES
        ),
        name="gather_start",
    )(conditions, project, output, expand, modulate, bias_piece, bias_own)


def head_window(head):
    start = lax.min(lax.div(head * HEAD_DIM, 128) * 128, D - 256)
    start = pl.multiple_of(start, 128)
    lane = iota((1, 256), 1) + start
    inside = (lane >= head * HEAD_DIM) & (lane < (head + 1) * HEAD_DIM)
    return start, inside.astype(full_type)


def window(ref, base, start):
    return ref[:, pl.ds(pl.multiple_of(base + start, 128), 256)]


def masked_probs(query, key, same):
    scores = jnp.where(same, contract(query, key, 1, 1) * HEAD_DIM ** (-0.5), -1e30)
    exponent = jnp.exp(scores - jnp.max(scores, axis=1, keepdims=True))
    return exponent / jnp.sum(exponent, axis=1, keepdims=True)


def attend_forward_kernel(packed, slot_row, slot_column, mixed, total):
    same = slot_column[...] == slot_row[...]
    total[...] = jnp.zeros_like(total)

    def head_step(head, carry):
        start, inside = head_window(head)
        keep = inside.astype(low_type)
        probs = masked_probs(window(packed, 0, start) * keep, window(packed, D, start), same)
        out = contract(probs.astype(low_type), window(packed, 2 * D, start) * keep, 1, 0)
        total[:, pl.ds(start, 256)] += out
        return carry

    lax.fori_loop(0, HEADS, head_step, 0, unroll=2)
    mixed[...] = total[...].astype(low_type)


def attend_forward(packed, slot_row, slot_column):
    return pl.pallas_call(
        attend_forward_kernel,
        out_shape=jax.ShapeDtypeStruct((ROW, D), low_type),
        in_specs=[vmem()] * 3,
        out_specs=vmem(),
        scratch_shapes=[pltpu.VMEM((ROW, D), full_type)],
        compiler_params=pltpu.CompilerParams(vmem_limit_bytes=VMEM_BYTES),
        name="attend_forward",
    )(packed, slot_row, slot_column)


def attend_backward_kernel(packed, grad_mixed, slot_row, slot_column, grads, total):
    same = slot_column[...] == slot_row[...]
    total[...] = jnp.zeros_like(total)
    scale = HEAD_DIM ** (-0.5)

    def head_step(head, carry):
        start, inside = head_window(head)
        keep = inside.astype(low_type)
        query = window(packed, 0, start) * keep
        key = window(packed, D, start)
        value = window(packed, 2 * D, start)
        grad = window(grad_mixed, 0, start) * keep
        probs = masked_probs(query, key, same)
        grad_probs = contract(grad, value, 1, 1)
        grad_scores = probs * (grad_probs - jnp.sum(probs * grad_probs, axis=1, keepdims=True))
        grad_scores = grad_scores.astype(low_type)
        total[:, pl.ds(start, 256)] += contract(grad_scores, key * keep, 1, 0) * scale
        total[:, pl.ds(pl.multiple_of(D + start, 128), 256)] += contract(grad_scores, query, 0, 0) * scale
        total[:, pl.ds(pl.multiple_of(2 * D + start, 128), 256)] += contract(probs.astype(low_type), grad, 0, 0)
        return carry

    lax.fori_loop(0, HEADS, head_step, 0, unroll=2)
    grads[...] = total[...].astype(low_type)


def attend_backward(packed, grad_mixed, slot_row, slot_column):
    return pl.pallas_call(
        attend_backward_kernel,
        out_shape=jax.ShapeDtypeStruct(packed.shape, low_type),
        in_specs=[vmem()] * 4,
        out_specs=vmem(),
        scratch_shapes=[pltpu.VMEM(packed.shape, full_type)],
        compiler_params=pltpu.CompilerParams(vmem_limit_bytes=VMEM_BYTES),
        name="attend_backward",
    )(packed, grad_mixed, slot_row, slot_column)


def feed_kernel(
    feed_own,
    grad_own,
    expand,
    shrink,
    bias,
    feed_out,
    grad_feed_in,
    grad_shrink,
    grad_expand,
    grad_bias,
    feed_all,
    grad_all,
    hidden_all,
    pre_all,
    slope_all,
    feed_parts,
    grad_parts,
    shrink_low,
    *scratch,
):
    feed_sends, feed_recvs, grad_sends, grad_recvs = scratch[0:4]
    feed_scatter = Scatter(feed_parts, *scratch[4:11], ROW, ROW // 2)
    grad_scatter = Scatter(grad_parts, *scratch[11:18], ROW, ROW // 2)
    place, layer, twin, across, along, corner = plane_places()
    feed_gather = Gather(feed_all.at[place], feed_all, feed_sends, feed_recvs, ROW, ROW // 2)
    grad_gather = Gather(grad_all.at[place], grad_all, grad_sends, grad_recvs, ROW, ROW // 2)
    feed_all[place] = feed_own[...]
    grad_all[place] = grad_own[...]
    shrink_low[...] = shrink[...].astype(low_type)
    greet([(twin, layer), (across, layer), (along, layer)])
    feed_gather.start_links()
    feed_gather.start_twin()
    grad_gather.start_twin()

    def ahead(slot):
        pre = contract(feed_all[slot], expand[...], 1, 0) + bias[...]
        tanh_part = jnp.tanh(tanh_scale * (pre + cubic_term * pre * pre * pre))
        hidden = (0.5 * pre * (1.0 + tanh_part)).astype(low_type)
        slope_all[slot] = 0.5 * (1.0 + tanh_part) + 0.5 * pre * (1.0 - tanh_part * tanh_part) * tanh_scale * (
            1.0 + 3.0 * cubic_term * pre * pre
        )
        hidden_all[slot] = hidden
        feed_parts[slot] = contract(hidden, shrink_low[...], 1, 0).astype(low_type)

    def back(slot):
        grad_hidden = contract(grad_all[slot], shrink_low[...], 1, 1)
        grad_pre = (grad_hidden * slope_all[slot]).astype(low_type)
        pre_all[slot] = grad_pre
        grad_parts[slot] = contract(grad_pre, expand[...], 1, 1).astype(low_type)

    ahead(place)
    feed_gather.arrived(2)
    ahead(twin)
    feed_gather.forward_near()
    grad_gather.start_links()
    ahead(across)
    ahead(along)
    feed_gather.forward_far()
    feed_gather.arrived(5, 6)
    ahead(twin_of(across))
    ahead(twin_of(along))
    ahead(corner)
    feed_gather.arrived(7, 8)
    ahead(twin_of(corner))
    feed_scatter.start_twin()
    back(place)
    grad_gather.arrived(2)
    back(twin)
    grad_gather.forward_near()
    back(across)
    back(along)
    grad_gather.forward_far()
    grad_gather.arrived(5, 6)
    back(twin_of(across))
    back(twin_of(along))
    back(corner)
    grad_gather.arrived(7, 8)
    back(twin_of(corner))
    grad_scatter.start_twin()
    grad_scatter.start_links()
    feed_scatter.start_links()

    units = hidden_all.shape[2]
    hidden = hidden_all[...].reshape(GROUP * ROW, units)
    grad_shrink[...] = contract(hidden, grad_all[...].reshape(GROUP * ROW, D), 0, 0).astype(low_type)
    grad_scatter.forward()
    grad_pre = pre_all[...].reshape(GROUP * ROW, units)
    grad_bias[...] = jnp.sum(grad_pre.astype(full_type), axis=0, keepdims=True)
    grad_expand[...] = contract(feed_all[...].reshape(GROUP * ROW, D), grad_pre, 0, 0).astype(low_type)
    grad_feed_in[...] = grad_scatter.finish()
    feed_scatter.forward()
    feed_out[...] = feed_scatter.finish()
    feed_gather.finish_sends()
    grad_gather.finish_sends()


def feed_call(feed_own, grad_own, expand, shrink, bias):
    units = expand.shape[1]
    shape = jax.ShapeDtypeStruct
    dma = pltpu.SemaphoreType.DMA
    return pl.pallas_call(
        feed_kernel,
        out_shape=(
            shape((ROW, D), full_type),
            shape((ROW, D), full_type),
            shape((units, D), low_type),
            shape((D, units), low_type),
            shape((1, units), full_type),
        ),
        in_specs=[vmem()] * 5,
        out_specs=(vmem(),) * 5,
        scratch_shapes=[
            pltpu.VMEM((GROUP, ROW, D), low_type),
            pltpu.VMEM((GROUP, ROW, D), low_type),
            pltpu.VMEM((GROUP, ROW, units), low_type),
            pltpu.VMEM((GROUP, ROW, units), low_type),
            pltpu.VMEM((GROUP, ROW, units), full_type),
            pltpu.VMEM((GROUP, ROW, D), low_type),
            pltpu.VMEM((GROUP, ROW, D), low_type),
            pltpu.VMEM((units, D), low_type),
            dma((9,)),
            dma((9,)),
            dma((9,)),
            dma((9,)),
            *scatter_scratch(ROW, ROW // 2, D),
            *scatter_scratch(ROW, ROW // 2, D),
        ],
        compiler_params=pltpu.CompilerParams(
            collective_id=1, has_side_effects=True, vmem_limit_bytes=VMEM_BYTES
        ),
        name="feed_forward",
    )(feed_own, grad_own, expand, shrink, bias)

def sample_compactor():
    row, column = iota((16, 32), 0), iota((16, 32), 1)
    return (column == (row >> 2) * 8 + (row & 3)).astype(full_type).astype(low_type)


def sample_scatterer():
    row, column = iota((256, 128), 0), iota((256, 128), 1)
    wanted = ((row >> 3) & 7) * 16 + (row >> 6) * 4 + (row & 7)
    return jnp.where(((row & 7) < 4) & (column == wanted), 1.0, 0.0).astype(low_type)


def square_sum(values):
    values = values.astype(full_type)
    squares = values * values
    while squares.ndim > 2:
        squares = jnp.sum(squares, axis=0)
    return jnp.sum(jnp.sum(squares, axis=0, keepdims=True), axis=1, keepdims=True)


def finish_kernel(
    project_parts,
    output_parts,
    expand_parts,
    shrink_part,
    bias_parts,
    samples,
    active,
    modulate,
    project_sum,
    output_sum,
    expand_sum,
    shrink_sum,
    bias_sum,
    modulate_sum,
    condition_sum,
    square_total,
    project_own,
    output_own,
    expand_own,
    project_mid,
    output_mid,
    expand_mid,
    shrink_mid,
    bias_recv,
    bias_all,
    sample_recv,
    group_all,
    term_send,
    term_recv,
    term_sum,
    square_send,
    square_recv,
    square_part,
    square_all,
    small_sends,
    small_recvs,
    pair_sends,
    pair_recvs,
    mid_sends,
    mid_recvs,
    local_sem,
    *scratch,
):
    place, layer, *_ = plane_places()
    plane = [lax.rem(place + step, GROUP) for step in range(1, GROUP)]
    column = [lax.rem(layer + step, DEPTH) for step in range(1, DEPTH)]
    rows = project_own.shape[0]
    pair = layer + 1 - 2 * lax.rem(layer, 2)
    across_middle = DEPTH - 1 - layer
    edge = (layer == 0) | (layer == DEPTH - 1)
    middle = jnp.logical_not(edge)

    chunks = []
    for step in range(4):
        part = pl.ds(step * rows, rows)
        chunks.append((shrink_part.at[part], shrink_sum.at[part], shrink_mid.at[part]))
    for step in range(4):
        part = pl.ds(2 * step, 2)
        chunks.append((expand_own.at[part], expand_sum.at[part], expand_mid.at[part]))
    chunks.append((output_own, output_sum, output_mid))
    for step in range(3):
        part = (slice(None), pl.ds(step * D, D))
        chunks.append((project_own.at[part], project_sum.at[part], project_mid.at[part]))

    def pair_copy(index):
        given, result, _ = chunks[index]
        return lambda source: pltpu.make_async_remote_copy(
            src_ref=source,
            dst_ref=result,
            send_sem=pair_sends.at[index],
            recv_sem=pair_recvs.at[index],
            device_id=(place, pair),
            device_id_type=MESH,
        )

    def middle_copy(index):
        given, _, other = chunks[index]
        return pltpu.make_async_remote_copy(
            src_ref=given,
            dst_ref=other,
            send_sem=mid_sends.at[index],
            recv_sem=mid_recvs.at[index],
            device_id=(place, across_middle),
            device_id_type=MESH,
        )

    def edge_send(indices):
        @pl.when(edge)
        def _():
            for index in indices:
                pair_copy(index)(chunks[index][0]).start()

    def middle_step(index):
        @pl.when(middle)
        def _():
            if index < len(chunks):
                given, result, _ = chunks[index]
                pair_copy(index)(result).wait_recv()
                given[...] = (given[...].astype(full_type) + result[...].astype(full_type)).astype(low_type)
                middle_copy(index).start()
            if index > 0:
                given, result, other = chunks[index - 1]
                middle_copy(index - 1).wait()
                result[...] = (given[...].astype(full_type) + other[...].astype(full_type)).astype(low_type)
                pair_copy(index - 1)(result).start()

    greet([(peer, layer) for peer in plane] + [(place, peer) for peer in column])

    waits = []

    def exchange(base, peers, source, target):
        copies = []
        for step, peer in enumerate(peers):
            where = (peer, layer) if peers is plane else (place, peer)
            copies.append(
                send(source(peer), target, small_sends.at[base + step], small_recvs.at[base + step], *where)
            )
        waits.extend(copies)
        return copies

    def arrive(copies):
        for copy in copies:
            copy.wait_recv()

    edge_send(range(0, 4))
    sample_copies = exchange(0, column, lambda peer: samples.at[peer], sample_recv.at[layer])
    project_scatter = Scatter(project_parts, *scratch[0:7], rows, 80)
    output_scatter = Scatter(output_parts, *scratch[7:14], rows, 64)
    project_scatter.start_twin()
    output_scatter.start_twin()
    bias_copies = exchange(3, plane, lambda peer: bias_parts.at[peer], bias_recv.at[place])
    expand_copies = exchange(10, plane, lambda peer: expand_parts.at[peer], expand_own.at[place])
    own_copy = pltpu.make_async_copy(expand_parts.at[place], expand_own.at[place], local_sem)
    own_copy.start()
    bias_recv[place] = bias_parts[place]
    sample_recv[layer] = samples[layer]

    arrive(sample_copies)
    group = contract(sample_compactor(), sample_recv[...].reshape(4 * 8, samples.shape[2]).astype(low_type), 1, 0)
    group_all[place] = group.astype(low_type)
    group_copies = exchange(17, plane, lambda peer: group_all.at[place], group_all.at[place])
    project_scatter.start_links()
    output_scatter.start_links()
    middle_step(0)
    arrive(bias_copies)
    total = bias_recv[0]
    for step in range(1, GROUP):
        total = total + bias_recv[step]
    bias_all[layer] = total
    bias_copies = exchange(24, column, lambda peer: bias_all.at[layer], bias_all.at[layer])

    arrive(group_copies)
    every = group_all[...].reshape(GROUP * 16, samples.shape[2])
    grad_modulate = contract(active[...], every, 0, 0)
    modulate_sum[...] = grad_modulate
    spread = contract(sample_scatterer(), every, 1, 0).astype(low_type)
    terms = contract(spread, modulate[...].astype(low_type), 1, 1)
    term_send[...] = terms.reshape(term_send.shape)
    term_copies = exchange(27, column, lambda peer: term_send.at[peer], term_recv.at[layer])
    term_recv[layer] = term_send[layer]
    middle_step(1)
    arrive(term_copies)
    term_sum[...] = (term_recv[0] + term_recv[1]) + (term_recv[2] + term_recv[3])
    last_copies = exchange(30, plane, lambda peer: term_sum.at[peer], condition_sum.at[place])
    condition_sum[place] = term_sum[place]
    arrive(bias_copies)
    bias_total = (bias_all[0] + bias_all[1]) + (bias_all[2] + bias_all[3])
    bias_sum[...] = bias_total
    middle_step(2)
    project_scatter.forward()
    output_scatter.forward()
    middle_step(3)
    arrive(expand_copies)
    own_copy.wait()
    edge_send(range(4, 8))
    middle_step(4)
    middle_step(5)
    output_own[...] = output_scatter.finish().astype(low_type)
    edge_send(range(8, 9))
    middle_step(6)
    project_own[...] = project_scatter.finish().astype(low_type)
    edge_send(range(9, 12))
    for step in range(7, 13):
        middle_step(step)

    @pl.when(edge)
    def _():
        for index in range(len(chunks)):
            pair_copy(index)(chunks[index][0]).wait()

    @pl.when(middle)
    def _():
        for index in range(len(chunks)):
            pair_copy(index)(chunks[index][1]).wait_send()

    trunk = (
        square_sum(project_sum[...])
        + square_sum(output_sum[...])
        + square_sum(expand_sum[...])
        + square_sum(shrink_sum[...])
        + square_sum(bias_sum[...])
    )
    square_send[0] = jnp.broadcast_to(trunk, (8, 128))
    square_send[1] = jnp.broadcast_to(square_sum(modulate_sum[...]), (8, 128))
    square_copies = exchange(37, plane, lambda peer: square_send, square_recv.at[place])
    square_recv[place] = square_send[...]
    arrive(square_copies)
    both = square_recv[0]
    for step in range(1, GROUP):
        both = both + square_recv[step]
    square_part[...] = both
    square_all[layer] = both
    square_copies = exchange(44, column, lambda peer: square_part, square_all.at[layer])
    arrive(square_copies)
    square_total[...] = both[0] + (square_all[0, 1] + square_all[1, 1] + (square_all[2, 1] + square_all[3, 1]))
    arrive(last_copies)
    for copy in waits:
        copy.wait_send()


def reduce_all(
    grad_project, grad_output, grad_expand, grad_shrink, bias_grads, sample_grads, active, modulate_weight
):
    rows, columns = modulate_weight.shape
    units = grad_expand.shape[1]
    shard = bias_grads.shape[0] // GROUP
    shape = jax.ShapeDtypeStruct
    dma = pltpu.SemaphoreType.DMA
    samples = sample_grads.astype(full_type).reshape(8, DEPTH, columns).transpose(1, 0, 2)
    sums = pl.pallas_call(
        finish_kernel,
        out_shape=(
            shape((rows, 3 * D), low_type),
            shape((rows, D), low_type),
            shape((GROUP, rows, units), low_type),
            shape((units, D), low_type),
            shape((1, shard), full_type),
            shape((rows, columns), full_type),
            shape((GROUP, 8, rows), full_type),
            shape((8, 128), full_type),
        ),
        in_specs=[vmem()] * 8,
        out_specs=(vmem(),) * 8,
        scratch_shapes=[
            pltpu.VMEM((rows, 3 * D), low_type),
            pltpu.VMEM((rows, D), low_type),
            pltpu.VMEM((GROUP, rows, units), low_type),
            pltpu.VMEM((rows, 3 * D), low_type),
            pltpu.VMEM((rows, D), low_type),
            pltpu.VMEM((GROUP, rows, units), low_type),
            pltpu.VMEM((units, D), low_type),
            pltpu.VMEM((GROUP, 1, shard), full_type),
            pltpu.VMEM((DEPTH, 1, shard), full_type),
            pltpu.VMEM((DEPTH, 8, columns), full_type),
            pltpu.VMEM((GROUP, 16, columns), low_type),
            pltpu.VMEM((DEPTH, GROUP, 8, rows), full_type),
            pltpu.VMEM((DEPTH, GROUP, 8, rows), full_type),
            pltpu.VMEM((GROUP, 8, rows), full_type),
            pltpu.VMEM((2, 8, 128), full_type),
            pltpu.VMEM((GROUP, 2, 8, 128), full_type),
            pltpu.VMEM((2, 8, 128), full_type),
            pltpu.VMEM((DEPTH, 2, 8, 128), full_type),
            dma((47,)),
            dma((47,)),
            dma((12,)),
            dma((12,)),
            dma((12,)),
            dma((12,)),
            dma,
            *scatter_scratch(rows, 80, 3 * D),
            *scatter_scratch(rows, 64, D),
        ],
        compiler_params=pltpu.CompilerParams(
            collective_id=2, has_side_effects=True, vmem_limit_bytes=VMEM_BYTES
        ),
        name="reduce_finish",
    )(
        grad_project.reshape(GROUP, rows, 3 * D),
        grad_output.reshape(GROUP, rows, D),
        grad_expand.reshape(GROUP, rows, units),
        grad_shrink,
        bias_grads.reshape(GROUP, 1, shard),
        samples,
        active,
        modulate_weight,
    )
    sum_expand = sums[2].transpose(1, 0, 2).reshape(rows, GROUP * units)
    conditions = sums[6][:, 0:IMG_ROW].transpose(1, 0, 2).reshape(IMG_ROW, D)
    return (
        sums[0].astype(full_type),
        sums[1].astype(full_type),
        sum_expand.astype(full_type),
        sums[3].astype(full_type),
        sums[5],
        sums[4][0],
        conditions,
        sums[7][0, 0],
    )


def per_slot(onehot, rows):
    return contract(onehot, rows, 1, 0)


def plane_body(
    tokens,
    conditions,
    image_lengths,
    cotangent,
    project_weight,
    project_moment,
    project_square,
    output_weight,
    output_moment,
    output_square,
    expand_weight,
    expand_moment,
    expand_square,
    shrink_weight,
    shrink_moment,
    shrink_square,
    modulate_weight,
    modulate_moment,
    modulate_square,
    bias_vector,
    bias_moment,
    bias_square,
):
    place = lax.axis_index("dp")
    layer = lax.axis_index("mod")
    shard = bias_vector.shape[0]
    columns = modulate_weight.shape[1]
    units = FF // GROUP
    mod_base = 4 * D + FF
    span = 10 * D + FF
    blank = jnp.zeros((span,), jnp.float32)
    around = jnp.concatenate([blank, bias_vector, blank])
    bias_piece = lax.dynamic_slice_in_dim(
        around, span + mod_base + layer * columns - place * shard, columns
    )[None, :]
    blocks = start_call(
        conditions, project_weight, output_weight, expand_weight, modulate_weight, bias_piece, bias_vector[None, :]
    )
    full_project = blocks[0].reshape(D, 3 * D)
    full_output = blocks[1].reshape(D, D)
    own_expand = blocks[2].reshape(D, units)
    own_mod = blocks[3].transpose(1, 0, 2).reshape(8, 6 * D)
    active = blocks[4]
    bias_full = blocks[5].reshape(span)
    bias_query = bias_full[0:D]
    bias_value = bias_full[D : 2 * D]
    bias_output = bias_full[2 * D : 3 * D]
    bias_expand = lax.dynamic_slice_in_dim(bias_full, 3 * D + place * units, units)[None, :]
    bias_shrink = bias_full[3 * D + FF : 4 * D + FF]

    slots = jnp.arange(IMG_ROW, dtype=jnp.int32)
    ends = jnp.sum(
        jnp.where(slots[:, None] <= slots[None, :], image_lengths[0][:, None], 0), axis=0, dtype=jnp.int32
    )
    positions = jnp.arange(ROW, dtype=jnp.int32)
    slot_of = jnp.sum(
        (positions[:, None] >= ends[None, :]).astype(jnp.int32), axis=1, dtype=jnp.int32
    )
    slot_match = (slot_of[:, None] == jnp.arange(8, dtype=jnp.int32)[None, :]) & (slot_of[:, None] < IMG_ROW)
    onehot = slot_match.astype(low_type)
    slot_row, slot_column = slot_of[None, :], slot_of[:, None]
    per_token = contract(onehot, own_mod.astype(low_type), 1, 0)
    shift_attend = per_token[:, 0:D]
    scale_attend = per_token[:, D : 2 * D]
    gate_attend = per_token[:, 2 * D : 3 * D]
    shift_feed = per_token[:, 3 * D : 4 * D]
    scale_feed = per_token[:, 4 * D : 5 * D]
    gate_feed = per_token[:, 5 * D : 6 * D]
    inputs = tokens.astype(jnp.float32)
    normed_attend, inverse_attend = normalize_rows(inputs)
    attend_in = (normed_attend * (1.0 + scale_attend) + shift_attend).astype(low_type)
    shift = jnp.concatenate([bias_query, jnp.zeros((D,), jnp.float32), bias_value])
    packed = (contract(attend_in, full_project, 1, 0) + shift).astype(low_type)
    mixed = attend_forward(packed, slot_row, slot_column)
    attend_out = contract(mixed, full_output, 1, 0) + bias_output
    resid = inputs + gate_attend * attend_out
    normed_feed, inverse_feed = normalize_rows(resid)
    feed_in = (normed_feed * (1.0 + scale_feed) + shift_feed).astype(low_type)
    grad_out = cotangent.astype(jnp.float32)
    grad_feed = (gate_feed * grad_out).astype(low_type)
    feed_sum, grad_feed_in, grad_shrink, grad_expand, grad_bias_expand = feed_call(
        feed_in, grad_feed, own_expand, shrink_weight, bias_expand
    )
    feed_out = feed_sum + bias_shrink
    block_output = (resid + gate_feed * feed_out).astype(low_type)
    grad_gate_feed = grad_out * feed_out
    grad_scale_feed = grad_feed_in * normed_feed
    grad_resid = grad_out + normalize_back(
        grad_feed_in * (1.0 + scale_feed), normed_feed, inverse_feed
    )
    grad_gate_attend = grad_resid * attend_out
    grad_attend = (gate_attend * grad_resid).astype(low_type)
    grad_output = contract(mixed, grad_attend, 0, 0).astype(low_type)
    grad_mixed = contract(grad_attend, full_output, 1, 1).astype(low_type)
    grad_packed = attend_backward(packed, grad_mixed, slot_row, slot_column)
    grad_project = contract(attend_in, grad_packed, 0, 0).astype(low_type)
    grad_attend_in = contract(grad_packed, full_project, 1, 1)
    grad_scale_attend = grad_attend_in * normed_attend
    token_grads = grad_resid + normalize_back(
        grad_attend_in * (1.0 + scale_attend), normed_attend, inverse_attend
    )
    token_mod_grads = jnp.concatenate(
        [
            grad_attend_in,
            grad_scale_attend,
            grad_gate_attend,
            grad_feed_in,
            grad_scale_feed,
            grad_gate_feed,
        ],
        axis=1,
    )
    sample_grads = contract(slot_match.astype(jnp.float32), token_mod_grads, 0, 0).astype(low_type)
    bias_grads = jnp.concatenate(
        [
            jnp.sum(grad_packed[:, 0:D], axis=0, dtype=jnp.float32),
            jnp.sum(grad_packed[:, 2 * D : 3 * D], axis=0, dtype=jnp.float32),
            jnp.sum(grad_attend, axis=0, dtype=jnp.float32),
            lax.dynamic_update_slice_in_dim(
                jnp.zeros((FF,), jnp.float32), grad_bias_expand[0], place * units, 0
            ),
            jnp.sum(grad_feed, axis=0, dtype=jnp.float32),
            jnp.sum(sample_grads, axis=0, dtype=jnp.float32),
        ],
        axis=0,
    )
    (
        sum_project,
        sum_output,
        sum_expand,
        sum_shrink,
        sum_modulate,
        sum_bias,
        condition_sum,
        square_total,
    ) = reduce_all(
        grad_project, grad_output, grad_expand, grad_shrink, bias_grads, sample_grads, active, modulate_weight
    )
    own_conditions = conditions.astype(jnp.float32)
    sigmoid_part = jax.nn.sigmoid(own_conditions)
    condition_grads = condition_sum * (sigmoid_part * (1.0 + own_conditions * (1.0 - sigmoid_part)))
    global_norm = jnp.sqrt(square_total)
    clip_factor = jnp.minimum(1.0, 1.0 / (global_norm + 1e-06))
    updated = (
        *adam_update(project_weight, project_moment, project_square, sum_project * clip_factor, D ** (-0.5)),
        *adam_update(output_weight, output_moment, output_square, sum_output * clip_factor, (D // 64) ** (-0.5)),
        *adam_update(expand_weight, expand_moment, expand_square, sum_expand * clip_factor, D ** (-0.5)),
        *adam_update(shrink_weight, shrink_moment, shrink_square, sum_shrink * clip_factor, FF ** (-0.5)),
        *adam_update(modulate_weight, modulate_moment, modulate_square, sum_modulate * clip_factor, D ** (-0.5)),
        *adam_update(bias_vector, bias_moment, bias_square, sum_bias * clip_factor, 0.3),
    )
    return (block_output, token_grads, condition_grads, global_norm, *updated)


def generic_body(
    tokens,
    conditions,
    image_lengths,
    cotangent,
    project_weight,
    project_moment,
    project_square,
    output_weight,
    output_moment,
    output_square,
    expand_weight,
    expand_moment,
    expand_square,
    shrink_weight,
    shrink_moment,
    shrink_square,
    modulate_weight,
    modulate_moment,
    modulate_square,
    bias_vector,
    bias_moment,
    bias_square,
):
    low_type = jnp.bfloat16
    group_size = lax.axis_size("mod")
    group_place = lax.axis_index("mod")
    columns = 6 * D // group_size
    full_project, full_output, full_expand, full_shrink, full_modulate, full_bias = (
        lax.all_gather(project_weight.astype(low_type), "dp", axis=0, tiled=True),
        lax.all_gather(output_weight.astype(low_type), "dp", axis=0, tiled=True),
        lax.all_gather(expand_weight.astype(low_type), "dp", axis=0, tiled=True),
        lax.all_gather(shrink_weight.astype(low_type), "dp", axis=0, tiled=True),
        lax.all_gather(modulate_weight.astype(low_type), "dp", axis=0, tiled=True),
        lax.all_gather(bias_vector.astype(low_type), "dp", axis=0, tiled=True),
    )
    bias_full = full_bias.astype(jnp.float32)
    bias_query = bias_full[0:D]
    bias_value = bias_full[D : 2 * D]
    bias_output = bias_full[2 * D : 3 * D]
    bias_expand = bias_full[3 * D : 3 * D + FF]
    bias_shrink = bias_full[3 * D + FF : 4 * D + FF]
    bias_modulate = lax.dynamic_slice_in_dim(bias_full, 4 * D + FF + group_place * columns, columns)
    group_conditions = lax.all_gather(conditions, "mod", axis=0, tiled=True)
    activated = jax.nn.silu(group_conditions.astype(jnp.float32)).astype(low_type)
    group_mod = (contract(activated, full_modulate, 1, 0) + bias_modulate).astype(low_type)
    own_mod = lax.all_to_all(group_mod, "mod", split_axis=0, concat_axis=1, tiled=True)
    slots = jnp.arange(IMG_ROW, dtype=jnp.int32)
    ends = jnp.sum(
        jnp.where(slots[:, None] <= slots[None, :], image_lengths[0][:, None], 0), axis=0, dtype=jnp.int32
    )
    positions = jnp.arange(ROW, dtype=jnp.int32)
    slot_of = jnp.sum(
        (positions[:, None] >= ends[None, :]).astype(jnp.int32), axis=1, dtype=jnp.int32
    )
    slot_match = slot_of[:, None] == jnp.arange(IMG_ROW, dtype=jnp.int32)[None, :]
    same_image = slot_of[:, None] == slot_of[None, :]
    per_token = contract(slot_match.astype(low_type), own_mod, 1, 0)
    shift_attend = per_token[:, 0:D]
    scale_attend = per_token[:, D : 2 * D]
    gate_attend = per_token[:, 2 * D : 3 * D]
    shift_feed = per_token[:, 3 * D : 4 * D]
    scale_feed = per_token[:, 4 * D : 5 * D]
    gate_feed = per_token[:, 5 * D : 6 * D]
    inputs = tokens.astype(jnp.float32)
    normed_attend, inverse_attend = normalize_rows(inputs)
    attend_in = (normed_attend * (1.0 + scale_attend) + shift_attend).astype(low_type)
    projected = contract(attend_in, full_project, 1, 0)
    query = (projected[:, 0:D] + bias_query).astype(low_type)
    keys = projected[:, D : 2 * D].astype(low_type)
    values = (projected[:, 2 * D : 3 * D] + bias_value).astype(low_type)
    head_scale = HEAD_DIM ** (-0.5)

    def split_heads(matrix):
        return matrix.reshape(ROW, HEADS, HEAD_DIM).transpose(1, 0, 2)

    def head_scores(query_head, key_head):
        return jnp.where(same_image, contract(query_head, key_head, 1, 1) * head_scale, -1e30)

    def attend_head(pieces):
        query_head, key_head, value_head = pieces
        scores = head_scores(query_head, key_head)
        row_top = jnp.max(scores, axis=1, keepdims=True)
        exponent = jnp.exp(scores - row_top)
        total = jnp.sum(exponent, axis=1, keepdims=True)
        probs = (exponent / total).astype(low_type)
        return (contract(probs, value_head, 1, 0), (row_top + jnp.log(total))[:, 0])

    heads_query = split_heads(query)
    heads_key = split_heads(keys)
    heads_value = split_heads(values)
    mixed_heads, log_totals = lax.map(attend_head, (heads_query, heads_key, heads_value))
    mixed = merge_heads(mixed_heads).astype(low_type)
    attend_out = contract(mixed, full_output, 1, 0) + bias_output
    resid = inputs + gate_attend * attend_out
    normed_feed, inverse_feed = normalize_rows(resid)
    feed_in = (normed_feed * (1.0 + scale_feed) + shift_feed).astype(low_type)
    hidden_pre = contract(feed_in, full_expand, 1, 0) + bias_expand
    tanh_part = jnp.tanh(
        tanh_scale * (hidden_pre + cubic_term * hidden_pre * hidden_pre * hidden_pre)
    )
    hidden = (0.5 * hidden_pre * (1.0 + tanh_part)).astype(low_type)
    feed_out = contract(hidden, full_shrink, 1, 0) + bias_shrink
    block_output = (resid + gate_feed * feed_out).astype(low_type)
    grad_out = cotangent.astype(jnp.float32)
    grad_gate_feed = grad_out * feed_out
    grad_feed = (gate_feed * grad_out).astype(low_type)
    grad_shrink = contract(hidden, grad_feed, 0, 0)
    grad_hidden = contract(grad_feed, full_shrink, 1, 1)
    slope = 0.5 * (1.0 + tanh_part) + 0.5 * hidden_pre * (
        1.0 - tanh_part * tanh_part
    ) * tanh_scale * (1.0 + 3.0 * cubic_term * hidden_pre * hidden_pre)
    grad_pre = (grad_hidden * slope).astype(low_type)
    grad_expand = contract(feed_in, grad_pre, 0, 0)
    grad_feed_in = contract(grad_pre, full_expand, 1, 1)
    grad_scale_feed = grad_feed_in * normed_feed
    grad_resid = grad_out + normalize_back(
        grad_feed_in * (1.0 + scale_feed), normed_feed, inverse_feed
    )
    grad_gate_attend = grad_resid * attend_out
    grad_attend = (gate_attend * grad_resid).astype(low_type)
    grad_output = contract(mixed, grad_attend, 0, 0)
    grad_mixed = contract(grad_attend, full_output, 1, 1).astype(low_type)

    def attend_back(pieces):
        query_head, key_head, value_head, grad_head, log_total = pieces
        probs = jnp.exp(head_scores(query_head, key_head) - log_total[:, None])
        grad_value = contract(probs.astype(low_type), grad_head, 0, 0)
        grad_probs = contract(grad_head, value_head, 1, 1)
        grad_scores = (
            probs * (grad_probs - jnp.sum(probs * grad_probs, axis=1, keepdims=True))
        ).astype(low_type)
        grad_query = contract(grad_scores, key_head, 1, 0) * head_scale
        grad_key = contract(grad_scores, query_head, 0, 0) * head_scale
        return (grad_query, grad_key, grad_value)

    heads_grad_query, heads_grad_key, heads_grad_value = lax.map(
        attend_back, (heads_query, heads_key, heads_value, split_heads(grad_mixed), log_totals)
    )
    grad_projected = jnp.concatenate(
        [merge_heads(heads_grad_query), merge_heads(heads_grad_key), merge_heads(heads_grad_value)],
        axis=1,
    ).astype(low_type)
    grad_project = contract(attend_in, grad_projected, 0, 0)
    grad_attend_in = contract(grad_projected, full_project, 1, 1)
    grad_scale_attend = grad_attend_in * normed_attend
    token_grads = grad_resid + normalize_back(
        grad_attend_in * (1.0 + scale_attend), normed_attend, inverse_attend
    )
    token_mod_grads = jnp.concatenate(
        [
            grad_attend_in,
            grad_scale_attend,
            grad_gate_attend,
            grad_feed_in,
            grad_scale_feed,
            grad_gate_feed,
        ],
        axis=1,
    )
    sample_grads = contract(slot_match.astype(jnp.float32), token_mod_grads, 0, 0).astype(low_type)
    group_grads = lax.all_to_all(sample_grads, "mod", split_axis=1, concat_axis=0, tiled=True)
    grad_modulate = contract(activated, group_grads, 0, 0)
    grad_bias_modulate = jnp.sum(group_grads, axis=0, dtype=jnp.float32)
    condition_terms = contract(group_grads, full_modulate, 1, 1)
    condition_sum = lax.psum_scatter(
        condition_terms.astype(jnp.bfloat16), "mod", scatter_dimension=0, tiled=True
    ).astype(jnp.float32)
    own_conditions = conditions.astype(jnp.float32)
    sigmoid_part = jax.nn.sigmoid(own_conditions)
    condition_grads = condition_sum * (sigmoid_part * (1.0 + own_conditions * (1.0 - sigmoid_part)))
    modulate_bias_grad = lax.dynamic_update_slice_in_dim(
        jnp.zeros((6 * D,), jnp.float32), grad_bias_modulate, group_place * columns, 0
    )
    grad_bias = jnp.concatenate(
        [
            jnp.sum(grad_projected[:, 0:D], axis=0, dtype=jnp.float32),
            jnp.sum(grad_projected[:, 2 * D : 3 * D], axis=0, dtype=jnp.float32),
            jnp.sum(grad_attend, axis=0, dtype=jnp.float32),
            jnp.sum(grad_pre, axis=0, dtype=jnp.float32),
            jnp.sum(grad_feed, axis=0, dtype=jnp.float32),
            modulate_bias_grad,
        ],
        axis=0,
    )
    summed = (
        lax.psum_scatter(
            grad_project.astype(jnp.bfloat16), "dp", scatter_dimension=0, tiled=True
        ).astype(jnp.float32),
        lax.psum_scatter(
            grad_output.astype(jnp.bfloat16), "dp", scatter_dimension=0, tiled=True
        ).astype(jnp.float32),
        lax.psum_scatter(
            grad_expand.astype(jnp.bfloat16), "dp", scatter_dimension=0, tiled=True
        ).astype(jnp.float32),
        lax.psum_scatter(
            grad_shrink.astype(jnp.bfloat16), "dp", scatter_dimension=0, tiled=True
        ).astype(jnp.float32),
        lax.psum_scatter(
            grad_modulate.astype(jnp.bfloat16), "dp", scatter_dimension=0, tiled=True
        ).astype(jnp.float32),
        lax.psum_scatter(
            grad_bias.astype(jnp.bfloat16), "dp", scatter_dimension=0, tiled=True
        ).astype(jnp.float32),
    )
    sum_project, sum_output, sum_expand, sum_shrink, sum_bias = (
        lax.psum(summed[0].astype(jnp.bfloat16), "mod").astype(jnp.float32),
        lax.psum(summed[1].astype(jnp.bfloat16), "mod").astype(jnp.float32),
        lax.psum(summed[2].astype(jnp.bfloat16), "mod").astype(jnp.float32),
        lax.psum(summed[3].astype(jnp.bfloat16), "mod").astype(jnp.float32),
        lax.psum(summed[5].astype(jnp.bfloat16), "mod").astype(jnp.float32),
    )
    sum_modulate = summed[4]
    trunk_square = (
        jnp.sum(sum_project * sum_project)
        + jnp.sum(sum_output * sum_output)
        + jnp.sum(sum_expand * sum_expand)
        + jnp.sum(sum_shrink * sum_shrink)
        + jnp.sum(sum_bias * sum_bias)
    )
    totals = lax.psum((trunk_square, jnp.sum(sum_modulate * sum_modulate)), ("dp", "mod"))
    global_norm = jnp.sqrt(totals[0] / group_size + totals[1])
    clip_factor = jnp.minimum(1.0, 1.0 / (global_norm + 1e-06))
    next_project, first_project, second_project = adam_update(
        project_weight, project_moment, project_square, sum_project * clip_factor, D ** (-0.5)
    )
    next_output, first_output, second_output = adam_update(
        output_weight, output_moment, output_square, sum_output * clip_factor, (D // 64) ** (-0.5)
    )
    next_expand, first_expand, second_expand = adam_update(
        expand_weight, expand_moment, expand_square, sum_expand * clip_factor, D ** (-0.5)
    )
    next_shrink, first_shrink, second_shrink = adam_update(
        shrink_weight, shrink_moment, shrink_square, sum_shrink * clip_factor, FF ** (-0.5)
    )
    next_modulate, first_modulate, second_modulate = adam_update(
        modulate_weight, modulate_moment, modulate_square, sum_modulate * clip_factor, D ** (-0.5)
    )
    next_biases, first_biases, second_biases = adam_update(
        bias_vector, bias_moment, bias_square, sum_bias * clip_factor, 0.3
    )
    return (
        block_output,
        token_grads,
        condition_grads,
        global_norm,
        next_project,
        first_project,
        second_project,
        next_output,
        first_output,
        second_output,
        next_expand,
        first_expand,
        second_expand,
        next_shrink,
        first_shrink,
        second_shrink,
        next_modulate,
        first_modulate,
        second_modulate,
        next_biases,
        first_biases,
        second_biases,
    )


def solution(mesh):
    return jax.shard_map(
        plane_body if mesh.shape["dp"] == GROUP and mesh.shape["mod"] == DEPTH else generic_body,
        mesh=mesh,
        in_specs=(
            P(("dp", "mod"), None),
            P(("dp", "mod"), None),
            P(("dp", "mod"), None),
            P(("dp", "mod"), None),
            P("dp", None),
            P("dp", None),
            P("dp", None),
            P("dp", None),
            P("dp", None),
            P("dp", None),
            P("dp", None),
            P("dp", None),
            P("dp", None),
            P("dp", None),
            P("dp", None),
            P("dp", None),
            P("dp", "mod"),
            P("dp", "mod"),
            P("dp", "mod"),
            P("dp"),
            P("dp"),
            P("dp"),
        ),
        out_specs=(
            P(("dp", "mod"), None),
            P(("dp", "mod"), None),
            P(("dp", "mod"), None),
            P(),
            P("dp", None),
            P("dp", None),
            P("dp", None),
            P("dp", None),
            P("dp", None),
            P("dp", None),
            P("dp", None),
            P("dp", None),
            P("dp", None),
            P("dp", None),
            P("dp", None),
            P("dp", None),
            P("dp", "mod"),
            P("dp", "mod"),
            P("dp", "mod"),
            P("dp"),
            P("dp"),
            P("dp"),
        ),
        check_vma=False,
    )
```

```python
import functools

import jax
import jax.numpy as jnp
from jax import lax
from jax.experimental import pallas as pl
from jax.experimental.pallas import tpu as pltpu
from jax.sharding import PartitionSpec as P

D = 1152
HEADS = 16
HEAD_DIM = 72
FF = 4608
ROW = 256
STEP = 10
IMG_ROW = 4


beta_first = 0.9
beta_second = 0.999
weight_decay = 0.01
adam_epsilon = 1e-08
tanh_scale = 0.7978845608028654
cubic_term = 0.044715


def contract(left, right, left_axis, right_axis):
    return lax.dot_general(
        left, right, (((left_axis,), (right_axis,)), ((), ())), preferred_element_type=jnp.float32
    )


def normalize_rows(values):
    center = values - jnp.mean(values, axis=-1, keepdims=True)
    inverse = lax.rsqrt(jnp.mean(center * center, axis=-1, keepdims=True) + 1e-06)
    return (center * inverse, inverse)


def normalize_back(grad_normed, normed, inverse):
    centered = grad_normed - jnp.mean(grad_normed, axis=-1, keepdims=True)
    return (centered - normed * jnp.mean(grad_normed * normed, axis=-1, keepdims=True)) * inverse


def adam_update(weight, moment, square, grad, rate):
    first = beta_first * moment + (1.0 - beta_first) * grad
    second = beta_second * square + (1.0 - beta_second) * grad * grad
    step_size = first / (1.0 - beta_first**STEP)
    divisor = jnp.sqrt(second / (1.0 - beta_second**STEP)) + adam_epsilon
    return (weight - rate * (step_size / divisor + weight_decay * weight), first, second)


def merge_heads(stacked):
    return stacked.transpose(1, 0, 2).reshape(stacked.shape[1], stacked.shape[0] * stacked.shape[2])


MESH = pl.DeviceIdType.MESH
GROUP = 8
DEPTH = 4
VMEM_BYTES = 60 << 20
low_type = jnp.bfloat16
full_type = jnp.float32


def vmem():
    return pl.BlockSpec(memory_space=pltpu.VMEM)


def anywhere():
    return pl.BlockSpec(memory_space=pl.ANY)


def plane_places():
    place = lax.axis_index("dp")
    layer = lax.axis_index("mod")
    twin = place + 1 - 2 * lax.rem(place, 2)
    side = 2 - 4 * lax.rem(lax.div(place, 2), 2)
    across = place + side
    along = place + 4 - 8 * lax.div(place, 4)
    corner = along + side
    return place, layer, twin, across, along, corner


def twin_of(place):
    return place + 1 - 2 * lax.rem(place, 2)


def send(source, target, send_sem, recv_sem, place, layer):
    copy = pltpu.make_async_remote_copy(
        src_ref=source,
        dst_ref=target,
        send_sem=send_sem,
        recv_sem=recv_sem,
        device_id=(place, layer),
        device_id_type=MESH,
    )
    copy.start()
    return copy


def greet(peers):
    barrier = pltpu.get_barrier_semaphore()
    for peer in peers:
        pl.semaphore_signal(barrier, inc=1, device_id=peer, device_id_type=MESH)
    pl.semaphore_wait(barrier, len(peers))


class Gather:
    def __init__(self, own, slots, sends, recvs, base, rows, cut):
        self.own, self.slots, self.sends, self.recvs = own, slots, sends, recvs
        self.whole = pl.ds(base, rows)
        self.first, self.second = pl.ds(base, cut), pl.ds(base + cut, rows - cut)
        self.place, self.layer, self.twin, self.across, self.along, self.corner = plane_places()
        self.copies = {}

    def push(self, index, slot, part, peer, own=False):
        target = self.slots.at[slot, part]
        source = self.own.at[part] if own else target
        self.copies[index] = send(
            source, target, self.sends.at[index], self.recvs.at[index], peer, self.layer
        )

    def start_twin(self):
        self.push(2, self.place, self.whole, self.twin, True)

    def start_links(self):
        self.push(0, self.place, self.whole, self.across, True)
        self.push(1, self.place, self.whole, self.along, True)

    def forward_near(self):
        self.copies[0].wait_recv()
        self.push(3, self.across, self.first, self.along)
        self.push(5, self.across, self.whole, self.twin)
        self.copies[1].wait_recv()
        self.push(4, self.along, self.second, self.across)
        self.push(6, self.along, self.whole, self.twin)

    def forward_far(self):
        self.copies[3].wait_recv()
        self.push(7, self.corner, self.first, self.twin)
        self.copies[4].wait_recv()
        self.push(8, self.corner, self.second, self.twin)

    def arrived(self, *indices):
        for index in indices:
            self.copies[index].wait_recv()

    def finish_sends(self):
        for index in range(9):
            self.copies[index].wait_send()


class Scatter:
    def __init__(
        self, parts, from_twin, half_across, half_along, whole_across, whole_along, sends, recvs, rows, cut, outgoing=None
    ):
        self.parts, self.from_twin = parts, from_twin
        self.outgoing = parts if outgoing is None else outgoing
        self.half_across, self.half_along = half_across, half_along
        self.whole_across, self.whole_along = whole_across, whole_along
        self.sends, self.recvs = sends, recvs
        self.first, self.second = pl.ds(0, cut), pl.ds(cut, rows - cut)
        self.place, self.layer, self.twin, self.across, self.along, self.corner = plane_places()
        self.places = (self.place, self.across, self.along, self.corner)
        self.slots = self.places if outgoing is None else (0, 1, 2, 3)
        self.copies = {}

    def push(self, index, source, target, peer):
        self.copies[index] = send(
            source, target, self.sends.at[index], self.recvs.at[index], peer, self.layer
        )

    def start_twin(self, *indices):
        for index in indices or (1, 2, 3, 0):
            self.push(index, self.outgoing.at[twin_of(self.places[index])], self.from_twin.at[index], self.twin)

    def add(self, slot, part, other):
        total = self.parts[slot, part].astype(full_type) + other.astype(full_type)
        self.parts[slot, part] = total.astype(self.parts.dtype)

    def merge_twin(self, index):
        self.copies[index].wait_recv()
        self.add(self.slots[index], slice(None), self.from_twin[index])

    def start_near(self):
        _, across, along, _ = self.slots
        self.merge_twin(1)
        self.push(6, self.parts.at[across, self.first], self.whole_across.at[self.first], self.across)
        self.merge_twin(2)
        self.push(7, self.parts.at[along, self.second], self.whole_along.at[self.second], self.along)

    def start_far(self):
        corner = self.slots[3]
        self.merge_twin(3)
        self.push(4, self.parts.at[corner, self.first], self.half_across, self.across)
        self.push(5, self.parts.at[corner, self.second], self.half_along, self.along)

    def forward(self):
        _, across, along, _ = self.slots
        self.copies[5].wait_recv()
        self.add(across, self.second, self.half_along[...])
        self.push(8, self.parts.at[across, self.second], self.whole_across.at[self.second], self.across)
        self.copies[4].wait_recv()
        self.add(along, self.first, self.half_across[...])
        self.push(9, self.parts.at[along, self.first], self.whole_along.at[self.first], self.along)

    def settle(self):
        for index in (0, 6, 8, 7, 9):
            self.copies[index].wait_recv()
        for index in range(10):
            self.copies[index].wait_send()

    def total(self, part=slice(None)):
        return (
            self.parts[self.slots[0], part].astype(full_type)
            + self.from_twin[0, part].astype(full_type)
            + (self.whole_across[part].astype(full_type) + self.whole_along[part].astype(full_type))
        )


def scatter_scratch(rows, cut, columns, lead=()):
    return [
        pltpu.VMEM(lead + (4, rows, columns), low_type),
        pltpu.VMEM(lead + (cut, columns), low_type),
        pltpu.VMEM(lead + (rows - cut, columns), low_type),
        pltpu.VMEM(lead + (rows, columns), low_type),
        pltpu.VMEM(lead + (rows, columns), low_type),
        pltpu.SemaphoreType.DMA(lead + (10,)),
        pltpu.SemaphoreType.DMA(lead + (10,)),
    ]


def iota(shape, axis):
    return lax.broadcasted_iota(jnp.int32, shape, axis)


def sample_picker():
    row, column = iota((128, 256), 0), iota((128, 256), 1)
    wanted = ((row >> 2) & 3) * 64 + (row >> 4) * 8 + (row & 3)
    return (column == wanted).astype(full_type).astype(low_type)


def slot_spreader():
    row, column = iota((32, 16), 0), iota((32, 16), 1)
    return jnp.where(((row & 7) < 4) & (column == (row >> 3) * 4 + (row & 7)), 1.0, 0.0).astype(low_type)


def start_kernel(
    conditions,
    project,
    output,
    expand,
    modulate,
    bias_piece,
    bias_own,
    project_out,
    output_out,
    expand_out,
    mod_out,
    active_out,
    bias_out,
    own_project,
    own_output,
    own_expand,
    cond_send,
    cond_plane,
    cond_all,
    part_send,
    part_recv,
    mod_send,
    mod_recv,
    bias_recv,
    small_send,
    small_recv,
    project_sends,
    project_recvs,
    output_sends,
    output_recvs,
    expand_sends,
    expand_recvs,
    local_sems,
):
    place, layer, *_ = plane_places()
    plane = [lax.rem(place + step, GROUP) for step in range(1, GROUP)]
    column = [lax.rem(layer + step, DEPTH) for step in range(1, DEPTH)]
    cut_columns = expand.shape[1] // GROUP
    cut_rows = project.shape[0]

    values = conditions[...].astype(full_type)
    active = (values * jax.nn.sigmoid(values)).astype(low_type).astype(full_type)
    cond_send[...] = jnp.zeros_like(cond_send)
    for step in range(GROUP):
        cond_send[step, 0:IMG_ROW, :] = active[:, step * cut_rows : (step + 1) * cut_rows]
    bias_recv[place] = bias_own[...].astype(low_type).astype(full_type)
    own_project[...] = project[...].astype(low_type)
    own_output[...] = output[...].astype(low_type)
    for step in range(GROUP):
        own_expand[step] = expand[:, step * cut_columns : (step + 1) * cut_columns].astype(low_type)

    greet([(peer, layer) for peer in plane] + [(place, peer) for peer in column])

    small = []
    for step, peer in enumerate(plane):
        small.append(
            send(cond_send.at[peer], cond_plane.at[place], small_send.at[step], small_recv.at[step], peer, layer)
        )
    third = cut_rows // 3
    project_gathers = [
        Gather(own_project, project_out, project_sends.at[step], project_recvs.at[step], step * third, third, 16 + 16 * (step % 2))
        for step in range(3)
    ]
    output_gather = Gather(own_output, output_out, output_sends, output_recvs, 0, cut_rows, 64)
    for gather in project_gathers:
        gather.start_twin()
    output_gather.start_twin()
    project_gathers[0].start_links()
    locals_ = [
        pltpu.make_async_copy(own_project, project_out.at[place], local_sems.at[0]),
        pltpu.make_async_copy(own_output, output_out.at[place], local_sems.at[1]),
        pltpu.make_async_copy(own_expand.at[place], expand_out.at[place], local_sems.at[2]),
    ]
    for copy in locals_:
        copy.start()

    cond_plane[place] = cond_send[place]
    for copy in small:
        copy.wait_recv()
    waits = list(small)
    project_gathers[1].start_links()
    small = []
    for step, peer in enumerate(column):
        small.append(
            send(cond_plane, cond_all.at[layer], small_send.at[7 + step], small_recv.at[7 + step], place, peer)
        )
    cond_all[layer] = cond_plane[...]
    for copy in small:
        copy.wait_recv()
    waits += small
    padded = cond_all[...].reshape(DEPTH * GROUP * 8, cut_rows).astype(low_type)
    picked = contract(sample_picker(), padded, 1, 0).astype(low_type)
    active_out[...] = picked
    partial = contract(picked, modulate[...].astype(low_type), 1, 0)
    partial = partial + bias_piece[...].astype(low_type).astype(full_type)
    part_send[...] = partial.reshape(part_send.shape)
    small = []
    for step, peer in enumerate(plane):
        small.append(
            send(part_send.at[peer], part_recv.at[place], small_send.at[10 + step], small_recv.at[10 + step], peer, layer)
        )
        small.append(
            send(bias_recv.at[place], bias_recv.at[place], small_send.at[20 + step], small_recv.at[20 + step], peer, layer)
        )
    part_recv[place] = part_send[place]
    project_gathers[2].start_links()
    output_gather.start_links()
    for copy in small:
        copy.wait_recv()
    waits += small
    total = part_recv[0]
    for step in range(1, GROUP):
        total = total + part_recv[step]
    spread = contract(slot_spreader(), total.astype(low_type), 1, 0)
    mod_send[...] = spread.reshape(mod_send.shape)
    small = []
    for step, peer in enumerate(column):
        small.append(
            send(mod_send.at[peer], mod_recv.at[layer], small_send.at[17 + step], small_recv.at[17 + step], place, peer)
        )
    mod_recv[layer] = mod_send[layer]

    project_gathers[0].forward_near()
    project_gathers[1].forward_near()
    for copy in small:
        copy.wait_recv()
    waits += small
    mod_out[...] = mod_recv[...]
    bias_out[...] = bias_recv[...]
    project_gathers[2].forward_near()
    output_gather.forward_near()
    exchange = []
    for step, peer in enumerate(plane):
        exchange.append(
            send(own_expand.at[peer], expand_out.at[place], expand_sends.at[step], expand_recvs.at[step], peer, layer)
        )
    for gather in (*project_gathers, output_gather):
        gather.forward_far()
    for gather in (*project_gathers, output_gather):
        gather.arrived(2, 5, 6, 7, 8)
        gather.finish_sends()
    for copy in exchange:
        copy.wait()
    for copy in waits:
        copy.wait_send()
    for copy in locals_:
        copy.wait()


def start_call(conditions, project, output, expand, modulate, bias_piece, bias_own):
    rows = project.shape[0]
    hidden = expand.shape[1] // GROUP
    columns = modulate.shape[1]
    shape = jax.ShapeDtypeStruct
    dma = pltpu.SemaphoreType.DMA
    return pl.pallas_call(
        start_kernel,
        out_shape=(
            shape((GROUP, rows, project.shape[1]), low_type),
            shape((GROUP, rows, output.shape[1]), low_type),
            shape((GROUP, rows, hidden), low_type),
            shape((DEPTH, 8, columns), full_type),
            shape((128, rows), low_type),
            shape((GROUP,) + bias_own.shape, full_type),
        ),
        in_specs=[vmem()] * 7,
        out_specs=(anywhere(), anywhere(), anywhere(), vmem(), vmem(), vmem()),
        scratch_shapes=[
            pltpu.VMEM(project.shape, low_type),
            pltpu.VMEM(output.shape, low_type),
            pltpu.VMEM((GROUP, rows, hidden), low_type),
            pltpu.VMEM((GROUP, 8, rows), full_type),
            pltpu.VMEM((GROUP, 8, rows), full_type),
            pltpu.VMEM((DEPTH, GROUP, 8, rows), full_type),
            pltpu.VMEM((GROUP, 16, columns), full_type),
            pltpu.VMEM((GROUP, 16, columns), full_type),
            pltpu.VMEM((DEPTH, 8, columns), full_type),
            pltpu.VMEM((DEPTH, 8, columns), full_type),
            pltpu.VMEM((GROUP,) + bias_own.shape, full_type),
            dma((27,)),
            dma((27,)),
            dma((3, 9)),
            dma((3, 9)),
            dma((9,)),
            dma((9,)),
            dma((7,)),
            dma((7,)),
            dma((3,)),
        ],
        compiler_params=pltpu.CompilerParams(
            collective_id=0, has_side_effects=True, vmem_limit_bytes=VMEM_BYTES
        ),
        name="gather_start",
    )(conditions, project, output, expand, modulate, bias_piece, bias_own)


def head_window(head):
    start = lax.min(lax.div(head * HEAD_DIM, 128) * 128, D - 256)
    start = pl.multiple_of(start, 128)
    lane = iota((1, 256), 1) + start
    inside = (lane >= head * HEAD_DIM) & (lane < (head + 1) * HEAD_DIM)
    return start, inside.astype(full_type)


def window(ref, base, start):
    return ref[:, pl.ds(pl.multiple_of(base + start, 128), 256)]


def masked_probs(query, key, same):
    scores = jnp.where(same, contract(query, key, 1, 1) * HEAD_DIM ** (-0.5), -1e30)
    exponent = jnp.exp(scores - jnp.max(scores, axis=1, keepdims=True))
    return exponent / jnp.sum(exponent, axis=1, keepdims=True)


def attend_forward_kernel(packed, slot_row, slot_column, mixed, total):
    same = slot_column[...] == slot_row[...]
    total[...] = jnp.zeros_like(total)

    def head_step(head, carry):
        start, inside = head_window(head)
        keep = inside.astype(low_type)
        probs = masked_probs(window(packed, 0, start) * keep, window(packed, D, start), same)
        out = contract(probs.astype(low_type), window(packed, 2 * D, start) * keep, 1, 0)
        total[:, pl.ds(start, 256)] += out
        return carry

    lax.fori_loop(0, HEADS, head_step, 0, unroll=2)
    mixed[...] = total[...].astype(low_type)


def attend_forward(packed, slot_row, slot_column):
    return pl.pallas_call(
        attend_forward_kernel,
        out_shape=jax.ShapeDtypeStruct((ROW, D), low_type),
        in_specs=[vmem()] * 3,
        out_specs=vmem(),
        scratch_shapes=[pltpu.VMEM((ROW, D), full_type)],
        compiler_params=pltpu.CompilerParams(vmem_limit_bytes=VMEM_BYTES),
        name="attend_forward",
    )(packed, slot_row, slot_column)


def feed_kernel(
    feed_own,
    grad_own,
    expand,
    shrink,
    bias,
    feed_parts,
    grad_feed_in,
    grad_shrink,
    grad_expand,
    grad_bias,
    feed_all,
    grad_all,
    hidden_all,
    pre_all,
    slope_all,
    grad_parts,
    shrink_low,
    *scratch,
):
    feed_sends, feed_recvs, grad_sends, grad_recvs = scratch[0:4]
    grad_scatter = Scatter(grad_parts, *scratch[4:11], ROW, ROW // 2)
    place, layer, twin, across, along, corner = plane_places()
    feed_gather = Gather(feed_own, feed_all, feed_sends, feed_recvs, 0, ROW, ROW // 2)
    grad_gather = Gather(grad_own, grad_all, grad_sends, grad_recvs, 0, ROW, ROW // 2)
    greet([(twin, layer), (across, layer), (along, layer)])
    feed_gather.start_links()
    feed_gather.start_twin()
    grad_gather.start_twin()
    feed_all[place] = feed_own[...]
    grad_all[place] = grad_own[...]
    shrink_low[...] = shrink[...].astype(low_type)

    def ahead(slot):
        pre = contract(feed_all[slot], expand[...], 1, 0) + bias[...]
        tanh_part = jnp.tanh(tanh_scale * (pre + cubic_term * pre * pre * pre))
        hidden = (0.5 * pre * (1.0 + tanh_part)).astype(low_type)
        slope_all[slot] = 0.5 * (1.0 + tanh_part) + 0.5 * pre * (1.0 - tanh_part * tanh_part) * tanh_scale * (
            1.0 + 3.0 * cubic_term * pre * pre
        )
        hidden_all[slot] = hidden
        feed_parts[slot] = contract(hidden, shrink_low[...], 1, 0).astype(low_type)

    def back(slot):
        grad_hidden = contract(grad_all[slot], shrink_low[...], 1, 1)
        grad_pre = (grad_hidden * slope_all[slot]).astype(low_type)
        pre_all[slot] = grad_pre
        grad_parts[slot] = contract(grad_pre, expand[...], 1, 1).astype(low_type)

    ahead(place)
    feed_gather.arrived(2)
    ahead(twin)
    feed_gather.forward_near()
    grad_gather.start_links()
    ahead(across)
    ahead(along)
    feed_gather.forward_far()
    feed_gather.arrived(5, 6)
    ahead(twin_of(across))
    ahead(twin_of(along))
    ahead(corner)
    feed_gather.arrived(7, 8)
    ahead(twin_of(corner))
    back(place)
    grad_gather.arrived(2)
    back(twin)
    grad_gather.forward_near()
    grad_gather.arrived(5, 6)
    back(twin_of(across))
    back(twin_of(along))
    grad_scatter.start_twin(1, 2)
    back(across)
    back(along)
    grad_gather.forward_far()
    grad_scatter.start_near()
    back(corner)
    grad_gather.arrived(7, 8)
    back(twin_of(corner))
    grad_scatter.start_twin(3, 0)
    grad_scatter.start_far()

    units = hidden_all.shape[2]
    hidden = hidden_all[...].reshape(GROUP * ROW, units)
    grad_shrink[...] = contract(hidden, grad_all[...].reshape(GROUP * ROW, D), 0, 0).astype(low_type)
    grad_scatter.forward()
    grad_pre = pre_all[...].reshape(GROUP * ROW, units)
    grad_bias[...] = jnp.sum(grad_pre.astype(full_type), axis=0, keepdims=True)
    grad_expand[...] = contract(feed_all[...].reshape(GROUP * ROW, D), grad_pre, 0, 0).astype(low_type)
    grad_scatter.settle()
    grad_feed_in[...] = grad_scatter.total()
    feed_gather.finish_sends()
    grad_gather.finish_sends()


def feed_call(feed_own, grad_own, expand, shrink, bias):
    units = expand.shape[1]
    shape = jax.ShapeDtypeStruct
    dma = pltpu.SemaphoreType.DMA
    return pl.pallas_call(
        feed_kernel,
        out_shape=(
            shape((GROUP, ROW, D), low_type),
            shape((ROW, D), full_type),
            shape((units, D), low_type),
            shape((D, units), low_type),
            shape((1, units), full_type),
        ),
        in_specs=[vmem()] * 5,
        out_specs=(vmem(),) * 5,
        scratch_shapes=[
            pltpu.VMEM((GROUP, ROW, D), low_type),
            pltpu.VMEM((GROUP, ROW, D), low_type),
            pltpu.VMEM((GROUP, ROW, units), low_type),
            pltpu.VMEM((GROUP, ROW, units), low_type),
            pltpu.VMEM((GROUP, ROW, units), full_type),
            pltpu.VMEM((GROUP, ROW, D), low_type),
            pltpu.VMEM((units, D), low_type),
            dma((9,)),
            dma((9,)),
            dma((9,)),
            dma((9,)),
            *scatter_scratch(ROW, ROW // 2, D),
        ],
        compiler_params=pltpu.CompilerParams(
            collective_id=1, has_side_effects=True, vmem_limit_bytes=VMEM_BYTES
        ),
        name="feed_forward",
    )(feed_own, grad_own, expand, shrink, bias)

def sample_compactor():
    row, column = iota((16, 32), 0), iota((16, 32), 1)
    return (column == (row >> 2) * 8 + (row & 3)).astype(full_type).astype(low_type)


def sample_scatterer():
    row, column = iota((256, 128), 0), iota((256, 128), 1)
    wanted = ((row >> 3) & 7) * 16 + (row >> 6) * 4 + (row & 7)
    return jnp.where(((row & 7) < 4) & (column == wanted), 1.0, 0.0).astype(low_type)


def square_sum(values):
    values = values.astype(full_type)
    squares = values * values
    while squares.ndim > 2:
        squares = jnp.sum(squares, axis=0)
    return jnp.sum(jnp.sum(squares, axis=0, keepdims=True), axis=1, keepdims=True)


def slot_sums(onehot, values):
    high = values.astype(low_type)
    rest = (values - high.astype(full_type)).astype(low_type)
    return contract(onehot, high, 0, 0) + contract(onehot, rest, 0, 0)


def column_sum(values):
    return jnp.sum(values.astype(full_type), axis=0, keepdims=True)


BLOCK = 64
BIAS_ROWS = 128
LANES = 128


def back_kernel(
    tokens,
    cotangent,
    modulation,
    slot_row,
    slot_column,
    packed,
    attend_in,
    mixed,
    attend_out,
    resid,
    grad_feed_in,
    bias_shrink,
    grad_bias_expand,
    active,
    modulate,
    full_output,
    full_project,
    feed_parts_in,
    grad_shrink,
    grad_expand,
    block_output,
    token_grads,
    project_sum,
    output_sum,
    expand_sum,
    shrink_sum,
    bias_sum,
    modulate_sum,
    condition_sum,
    square_total,
    output_store,
    project_store,
    feed_parts,
    shrink_own,
    grad_resid,
    grad_attend,
    grad_mixed,
    grad_packed,
    slot_grads,
    project_own,
    output_own,
    expand_own,
    project_mid,
    output_mid,
    expand_mid,
    shrink_mid,
    bias_own,
    bias_recv,
    bias_layers,
    sample_send,
    sample_recv,
    group_all,
    term_send,
    term_recv,
    term_sum,
    square_send,
    square_recv,
    square_part,
    square_all,
    small_sends,
    small_recvs,
    pair_sends,
    pair_recvs,
    mid_sends,
    mid_recvs,
    local_sems,
    *scratch,
):
    place, layer, *_ = plane_places()
    plane = [lax.rem(place + step, GROUP) for step in range(1, GROUP)]
    column = [lax.rem(layer + step, DEPTH) for step in range(1, DEPTH)]
    rows = output_own.shape[0]
    pair = layer + 1 - 2 * lax.rem(layer, 2)
    across_middle = DEPTH - 1 - layer
    edge = (layer == 0) | (layer == DEPTH - 1)
    middle = jnp.logical_not(edge)
    scale = HEAD_DIM ** (-0.5)

    chunks = []
    for step in range(4):
        part = pl.ds(step * rows, rows)
        chunks.append((shrink_own.at[part], shrink_sum.at[part], shrink_mid.at[part]))
    for step in range(4):
        part = pl.ds(2 * step, 2)
        chunks.append((expand_own.at[part], expand_sum.at[part], expand_mid.at[part]))
    chunks.append((output_own, output_sum, output_mid))
    for step in range(3):
        chunks.append((project_own.at[step], project_sum.at[step], project_mid.at[step]))

    def pair_copy(index, source):
        return pltpu.make_async_remote_copy(
            src_ref=source,
            dst_ref=chunks[index][1],
            send_sem=pair_sends.at[index],
            recv_sem=pair_recvs.at[index],
            device_id=(place, pair),
            device_id_type=MESH,
        )

    def middle_copy(index):
        return pltpu.make_async_remote_copy(
            src_ref=chunks[index][0],
            dst_ref=chunks[index][2],
            send_sem=mid_sends.at[index],
            recv_sem=mid_recvs.at[index],
            device_id=(place, across_middle),
            device_id_type=MESH,
        )

    def edge_send(*indices):
        @pl.when(edge)
        def _():
            for index in indices:
                pair_copy(index, chunks[index][0]).start()

    def middle_step(*indices):
        @pl.when(middle)
        def _():
            for index in indices:
                if index < len(chunks):
                    given, result, _ = chunks[index]
                    pair_copy(index, result).wait_recv()
                    given[...] = (given[...].astype(full_type) + result[...].astype(full_type)).astype(low_type)
                    middle_copy(index).start()
                if index > 0:
                    given, result, other = chunks[index - 1]
                    middle_copy(index - 1).wait()
                    result[...] = (given[...].astype(full_type) + other[...].astype(full_type)).astype(low_type)
                    pair_copy(index - 1, result).start()

    waits = []

    def exchange(base, peers, source, target):
        copies = []
        for step, peer in enumerate(peers):
            where = (peer, layer) if peers is plane else (place, peer)
            copies.append(
                send(source(peer), target, small_sends.at[base + step], small_recvs.at[base + step], *where)
            )
        waits.extend(copies)
        return copies

    def arrive(copies):
        for copy in copies:
            copy.wait_recv()

    def load(index, source, target):
        copy = pltpu.make_async_copy(source, target, local_sems.at[index])
        copy.start()
        return copy

    feed_scatter = Scatter(feed_parts, *scratch[0:7], ROW, ROW // 2, outgoing=feed_parts_in)
    output_scatter = Scatter(output_store, *scratch[7:14], rows, 64)
    project_scatters = [
        Scatter(project_store.at[step], *(ref.at[step] for ref in scratch[14:21]), rows, 64) for step in range(3)
    ]
    shrink_load = load(0, grad_shrink, shrink_own)
    expand_load = load(1, grad_expand.at[place], expand_own.at[place])
    output_load = load(2, full_output, output_store)
    feed_loads = [
        load(3 + step, feed_parts_in.at[feed_scatter.places[step]], feed_parts.at[step]) for step in range(4)
    ]
    project_loads = [
        load(7 + step, full_project.at[:, :, pl.ds(step * D, D)], project_store.at[step]) for step in range(3)
    ]

    greet([(peer, layer) for peer in plane] + [(place, peer) for peer in column])

    feed_scatter.start_twin()
    expand_copies = exchange(0, plane, lambda peer: grad_expand.at[peer], expand_own.at[place])
    shrink_load.wait()
    edge_send(0, 1, 2, 3)
    slot_grads[...] = jnp.zeros_like(slot_grads)
    bias_own[...] = jnp.zeros_like(bias_own)
    grad_packed[...] = jnp.zeros_like(grad_packed)

    def block_parts(step):
        part = pl.ds(pl.multiple_of(step * BLOCK, BLOCK), BLOCK)
        slots = slot_column[part, :]
        onehot = jnp.where((slots == iota((BLOCK, 8), 1)) & (slots < IMG_ROW), 1.0, 0.0)
        return part, onehot.astype(low_type)

    def spread_slots(onehot, index):
        return contract(onehot, modulation[:, index * D : (index + 1) * D].astype(low_type), 1, 0)

    def feed_step(step, carry):
        part, onehot = block_parts(step)
        normed, inverse = normalize_rows(resid[part, :])
        grad_in = grad_feed_in[part, :]
        slot_grads[3] += slot_sums(onehot, grad_in)
        slot_grads[4] += slot_sums(onehot, grad_in * normed)
        grad = cotangent[part, :].astype(full_type) + normalize_back(
            grad_in * (1.0 + spread_slots(onehot, 4)), normed, inverse
        )
        grad_resid[part, :] = grad
        slot_grads[2] += slot_sums(onehot, grad * attend_out[part, :])
        grad_attend[part, :] = (spread_slots(onehot, 2) * grad).astype(low_type)
        return carry

    lax.fori_loop(0, ROW // BLOCK, feed_step, 0)
    for copy in feed_loads:
        copy.wait()
    feed_scatter.start_far()
    feed_scatter.start_near()
    output_load.wait()
    grad_mixed[...] = contract(grad_attend[...], output_store[...].reshape(D, D), 1, 1).astype(low_type)
    middle_step(0)

    same = slot_column[...] == slot_row[...]

    def head_step(head, carry):
        start, inside = head_window(head)
        keep = inside.astype(low_type)
        query = window(packed, 0, start) * keep
        key = window(packed, D, start)
        value = window(packed, 2 * D, start)
        grad = window(grad_mixed, 0, start) * keep
        probs = masked_probs(query, key, same)
        grad_probs = contract(grad, value, 1, 1)
        grad_scores = probs * (grad_probs - jnp.sum(probs * grad_probs, axis=1, keepdims=True))
        grad_scores = grad_scores.astype(low_type)

        def put(base, values):
            where = pl.ds(pl.multiple_of(base + start, 128), 256)
            grad_packed[:, where] = (grad_packed[:, where].astype(full_type) + values).astype(low_type)

        put(0, contract(grad_scores, key * keep, 1, 0) * scale)
        put(D, contract(grad_scores, query, 0, 0) * scale)
        put(2 * D, contract(probs.astype(low_type), grad, 0, 0))
        return carry

    def heads(first, last):
        lax.fori_loop(first, last, head_step, 0, unroll=2)

    def weight_step(left, right, target, step, carry):
        where = pl.ds(pl.multiple_of(step * 384, 128), 384)
        values = contract(left[...], right[:, where], 0, 0).astype(low_type)
        target[:, :, where] = values.reshape(GROUP, rows, 384)
        return carry

    heads(0, 4)
    middle_step(1)
    lax.fori_loop(0, 3, functools.partial(weight_step, mixed, grad_attend, output_store), 0)
    output_scatter.start_twin()
    heads(4, 8)
    middle_step(2)
    output_scatter.start_far()
    output_scatter.start_near()
    heads(8, 12)
    feed_scatter.forward()
    middle_step(3)
    arrive(expand_copies)
    expand_load.wait()
    edge_send(4, 5)
    heads(12, 16)
    middle_step(4)
    for copy in project_loads:
        copy.wait()
    for step in range(3):
        piece = contract(
            grad_packed[:, step * D : (step + 1) * D], project_store[step].reshape(D, D), 1, 1
        )
        token_grads[...] = piece if step == 0 else token_grads[...] + piece
    for step in range(3):
        lax.fori_loop(
            0,
            3,
            functools.partial(
                weight_step, attend_in, grad_packed.at[:, pl.ds(step * D, D)], project_store.at[step]
            ),
            0,
        )
        project_scatters[step].start_twin()
    project_scatters[0].start_far()
    project_scatters[0].start_near()
    middle_step(5)

    def attend_step(step, carry):
        part, onehot = block_parts(step)
        normed, inverse = normalize_rows(tokens[part, :].astype(full_type))
        grad_in = token_grads[part, :]
        slot_grads[0] += slot_sums(onehot, grad_in)
        slot_grads[1] += slot_sums(onehot, grad_in * normed)
        token_grads[part, :] = grad_resid[part, :] + normalize_back(
            grad_in * (1.0 + spread_slots(onehot, 1)), normed, inverse
        )
        return carry

    lax.fori_loop(0, ROW // BLOCK, attend_step, 0)
    project_scatters[1].start_far()
    project_scatters[1].start_near()
    output_scatter.forward()
    feed_scatter.settle()

    def put_rows(base, values):
        for step in range(values.shape[1] // LANES):
            bias_own[base + step : base + step + 1, :] = values[:, step * LANES : (step + 1) * LANES]

    def output_step(step, carry):
        part, onehot = block_parts(step)
        feed_out = feed_scatter.total(part) + bias_shrink[...]
        grad = cotangent[part, :].astype(full_type)
        gate = spread_slots(onehot, 5)
        block_output[part, :] = (resid[part, :] + gate * feed_out).astype(low_type)
        slot_grads[5] += slot_sums(onehot, grad * feed_out)
        return carry + column_sum((gate * grad).astype(low_type))

    feed_bias = lax.fori_loop(0, ROW // BLOCK, output_step, jnp.zeros((1, D), full_type))
    rounded = [slot_grads[step].astype(low_type).astype(full_type) for step in range(6)]
    half = D // 2
    for block in range(DEPTH):
        for step in range(3):
            piece, side = divmod(3 * block + step, 2)
            sample_send[block, :, step * half : (step + 1) * half] = rounded[piece][:, side * half : (side + 1) * half]
    sample_copies = exchange(7, column, lambda peer: sample_send.at[peer], sample_recv.at[layer])
    sample_recv[layer] = sample_send[layer]
    edge_send(6, 7)
    put_rows(0, column_sum(grad_packed[:, 0:D]))
    put_rows(9, column_sum(grad_packed[:, 2 * D : 3 * D]))
    put_rows(18, column_sum(grad_attend[...]))
    put_rows(27, feed_bias)
    for step in range(6):
        put_rows(36 + 9 * step, column_sum(rounded[step]))
    bias_recv[place] = bias_own[pl.ds(pl.multiple_of(place * 16, 16), 16), :]
    bias_copies = exchange(
        10, plane, lambda peer: bias_own.at[pl.ds(pl.multiple_of(peer * 16, 16), 16)], bias_recv.at[place]
    )
    middle_step(6)
    output_scatter.settle()
    output_own[...] = output_scatter.total().astype(low_type)
    arrive(sample_copies)
    group = contract(sample_compactor(), sample_recv[...].reshape(DEPTH * 8, sample_recv.shape[2]).astype(low_type), 1, 0)
    group_all[place] = group.astype(low_type)
    group_copies = exchange(17, plane, lambda peer: group_all.at[place], group_all.at[place])
    project_scatters[2].start_far()
    project_scatters[2].start_near()
    edge_send(8)
    middle_step(7)
    project_scatters[0].forward()
    arrive(bias_copies)
    total = bias_recv[0]
    for step in range(1, GROUP):
        total = total + bias_recv[step]
    bias_layers[layer, 0:16, :] = total
    bias_layers[layer, 16:24, :] = jnp.zeros((8, LANES), full_type)
    for step in range(4):
        bias_layers[layer, 16 + step : 17 + step, :] = grad_bias_expand[:, step * LANES : (step + 1) * LANES]
    bias_layers[layer, 20:21, 0:64] = grad_bias_expand[:, 512:576]
    layer_copies = exchange(24, column, lambda peer: bias_layers.at[layer], bias_layers.at[layer])
    middle_step(8)
    project_scatters[1].forward()

    arrive(group_copies)
    every = group_all[...].reshape(GROUP * 16, group_all.shape[2])
    modulate_sum[...] = contract(active[...], every, 0, 0)
    spread = contract(sample_scatterer(), every, 1, 0).astype(low_type)
    terms = contract(spread, modulate[...].astype(low_type), 1, 1)
    term_send[...] = terms.reshape(term_send.shape)
    term_copies = exchange(27, column, lambda peer: term_send.at[peer], term_recv.at[layer])
    term_recv[layer] = term_send[layer]
    project_scatters[0].settle()
    project_own[0] = project_scatters[0].total().astype(low_type)
    edge_send(9)
    middle_step(9)
    project_scatters[2].forward()
    arrive(layer_copies)
    total = (bias_layers[0] + bias_layers[1]) + (bias_layers[2] + bias_layers[3])
    bias_sum[place] = total
    bias_copies = exchange(30, plane, lambda peer: bias_sum.at[place], bias_sum.at[place])
    arrive(term_copies)
    term_sum[...] = (term_recv[0] + term_recv[1]) + (term_recv[2] + term_recv[3])
    last_copies = exchange(37, plane, lambda peer: term_sum.at[peer], condition_sum.at[place])
    condition_sum[place] = term_sum[place]
    project_scatters[1].settle()
    project_own[1] = project_scatters[1].total().astype(low_type)
    edge_send(10)
    middle_step(10)
    project_scatters[2].settle()
    project_own[2] = project_scatters[2].total().astype(low_type)
    edge_send(11)
    modulate_square = square_sum(modulate_sum[...])
    arrive(bias_copies)
    middle_step(11, 12)

    @pl.when(edge)
    def _():
        for index in range(len(chunks)):
            pair_copy(index, chunks[index][0]).wait()

    @pl.when(middle)
    def _():
        for index in range(len(chunks)):
            pair_copy(index, chunks[index][1]).wait_send()

    trunk = (
        square_sum(project_sum[...])
        + square_sum(output_sum[...])
        + square_sum(expand_sum[...])
        + square_sum(shrink_sum[...])
        + square_sum(bias_sum[place])
    )
    square_send[0] = jnp.broadcast_to(trunk, (8, 128))
    square_send[1] = jnp.broadcast_to(modulate_square, (8, 128))
    square_copies = exchange(44, plane, lambda peer: square_send, square_recv.at[place])
    square_recv[place] = square_send[...]
    arrive(square_copies)
    both = square_recv[0]
    for step in range(1, GROUP):
        both = both + square_recv[step]
    square_part[...] = both
    square_all[layer] = both
    square_copies = exchange(51, column, lambda peer: square_part, square_all.at[layer])
    arrive(square_copies)
    square_total[...] = both[0] + ((square_all[0, 1] + square_all[1, 1]) + (square_all[2, 1] + square_all[3, 1]))
    arrive(last_copies)
    for copy in waits:
        copy.wait_send()


def back_call(
    tokens,
    cotangent,
    modulation,
    slot_row,
    slot_column,
    packed,
    attend_in,
    mixed,
    attend_out,
    resid,
    grad_feed_in,
    bias_shrink,
    grad_bias_expand,
    active,
    modulate,
    full_output,
    full_project,
    feed_parts,
    grad_shrink,
    grad_expand,
):
    rows, columns = modulate.shape
    units = grad_expand.shape[2]
    shape = jax.ShapeDtypeStruct
    dma = pltpu.SemaphoreType.DMA
    return pl.pallas_call(
        back_kernel,
        out_shape=(
            shape((ROW, D), low_type),
            shape((ROW, D), full_type),
            shape((3, rows, D), low_type),
            shape((rows, D), low_type),
            shape((GROUP, rows, units), low_type),
            shape((units, D), low_type),
            shape((GROUP, 24, LANES), full_type),
            shape((rows, columns), full_type),
            shape((GROUP, 8, rows), full_type),
            shape((8, LANES), full_type),
        ),
        in_specs=[vmem()] * 15 + [anywhere()] * 5,
        out_specs=(vmem(),) * 10,
        scratch_shapes=[
            pltpu.VMEM((GROUP, rows, D), low_type),
            pltpu.VMEM((3, GROUP, rows, D), low_type),
            pltpu.VMEM((4, ROW, D), low_type),
            pltpu.VMEM((units, D), low_type),
            pltpu.VMEM((ROW, D), full_type),
            pltpu.VMEM((ROW, D), low_type),
            pltpu.VMEM((ROW, D), low_type),
            pltpu.VMEM((ROW, 3 * D), low_type),
            pltpu.VMEM((6, 8, D), full_type),
            pltpu.VMEM((3, rows, D), low_type),
            pltpu.VMEM((rows, D), low_type),
            pltpu.VMEM((GROUP, rows, units), low_type),
            pltpu.VMEM((3, rows, D), low_type),
            pltpu.VMEM((rows, D), low_type),
            pltpu.VMEM((GROUP, rows, units), low_type),
            pltpu.VMEM((units, D), low_type),
            pltpu.VMEM((BIAS_ROWS, LANES), full_type),
            pltpu.VMEM((GROUP, 16, LANES), full_type),
            pltpu.VMEM((DEPTH, 24, LANES), full_type),
            pltpu.VMEM((DEPTH, 8, columns), full_type),
            pltpu.VMEM((DEPTH, 8, columns), full_type),
            pltpu.VMEM((GROUP, 16, columns), low_type),
            pltpu.VMEM((DEPTH, GROUP, 8, rows), full_type),
            pltpu.VMEM((DEPTH, GROUP, 8, rows), full_type),
            pltpu.VMEM((GROUP, 8, rows), full_type),
            pltpu.VMEM((2, 8, LANES), full_type),
            pltpu.VMEM((GROUP, 2, 8, LANES), full_type),
            pltpu.VMEM((2, 8, LANES), full_type),
            pltpu.VMEM((DEPTH, 2, 8, LANES), full_type),
            dma((54,)),
            dma((54,)),
            dma((12,)),
            dma((12,)),
            dma((12,)),
            dma((12,)),
            dma((10,)),
            *scatter_scratch(ROW, ROW // 2, D),
            *scatter_scratch(rows, 64, D),
            *scatter_scratch(rows, 64, D, (3,)),
        ],
        compiler_params=pltpu.CompilerParams(
            collective_id=2, has_side_effects=True, vmem_limit_bytes=VMEM_BYTES
        ),
        name="backward",
    )(
        tokens,
        cotangent,
        modulation,
        slot_row,
        slot_column,
        packed,
        attend_in,
        mixed,
        attend_out,
        resid,
        grad_feed_in,
        bias_shrink,
        grad_bias_expand,
        active,
        modulate,
        full_output,
        full_project,
        feed_parts,
        grad_shrink,
        grad_expand,
    )


def per_slot(onehot, rows):
    return contract(onehot, rows, 1, 0)


def plane_body(
    tokens,
    conditions,
    image_lengths,
    cotangent,
    project_weight,
    project_moment,
    project_square,
    output_weight,
    output_moment,
    output_square,
    expand_weight,
    expand_moment,
    expand_square,
    shrink_weight,
    shrink_moment,
    shrink_square,
    modulate_weight,
    modulate_moment,
    modulate_square,
    bias_vector,
    bias_moment,
    bias_square,
):
    place = lax.axis_index("dp")
    layer = lax.axis_index("mod")
    shard = bias_vector.shape[0]
    columns = modulate_weight.shape[1]
    units = FF // GROUP
    mod_base = 4 * D + FF
    span = 10 * D + FF
    blank = jnp.zeros((span,), jnp.float32)
    around = jnp.concatenate([blank, bias_vector, blank])
    bias_piece = lax.dynamic_slice_in_dim(
        around, span + mod_base + layer * columns - place * shard, columns
    )[None, :]
    blocks = start_call(
        conditions, project_weight, output_weight, expand_weight, modulate_weight, bias_piece, bias_vector[None, :]
    )
    full_project = blocks[0].reshape(D, 3 * D)
    full_output = blocks[1].reshape(D, D)
    own_expand = blocks[2].reshape(D, units)
    own_mod = blocks[3].transpose(1, 0, 2).reshape(8, 6 * D)
    active = blocks[4]
    bias_full = blocks[5].reshape(span)
    bias_query = bias_full[0:D]
    bias_value = bias_full[D : 2 * D]
    bias_output = bias_full[2 * D : 3 * D]
    bias_expand = lax.dynamic_slice_in_dim(bias_full, 3 * D + place * units, units)[None, :]
    bias_shrink = bias_full[3 * D + FF : 4 * D + FF]

    slots = jnp.arange(IMG_ROW, dtype=jnp.int32)
    ends = jnp.sum(
        jnp.where(slots[:, None] <= slots[None, :], image_lengths[0][:, None], 0), axis=0, dtype=jnp.int32
    )
    positions = jnp.arange(ROW, dtype=jnp.int32)
    slot_of = jnp.sum(
        (positions[:, None] >= ends[None, :]).astype(jnp.int32), axis=1, dtype=jnp.int32
    )
    slot_match = (slot_of[:, None] == jnp.arange(8, dtype=jnp.int32)[None, :]) & (slot_of[:, None] < IMG_ROW)
    onehot = slot_match.astype(low_type)
    slot_row, slot_column = slot_of[None, :], slot_of[:, None]
    per_token = contract(onehot, own_mod.astype(low_type), 1, 0)
    shift_attend = per_token[:, 0:D]
    scale_attend = per_token[:, D : 2 * D]
    gate_attend = per_token[:, 2 * D : 3 * D]
    shift_feed = per_token[:, 3 * D : 4 * D]
    scale_feed = per_token[:, 4 * D : 5 * D]
    gate_feed = per_token[:, 5 * D : 6 * D]
    inputs = tokens.astype(jnp.float32)
    normed_attend, inverse_attend = normalize_rows(inputs)
    attend_in = (normed_attend * (1.0 + scale_attend) + shift_attend).astype(low_type)
    shift = jnp.concatenate([bias_query, jnp.zeros((D,), jnp.float32), bias_value])
    packed = (contract(attend_in, full_project, 1, 0) + shift).astype(low_type)
    mixed = attend_forward(packed, slot_row, slot_column)
    attend_out = contract(mixed, full_output, 1, 0) + bias_output
    resid = inputs + gate_attend * attend_out
    normed_feed, inverse_feed = normalize_rows(resid)
    feed_in = (normed_feed * (1.0 + scale_feed) + shift_feed).astype(low_type)
    grad_out = cotangent.astype(jnp.float32)
    grad_feed = (gate_feed * grad_out).astype(low_type)
    feed_parts, grad_feed_in, grad_shrink, grad_expand, grad_bias_expand = feed_call(
        feed_in, grad_feed, own_expand, shrink_weight, bias_expand
    )
    rows = project_weight.shape[0]
    (
        block_output,
        token_grads,
        sum_project,
        sum_output,
        sum_expand,
        sum_shrink,
        bias_sums,
        sum_modulate,
        condition_parts,
        square_total,
    ) = back_call(
        tokens,
        cotangent,
        own_mod,
        slot_row,
        slot_column,
        packed,
        attend_in,
        mixed,
        attend_out,
        resid,
        grad_feed_in,
        bias_shrink[None, :],
        grad_bias_expand,
        active,
        modulate_weight,
        blocks[1],
        blocks[0],
        feed_parts,
        grad_shrink,
        grad_expand.reshape(GROUP, rows, units),
    )
    square_total = square_total[0, 0]
    sum_project = sum_project.transpose(1, 0, 2).reshape(rows, 3 * D).astype(jnp.float32)
    sum_output = sum_output.astype(jnp.float32)
    sum_expand = sum_expand.transpose(1, 0, 2).reshape(rows, FF).astype(jnp.float32)
    sum_shrink = sum_shrink.astype(jnp.float32)
    common = bias_sums[:, 0:16].reshape(BIAS_ROWS * LANES)
    every_bias = jnp.concatenate(
        [common[0 : 3 * D], bias_sums[:, 16:24].reshape(GROUP, 8 * LANES)[:, 0:units].reshape(FF), common[3 * D : 10 * D]]
    )
    sum_bias = lax.dynamic_slice_in_dim(every_bias, place * shard, shard)
    condition_sum = condition_parts[:, 0:IMG_ROW].transpose(1, 0, 2).reshape(IMG_ROW, D)
    own_conditions = conditions.astype(jnp.float32)
    sigmoid_part = jax.nn.sigmoid(own_conditions)
    condition_grads = condition_sum * (sigmoid_part * (1.0 + own_conditions * (1.0 - sigmoid_part)))
    global_norm = jnp.sqrt(square_total)
    clip_factor = jnp.minimum(1.0, 1.0 / (global_norm + 1e-06))
    updated = (
        *adam_update(project_weight, project_moment, project_square, sum_project * clip_factor, D ** (-0.5)),
        *adam_update(output_weight, output_moment, output_square, sum_output * clip_factor, (D // 64) ** (-0.5)),
        *adam_update(expand_weight, expand_moment, expand_square, sum_expand * clip_factor, D ** (-0.5)),
        *adam_update(shrink_weight, shrink_moment, shrink_square, sum_shrink * clip_factor, FF ** (-0.5)),
        *adam_update(modulate_weight, modulate_moment, modulate_square, sum_modulate * clip_factor, D ** (-0.5)),
        *adam_update(bias_vector, bias_moment, bias_square, sum_bias * clip_factor, 0.3),
    )
    return (block_output, token_grads, condition_grads, global_norm, *updated)


def generic_body(
    tokens,
    conditions,
    image_lengths,
    cotangent,
    project_weight,
    project_moment,
    project_square,
    output_weight,
    output_moment,
    output_square,
    expand_weight,
    expand_moment,
    expand_square,
    shrink_weight,
    shrink_moment,
    shrink_square,
    modulate_weight,
    modulate_moment,
    modulate_square,
    bias_vector,
    bias_moment,
    bias_square,
):
    low_type = jnp.bfloat16
    group_size = lax.axis_size("mod")
    group_place = lax.axis_index("mod")
    columns = 6 * D // group_size
    full_project, full_output, full_expand, full_shrink, full_modulate, full_bias = (
        lax.all_gather(project_weight.astype(low_type), "dp", axis=0, tiled=True),
        lax.all_gather(output_weight.astype(low_type), "dp", axis=0, tiled=True),
        lax.all_gather(expand_weight.astype(low_type), "dp", axis=0, tiled=True),
        lax.all_gather(shrink_weight.astype(low_type), "dp", axis=0, tiled=True),
        lax.all_gather(modulate_weight.astype(low_type), "dp", axis=0, tiled=True),
        lax.all_gather(bias_vector.astype(low_type), "dp", axis=0, tiled=True),
    )
    bias_full = full_bias.astype(jnp.float32)
    bias_query = bias_full[0:D]
    bias_value = bias_full[D : 2 * D]
    bias_output = bias_full[2 * D : 3 * D]
    bias_expand = bias_full[3 * D : 3 * D + FF]
    bias_shrink = bias_full[3 * D + FF : 4 * D + FF]
    bias_modulate = lax.dynamic_slice_in_dim(bias_full, 4 * D + FF + group_place * columns, columns)
    group_conditions = lax.all_gather(conditions, "mod", axis=0, tiled=True)
    activated = jax.nn.silu(group_conditions.astype(jnp.float32)).astype(low_type)
    group_mod = (contract(activated, full_modulate, 1, 0) + bias_modulate).astype(low_type)
    own_mod = lax.all_to_all(group_mod, "mod", split_axis=0, concat_axis=1, tiled=True)
    slots = jnp.arange(IMG_ROW, dtype=jnp.int32)
    ends = jnp.sum(
        jnp.where(slots[:, None] <= slots[None, :], image_lengths[0][:, None], 0), axis=0, dtype=jnp.int32
    )
    positions = jnp.arange(ROW, dtype=jnp.int32)
    slot_of = jnp.sum(
        (positions[:, None] >= ends[None, :]).astype(jnp.int32), axis=1, dtype=jnp.int32
    )
    slot_match = slot_of[:, None] == jnp.arange(IMG_ROW, dtype=jnp.int32)[None, :]
    same_image = slot_of[:, None] == slot_of[None, :]
    per_token = contract(slot_match.astype(low_type), own_mod, 1, 0)
    shift_attend = per_token[:, 0:D]
    scale_attend = per_token[:, D : 2 * D]
    gate_attend = per_token[:, 2 * D : 3 * D]
    shift_feed = per_token[:, 3 * D : 4 * D]
    scale_feed = per_token[:, 4 * D : 5 * D]
    gate_feed = per_token[:, 5 * D : 6 * D]
    inputs = tokens.astype(jnp.float32)
    normed_attend, inverse_attend = normalize_rows(inputs)
    attend_in = (normed_attend * (1.0 + scale_attend) + shift_attend).astype(low_type)
    projected = contract(attend_in, full_project, 1, 0)
    query = (projected[:, 0:D] + bias_query).astype(low_type)
    keys = projected[:, D : 2 * D].astype(low_type)
    values = (projected[:, 2 * D : 3 * D] + bias_value).astype(low_type)
    head_scale = HEAD_DIM ** (-0.5)

    def split_heads(matrix):
        return matrix.reshape(ROW, HEADS, HEAD_DIM).transpose(1, 0, 2)

    def head_scores(query_head, key_head):
        return jnp.where(same_image, contract(query_head, key_head, 1, 1) * head_scale, -1e30)

    def attend_head(pieces):
        query_head, key_head, value_head = pieces
        scores = head_scores(query_head, key_head)
        row_top = jnp.max(scores, axis=1, keepdims=True)
        exponent = jnp.exp(scores - row_top)
        total = jnp.sum(exponent, axis=1, keepdims=True)
        probs = (exponent / total).astype(low_type)
        return (contract(probs, value_head, 1, 0), (row_top + jnp.log(total))[:, 0])

    heads_query = split_heads(query)
    heads_key = split_heads(keys)
    heads_value = split_heads(values)
    mixed_heads, log_totals = lax.map(attend_head, (heads_query, heads_key, heads_value))
    mixed = merge_heads(mixed_heads).astype(low_type)
    attend_out = contract(mixed, full_output, 1, 0) + bias_output
    resid = inputs + gate_attend * attend_out
    normed_feed, inverse_feed = normalize_rows(resid)
    feed_in = (normed_feed * (1.0 + scale_feed) + shift_feed).astype(low_type)
    hidden_pre = contract(feed_in, full_expand, 1, 0) + bias_expand
    tanh_part = jnp.tanh(
        tanh_scale * (hidden_pre + cubic_term * hidden_pre * hidden_pre * hidden_pre)
    )
    hidden = (0.5 * hidden_pre * (1.0 + tanh_part)).astype(low_type)
    feed_out = contract(hidden, full_shrink, 1, 0) + bias_shrink
    block_output = (resid + gate_feed * feed_out).astype(low_type)
    grad_out = cotangent.astype(jnp.float32)
    grad_gate_feed = grad_out * feed_out
    grad_feed = (gate_feed * grad_out).astype(low_type)
    grad_shrink = contract(hidden, grad_feed, 0, 0)
    grad_hidden = contract(grad_feed, full_shrink, 1, 1)
    slope = 0.5 * (1.0 + tanh_part) + 0.5 * hidden_pre * (
        1.0 - tanh_part * tanh_part
    ) * tanh_scale * (1.0 + 3.0 * cubic_term * hidden_pre * hidden_pre)
    grad_pre = (grad_hidden * slope).astype(low_type)
    grad_expand = contract(feed_in, grad_pre, 0, 0)
    grad_feed_in = contract(grad_pre, full_expand, 1, 1)
    grad_scale_feed = grad_feed_in * normed_feed
    grad_resid = grad_out + normalize_back(
        grad_feed_in * (1.0 + scale_feed), normed_feed, inverse_feed
    )
    grad_gate_attend = grad_resid * attend_out
    grad_attend = (gate_attend * grad_resid).astype(low_type)
    grad_output = contract(mixed, grad_attend, 0, 0)
    grad_mixed = contract(grad_attend, full_output, 1, 1).astype(low_type)

    def attend_back(pieces):
        query_head, key_head, value_head, grad_head, log_total = pieces
        probs = jnp.exp(head_scores(query_head, key_head) - log_total[:, None])
        grad_value = contract(probs.astype(low_type), grad_head, 0, 0)
        grad_probs = contract(grad_head, value_head, 1, 1)
        grad_scores = (
            probs * (grad_probs - jnp.sum(probs * grad_probs, axis=1, keepdims=True))
        ).astype(low_type)
        grad_query = contract(grad_scores, key_head, 1, 0) * head_scale
        grad_key = contract(grad_scores, query_head, 0, 0) * head_scale
        return (grad_query, grad_key, grad_value)

    heads_grad_query, heads_grad_key, heads_grad_value = lax.map(
        attend_back, (heads_query, heads_key, heads_value, split_heads(grad_mixed), log_totals)
    )
    grad_projected = jnp.concatenate(
        [merge_heads(heads_grad_query), merge_heads(heads_grad_key), merge_heads(heads_grad_value)],
        axis=1,
    ).astype(low_type)
    grad_project = contract(attend_in, grad_projected, 0, 0)
    grad_attend_in = contract(grad_projected, full_project, 1, 1)
    grad_scale_attend = grad_attend_in * normed_attend
    token_grads = grad_resid + normalize_back(
        grad_attend_in * (1.0 + scale_attend), normed_attend, inverse_attend
    )
    token_mod_grads = jnp.concatenate(
        [
            grad_attend_in,
            grad_scale_attend,
            grad_gate_attend,
            grad_feed_in,
            grad_scale_feed,
            grad_gate_feed,
        ],
        axis=1,
    )
    sample_grads = contract(slot_match.astype(jnp.float32), token_mod_grads, 0, 0).astype(low_type)
    group_grads = lax.all_to_all(sample_grads, "mod", split_axis=1, concat_axis=0, tiled=True)
    grad_modulate = contract(activated, group_grads, 0, 0)
    grad_bias_modulate = jnp.sum(group_grads, axis=0, dtype=jnp.float32)
    condition_terms = contract(group_grads, full_modulate, 1, 1)
    condition_sum = lax.psum_scatter(
        condition_terms.astype(jnp.bfloat16), "mod", scatter_dimension=0, tiled=True
    ).astype(jnp.float32)
    own_conditions = conditions.astype(jnp.float32)
    sigmoid_part = jax.nn.sigmoid(own_conditions)
    condition_grads = condition_sum * (sigmoid_part * (1.0 + own_conditions * (1.0 - sigmoid_part)))
    modulate_bias_grad = lax.dynamic_update_slice_in_dim(
        jnp.zeros((6 * D,), jnp.float32), grad_bias_modulate, group_place * columns, 0
    )
    grad_bias = jnp.concatenate(
        [
            jnp.sum(grad_projected[:, 0:D], axis=0, dtype=jnp.float32),
            jnp.sum(grad_projected[:, 2 * D : 3 * D], axis=0, dtype=jnp.float32),
            jnp.sum(grad_attend, axis=0, dtype=jnp.float32),
            jnp.sum(grad_pre, axis=0, dtype=jnp.float32),
            jnp.sum(grad_feed, axis=0, dtype=jnp.float32),
            modulate_bias_grad,
        ],
        axis=0,
    )
    summed = (
        lax.psum_scatter(
            grad_project.astype(jnp.bfloat16), "dp", scatter_dimension=0, tiled=True
        ).astype(jnp.float32),
        lax.psum_scatter(
            grad_output.astype(jnp.bfloat16), "dp", scatter_dimension=0, tiled=True
        ).astype(jnp.float32),
        lax.psum_scatter(
            grad_expand.astype(jnp.bfloat16), "dp", scatter_dimension=0, tiled=True
        ).astype(jnp.float32),
        lax.psum_scatter(
            grad_shrink.astype(jnp.bfloat16), "dp", scatter_dimension=0, tiled=True
        ).astype(jnp.float32),
        lax.psum_scatter(
            grad_modulate.astype(jnp.bfloat16), "dp", scatter_dimension=0, tiled=True
        ).astype(jnp.float32),
        lax.psum_scatter(
            grad_bias.astype(jnp.bfloat16), "dp", scatter_dimension=0, tiled=True
        ).astype(jnp.float32),
    )
    sum_project, sum_output, sum_expand, sum_shrink, sum_bias = (
        lax.psum(summed[0].astype(jnp.bfloat16), "mod").astype(jnp.float32),
        lax.psum(summed[1].astype(jnp.bfloat16), "mod").astype(jnp.float32),
        lax.psum(summed[2].astype(jnp.bfloat16), "mod").astype(jnp.float32),
        lax.psum(summed[3].astype(jnp.bfloat16), "mod").astype(jnp.float32),
        lax.psum(summed[5].astype(jnp.bfloat16), "mod").astype(jnp.float32),
    )
    sum_modulate = summed[4]
    trunk_square = (
        jnp.sum(sum_project * sum_project)
        + jnp.sum(sum_output * sum_output)
        + jnp.sum(sum_expand * sum_expand)
        + jnp.sum(sum_shrink * sum_shrink)
        + jnp.sum(sum_bias * sum_bias)
    )
    totals = lax.psum((trunk_square, jnp.sum(sum_modulate * sum_modulate)), ("dp", "mod"))
    global_norm = jnp.sqrt(totals[0] / group_size + totals[1])
    clip_factor = jnp.minimum(1.0, 1.0 / (global_norm + 1e-06))
    next_project, first_project, second_project = adam_update(
        project_weight, project_moment, project_square, sum_project * clip_factor, D ** (-0.5)
    )
    next_output, first_output, second_output = adam_update(
        output_weight, output_moment, output_square, sum_output * clip_factor, (D // 64) ** (-0.5)
    )
    next_expand, first_expand, second_expand = adam_update(
        expand_weight, expand_moment, expand_square, sum_expand * clip_factor, D ** (-0.5)
    )
    next_shrink, first_shrink, second_shrink = adam_update(
        shrink_weight, shrink_moment, shrink_square, sum_shrink * clip_factor, FF ** (-0.5)
    )
    next_modulate, first_modulate, second_modulate = adam_update(
        modulate_weight, modulate_moment, modulate_square, sum_modulate * clip_factor, D ** (-0.5)
    )
    next_biases, first_biases, second_biases = adam_update(
        bias_vector, bias_moment, bias_square, sum_bias * clip_factor, 0.3
    )
    return (
        block_output,
        token_grads,
        condition_grads,
        global_norm,
        next_project,
        first_project,
        second_project,
        next_output,
        first_output,
        second_output,
        next_expand,
        first_expand,
        second_expand,
        next_shrink,
        first_shrink,
        second_shrink,
        next_modulate,
        first_modulate,
        second_modulate,
        next_biases,
        first_biases,
        second_biases,
    )


def solution(mesh):
    return jax.shard_map(
        plane_body if mesh.shape["dp"] == GROUP and mesh.shape["mod"] == DEPTH else generic_body,
        mesh=mesh,
        in_specs=(
            P(("dp", "mod"), None),
            P(("dp", "mod"), None),
            P(("dp", "mod"), None),
            P(("dp", "mod"), None),
            P("dp", None),
            P("dp", None),
            P("dp", None),
            P("dp", None),
            P("dp", None),
            P("dp", None),
            P("dp", None),
            P("dp", None),
            P("dp", None),
            P("dp", None),
            P("dp", None),
            P("dp", None),
            P("dp", "mod"),
            P("dp", "mod"),
            P("dp", "mod"),
            P("dp"),
            P("dp"),
            P("dp"),
        ),
        out_specs=(
            P(("dp", "mod"), None),
            P(("dp", "mod"), None),
            P(("dp", "mod"), None),
            P(),
            P("dp", None),
            P("dp", None),
            P("dp", None),
            P("dp", None),
            P("dp", None),
            P("dp", None),
            P("dp", None),
            P("dp", None),
            P("dp", None),
            P("dp", None),
            P("dp", None),
            P("dp", None),
            P("dp", "mod"),
            P("dp", "mod"),
            P("dp", "mod"),
            P("dp"),
            P("dp"),
            P("dp"),
        ),
        check_vma=False,
    )
```

```python
import functools

import jax
import jax.numpy as jnp
from jax import lax
from jax.experimental import pallas as pl
from jax.experimental.pallas import tpu as pltpu
from jax.sharding import PartitionSpec as P

D = 1152
HEADS = 16
HEAD_DIM = 72
FF = 4608
ROW = 256
STEP = 10
IMG_ROW = 4


beta_first = 0.9
beta_second = 0.999
weight_decay = 0.01
adam_epsilon = 1e-08
tanh_scale = 0.7978845608028654
cubic_term = 0.044715


def contract(left, right, left_axis, right_axis):
    return lax.dot_general(
        left, right, (((left_axis,), (right_axis,)), ((), ())), preferred_element_type=jnp.float32
    )


def normalize_rows(values):
    center = values - jnp.mean(values, axis=-1, keepdims=True)
    inverse = lax.rsqrt(jnp.mean(center * center, axis=-1, keepdims=True) + 1e-06)
    return (center * inverse, inverse)


def normalize_back(grad_normed, normed, inverse):
    centered = grad_normed - jnp.mean(grad_normed, axis=-1, keepdims=True)
    return (centered - normed * jnp.mean(grad_normed * normed, axis=-1, keepdims=True)) * inverse


def adam_update(weight, moment, square, grad, rate):
    first = beta_first * moment + (1.0 - beta_first) * grad
    second = beta_second * square + (1.0 - beta_second) * grad * grad
    step_size = first / (1.0 - beta_first**STEP)
    divisor = jnp.sqrt(second / (1.0 - beta_second**STEP)) + adam_epsilon
    return (weight - rate * (step_size / divisor + weight_decay * weight), first, second)


def merge_heads(stacked):
    return stacked.transpose(1, 0, 2).reshape(stacked.shape[1], stacked.shape[0] * stacked.shape[2])


MESH = pl.DeviceIdType.MESH
GROUP = 8
DEPTH = 4
VMEM_BYTES = 60 << 20
low_type = jnp.bfloat16
full_type = jnp.float32


def vmem():
    return pl.BlockSpec(memory_space=pltpu.VMEM)


def anywhere():
    return pl.BlockSpec(memory_space=pl.ANY)


def plane_places():
    place = lax.axis_index("dp")
    layer = lax.axis_index("mod")
    twin = place + 1 - 2 * lax.rem(place, 2)
    side = 2 - 4 * lax.rem(lax.div(place, 2), 2)
    across = place + side
    along = place + 4 - 8 * lax.div(place, 4)
    corner = along + side
    return place, layer, twin, across, along, corner


def twin_of(place):
    return place + 1 - 2 * lax.rem(place, 2)


def send(source, target, send_sem, recv_sem, place, layer):
    copy = pltpu.make_async_remote_copy(
        src_ref=source,
        dst_ref=target,
        send_sem=send_sem,
        recv_sem=recv_sem,
        device_id=(place, layer),
        device_id_type=MESH,
    )
    copy.start()
    return copy


def greet(peers):
    barrier = pltpu.get_barrier_semaphore()
    for peer in peers:
        pl.semaphore_signal(barrier, inc=1, device_id=peer, device_id_type=MESH)
    pl.semaphore_wait(barrier, len(peers))


class Gather:
    def __init__(self, own, slots, sends, recvs, base, rows, cut):
        self.own, self.slots, self.sends, self.recvs = own, slots, sends, recvs
        self.whole = pl.ds(base, rows)
        self.first, self.second = pl.ds(base, cut), pl.ds(base + cut, rows - cut)
        self.place, self.layer, self.twin, self.across, self.along, self.corner = plane_places()
        self.copies = {}

    def push(self, index, slot, part, peer, own=False):
        target = self.slots.at[slot, part]
        source = self.own.at[part] if own else target
        self.copies[index] = send(
            source, target, self.sends.at[index], self.recvs.at[index], peer, self.layer
        )

    def start_twin(self):
        self.push(2, self.place, self.whole, self.twin, True)

    def start_links(self):
        self.push(0, self.place, self.whole, self.across, True)
        self.push(1, self.place, self.whole, self.along, True)

    def forward_near(self):
        self.copies[0].wait_recv()
        self.push(3, self.across, self.first, self.along)
        self.push(5, self.across, self.whole, self.twin)
        self.copies[1].wait_recv()
        self.push(4, self.along, self.second, self.across)
        self.push(6, self.along, self.whole, self.twin)

    def forward_far(self):
        self.copies[3].wait_recv()
        self.push(7, self.corner, self.first, self.twin)
        self.copies[4].wait_recv()
        self.push(8, self.corner, self.second, self.twin)

    def arrived(self, *indices):
        for index in indices:
            self.copies[index].wait_recv()

    def finish_sends(self):
        for index in range(9):
            self.copies[index].wait_send()


class Scatter:
    def __init__(
        self, parts, from_twin, half_across, half_along, whole_across, whole_along, sends, recvs, rows, cut, outgoing=None
    ):
        self.parts, self.from_twin = parts, from_twin
        self.outgoing = parts if outgoing is None else outgoing
        self.half_across, self.half_along = half_across, half_along
        self.whole_across, self.whole_along = whole_across, whole_along
        self.sends, self.recvs = sends, recvs
        self.first, self.second = pl.ds(0, cut), pl.ds(cut, rows - cut)
        self.place, self.layer, self.twin, self.across, self.along, self.corner = plane_places()
        self.places = (self.place, self.across, self.along, self.corner)
        self.slots = self.places if outgoing is None else (0, 1, 2, 3)
        self.copies = {}

    def push(self, index, source, target, peer):
        self.copies[index] = send(
            source, target, self.sends.at[index], self.recvs.at[index], peer, self.layer
        )

    def start_twin(self, *indices):
        for index in indices or (1, 2, 3, 0):
            self.push(index, self.outgoing.at[twin_of(self.places[index])], self.from_twin.at[index], self.twin)

    def add(self, slot, part, other):
        total = self.parts[slot, part].astype(full_type) + other.astype(full_type)
        self.parts[slot, part] = total.astype(self.parts.dtype)

    def merge_twin(self, index):
        self.copies[index].wait_recv()
        self.add(self.slots[index], slice(None), self.from_twin[index])

    def start_near(self):
        _, across, along, _ = self.slots
        self.merge_twin(1)
        self.push(6, self.parts.at[across, self.first], self.whole_across.at[self.first], self.across)
        self.merge_twin(2)
        self.push(7, self.parts.at[along, self.second], self.whole_along.at[self.second], self.along)

    def start_far(self):
        corner = self.slots[3]
        self.merge_twin(3)
        self.push(4, self.parts.at[corner, self.first], self.half_across, self.across)
        self.push(5, self.parts.at[corner, self.second], self.half_along, self.along)

    def forward(self):
        _, across, along, _ = self.slots
        self.copies[5].wait_recv()
        self.add(across, self.second, self.half_along[...])
        self.push(8, self.parts.at[across, self.second], self.whole_across.at[self.second], self.across)
        self.copies[4].wait_recv()
        self.add(along, self.first, self.half_across[...])
        self.push(9, self.parts.at[along, self.first], self.whole_along.at[self.first], self.along)

    def settle(self):
        for index in (0, 6, 8, 7, 9):
            self.copies[index].wait_recv()
        for index in range(10):
            self.copies[index].wait_send()

    def total(self, part=slice(None)):
        return (
            self.parts[self.slots[0], part].astype(full_type)
            + self.from_twin[0, part].astype(full_type)
            + (self.whole_across[part].astype(full_type) + self.whole_along[part].astype(full_type))
        )


def scatter_scratch(rows, cut, columns, lead=()):
    return [
        pltpu.VMEM(lead + (4, rows, columns), low_type),
        pltpu.VMEM(lead + (cut, columns), low_type),
        pltpu.VMEM(lead + (rows - cut, columns), low_type),
        pltpu.VMEM(lead + (rows, columns), low_type),
        pltpu.VMEM(lead + (rows, columns), low_type),
        pltpu.SemaphoreType.DMA(lead + (10,)),
        pltpu.SemaphoreType.DMA(lead + (10,)),
    ]


def iota(shape, axis):
    return lax.broadcasted_iota(jnp.int32, shape, axis)


def sample_picker():
    row, column = iota((128, 256), 0), iota((128, 256), 1)
    wanted = ((row >> 2) & 3) * 64 + (row >> 4) * 8 + (row & 3)
    return (column == wanted).astype(full_type).astype(low_type)


def slot_spreader():
    row, column = iota((32, 16), 0), iota((32, 16), 1)
    return jnp.where(((row & 7) < 4) & (column == (row >> 3) * 4 + (row & 7)), 1.0, 0.0).astype(low_type)


def head_window(head):
    start = lax.min(lax.div(head * HEAD_DIM, 128) * 128, D - 256)
    start = pl.multiple_of(start, 128)
    lane = iota((1, 256), 1) + start
    inside = (lane >= head * HEAD_DIM) & (lane < (head + 1) * HEAD_DIM)
    return start, inside.astype(full_type)


def window(ref, base, start):
    return ref[:, pl.ds(pl.multiple_of(base + start, 128), 256)]


def masked_probs(query, key, same):
    scores = jnp.where(same, contract(query, key, 1, 1) * HEAD_DIM ** (-0.5), -1e30)
    exponent = jnp.exp(scores - jnp.max(scores, axis=1, keepdims=True))
    return exponent / jnp.sum(exponent, axis=1, keepdims=True)


BLOCK = 64


def slot_numbers(lengths, shape, axis):
    position = iota(shape, axis)
    slot, end = jnp.zeros(shape, jnp.int32), 0
    for step in range(IMG_ROW):
        end = end + lengths[0, step]
        slot = slot + jnp.where(position >= end, 1, 0)
    return slot


def slot_onehot(slots):
    matched = (slots == iota((slots.shape[0], 8), 1)) & (slots < IMG_ROW)
    return jnp.where(matched, 1.0, 0.0).astype(low_type)


def block_part(step):
    return pl.ds(pl.multiple_of(step * BLOCK, BLOCK), BLOCK)


def spread_slots(onehot, modulation, index):
    return contract(onehot, modulation[index].astype(low_type), 1, 0)


def front_kernel(
    lengths,
    tokens,
    cotangent,
    conditions,
    bias_own,
    project,
    output,
    expand,
    modulate,
    packed,
    attend_in,
    mixed,
    attend_out,
    resid,
    feed_in,
    modulation,
    active_out,
    bias_expand,
    bias_shrink,
    weights_out,
    expand_out,
    grad_all,
    project_load,
    output_load,
    expand_load,
    modulate_load,
    weights_own,
    weights_all,
    expand_own,
    grad_own,
    cond_send,
    cond_plane,
    cond_all,
    part_send,
    twin_recv,
    part_recv,
    mod_send,
    mod_recv,
    bias_recv,
    bias_flat,
    small_sends,
    small_recvs,
    near_sends,
    near_recvs,
    base_sends,
    base_recvs,
    far_sends,
    far_recvs,
    grad_sends,
    grad_recvs,
    local_sems,
):
    place, layer, twin, across, along, corner = plane_places()
    places = (place, across, along, corner)
    plane = [lax.rem(place + step, GROUP) for step in range(1, GROUP)]
    column = [lax.rem(layer + step, DEPTH) for step in range(1, DEPTH)]
    pair = layer + 1 - 2 * lax.rem(layer, 2)
    inner = jnp.where((layer == 0) | (layer == DEPTH - 1), 0, 1)
    rows = weights_own.shape[0]
    third = rows // 3
    shard = bias_own.shape[1]
    columns = modulate_load.shape[1]
    units = expand_own.shape[2]

    def load(index, source, target):
        copy = pltpu.make_async_copy(source, target, local_sems.at[index])
        copy.start()
        return copy

    loads = [
        load(0, project, project_load),
        load(1, modulate, modulate_load),
        load(2, output, output_load),
        load(3, expand, expand_load),
    ]
    peers = [(peer, layer) for peer in plane] + [(place, peer) for peer in column]
    barrier = pltpu.get_barrier_semaphore()
    for peer in peers:
        pl.semaphore_signal(barrier, inc=1, device_id=peer, device_id_type=MESH)
    values = conditions[...].astype(full_type)
    active = (values * jax.nn.sigmoid(values)).astype(low_type).astype(full_type)
    cond_send[...] = jnp.zeros_like(cond_send)
    for step in range(GROUP):
        cond_send[step, 0:IMG_ROW, :] = active[:, step * rows : (step + 1) * rows]
    bias_recv[place] = bias_own[...].astype(low_type).astype(full_type)
    pl.semaphore_wait(barrier, len(peers))

    waits = []

    def exchange(base, peers, source, target):
        copies = []
        for step, peer in enumerate(peers):
            where = (peer, layer) if peers is plane else (place, peer)
            copies.append(
                send(source(peer), target, small_sends.at[base + step], small_recvs.at[base + step], *where)
            )
        waits.extend(copies)
        return copies

    def arrive(copies):
        for copy in copies:
            copy.wait_recv()

    cond_copies = exchange(0, plane, lambda peer: cond_send.at[peer], cond_plane.at[place])
    cond_plane[place] = cond_send[place]
    bias_copies = exchange(7, plane, lambda peer: bias_recv.at[place], bias_recv.at[place])
    loads[0].wait()
    weights_own[:, 0 : 3 * D] = project_load[...].astype(low_type)
    loads[2].wait()
    weights_own[:, 3 * D : 4 * D] = output_load[...].astype(low_type)
    second = pl.multiple_of(third * (1 + inner), 16)
    last = pl.multiple_of(third * (2 - inner), 16)
    near = Gather(weights_own, weights_all, near_sends, near_recvs, second, third, 32)
    base = Gather(weights_own, weights_all, base_sends, base_recvs, 0, third, 16)
    near.start_links()
    near.start_twin()
    base.start_twin()
    whole = pl.ds(last, third)

    def far_copy(index, slot, part, where):
        return send(
            weights_all.at[slot, part],
            weights_all.at[slot, part],
            far_sends.at[index],
            far_recvs.at[index],
            *where,
        )

    far = [
        send(
            weights_own.at[whole], weights_all.at[place, whole], far_sends.at[0], far_recvs.at[0], twin, layer
        )
    ]
    arrive(cond_copies)
    cond_copies = exchange(14, column, lambda peer: cond_plane, cond_all.at[layer])
    cond_all[layer] = cond_plane[...]
    weights_all[place] = weights_own[...]
    loads[1].wait()
    arrive(cond_copies)
    padded = cond_all[...].reshape(DEPTH * GROUP * 8, rows).astype(low_type)
    picked = contract(sample_picker(), padded, 1, 0).astype(low_type)
    active_out[...] = picked
    partial = contract(picked, modulate_load[...].astype(low_type), 1, 0)
    part_send[...] = partial.reshape(part_send.shape)
    twin_copies = []
    for step in (1, 2, 3, 0):
        twin_copies.append(
            send(
                part_send.at[twin_of(places[step])],
                twin_recv.at[step],
                small_sends.at[17 + step],
                small_recvs.at[17 + step],
                twin,
                layer,
            )
        )
    part_copies = []
    for step, copy in zip((1, 2, 3), twin_copies):
        copy.wait_recv()
        part_send[places[step]] = part_send[places[step]] + twin_recv[step]
        part_copies.append(
            send(
                part_send.at[places[step]],
                part_recv.at[step - 1],
                small_sends.at[21 + step],
                small_recvs.at[21 + step],
                places[step],
                layer,
            )
        )
    waits += twin_copies + part_copies
    base.start_links()
    arrive(bias_copies)
    for step in range(GROUP):
        bias_flat[:, step * shard : (step + 1) * shard] = bias_recv[step]
    start = pl.multiple_of(4 * D + FF + 2 * columns * lax.div(layer, 2), 128)
    both = bias_flat[:, pl.ds(start, 2 * columns)]
    bias_modulate = jnp.where(lax.rem(layer, 2) == 0, both[:, 0:columns], both[:, columns : 2 * columns])
    start = pl.multiple_of(3 * D + 2 * units * lax.div(place, 2), 128)
    both = bias_flat[:, pl.ds(start, 2 * units)]
    bias_expand[...] = jnp.where(lax.rem(place, 2) == 0, both[:, 0:units], both[:, units : 2 * units])
    bias_shrink[...] = bias_flat[:, 3 * D + FF : 4 * D + FF]
    arrive(twin_copies[3:] + part_copies)
    total = (part_send[place] + twin_recv[0]) + ((part_recv[0] + part_recv[1]) + part_recv[2]) + bias_modulate
    spread = contract(slot_spreader(), total.astype(low_type), 1, 0)
    mod_send[...] = spread.reshape(mod_send.shape)
    mod_copies = exchange(25, column, lambda peer: mod_send.at[peer], mod_recv.at[layer])
    mod_recv[layer] = mod_send[layer]

    near.forward_near()
    up = (place, pair)
    far.append(far_copy(1, across, near.whole, up))
    far.append(far_copy(2, along, near.whole, up))
    loads[3].wait()
    for step in range(GROUP):
        expand_own[step] = expand_load[:, step * units : (step + 1) * units].astype(low_type)
    arrive(mod_copies)
    half = D // 2
    for block in range(DEPTH):
        for step in range(3):
            piece, side = divmod(3 * block + step, 2)
            modulation[piece, :, side * half : (side + 1) * half] = mod_recv[block, :, step * half : (step + 1) * half]
    base.forward_near()
    near.forward_far()
    far.append(far_copy(3, corner, near.whole, up))
    slot_row = slot_numbers(lengths, (1, ROW), 1)
    slot_column = slot_numbers(lengths, (ROW, 1), 0)
    onehot = slot_onehot(slot_column)

    def first_step(step):
        part = pl.ds(step * BLOCK, BLOCK)
        picked = onehot[step * BLOCK : (step + 1) * BLOCK]
        normed, _ = normalize_rows(tokens[part, :].astype(full_type))
        attend_in[part, :] = (
            normed * (1.0 + spread_slots(picked, modulation, 1)) + spread_slots(picked, modulation, 0)
        ).astype(low_type)
        grad_own[part, :] = (spread_slots(picked, modulation, 5) * cotangent[part, :].astype(full_type)).astype(low_type)

    for step in range(ROW // BLOCK):
        first_step(step)
    base.forward_far()
    grad_gather = Gather(grad_own, grad_all, grad_sends, grad_recvs, 0, ROW, ROW // 2)
    grad_gather.start_links()
    grad_gather.start_twin()
    expand_copies = exchange(28, plane, lambda peer: expand_own.at[peer], expand_out.at[place])
    keeps = [
        load(4, grad_own, grad_all.at[place]),
        load(5, expand_own.at[place], expand_out.at[place]),
    ]
    for index, slot in ((1, across), (2, along), (3, corner)):
        far[index].wait_recv()
        far.append(far_copy(3 + index, slot, whole, (twin, layer)))
    near.arrived(2, 5, 6, 7, 8)
    base.arrived(2, 5, 6, 7, 8)
    for index in (0, 4, 5, 6):
        far[index].wait_recv()
    keeps.append(load(6, weights_all, weights_out))

    mixed[...] = jnp.zeros_like(mixed)

    def query_step(step, carry):
        where = pl.ds(pl.multiple_of(step * 384, 128), 384)
        values = contract(attend_in[...], weights_all[:, :, where].reshape(D, 384), 1, 0)
        packed[:, where] = values.astype(low_type)
        return carry

    def biased_step(step, base, carry):
        where = pl.ds(pl.multiple_of(base + step * 384, 128), 384)
        shift = bias_flat[:, pl.ds(pl.multiple_of(lax.div(base, 2) + step * 384, 128), 384)]
        values = contract(attend_in[...], weights_all[:, :, where].reshape(D, 384), 1, 0)
        packed[:, where] = (values + shift).astype(low_type)
        return carry

    lax.fori_loop(0, 3, lambda step, carry: biased_step(step, 0, carry), 0)
    lax.fori_loop(3, 6, query_step, 0)
    lax.fori_loop(0, 3, lambda step, carry: biased_step(step, 2 * D, carry), 0)
    same = slot_column == slot_row

    def head_step(head, carry):
        start, inside = head_window(head)
        keep = inside.astype(low_type)
        probs = masked_probs(window(packed, 0, start) * keep, window(packed, D, start), same)
        out = contract(probs.astype(low_type), window(packed, 2 * D, start) * keep, 1, 0)
        where = pl.ds(start, 256)
        mixed[:, where] = (mixed[:, where].astype(full_type) + out).astype(low_type)
        return carry

    lax.fori_loop(0, 8, head_step, 0, unroll=2)
    grad_gather.forward_near()
    lax.fori_loop(8, HEADS, head_step, 0, unroll=2)

    def out_step(step, carry):
        where = pl.ds(pl.multiple_of(step * 384, 128), 384)
        source = pl.ds(pl.multiple_of(3 * D + step * 384, 128), 384)
        shift = bias_flat[:, pl.ds(pl.multiple_of(2 * D + step * 384, 128), 384)]
        attend_out[:, where] = contract(mixed[...], weights_all[:, :, source].reshape(D, 384), 1, 0) + shift
        return carry

    lax.fori_loop(0, 3, out_step, 0)
    for step in range(ROW // BLOCK):
        part = pl.ds(step * BLOCK, BLOCK)
        picked = onehot[step * BLOCK : (step + 1) * BLOCK]
        joined = tokens[part, :].astype(full_type) + spread_slots(picked, modulation, 2) * attend_out[part, :]
        resid[part, :] = joined
        normed, _ = normalize_rows(joined)
        feed_in[part, :] = (
            normed * (1.0 + spread_slots(picked, modulation, 4)) + spread_slots(picked, modulation, 3)
        ).astype(low_type)
    grad_gather.forward_far()
    grad_gather.arrived(2, 5, 6, 7, 8)
    arrive(expand_copies)
    for gather in (near, base, grad_gather):
        gather.finish_sends()
    for copy in far + waits:
        copy.wait_send()
    for copy in keeps:
        copy.wait()


def front_call(lengths, tokens, cotangent, conditions, bias_own, project, output, expand, modulate):
    rows, columns = modulate.shape
    units = expand.shape[1] // GROUP
    shard = bias_own.shape[1]
    shape = jax.ShapeDtypeStruct
    dma = pltpu.SemaphoreType.DMA
    return pl.pallas_call(
        front_kernel,
        out_shape=(
            shape((ROW, 3 * D), low_type),
            shape((ROW, D), low_type),
            shape((ROW, D), low_type),
            shape((ROW, D), full_type),
            shape((ROW, D), full_type),
            shape((ROW, D), low_type),
            shape((6, 8, D), full_type),
            shape((GROUP * 16, rows), low_type),
            shape((1, units), full_type),
            shape((1, D), full_type),
            shape((GROUP, rows, 4 * D), low_type),
            shape((GROUP, rows, units), low_type),
            shape((GROUP, ROW, D), low_type),
        ),
        in_specs=[pl.BlockSpec(memory_space=pltpu.SMEM)] + [vmem()] * 4 + [anywhere()] * 4,
        out_specs=(vmem(),) * 10 + (anywhere(),) * 3,
        scratch_shapes=[
            pltpu.VMEM(project.shape, full_type),
            pltpu.VMEM(output.shape, full_type),
            pltpu.VMEM(expand.shape, full_type),
            pltpu.VMEM(modulate.shape, full_type),
            pltpu.VMEM((rows, 4 * D), low_type),
            pltpu.VMEM((GROUP, rows, 4 * D), low_type),
            pltpu.VMEM((GROUP, rows, units), low_type),
            pltpu.VMEM((ROW, D), low_type),
            pltpu.VMEM((GROUP, 8, rows), full_type),
            pltpu.VMEM((GROUP, 8, rows), full_type),
            pltpu.VMEM((DEPTH, GROUP, 8, rows), full_type),
            pltpu.VMEM((GROUP, 16, columns), full_type),
            pltpu.VMEM((4, 16, columns), full_type),
            pltpu.VMEM((3, 16, columns), full_type),
            pltpu.VMEM((DEPTH, 8, columns), full_type),
            pltpu.VMEM((DEPTH, 8, columns), full_type),
            pltpu.VMEM((GROUP, 1, shard), full_type),
            pltpu.VMEM((1, GROUP * shard), full_type),
            dma((35,)),
            dma((35,)),
            dma((9,)),
            dma((9,)),
            dma((9,)),
            dma((9,)),
            dma((7,)),
            dma((7,)),
            dma((9,)),
            dma((9,)),
            dma((7,)),
        ],
        compiler_params=pltpu.CompilerParams(
            collective_id=0, has_side_effects=True, vmem_limit_bytes=VMEM_BYTES
        ),
        name="forward",
    )(lengths, tokens, cotangent, conditions, bias_own, project, output, expand, modulate)


def feed_kernel(
    feed_own,
    expand,
    bias,
    shrink,
    grads,
    feed_parts,
    grad_feed_in,
    grad_shrink,
    grad_expand,
    grad_bias,
    feed_all,
    grad_all,
    hidden_all,
    pre_all,
    grad_parts,
    shrink_full,
    shrink_low,
    local_sems,
    feed_sends,
    feed_recvs,
    *scratch,
):
    grad_scatter = Scatter(grad_parts, *scratch, ROW, ROW // 2)
    place, layer, twin, across, along, corner = plane_places()
    feed_gather = Gather(feed_own, feed_all, feed_sends, feed_recvs, 0, ROW, ROW // 2)
    shrink_copy = pltpu.make_async_copy(shrink, shrink_full, local_sems.at[0])
    grad_copy = pltpu.make_async_copy(grads, grad_all, local_sems.at[1])
    shrink_copy.start()
    grad_copy.start()
    greet([(twin, layer), (across, layer), (along, layer)])
    feed_gather.start_links()
    feed_gather.start_twin()
    feed_all[place] = feed_own[...]
    shrink_copy.wait()
    shrink_low[...] = shrink_full[...].astype(low_type)
    grad_copy.wait()

    def through(slot):
        pre = contract(feed_all[slot], expand[...], 1, 0) + bias[...]
        tanh_part = jnp.tanh(tanh_scale * (pre + cubic_term * pre * pre * pre))
        hidden = (0.5 * pre * (1.0 + tanh_part)).astype(low_type)
        slope = 0.5 * (1.0 + tanh_part) + 0.5 * pre * (1.0 - tanh_part * tanh_part) * tanh_scale * (
            1.0 + 3.0 * cubic_term * pre * pre
        )
        hidden_all[slot] = hidden
        grad_hidden = contract(grad_all[slot], shrink_low[...], 1, 1)
        grad_pre = (grad_hidden * slope).astype(low_type)
        pre_all[slot] = grad_pre
        grad_parts[slot] = contract(grad_pre, expand[...], 1, 1).astype(low_type)

    through(place)
    feed_gather.arrived(2)
    through(twin)
    feed_gather.forward_near()
    through(across)
    through(along)
    feed_gather.arrived(5, 6)
    through(twin_of(across))
    feed_gather.forward_far()
    through(twin_of(along))
    grad_scatter.start_twin(1, 2)
    through(corner)
    grad_scatter.start_near()
    feed_gather.arrived(7, 8)
    through(twin_of(corner))
    grad_scatter.start_twin(3, 0)
    grad_scatter.start_far()

    units = hidden_all.shape[2]
    hidden = hidden_all[...].reshape(GROUP * ROW, units)
    grad_shrink[...] = contract(hidden, grad_all[...].reshape(GROUP * ROW, D), 0, 0).astype(low_type)
    grad_scatter.forward()
    grad_pre = pre_all[...].reshape(GROUP * ROW, units)
    grad_bias[...] = jnp.sum(grad_pre.astype(full_type), axis=0, keepdims=True)
    grad_expand[...] = contract(feed_all[...].reshape(GROUP * ROW, D), grad_pre, 0, 0).astype(low_type)

    def part_step(slot, carry):
        feed_parts[slot] = contract(hidden_all[slot], shrink_low[...], 1, 0).astype(low_type)
        return carry

    lax.fori_loop(0, GROUP, part_step, 0)
    grad_scatter.settle()
    grad_feed_in[...] = grad_scatter.total()
    feed_gather.finish_sends()


def feed_call(feed_own, expand, bias, shrink, grads):
    units = expand.shape[1]
    shape = jax.ShapeDtypeStruct
    dma = pltpu.SemaphoreType.DMA
    return pl.pallas_call(
        feed_kernel,
        out_shape=(
            shape((GROUP, ROW, D), low_type),
            shape((ROW, D), full_type),
            shape((units, D), low_type),
            shape((D, units), low_type),
            shape((1, units), full_type),
        ),
        in_specs=[vmem()] * 3 + [anywhere()] * 2,
        out_specs=(vmem(),) * 5,
        scratch_shapes=[
            pltpu.VMEM((GROUP, ROW, D), low_type),
            pltpu.VMEM((GROUP, ROW, D), low_type),
            pltpu.VMEM((GROUP, ROW, units), low_type),
            pltpu.VMEM((GROUP, ROW, units), low_type),
            pltpu.VMEM((GROUP, ROW, D), low_type),
            pltpu.VMEM((units, D), full_type),
            pltpu.VMEM((units, D), low_type),
            dma((2,)),
            dma((9,)),
            dma((9,)),
            *scatter_scratch(ROW, ROW // 2, D),
        ],
        compiler_params=pltpu.CompilerParams(
            collective_id=1, has_side_effects=True, vmem_limit_bytes=VMEM_BYTES
        ),
        name="feed_forward",
    )(feed_own, expand, bias, shrink, grads)


def sample_compactor():
    row, column = iota((16, 32), 0), iota((16, 32), 1)
    return (column == (row >> 2) * 8 + (row & 3)).astype(full_type).astype(low_type)


def sample_scatterer():
    row, column = iota((256, 128), 0), iota((256, 128), 1)
    wanted = ((row >> 3) & 7) * 16 + (row >> 6) * 4 + (row & 7)
    return jnp.where(((row & 7) < 4) & (column == wanted), 1.0, 0.0).astype(low_type)


def square_sum(values):
    values = values.astype(full_type)
    squares = values * values
    while squares.ndim > 2:
        squares = jnp.sum(squares, axis=0)
    return jnp.sum(jnp.sum(squares, axis=0, keepdims=True), axis=1, keepdims=True)


def slot_sums(onehot, values):
    high = values.astype(low_type)
    rest = (values - high.astype(full_type)).astype(low_type)
    return contract(onehot, high, 0, 0) + contract(onehot, rest, 0, 0)


def column_sum(values):
    return jnp.sum(values.astype(full_type), axis=0, keepdims=True)


BIAS_ROWS = 128
LANES = 128


def back_kernel(
    lengths,
    tokens,
    cotangent,
    modulation,
    packed,
    attend_in,
    mixed,
    attend_out,
    resid,
    grad_feed_in,
    bias_shrink,
    grad_bias_expand,
    active,
    modulate,
    full_weights,
    feed_parts_in,
    grad_shrink,
    grad_expand,
    block_output,
    token_grads,
    project_sum,
    output_sum,
    expand_sum,
    shrink_sum,
    bias_sum,
    modulate_sum,
    condition_sum,
    square_total,
    output_store,
    project_store,
    feed_parts,
    shrink_own,
    grad_resid,
    grad_attend,
    grad_mixed,
    grad_packed,
    slot_grads,
    project_own,
    output_own,
    expand_own,
    project_mid,
    output_mid,
    expand_mid,
    shrink_mid,
    bias_own,
    bias_recv,
    bias_layers,
    sample_send,
    sample_recv,
    group_all,
    term_send,
    term_recv,
    term_sum,
    square_send,
    square_recv,
    square_part,
    square_all,
    small_sends,
    small_recvs,
    pair_sends,
    pair_recvs,
    mid_sends,
    mid_recvs,
    local_sems,
    slots,
    *scratch,
):
    place, layer, *_ = plane_places()
    plane = [lax.rem(place + step, GROUP) for step in range(1, GROUP)]
    column = [lax.rem(layer + step, DEPTH) for step in range(1, DEPTH)]
    rows = output_own.shape[0]
    pair = layer + 1 - 2 * lax.rem(layer, 2)
    across_middle = DEPTH - 1 - layer
    edge = (layer == 0) | (layer == DEPTH - 1)
    middle = jnp.logical_not(edge)
    scale = HEAD_DIM ** (-0.5)

    chunks = []
    for step in range(4):
        part = pl.ds(step * rows, rows)
        chunks.append((shrink_own.at[part], shrink_sum.at[part], shrink_mid.at[part]))
    for step in range(4):
        part = pl.ds(2 * step, 2)
        chunks.append((expand_own.at[part], expand_sum.at[part], expand_mid.at[part]))
    chunks.append((output_own, output_sum, output_mid))
    for step in range(3):
        chunks.append((project_own.at[step], project_sum.at[step], project_mid.at[step]))

    def pair_copy(index, source):
        return pltpu.make_async_remote_copy(
            src_ref=source,
            dst_ref=chunks[index][1],
            send_sem=pair_sends.at[index],
            recv_sem=pair_recvs.at[index],
            device_id=(place, pair),
            device_id_type=MESH,
        )

    def middle_copy(index):
        return pltpu.make_async_remote_copy(
            src_ref=chunks[index][0],
            dst_ref=chunks[index][2],
            send_sem=mid_sends.at[index],
            recv_sem=mid_recvs.at[index],
            device_id=(place, across_middle),
            device_id_type=MESH,
        )

    def edge_send(*indices):
        @pl.when(edge)
        def _():
            for index in indices:
                pair_copy(index, chunks[index][0]).start()

    def middle_step(*indices):
        @pl.when(middle)
        def _():
            for index in indices:
                if index < len(chunks):
                    given, result, _ = chunks[index]
                    pair_copy(index, result).wait_recv()
                    given[...] = (given[...].astype(full_type) + result[...].astype(full_type)).astype(low_type)
                    middle_copy(index).start()
                if index > 0:
                    given, result, other = chunks[index - 1]
                    middle_copy(index - 1).wait()
                    result[...] = (given[...].astype(full_type) + other[...].astype(full_type)).astype(low_type)
                    pair_copy(index - 1, result).start()

    waits = []

    def exchange(base, peers, source, target):
        copies = []
        for step, peer in enumerate(peers):
            where = (peer, layer) if peers is plane else (place, peer)
            copies.append(
                send(source(peer), target, small_sends.at[base + step], small_recvs.at[base + step], *where)
            )
        waits.extend(copies)
        return copies

    def arrive(copies):
        for copy in copies:
            copy.wait_recv()

    def load(index, source, target):
        copy = pltpu.make_async_copy(source, target, local_sems.at[index])
        copy.start()
        return copy

    feed_scatter = Scatter(feed_parts, *scratch[0:7], ROW, ROW // 2, outgoing=feed_parts_in)
    output_scatter = Scatter(output_store, *scratch[7:14], rows, 64)
    project_scatters = [
        Scatter(project_store.at[step], *(ref.at[step] for ref in scratch[14:21]), rows, 64) for step in range(3)
    ]
    shrink_load = load(0, grad_shrink, shrink_own)
    expand_load = load(1, grad_expand.at[place], expand_own.at[place])
    output_load = load(2, full_weights.at[:, :, pl.ds(3 * D, D)], output_store)
    feed_loads = [
        load(3 + step, feed_parts_in.at[feed_scatter.places[step]], feed_parts.at[step]) for step in range(4)
    ]
    project_loads = [
        load(7 + step, full_weights.at[:, :, pl.ds(step * D, D)], project_store.at[step]) for step in range(3)
    ]

    greet([(peer, layer) for peer in plane] + [(place, peer) for peer in column])

    feed_scatter.start_twin()
    expand_copies = exchange(0, plane, lambda peer: grad_expand.at[peer], expand_own.at[place])
    shrink_load.wait()
    edge_send(0, 1, 2, 3)
    slot_grads[...] = jnp.zeros_like(slot_grads)
    bias_own[...] = jnp.zeros_like(bias_own)
    grad_packed[...] = jnp.zeros_like(grad_packed)

    slot_row = slot_numbers(lengths, (1, ROW), 1)
    slot_column = slot_numbers(lengths, (ROW, 1), 0)
    slots[...] = slot_column

    def block_parts(step):
        part = block_part(step)
        return part, slot_onehot(slots[part, :])

    def feed_step(step, carry):
        part, onehot = block_parts(step)
        normed, inverse = normalize_rows(resid[part, :])
        grad_in = grad_feed_in[part, :]
        slot_grads[3] += slot_sums(onehot, grad_in)
        slot_grads[4] += slot_sums(onehot, grad_in * normed)
        grad = cotangent[part, :].astype(full_type) + normalize_back(
            grad_in * (1.0 + spread_slots(onehot, modulation, 4)), normed, inverse
        )
        grad_resid[part, :] = grad
        slot_grads[2] += slot_sums(onehot, grad * attend_out[part, :])
        grad_attend[part, :] = (spread_slots(onehot, modulation, 2) * grad).astype(low_type)
        return carry

    lax.fori_loop(0, ROW // BLOCK, feed_step, 0)
    for copy in feed_loads:
        copy.wait()
    feed_scatter.start_far()
    feed_scatter.start_near()
    output_load.wait()
    grad_mixed[...] = contract(grad_attend[...], output_store[...].reshape(D, D), 1, 1).astype(low_type)
    middle_step(0)

    same = slot_column == slot_row

    def head_step(head, carry):
        start, inside = head_window(head)
        keep = inside.astype(low_type)
        query = window(packed, 0, start) * keep
        key = window(packed, D, start)
        value = window(packed, 2 * D, start)
        grad = window(grad_mixed, 0, start) * keep
        probs = masked_probs(query, key, same)
        grad_probs = contract(grad, value, 1, 1)
        grad_scores = probs * (grad_probs - jnp.sum(probs * grad_probs, axis=1, keepdims=True))
        grad_scores = grad_scores.astype(low_type)

        def put(base, values):
            where = pl.ds(pl.multiple_of(base + start, 128), 256)
            grad_packed[:, where] = (grad_packed[:, where].astype(full_type) + values).astype(low_type)

        put(0, contract(grad_scores, key * keep, 1, 0) * scale)
        put(D, contract(grad_scores, query, 0, 0) * scale)
        put(2 * D, contract(probs.astype(low_type), grad, 0, 0))
        return carry

    def heads(first, last):
        lax.fori_loop(first, last, head_step, 0, unroll=2)

    def weight_step(left, right, target, step, carry):
        where = pl.ds(pl.multiple_of(step * 384, 128), 384)
        values = contract(left[...], right[:, where], 0, 0).astype(low_type)
        target[:, :, where] = values.reshape(GROUP, rows, 384)
        return carry

    heads(0, 4)
    middle_step(1)
    lax.fori_loop(0, 3, functools.partial(weight_step, mixed, grad_attend, output_store), 0)
    output_scatter.start_twin()
    heads(4, 8)
    middle_step(2)
    output_scatter.start_far()
    output_scatter.start_near()
    heads(8, 12)
    feed_scatter.forward()
    middle_step(3)
    arrive(expand_copies)
    expand_load.wait()
    edge_send(4, 5)
    heads(12, 16)
    middle_step(4)
    for copy in project_loads:
        copy.wait()
    for step in range(3):
        piece = contract(
            grad_packed[:, step * D : (step + 1) * D], project_store[step].reshape(D, D), 1, 1
        )
        token_grads[...] = piece if step == 0 else token_grads[...] + piece
    for step in range(3):
        lax.fori_loop(
            0,
            3,
            functools.partial(
                weight_step, attend_in, grad_packed.at[:, pl.ds(step * D, D)], project_store.at[step]
            ),
            0,
        )
        project_scatters[step].start_twin()
    project_scatters[0].start_far()
    project_scatters[0].start_near()
    middle_step(5)

    def attend_step(step, carry):
        part, onehot = block_parts(step)
        normed, inverse = normalize_rows(tokens[part, :].astype(full_type))
        grad_in = token_grads[part, :]
        slot_grads[0] += slot_sums(onehot, grad_in)
        slot_grads[1] += slot_sums(onehot, grad_in * normed)
        token_grads[part, :] = grad_resid[part, :] + normalize_back(
            grad_in * (1.0 + spread_slots(onehot, modulation, 1)), normed, inverse
        )
        return carry

    lax.fori_loop(0, ROW // BLOCK, attend_step, 0)
    project_scatters[1].start_far()
    project_scatters[1].start_near()
    output_scatter.forward()
    feed_scatter.settle()

    def put_rows(base, values):
        for step in range(values.shape[1] // LANES):
            bias_own[base + step : base + step + 1, :] = values[:, step * LANES : (step + 1) * LANES]

    def output_step(step, carry):
        part, onehot = block_parts(step)
        feed_out = feed_scatter.total(part) + bias_shrink[...]
        grad = cotangent[part, :].astype(full_type)
        gate = spread_slots(onehot, modulation, 5)
        block_output[part, :] = (resid[part, :] + gate * feed_out).astype(low_type)
        slot_grads[5] += slot_sums(onehot, grad * feed_out)
        return carry + column_sum((gate * grad).astype(low_type))

    feed_bias = lax.fori_loop(0, ROW // BLOCK, output_step, jnp.zeros((1, D), full_type))
    rounded = [slot_grads[step].astype(low_type).astype(full_type) for step in range(6)]
    half = D // 2
    for block in range(DEPTH):
        for step in range(3):
            piece, side = divmod(3 * block + step, 2)
            sample_send[block, :, step * half : (step + 1) * half] = rounded[piece][:, side * half : (side + 1) * half]
    sample_copies = exchange(7, column, lambda peer: sample_send.at[peer], sample_recv.at[layer])
    sample_recv[layer] = sample_send[layer]
    edge_send(6, 7)
    put_rows(0, column_sum(grad_packed[:, 0:D]))
    put_rows(9, column_sum(grad_packed[:, 2 * D : 3 * D]))
    put_rows(18, column_sum(grad_attend[...]))
    put_rows(27, feed_bias)
    for step in range(6):
        put_rows(36 + 9 * step, column_sum(rounded[step]))
    bias_recv[place] = bias_own[pl.ds(pl.multiple_of(place * 16, 16), 16), :]
    bias_copies = exchange(
        10, plane, lambda peer: bias_own.at[pl.ds(pl.multiple_of(peer * 16, 16), 16)], bias_recv.at[place]
    )
    middle_step(6)
    output_scatter.settle()
    output_own[...] = output_scatter.total().astype(low_type)
    arrive(sample_copies)
    group = contract(sample_compactor(), sample_recv[...].reshape(DEPTH * 8, sample_recv.shape[2]).astype(low_type), 1, 0)
    group_all[place] = group.astype(low_type)
    group_copies = exchange(17, plane, lambda peer: group_all.at[place], group_all.at[place])
    project_scatters[2].start_far()
    project_scatters[2].start_near()
    edge_send(8)
    middle_step(7)
    project_scatters[0].forward()
    arrive(bias_copies)
    total = bias_recv[0]
    for step in range(1, GROUP):
        total = total + bias_recv[step]
    bias_layers[layer, 0:16, :] = total
    bias_layers[layer, 16:24, :] = jnp.zeros((8, LANES), full_type)
    for step in range(4):
        bias_layers[layer, 16 + step : 17 + step, :] = grad_bias_expand[:, step * LANES : (step + 1) * LANES]
    bias_layers[layer, 20:21, 0:64] = grad_bias_expand[:, 512:576]
    layer_copies = exchange(24, column, lambda peer: bias_layers.at[layer], bias_layers.at[layer])
    middle_step(8)
    project_scatters[1].forward()

    arrive(group_copies)
    every = group_all[...].reshape(GROUP * 16, group_all.shape[2])
    modulate_sum[...] = contract(active[...], every, 0, 0)
    spread = contract(sample_scatterer(), every, 1, 0).astype(low_type)
    terms = contract(spread, modulate[...].astype(low_type), 1, 1)
    term_send[...] = terms.reshape(term_send.shape)
    term_copies = exchange(27, column, lambda peer: term_send.at[peer], term_recv.at[layer])
    term_recv[layer] = term_send[layer]
    project_scatters[0].settle()
    project_own[0] = project_scatters[0].total().astype(low_type)
    edge_send(9)
    middle_step(9)
    project_scatters[2].forward()
    arrive(layer_copies)
    total = (bias_layers[0] + bias_layers[1]) + (bias_layers[2] + bias_layers[3])
    bias_sum[place] = total
    bias_copies = exchange(30, plane, lambda peer: bias_sum.at[place], bias_sum.at[place])
    arrive(term_copies)
    term_sum[...] = (term_recv[0] + term_recv[1]) + (term_recv[2] + term_recv[3])
    last_copies = exchange(37, plane, lambda peer: term_sum.at[peer], condition_sum.at[place])
    condition_sum[place] = term_sum[place]
    project_scatters[1].settle()
    project_own[1] = project_scatters[1].total().astype(low_type)
    edge_send(10)
    middle_step(10)
    project_scatters[2].settle()
    project_own[2] = project_scatters[2].total().astype(low_type)
    edge_send(11)
    modulate_square = square_sum(modulate_sum[...])
    arrive(bias_copies)
    middle_step(11, 12)

    @pl.when(edge)
    def _():
        for index in range(len(chunks)):
            pair_copy(index, chunks[index][0]).wait()

    @pl.when(middle)
    def _():
        for index in range(len(chunks)):
            pair_copy(index, chunks[index][1]).wait_send()

    trunk = (
        square_sum(project_sum[...])
        + square_sum(output_sum[...])
        + square_sum(expand_sum[...])
        + square_sum(shrink_sum[...])
        + square_sum(bias_sum[place])
    )
    square_send[0] = jnp.broadcast_to(trunk, (8, 128))
    square_send[1] = jnp.broadcast_to(modulate_square, (8, 128))
    square_copies = exchange(44, plane, lambda peer: square_send, square_recv.at[place])
    square_recv[place] = square_send[...]
    arrive(square_copies)
    both = square_recv[0]
    for step in range(1, GROUP):
        both = both + square_recv[step]
    square_part[...] = both
    square_all[layer] = both
    square_copies = exchange(51, column, lambda peer: square_part, square_all.at[layer])
    arrive(square_copies)
    square_total[...] = both[0] + ((square_all[0, 1] + square_all[1, 1]) + (square_all[2, 1] + square_all[3, 1]))
    arrive(last_copies)
    for copy in waits:
        copy.wait_send()


def back_call(
    lengths,
    tokens,
    cotangent,
    modulation,
    packed,
    attend_in,
    mixed,
    attend_out,
    resid,
    grad_feed_in,
    bias_shrink,
    grad_bias_expand,
    active,
    modulate,
    full_weights,
    feed_parts,
    grad_shrink,
    grad_expand,
):
    rows, columns = modulate.shape
    units = grad_expand.shape[2]
    shape = jax.ShapeDtypeStruct
    dma = pltpu.SemaphoreType.DMA
    return pl.pallas_call(
        back_kernel,
        out_shape=(
            shape((ROW, D), low_type),
            shape((ROW, D), full_type),
            shape((3, rows, D), low_type),
            shape((rows, D), low_type),
            shape((GROUP, rows, units), low_type),
            shape((units, D), low_type),
            shape((GROUP, 24, LANES), full_type),
            shape((rows, columns), full_type),
            shape((GROUP, 8, rows), full_type),
            shape((8, LANES), full_type),
        ),
        in_specs=[pl.BlockSpec(memory_space=pltpu.SMEM)] + [vmem()] * 13 + [anywhere()] * 4,
        out_specs=(vmem(),) * 10,
        scratch_shapes=[
            pltpu.VMEM((GROUP, rows, D), low_type),
            pltpu.VMEM((3, GROUP, rows, D), low_type),
            pltpu.VMEM((4, ROW, D), low_type),
            pltpu.VMEM((units, D), low_type),
            pltpu.VMEM((ROW, D), full_type),
            pltpu.VMEM((ROW, D), low_type),
            pltpu.VMEM((ROW, D), low_type),
            pltpu.VMEM((ROW, 3 * D), low_type),
            pltpu.VMEM((6, 8, D), full_type),
            pltpu.VMEM((3, rows, D), low_type),
            pltpu.VMEM((rows, D), low_type),
            pltpu.VMEM((GROUP, rows, units), low_type),
            pltpu.VMEM((3, rows, D), low_type),
            pltpu.VMEM((rows, D), low_type),
            pltpu.VMEM((GROUP, rows, units), low_type),
            pltpu.VMEM((units, D), low_type),
            pltpu.VMEM((BIAS_ROWS, LANES), full_type),
            pltpu.VMEM((GROUP, 16, LANES), full_type),
            pltpu.VMEM((DEPTH, 24, LANES), full_type),
            pltpu.VMEM((DEPTH, 8, columns), full_type),
            pltpu.VMEM((DEPTH, 8, columns), full_type),
            pltpu.VMEM((GROUP, 16, columns), low_type),
            pltpu.VMEM((DEPTH, GROUP, 8, rows), full_type),
            pltpu.VMEM((DEPTH, GROUP, 8, rows), full_type),
            pltpu.VMEM((GROUP, 8, rows), full_type),
            pltpu.VMEM((2, 8, LANES), full_type),
            pltpu.VMEM((GROUP, 2, 8, LANES), full_type),
            pltpu.VMEM((2, 8, LANES), full_type),
            pltpu.VMEM((DEPTH, 2, 8, LANES), full_type),
            dma((54,)),
            dma((54,)),
            dma((12,)),
            dma((12,)),
            dma((12,)),
            dma((12,)),
            dma((10,)),
            pltpu.VMEM((ROW, 1), jnp.int32),
            *scatter_scratch(ROW, ROW // 2, D),
            *scatter_scratch(rows, 64, D),
            *scatter_scratch(rows, 64, D, (3,)),
        ],
        compiler_params=pltpu.CompilerParams(
            collective_id=2, has_side_effects=True, vmem_limit_bytes=VMEM_BYTES
        ),
        name="backward",
    )(
        lengths,
        tokens,
        cotangent,
        modulation,
        packed,
        attend_in,
        mixed,
        attend_out,
        resid,
        grad_feed_in,
        bias_shrink,
        grad_bias_expand,
        active,
        modulate,
        full_weights,
        feed_parts,
        grad_shrink,
        grad_expand,
    )


def plane_body(
    tokens,
    conditions,
    image_lengths,
    cotangent,
    project_weight,
    project_moment,
    project_square,
    output_weight,
    output_moment,
    output_square,
    expand_weight,
    expand_moment,
    expand_square,
    shrink_weight,
    shrink_moment,
    shrink_square,
    modulate_weight,
    modulate_moment,
    modulate_square,
    bias_vector,
    bias_moment,
    bias_square,
):
    place = lax.axis_index("dp")
    shard = bias_vector.shape[0]
    units = FF // GROUP
    (
        packed,
        attend_in,
        mixed,
        attend_out,
        resid,
        feed_in,
        modulation,
        active,
        bias_expand,
        bias_shrink,
        full_weights,
        own_expand,
        grad_all,
    ) = front_call(
        image_lengths,
        tokens,
        cotangent,
        conditions,
        bias_vector[None, :],
        project_weight,
        output_weight,
        expand_weight,
        modulate_weight,
    )
    feed_parts, grad_feed_in, grad_shrink, grad_expand, grad_bias_expand = feed_call(
        feed_in, own_expand.reshape(D, units), bias_expand, shrink_weight, grad_all
    )
    rows = project_weight.shape[0]
    (
        block_output,
        token_grads,
        sum_project,
        sum_output,
        sum_expand,
        sum_shrink,
        bias_sums,
        sum_modulate,
        condition_parts,
        square_total,
    ) = back_call(
        image_lengths,
        tokens,
        cotangent,
        modulation,
        packed,
        attend_in,
        mixed,
        attend_out,
        resid,
        grad_feed_in,
        bias_shrink,
        grad_bias_expand,
        active,
        modulate_weight,
        full_weights,
        feed_parts,
        grad_shrink,
        grad_expand.reshape(GROUP, rows, units),
    )
    square_total = square_total[0, 0]
    sum_project = sum_project.transpose(1, 0, 2).reshape(rows, 3 * D).astype(jnp.float32)
    sum_output = sum_output.astype(jnp.float32)
    sum_expand = sum_expand.transpose(1, 0, 2).reshape(rows, FF).astype(jnp.float32)
    sum_shrink = sum_shrink.astype(jnp.float32)
    common = bias_sums[:, 0:16].reshape(BIAS_ROWS * LANES)
    every_bias = jnp.concatenate(
        [common[0 : 3 * D], bias_sums[:, 16:24].reshape(GROUP, 8 * LANES)[:, 0:units].reshape(FF), common[3 * D : 10 * D]]
    )
    sum_bias = lax.dynamic_slice_in_dim(every_bias, place * shard, shard)
    condition_sum = condition_parts[:, 0:IMG_ROW].transpose(1, 0, 2).reshape(IMG_ROW, D)
    own_conditions = conditions.astype(jnp.float32)
    sigmoid_part = jax.nn.sigmoid(own_conditions)
    condition_grads = condition_sum * (sigmoid_part * (1.0 + own_conditions * (1.0 - sigmoid_part)))
    global_norm = jnp.sqrt(square_total)
    clip_factor = jnp.minimum(1.0, 1.0 / (global_norm + 1e-06))
    updated = (
        *adam_update(project_weight, project_moment, project_square, sum_project * clip_factor, D ** (-0.5)),
        *adam_update(output_weight, output_moment, output_square, sum_output * clip_factor, (D // 64) ** (-0.5)),
        *adam_update(expand_weight, expand_moment, expand_square, sum_expand * clip_factor, D ** (-0.5)),
        *adam_update(shrink_weight, shrink_moment, shrink_square, sum_shrink * clip_factor, FF ** (-0.5)),
        *adam_update(modulate_weight, modulate_moment, modulate_square, sum_modulate * clip_factor, D ** (-0.5)),
        *adam_update(bias_vector, bias_moment, bias_square, sum_bias * clip_factor, 0.3),
    )
    return (block_output, token_grads, condition_grads, global_norm, *updated)


def generic_body(
    tokens,
    conditions,
    image_lengths,
    cotangent,
    project_weight,
    project_moment,
    project_square,
    output_weight,
    output_moment,
    output_square,
    expand_weight,
    expand_moment,
    expand_square,
    shrink_weight,
    shrink_moment,
    shrink_square,
    modulate_weight,
    modulate_moment,
    modulate_square,
    bias_vector,
    bias_moment,
    bias_square,
):
    low_type = jnp.bfloat16
    group_size = lax.axis_size("mod")
    group_place = lax.axis_index("mod")
    columns = 6 * D // group_size
    full_project, full_output, full_expand, full_shrink, full_modulate, full_bias = (
        lax.all_gather(project_weight.astype(low_type), "dp", axis=0, tiled=True),
        lax.all_gather(output_weight.astype(low_type), "dp", axis=0, tiled=True),
        lax.all_gather(expand_weight.astype(low_type), "dp", axis=0, tiled=True),
        lax.all_gather(shrink_weight.astype(low_type), "dp", axis=0, tiled=True),
        lax.all_gather(modulate_weight.astype(low_type), "dp", axis=0, tiled=True),
        lax.all_gather(bias_vector.astype(low_type), "dp", axis=0, tiled=True),
    )
    bias_full = full_bias.astype(jnp.float32)
    bias_query = bias_full[0:D]
    bias_value = bias_full[D : 2 * D]
    bias_output = bias_full[2 * D : 3 * D]
    bias_expand = bias_full[3 * D : 3 * D + FF]
    bias_shrink = bias_full[3 * D + FF : 4 * D + FF]
    bias_modulate = lax.dynamic_slice_in_dim(bias_full, 4 * D + FF + group_place * columns, columns)
    group_conditions = lax.all_gather(conditions, "mod", axis=0, tiled=True)
    activated = jax.nn.silu(group_conditions.astype(jnp.float32)).astype(low_type)
    group_mod = (contract(activated, full_modulate, 1, 0) + bias_modulate).astype(low_type)
    own_mod = lax.all_to_all(group_mod, "mod", split_axis=0, concat_axis=1, tiled=True)
    slots = jnp.arange(IMG_ROW, dtype=jnp.int32)
    ends = jnp.sum(
        jnp.where(slots[:, None] <= slots[None, :], image_lengths[0][:, None], 0), axis=0, dtype=jnp.int32
    )
    positions = jnp.arange(ROW, dtype=jnp.int32)
    slot_of = jnp.sum(
        (positions[:, None] >= ends[None, :]).astype(jnp.int32), axis=1, dtype=jnp.int32
    )
    slot_match = slot_of[:, None] == jnp.arange(IMG_ROW, dtype=jnp.int32)[None, :]
    same_image = slot_of[:, None] == slot_of[None, :]
    per_token = contract(slot_match.astype(low_type), own_mod, 1, 0)
    shift_attend = per_token[:, 0:D]
    scale_attend = per_token[:, D : 2 * D]
    gate_attend = per_token[:, 2 * D : 3 * D]
    shift_feed = per_token[:, 3 * D : 4 * D]
    scale_feed = per_token[:, 4 * D : 5 * D]
    gate_feed = per_token[:, 5 * D : 6 * D]
    inputs = tokens.astype(jnp.float32)
    normed_attend, inverse_attend = normalize_rows(inputs)
    attend_in = (normed_attend * (1.0 + scale_attend) + shift_attend).astype(low_type)
    projected = contract(attend_in, full_project, 1, 0)
    query = (projected[:, 0:D] + bias_query).astype(low_type)
    keys = projected[:, D : 2 * D].astype(low_type)
    values = (projected[:, 2 * D : 3 * D] + bias_value).astype(low_type)
    head_scale = HEAD_DIM ** (-0.5)

    def split_heads(matrix):
        return matrix.reshape(ROW, HEADS, HEAD_DIM).transpose(1, 0, 2)

    def head_scores(query_head, key_head):
        return jnp.where(same_image, contract(query_head, key_head, 1, 1) * head_scale, -1e30)

    def attend_head(pieces):
        query_head, key_head, value_head = pieces
        scores = head_scores(query_head, key_head)
        row_top = jnp.max(scores, axis=1, keepdims=True)
        exponent = jnp.exp(scores - row_top)
        total = jnp.sum(exponent, axis=1, keepdims=True)
        probs = (exponent / total).astype(low_type)
        return (contract(probs, value_head, 1, 0), (row_top + jnp.log(total))[:, 0])

    heads_query = split_heads(query)
    heads_key = split_heads(keys)
    heads_value = split_heads(values)
    mixed_heads, log_totals = lax.map(attend_head, (heads_query, heads_key, heads_value))
    mixed = merge_heads(mixed_heads).astype(low_type)
    attend_out = contract(mixed, full_output, 1, 0) + bias_output
    resid = inputs + gate_attend * attend_out
    normed_feed, inverse_feed = normalize_rows(resid)
    feed_in = (normed_feed * (1.0 + scale_feed) + shift_feed).astype(low_type)
    hidden_pre = contract(feed_in, full_expand, 1, 0) + bias_expand
    tanh_part = jnp.tanh(
        tanh_scale * (hidden_pre + cubic_term * hidden_pre * hidden_pre * hidden_pre)
    )
    hidden = (0.5 * hidden_pre * (1.0 + tanh_part)).astype(low_type)
    feed_out = contract(hidden, full_shrink, 1, 0) + bias_shrink
    block_output = (resid + gate_feed * feed_out).astype(low_type)
    grad_out = cotangent.astype(jnp.float32)
    grad_gate_feed = grad_out * feed_out
    grad_feed = (gate_feed * grad_out).astype(low_type)
    grad_shrink = contract(hidden, grad_feed, 0, 0)
    grad_hidden = contract(grad_feed, full_shrink, 1, 1)
    slope = 0.5 * (1.0 + tanh_part) + 0.5 * hidden_pre * (
        1.0 - tanh_part * tanh_part
    ) * tanh_scale * (1.0 + 3.0 * cubic_term * hidden_pre * hidden_pre)
    grad_pre = (grad_hidden * slope).astype(low_type)
    grad_expand = contract(feed_in, grad_pre, 0, 0)
    grad_feed_in = contract(grad_pre, full_expand, 1, 1)
    grad_scale_feed = grad_feed_in * normed_feed
    grad_resid = grad_out + normalize_back(
        grad_feed_in * (1.0 + scale_feed), normed_feed, inverse_feed
    )
    grad_gate_attend = grad_resid * attend_out
    grad_attend = (gate_attend * grad_resid).astype(low_type)
    grad_output = contract(mixed, grad_attend, 0, 0)
    grad_mixed = contract(grad_attend, full_output, 1, 1).astype(low_type)

    def attend_back(pieces):
        query_head, key_head, value_head, grad_head, log_total = pieces
        probs = jnp.exp(head_scores(query_head, key_head) - log_total[:, None])
        grad_value = contract(probs.astype(low_type), grad_head, 0, 0)
        grad_probs = contract(grad_head, value_head, 1, 1)
        grad_scores = (
            probs * (grad_probs - jnp.sum(probs * grad_probs, axis=1, keepdims=True))
        ).astype(low_type)
        grad_query = contract(grad_scores, key_head, 1, 0) * head_scale
        grad_key = contract(grad_scores, query_head, 0, 0) * head_scale
        return (grad_query, grad_key, grad_value)

    heads_grad_query, heads_grad_key, heads_grad_value = lax.map(
        attend_back, (heads_query, heads_key, heads_value, split_heads(grad_mixed), log_totals)
    )
    grad_projected = jnp.concatenate(
        [merge_heads(heads_grad_query), merge_heads(heads_grad_key), merge_heads(heads_grad_value)],
        axis=1,
    ).astype(low_type)
    grad_project = contract(attend_in, grad_projected, 0, 0)
    grad_attend_in = contract(grad_projected, full_project, 1, 1)
    grad_scale_attend = grad_attend_in * normed_attend
    token_grads = grad_resid + normalize_back(
        grad_attend_in * (1.0 + scale_attend), normed_attend, inverse_attend
    )
    token_mod_grads = jnp.concatenate(
        [
            grad_attend_in,
            grad_scale_attend,
            grad_gate_attend,
            grad_feed_in,
            grad_scale_feed,
            grad_gate_feed,
        ],
        axis=1,
    )
    sample_grads = contract(slot_match.astype(jnp.float32), token_mod_grads, 0, 0).astype(low_type)
    group_grads = lax.all_to_all(sample_grads, "mod", split_axis=1, concat_axis=0, tiled=True)
    grad_modulate = contract(activated, group_grads, 0, 0)
    grad_bias_modulate = jnp.sum(group_grads, axis=0, dtype=jnp.float32)
    condition_terms = contract(group_grads, full_modulate, 1, 1)
    condition_sum = lax.psum_scatter(
        condition_terms.astype(jnp.bfloat16), "mod", scatter_dimension=0, tiled=True
    ).astype(jnp.float32)
    own_conditions = conditions.astype(jnp.float32)
    sigmoid_part = jax.nn.sigmoid(own_conditions)
    condition_grads = condition_sum * (sigmoid_part * (1.0 + own_conditions * (1.0 - sigmoid_part)))
    modulate_bias_grad = lax.dynamic_update_slice_in_dim(
        jnp.zeros((6 * D,), jnp.float32), grad_bias_modulate, group_place * columns, 0
    )
    grad_bias = jnp.concatenate(
        [
            jnp.sum(grad_projected[:, 0:D], axis=0, dtype=jnp.float32),
            jnp.sum(grad_projected[:, 2 * D : 3 * D], axis=0, dtype=jnp.float32),
            jnp.sum(grad_attend, axis=0, dtype=jnp.float32),
            jnp.sum(grad_pre, axis=0, dtype=jnp.float32),
            jnp.sum(grad_feed, axis=0, dtype=jnp.float32),
            modulate_bias_grad,
        ],
        axis=0,
    )
    summed = (
        lax.psum_scatter(
            grad_project.astype(jnp.bfloat16), "dp", scatter_dimension=0, tiled=True
        ).astype(jnp.float32),
        lax.psum_scatter(
            grad_output.astype(jnp.bfloat16), "dp", scatter_dimension=0, tiled=True
        ).astype(jnp.float32),
        lax.psum_scatter(
            grad_expand.astype(jnp.bfloat16), "dp", scatter_dimension=0, tiled=True
        ).astype(jnp.float32),
        lax.psum_scatter(
            grad_shrink.astype(jnp.bfloat16), "dp", scatter_dimension=0, tiled=True
        ).astype(jnp.float32),
        lax.psum_scatter(
            grad_modulate.astype(jnp.bfloat16), "dp", scatter_dimension=0, tiled=True
        ).astype(jnp.float32),
        lax.psum_scatter(
            grad_bias.astype(jnp.bfloat16), "dp", scatter_dimension=0, tiled=True
        ).astype(jnp.float32),
    )
    sum_project, sum_output, sum_expand, sum_shrink, sum_bias = (
        lax.psum(summed[0].astype(jnp.bfloat16), "mod").astype(jnp.float32),
        lax.psum(summed[1].astype(jnp.bfloat16), "mod").astype(jnp.float32),
        lax.psum(summed[2].astype(jnp.bfloat16), "mod").astype(jnp.float32),
        lax.psum(summed[3].astype(jnp.bfloat16), "mod").astype(jnp.float32),
        lax.psum(summed[5].astype(jnp.bfloat16), "mod").astype(jnp.float32),
    )
    sum_modulate = summed[4]
    trunk_square = (
        jnp.sum(sum_project * sum_project)
        + jnp.sum(sum_output * sum_output)
        + jnp.sum(sum_expand * sum_expand)
        + jnp.sum(sum_shrink * sum_shrink)
        + jnp.sum(sum_bias * sum_bias)
    )
    totals = lax.psum((trunk_square, jnp.sum(sum_modulate * sum_modulate)), ("dp", "mod"))
    global_norm = jnp.sqrt(totals[0] / group_size + totals[1])
    clip_factor = jnp.minimum(1.0, 1.0 / (global_norm + 1e-06))
    next_project, first_project, second_project = adam_update(
        project_weight, project_moment, project_square, sum_project * clip_factor, D ** (-0.5)
    )
    next_output, first_output, second_output = adam_update(
        output_weight, output_moment, output_square, sum_output * clip_factor, (D // 64) ** (-0.5)
    )
    next_expand, first_expand, second_expand = adam_update(
        expand_weight, expand_moment, expand_square, sum_expand * clip_factor, D ** (-0.5)
    )
    next_shrink, first_shrink, second_shrink = adam_update(
        shrink_weight, shrink_moment, shrink_square, sum_shrink * clip_factor, FF ** (-0.5)
    )
    next_modulate, first_modulate, second_modulate = adam_update(
        modulate_weight, modulate_moment, modulate_square, sum_modulate * clip_factor, D ** (-0.5)
    )
    next_biases, first_biases, second_biases = adam_update(
        bias_vector, bias_moment, bias_square, sum_bias * clip_factor, 0.3
    )
    return (
        block_output,
        token_grads,
        condition_grads,
        global_norm,
        next_project,
        first_project,
        second_project,
        next_output,
        first_output,
        second_output,
        next_expand,
        first_expand,
        second_expand,
        next_shrink,
        first_shrink,
        second_shrink,
        next_modulate,
        first_modulate,
        second_modulate,
        next_biases,
        first_biases,
        second_biases,
    )


def solution(mesh):
    return jax.shard_map(
        plane_body if mesh.shape["dp"] == GROUP and mesh.shape["mod"] == DEPTH else generic_body,
        mesh=mesh,
        in_specs=(
            P(("dp", "mod"), None),
            P(("dp", "mod"), None),
            P(("dp", "mod"), None),
            P(("dp", "mod"), None),
            P("dp", None),
            P("dp", None),
            P("dp", None),
            P("dp", None),
            P("dp", None),
            P("dp", None),
            P("dp", None),
            P("dp", None),
            P("dp", None),
            P("dp", None),
            P("dp", None),
            P("dp", None),
            P("dp", "mod"),
            P("dp", "mod"),
            P("dp", "mod"),
            P("dp"),
            P("dp"),
            P("dp"),
        ),
        out_specs=(
            P(("dp", "mod"), None),
            P(("dp", "mod"), None),
            P(("dp", "mod"), None),
            P(),
            P("dp", None),
            P("dp", None),
            P("dp", None),
            P("dp", None),
            P("dp", None),
            P("dp", None),
            P("dp", None),
            P("dp", None),
            P("dp", None),
            P("dp", None),
            P("dp", None),
            P("dp", None),
            P("dp", "mod"),
            P("dp", "mod"),
            P("dp", "mod"),
            P("dp"),
            P("dp"),
            P("dp"),
        ),
        check_vma=False,
    )
```

```python
import functools

import jax
import jax.numpy as jnp
from jax import lax
from jax.experimental import pallas as pl
from jax.experimental.pallas import tpu as pltpu
from jax.sharding import PartitionSpec as P

D = 1152
HEADS = 16
HEAD_DIM = 72
FF = 4608
ROW = 256
STEP = 10
IMG_ROW = 4


beta_first = 0.9
beta_second = 0.999
weight_decay = 0.01
adam_epsilon = 1e-08
tanh_scale = 0.7978845608028654
cubic_term = 0.044715


def contract(left, right, left_axis, right_axis):
    return lax.dot_general(
        left, right, (((left_axis,), (right_axis,)), ((), ())), preferred_element_type=jnp.float32
    )


def normalize_rows(values):
    center = values - jnp.mean(values, axis=-1, keepdims=True)
    inverse = lax.rsqrt(jnp.mean(center * center, axis=-1, keepdims=True) + 1e-06)
    return (center * inverse, inverse)


def normalize_back(grad_normed, normed, inverse):
    centered = grad_normed - jnp.mean(grad_normed, axis=-1, keepdims=True)
    return (centered - normed * jnp.mean(grad_normed * normed, axis=-1, keepdims=True)) * inverse


def adam_update(weight, moment, square, grad, rate):
    first = beta_first * moment + (1.0 - beta_first) * grad
    second = beta_second * square + (1.0 - beta_second) * grad * grad
    step_size = first / (1.0 - beta_first**STEP)
    divisor = jnp.sqrt(second / (1.0 - beta_second**STEP)) + adam_epsilon
    return (weight - rate * (step_size / divisor + weight_decay * weight), first, second)


def merge_heads(stacked):
    return stacked.transpose(1, 0, 2).reshape(stacked.shape[1], stacked.shape[0] * stacked.shape[2])


MESH = pl.DeviceIdType.MESH
GROUP = 8
DEPTH = 4
VMEM_BYTES = 60 << 20
low_type = jnp.bfloat16
full_type = jnp.float32


def vmem():
    return pl.BlockSpec(memory_space=pltpu.VMEM)


def anywhere():
    return pl.BlockSpec(memory_space=pl.ANY)


def plane_places():
    place = lax.axis_index("dp")
    layer = lax.axis_index("mod")
    twin = place + 1 - 2 * lax.rem(place, 2)
    side = 2 - 4 * lax.rem(lax.div(place, 2), 2)
    across = place + side
    along = place + 4 - 8 * lax.div(place, 4)
    corner = along + side
    return place, layer, twin, across, along, corner


def twin_of(place):
    return place + 1 - 2 * lax.rem(place, 2)


def send(source, target, send_sem, recv_sem, place, layer):
    copy = pltpu.make_async_remote_copy(
        src_ref=source,
        dst_ref=target,
        send_sem=send_sem,
        recv_sem=recv_sem,
        device_id=(place, layer),
        device_id_type=MESH,
    )
    copy.start()
    return copy


def greet(peers):
    barrier = pltpu.get_barrier_semaphore()
    for peer in peers:
        pl.semaphore_signal(barrier, inc=1, device_id=peer, device_id_type=MESH)
    pl.semaphore_wait(barrier, len(peers))


class Gather:
    def __init__(self, own, slots, sends, recvs, base, rows, cut):
        self.own, self.slots, self.sends, self.recvs = own, slots, sends, recvs
        self.whole = pl.ds(base, rows)
        self.first, self.second = pl.ds(base, cut), pl.ds(base + cut, rows - cut)
        self.place, self.layer, self.twin, self.across, self.along, self.corner = plane_places()
        self.copies = {}

    def push(self, index, slot, part, peer, own=False):
        target = self.slots.at[slot, part]
        source = self.own.at[part] if own else target
        self.copies[index] = send(
            source, target, self.sends.at[index], self.recvs.at[index], peer, self.layer
        )

    def start_twin(self):
        self.push(2, self.place, self.whole, self.twin, True)

    def start_links(self):
        self.push(0, self.place, self.whole, self.across, True)
        self.push(1, self.place, self.whole, self.along, True)

    def forward_near(self):
        self.copies[0].wait_recv()
        self.push(3, self.across, self.first, self.along)
        self.push(5, self.across, self.whole, self.twin)
        self.copies[1].wait_recv()
        self.push(4, self.along, self.second, self.across)
        self.push(6, self.along, self.whole, self.twin)

    def forward_far(self):
        self.copies[3].wait_recv()
        self.push(7, self.corner, self.first, self.twin)
        self.copies[4].wait_recv()
        self.push(8, self.corner, self.second, self.twin)

    def arrived(self, *indices):
        for index in indices:
            self.copies[index].wait_recv()

    def finish_sends(self):
        for index in range(9):
            self.copies[index].wait_send()


class Scatter:
    def __init__(self, parts, buffers, rows, cut, outgoing=None, columns=None):
        from_twin, half_across, half_along, whole_across, whole_along, self.sends, self.recvs = buffers
        self.first, self.second, self.rows = pl.ds(0, cut), pl.ds(cut, rows - cut), pl.ds(0, rows)
        self.place, self.layer, self.twin, self.across, self.along, self.corner = plane_places()
        self.places = (self.place, self.across, self.along, self.corner)
        self.slots = self.places if outgoing is None else (0, 1, 2, 3)
        outgoing = parts if outgoing is None else outgoing
        if columns is None:
            self.part = lambda slot, part: parts.at[slot, part]
            self.given = lambda slot: outgoing.at[slot]
            self.twin_part = lambda index, part: from_twin.at[index, part]
            self.half = (half_across, half_along)
            self.whole = (lambda part: whole_across.at[part], lambda part: whole_along.at[part])
        else:
            every = slice(None)
            self.part = lambda slot, part: parts.at[every, slot, part, columns]
            self.given = lambda slot: outgoing.at[every, slot, every, columns]
            self.twin_part = lambda index, part: from_twin.at[index, every, part, columns]
            self.half = (half_across.at[every, every, columns], half_along.at[every, every, columns])
            self.whole = (
                lambda part: whole_across.at[every, part, columns],
                lambda part: whole_along.at[every, part, columns],
            )
        self.copies = {}

    def push(self, index, source, target, peer):
        self.copies[index] = send(
            source, target, self.sends.at[index], self.recvs.at[index], peer, self.layer
        )

    def start_twin(self, *indices):
        for index in indices or (3, 1, 2, 0):
            self.push(index, self.given(twin_of(self.places[index])), self.twin_part(index, self.rows), self.twin)

    def add(self, slot, part, other):
        target = self.part(slot, part)
        target[...] = (target[...].astype(full_type) + other[...].astype(full_type)).astype(low_type)

    def merge_twin(self, index):
        self.copies[index].wait_recv()
        self.add(self.slots[index], self.rows, self.twin_part(index, self.rows))

    def start_near(self):
        _, across, along, _ = self.slots
        self.merge_twin(1)
        self.push(6, self.part(across, self.first), self.whole[0](self.first), self.across)
        self.merge_twin(2)
        self.push(7, self.part(along, self.second), self.whole[1](self.second), self.along)

    def start_far(self):
        corner = self.slots[3]
        self.merge_twin(3)
        self.push(4, self.part(corner, self.first), self.half[0], self.across)
        self.push(5, self.part(corner, self.second), self.half[1], self.along)

    def forward(self):
        _, across, along, _ = self.slots
        self.copies[5].wait_recv()
        self.add(across, self.second, self.half[1])
        self.push(8, self.part(across, self.second), self.whole[0](self.second), self.across)
        self.copies[4].wait_recv()
        self.add(along, self.first, self.half[0])
        self.push(9, self.part(along, self.first), self.whole[1](self.first), self.along)

    def settle(self):
        for index in (0, 6, 8, 7, 9):
            self.copies[index].wait_recv()
        for index in range(10):
            self.copies[index].wait_send()

    def total(self, part=None):
        part = self.rows if part is None else part
        return (
            self.part(self.slots[0], part)[...].astype(full_type)
            + self.twin_part(0, part)[...].astype(full_type)
            + (self.whole[0](part)[...].astype(full_type) + self.whole[1](part)[...].astype(full_type))
        )


def scatter_scratch(rows, cut, columns, copies=()):
    dma = pltpu.SemaphoreType.DMA
    lead = (3,) if copies else ()
    return [
        pltpu.VMEM((4,) + lead + (rows, columns), low_type),
        pltpu.VMEM(lead + (cut, columns), low_type),
        pltpu.VMEM(lead + (rows - cut, columns), low_type),
        pltpu.VMEM(lead + (rows, columns), low_type),
        pltpu.VMEM(lead + (rows, columns), low_type),
        dma(copies + (10,)),
        dma(copies + (10,)),
    ]


def iota(shape, axis):
    return lax.broadcasted_iota(jnp.int32, shape, axis)


def sample_picker():
    row, column = iota((128, 256), 0), iota((128, 256), 1)
    wanted = ((row >> 2) & 3) * 64 + (row >> 4) * 8 + (row & 3)
    return (column == wanted).astype(full_type).astype(low_type)


def slot_spreader():
    row, column = iota((32, 16), 0), iota((32, 16), 1)
    return jnp.where(((row & 7) < 4) & (column == (row >> 3) * 4 + (row & 7)), 1.0, 0.0).astype(low_type)


def head_window(head):
    start = lax.min(lax.div(head * HEAD_DIM, 128) * 128, D - 256)
    start = pl.multiple_of(start, 128)
    lane = iota((1, 256), 1) + start
    inside = (lane >= head * HEAD_DIM) & (lane < (head + 1) * HEAD_DIM)
    return start, inside.astype(full_type)


def window(ref, base, start):
    return ref[:, pl.ds(pl.multiple_of(base + start, 128), 256)]


def masked_probs(query, key, same):
    scores = jnp.where(same, contract(query, key, 1, 1) * HEAD_DIM ** (-0.5), -1e30)
    exponent = jnp.exp(scores - jnp.max(scores, axis=1, keepdims=True))
    return exponent / jnp.sum(exponent, axis=1, keepdims=True)


BLOCK = 64
LANES = 128


def slot_numbers(lengths, shape, axis):
    position = iota(shape, axis)
    slot, end = jnp.zeros(shape, jnp.int32), 0
    for step in range(IMG_ROW):
        end = end + lengths[0, step]
        slot = slot + jnp.where(position >= end, 1, 0)
    return slot


def slot_onehot(slots):
    matched = (slots == iota((slots.shape[0], 8), 1)) & (slots < IMG_ROW)
    return jnp.where(matched, 1.0, 0.0).astype(low_type)


def block_part(step):
    return pl.ds(pl.multiple_of(step * BLOCK, BLOCK), BLOCK)


def spread_slots(onehot, modulation, index):
    return contract(onehot, modulation[index].astype(low_type), 1, 0)


def front_kernel(
    lengths,
    tokens,
    cotangent,
    conditions,
    bias_own,
    project,
    output,
    expand,
    modulate,
    packed,
    attend_in,
    mixed,
    attend_out,
    resid,
    feed_in,
    modulation,
    active_out,
    bias_expand,
    bias_shrink,
    weights_out,
    expand_out,
    grad_all,
    project_load,
    output_load,
    expand_load,
    modulate_load,
    weights_own,
    weights_all,
    expand_own,
    grad_own,
    cond_send,
    cond_plane,
    cond_all,
    part_send,
    twin_recv,
    part_recv,
    mod_send,
    mod_recv,
    bias_recv,
    bias_flat,
    small_sends,
    small_recvs,
    near_sends,
    near_recvs,
    base_sends,
    base_recvs,
    far_sends,
    far_recvs,
    grad_sends,
    grad_recvs,
    local_sems,
):
    place, layer, twin, across, along, corner = plane_places()
    places = (place, across, along, corner)
    plane = [lax.rem(place + step, GROUP) for step in range(1, GROUP)]
    column = [lax.rem(layer + step, DEPTH) for step in range(1, DEPTH)]
    pair = layer + 1 - 2 * lax.rem(layer, 2)
    inner = jnp.where((layer == 0) | (layer == DEPTH - 1), 0, 1)
    rows = weights_own.shape[0]
    third = rows // 3
    shard = bias_own.shape[1]
    columns = modulate_load.shape[1]
    units = expand_own.shape[2]

    def load(index, source, target):
        copy = pltpu.make_async_copy(source, target, local_sems.at[index])
        copy.start()
        return copy

    loads = [
        load(0, project, project_load),
        load(1, modulate, modulate_load),
        load(2, output, output_load),
        load(3, expand, expand_load),
    ]
    peers = [(peer, layer) for peer in plane] + [(place, peer) for peer in column]
    barrier = pltpu.get_barrier_semaphore()
    for peer in peers:
        pl.semaphore_signal(barrier, inc=1, device_id=peer, device_id_type=MESH)
    values = conditions[...].astype(full_type)
    active = (values * jax.nn.sigmoid(values)).astype(low_type).astype(full_type)
    cond_send[...] = jnp.zeros_like(cond_send)
    for step in range(GROUP):
        cond_send[step, 0:IMG_ROW, :] = active[:, step * rows : (step + 1) * rows]
    bias_recv[place] = bias_own[...].astype(low_type).astype(full_type)
    pl.semaphore_wait(barrier, len(peers))

    waits = []

    def exchange(base, peers, source, target):
        copies = []
        for step, peer in enumerate(peers):
            where = (peer, layer) if peers is plane else (place, peer)
            copies.append(
                send(source(peer), target, small_sends.at[base + step], small_recvs.at[base + step], *where)
            )
        waits.extend(copies)
        return copies

    def arrive(copies):
        for copy in copies:
            copy.wait_recv()

    cond_copies = exchange(0, plane, lambda peer: cond_send.at[peer], cond_plane.at[place])
    cond_plane[place] = cond_send[place]
    bias_copies = exchange(7, plane, lambda peer: bias_recv.at[place], bias_recv.at[place])
    loads[0].wait()
    weights_own[:, 0 : 3 * D] = project_load[...].astype(low_type)
    loads[2].wait()
    weights_own[:, 3 * D : 4 * D] = output_load[...].astype(low_type)
    second = pl.multiple_of(third * (1 + inner), 16)
    last = pl.multiple_of(third * (2 - inner), 16)
    near = Gather(weights_own, weights_all, near_sends, near_recvs, second, third, 32)
    base = Gather(weights_own, weights_all, base_sends, base_recvs, 0, third, 16)
    near.start_links()
    near.start_twin()
    base.start_twin()
    whole = pl.ds(last, third)

    def far_copy(index, slot, part, where):
        return send(
            weights_all.at[slot, part],
            weights_all.at[slot, part],
            far_sends.at[index],
            far_recvs.at[index],
            *where,
        )

    far = [
        send(
            weights_own.at[whole], weights_all.at[place, whole], far_sends.at[0], far_recvs.at[0], twin, layer
        )
    ]
    arrive(cond_copies)
    cond_copies = exchange(14, column, lambda peer: cond_plane, cond_all.at[layer])
    cond_all[layer] = cond_plane[...]
    weights_all[place] = weights_own[...]
    loads[1].wait()
    arrive(cond_copies)
    padded = cond_all[...].reshape(DEPTH * GROUP * 8, rows).astype(low_type)
    picked = contract(sample_picker(), padded, 1, 0).astype(low_type)
    active_out[...] = picked
    partial = contract(picked, modulate_load[...].astype(low_type), 1, 0)
    part_send[...] = partial.reshape(part_send.shape)
    twin_copies = []
    for step in (1, 2, 3, 0):
        twin_copies.append(
            send(
                part_send.at[twin_of(places[step])],
                twin_recv.at[step],
                small_sends.at[17 + step],
                small_recvs.at[17 + step],
                twin,
                layer,
            )
        )
    part_copies = []
    for step, copy in zip((1, 2, 3), twin_copies):
        copy.wait_recv()
        part_send[places[step]] = part_send[places[step]] + twin_recv[step]
        part_copies.append(
            send(
                part_send.at[places[step]],
                part_recv.at[step - 1],
                small_sends.at[21 + step],
                small_recvs.at[21 + step],
                places[step],
                layer,
            )
        )
    waits += twin_copies + part_copies
    near.forward_near()
    up = (place, pair)
    far.append(far_copy(1, across, near.whole, up))
    base.start_links()
    arrive(bias_copies)
    for step in range(GROUP):
        bias_flat[:, step * shard : (step + 1) * shard] = bias_recv[step]
    start = pl.multiple_of(4 * D + FF + 2 * columns * lax.div(layer, 2), 128)
    both = bias_flat[:, pl.ds(start, 2 * columns)]
    bias_modulate = jnp.where(lax.rem(layer, 2) == 0, both[:, 0:columns], both[:, columns : 2 * columns])
    start = pl.multiple_of(3 * D + 2 * units * lax.div(place, 2), 128)
    both = bias_flat[:, pl.ds(start, 2 * units)]
    bias_expand[...] = jnp.where(lax.rem(place, 2) == 0, both[:, 0:units], both[:, units : 2 * units])
    bias_shrink[...] = bias_flat[:, 3 * D + FF : 4 * D + FF]
    arrive(twin_copies[3:] + part_copies)
    total = (part_send[place] + twin_recv[0]) + ((part_recv[0] + part_recv[1]) + part_recv[2]) + bias_modulate
    spread = contract(slot_spreader(), total.astype(low_type), 1, 0)
    mod_send[...] = spread.reshape(mod_send.shape)
    mod_copies = exchange(25, column, lambda peer: mod_send.at[peer], mod_recv.at[layer])
    mod_recv[layer] = mod_send[layer]

    far.append(far_copy(2, along, near.whole, up))
    near.forward_far()
    far.append(far_copy(3, corner, near.whole, up))
    loads[3].wait()
    for step in range(GROUP):
        expand_own[step] = expand_load[:, step * units : (step + 1) * units].astype(low_type)
    base.forward_near()

    def expand_copy(index, source, target, where):
        copy = send(source, target, small_sends.at[28 + index], small_recvs.at[28 + index], *where)
        waits.append(copy)
        return copy

    sources = [slot + (twin_of(slot) - slot) * inner for slot in (across, along, corner)]
    expand_copies = [
        expand_copy(step, expand_own.at[slot], expand_out.at[place], (slot, layer)) for step, slot in enumerate(sources)
    ]
    expand_copies.append(expand_copy(3, expand_own.at[twin], expand_out.at[place], (twin, layer)))
    arrive(mod_copies)
    half = D // 2
    for block in range(DEPTH):
        for step in range(3):
            piece, side = divmod(3 * block + step, 2)
            modulation[piece, :, side * half : (side + 1) * half] = mod_recv[block, :, step * half : (step + 1) * half]
    slot_row = slot_numbers(lengths, (1, ROW), 1)
    slot_column = slot_numbers(lengths, (ROW, 1), 0)
    onehot = slot_onehot(slot_column)

    def first_step(step):
        part = pl.ds(step * BLOCK, BLOCK)
        picked = onehot[step * BLOCK : (step + 1) * BLOCK]
        normed, _ = normalize_rows(tokens[part, :].astype(full_type))
        attend_in[part, :] = (
            normed * (1.0 + spread_slots(picked, modulation, 1)) + spread_slots(picked, modulation, 0)
        ).astype(low_type)
        grad_own[part, :] = (spread_slots(picked, modulation, 5) * cotangent[part, :].astype(full_type)).astype(low_type)

    for step in range(ROW // BLOCK):
        first_step(step)
    base.forward_far()
    grad_gather = Gather(grad_own, grad_all, grad_sends, grad_recvs, 0, ROW, ROW // 2)
    grad_gather.start_links()
    grad_gather.start_twin()
    keeps = [
        load(4, grad_own, grad_all.at[place]),
        load(5, expand_own.at[place], expand_out.at[place]),
    ]
    for index, slot in ((1, across), (2, along), (3, corner)):
        far[index].wait_recv()
        far.append(far_copy(3 + index, slot, whole, (twin, layer)))
    near.arrived(2, 5, 6, 7, 8)
    base.arrived(2, 5, 6, 7, 8)
    for index in (0, 4, 5, 6):
        far[index].wait_recv()
    for step, slot in enumerate(sources):
        expand_copies[step].wait_recv()
        expand_copies.append(expand_copy(4 + step, expand_out.at[slot], expand_out.at[slot], up))
    keeps.append(load(6, weights_all, weights_out))

    mixed[...] = jnp.zeros_like(mixed)

    def query_step(step, carry):
        where = pl.ds(pl.multiple_of(step * 384, 128), 384)
        values = contract(attend_in[...], weights_all[:, :, where].reshape(D, 384), 1, 0)
        packed[:, where] = values.astype(low_type)
        return carry

    def biased_step(step, base, carry):
        where = pl.ds(pl.multiple_of(base + step * 384, 128), 384)
        shift = bias_flat[:, pl.ds(pl.multiple_of(lax.div(base, 2) + step * 384, 128), 384)]
        values = contract(attend_in[...], weights_all[:, :, where].reshape(D, 384), 1, 0)
        packed[:, where] = (values + shift).astype(low_type)
        return carry

    lax.fori_loop(0, 3, lambda step, carry: biased_step(step, 0, carry), 0)
    lax.fori_loop(3, 6, query_step, 0)
    lax.fori_loop(0, 3, lambda step, carry: biased_step(step, 2 * D, carry), 0)
    same = slot_column == slot_row

    def head_step(head, carry):
        start, inside = head_window(head)
        keep = inside.astype(low_type)
        probs = masked_probs(window(packed, 0, start) * keep, window(packed, D, start), same)
        out = contract(probs.astype(low_type), window(packed, 2 * D, start) * keep, 1, 0)
        where = pl.ds(start, 256)
        mixed[:, where] = (mixed[:, where].astype(full_type) + out).astype(low_type)
        return carry

    lax.fori_loop(0, 8, head_step, 0, unroll=2)
    grad_gather.forward_near()
    lax.fori_loop(8, HEADS, head_step, 0, unroll=2)

    def out_step(step, carry):
        where = pl.ds(pl.multiple_of(step * 384, 128), 384)
        source = pl.ds(pl.multiple_of(3 * D + step * 384, 128), 384)
        shift = bias_flat[:, pl.ds(pl.multiple_of(2 * D + step * 384, 128), 384)]
        attend_out[:, where] = contract(mixed[...], weights_all[:, :, source].reshape(D, 384), 1, 0) + shift
        return carry

    lax.fori_loop(0, 3, out_step, 0)
    for step in range(ROW // BLOCK):
        part = pl.ds(step * BLOCK, BLOCK)
        picked = onehot[step * BLOCK : (step + 1) * BLOCK]
        joined = tokens[part, :].astype(full_type) + spread_slots(picked, modulation, 2) * attend_out[part, :]
        resid[part, :] = joined
        normed, _ = normalize_rows(joined)
        feed_in[part, :] = (
            normed * (1.0 + spread_slots(picked, modulation, 4)) + spread_slots(picked, modulation, 3)
        ).astype(low_type)
    grad_gather.forward_far()
    grad_gather.arrived(2, 5, 6, 7, 8)
    arrive(expand_copies[3:])
    for gather in (near, base, grad_gather):
        gather.finish_sends()
    for copy in far + waits:
        copy.wait_send()
    for copy in keeps:
        copy.wait()


def front_call(lengths, tokens, cotangent, conditions, bias_own, project, output, expand, modulate):
    rows, columns = modulate.shape
    units = expand.shape[1] // GROUP
    shard = bias_own.shape[1]
    shape = jax.ShapeDtypeStruct
    dma = pltpu.SemaphoreType.DMA
    return pl.pallas_call(
        front_kernel,
        out_shape=(
            shape((ROW, 3 * D), low_type),
            shape((ROW, D), low_type),
            shape((ROW, D), low_type),
            shape((ROW, D), full_type),
            shape((ROW, D), full_type),
            shape((ROW, D), low_type),
            shape((6, 8, D), full_type),
            shape((GROUP * 16, rows), low_type),
            shape((1, units), full_type),
            shape((1, D), full_type),
            shape((GROUP, rows, 4 * D), low_type),
            shape((GROUP, rows, units), low_type),
            shape((GROUP, ROW, D), low_type),
        ),
        in_specs=[pl.BlockSpec(memory_space=pltpu.SMEM)] + [vmem()] * 4 + [anywhere()] * 4,
        out_specs=(vmem(),) * 10 + (anywhere(),) * 3,
        scratch_shapes=[
            pltpu.VMEM(project.shape, full_type),
            pltpu.VMEM(output.shape, full_type),
            pltpu.VMEM(expand.shape, full_type),
            pltpu.VMEM(modulate.shape, full_type),
            pltpu.VMEM((rows, 4 * D), low_type),
            pltpu.VMEM((GROUP, rows, 4 * D), low_type),
            pltpu.VMEM((GROUP, rows, units), low_type),
            pltpu.VMEM((ROW, D), low_type),
            pltpu.VMEM((GROUP, 8, rows), full_type),
            pltpu.VMEM((GROUP, 8, rows), full_type),
            pltpu.VMEM((DEPTH, GROUP, 8, rows), full_type),
            pltpu.VMEM((GROUP, 16, columns), full_type),
            pltpu.VMEM((4, 16, columns), full_type),
            pltpu.VMEM((3, 16, columns), full_type),
            pltpu.VMEM((DEPTH, 8, columns), full_type),
            pltpu.VMEM((DEPTH, 8, columns), full_type),
            pltpu.VMEM((GROUP, 1, shard), full_type),
            pltpu.VMEM((1, GROUP * shard), full_type),
            dma((35,)),
            dma((35,)),
            dma((9,)),
            dma((9,)),
            dma((9,)),
            dma((9,)),
            dma((7,)),
            dma((7,)),
            dma((9,)),
            dma((9,)),
            dma((7,)),
        ],
        compiler_params=pltpu.CompilerParams(
            collective_id=0, has_side_effects=True, vmem_limit_bytes=VMEM_BYTES
        ),
        name="forward",
    )(lengths, tokens, cotangent, conditions, bias_own, project, output, expand, modulate)


def square_sum(values):
    values = values.astype(full_type)
    squares = values * values
    while squares.ndim > 2:
        squares = jnp.sum(squares, axis=0)
    return jnp.sum(jnp.sum(squares, axis=0, keepdims=True), axis=1, keepdims=True)


class Chain:
    def __init__(self, chunks, pair_sends, pair_recvs, mid_sends, mid_recvs):
        self.chunks = chunks
        self.place, self.layer = lax.axis_index("dp"), lax.axis_index("mod")
        self.pair = self.layer + 1 - 2 * lax.rem(self.layer, 2)
        self.edge = (self.layer == 0) | (self.layer == DEPTH - 1)
        self.middle = jnp.logical_not(self.edge)
        self.sems = (pair_sends, pair_recvs, mid_sends, mid_recvs)

    def pair_copy(self, index, source):
        return pltpu.make_async_remote_copy(
            src_ref=source,
            dst_ref=self.chunks[index][1],
            send_sem=self.sems[0].at[index],
            recv_sem=self.sems[1].at[index],
            device_id=(self.place, self.pair),
            device_id_type=MESH,
        )

    def middle_copy(self, index):
        return pltpu.make_async_remote_copy(
            src_ref=self.chunks[index][0],
            dst_ref=self.chunks[index][2],
            send_sem=self.sems[2].at[index],
            recv_sem=self.sems[3].at[index],
            device_id=(self.place, DEPTH - 1 - self.layer),
            device_id_type=MESH,
        )

    def edge_send(self, *indices):
        @pl.when(self.edge)
        def _():
            for index in indices:
                self.pair_copy(index, self.chunks[index][0]).start()

    def inward(self, *indices):
        @pl.when(self.middle)
        def _():
            for index in indices:
                given, result, _ = self.chunks[index]
                self.pair_copy(index, result).wait_recv()
                given[...] = (given[...].astype(full_type) + result[...].astype(full_type)).astype(low_type)
                self.middle_copy(index).start()

    def outward(self, *indices):
        @pl.when(self.middle)
        def _():
            for index in indices:
                given, result, other = self.chunks[index]
                self.middle_copy(index).wait()
                result[...] = (given[...].astype(full_type) + other[...].astype(full_type)).astype(low_type)
                self.pair_copy(index, result).start()

    def finish(self):
        @pl.when(self.edge)
        def _():
            for index in range(len(self.chunks)):
                self.pair_copy(index, self.chunks[index][0]).wait()

        @pl.when(self.middle)
        def _():
            for index in range(len(self.chunks)):
                self.pair_copy(index, self.chunks[index][1]).wait_send()


def slot_sums(onehot, values):
    high = values.astype(low_type)
    rest = (values - high.astype(full_type)).astype(low_type)
    return contract(onehot, high, 0, 0) + contract(onehot, rest, 0, 0)


def feed_kernel(
    lengths,
    feed_own,
    expand,
    bias,
    modulation,
    cotangent_in,
    attend_out_in,
    resid_in,
    mixed_in,
    shrink,
    grads,
    full_weights,
    feed_parts,
    shrink_sum,
    shrink_rest,
    shrink_square,
    expand_own,
    grad_bias,
    grad_resid,
    grad_attend,
    grad_mixed,
    output_parts,
    slot_grads,
    feed_all,
    grad_all,
    hidden_all,
    pre_all,
    grad_parts,
    shrink_full,
    shrink_low,
    grad_shrink,
    shrink_mid,
    grad_expand,
    output_weight,
    slots,
    cotangent,
    attend_out,
    resid,
    mixed,
    local_sems,
    feed_sends,
    feed_recvs,
    expand_sends,
    expand_recvs,
    chain_sems,
    *scratch,
):
    grad_scatter = Scatter(grad_parts, scratch, ROW, ROW // 2)
    place, layer, twin, across, along, corner = plane_places()
    plane = [lax.rem(place + step, GROUP) for step in range(1, GROUP)]
    column = [lax.rem(layer + step, DEPTH) for step in range(1, DEPTH)]
    rows = output_parts.shape[1]
    units = hidden_all.shape[2]
    feed_gather = Gather(feed_own, feed_all, feed_sends, feed_recvs, 0, ROW, ROW // 2)
    chunks, start = [], 0
    for step in range(4):
        size = 64 + 16 * (step % 2)
        part = pl.ds(start, size)
        start += size
        chunks.append((grad_shrink.at[part], shrink_sum.at[part], shrink_mid.at[part]))
    chain = Chain(chunks, *(chain_sems.at[step] for step in range(4)))
    shrink_copy = pltpu.make_async_copy(shrink, shrink_full, local_sems.at[0])
    grad_copy = pltpu.make_async_copy(grads, grad_all, local_sems.at[1])
    weight_copy = pltpu.make_async_copy(full_weights.at[:, :, pl.ds(3 * D, D)], output_weight, local_sems.at[2])
    shrink_copy.start()
    grad_copy.start()
    weight_copy.start()
    late_copies = [
        pltpu.make_async_copy(given, held, local_sems.at[5 + step])
        for step, (given, held) in enumerate(
            ((cotangent_in, cotangent), (attend_out_in, attend_out), (resid_in, resid), (mixed_in, mixed))
        )
    ]
    for copy in late_copies:
        copy.start()
    greet([(peer, layer) for peer in plane] + [(place, peer) for peer in column])
    feed_gather.start_links()
    feed_gather.start_twin()
    feed_all[place] = feed_own[...]
    shrink_copy.wait()
    shrink_low[...] = shrink_full[...].astype(low_type)
    slots[...] = slot_numbers(lengths, (ROW, 1), 0)
    slot_grads[...] = jnp.zeros_like(slot_grads)
    grad_copy.wait()

    def through(slot):
        both = pl.ds(2 * lax.div(slot, 2), 2)
        pre = contract(feed_all[both].reshape(2 * ROW, D), expand[...], 1, 0) + bias[...]
        tanh_part = jnp.tanh(tanh_scale * (pre + cubic_term * pre * pre * pre))
        hidden = (0.5 * pre * (1.0 + tanh_part)).astype(low_type)
        slope = 0.5 * (1.0 + tanh_part) + 0.5 * pre * (1.0 - tanh_part * tanh_part) * tanh_scale * (
            1.0 + 3.0 * cubic_term * pre * pre
        )
        hidden_all[both] = hidden.reshape(2, ROW, units)
        grad_hidden = contract(grad_all[both].reshape(2 * ROW, D), shrink_low[...], 1, 1)
        grad_pre = (grad_hidden * slope).astype(low_type)
        pre_all[both] = grad_pre.reshape(2, ROW, units)
        grad_parts[both] = contract(grad_pre, expand[...], 1, 1).astype(low_type).reshape(2, ROW, D)

    feed_gather.arrived(2)
    through(place)
    feed_gather.forward_near()
    feed_gather.arrived(5)
    through(across)
    grad_scatter.start_twin(1)
    feed_gather.arrived(6)
    through(along)
    grad_scatter.start_twin(2)
    feed_gather.forward_far()
    grad_scatter.start_near()
    feed_gather.arrived(7, 8)
    through(corner)
    grad_scatter.start_twin(3, 0)
    grad_scatter.start_far()

    hidden = hidden_all[...].reshape(GROUP * ROW, units)
    grad_shrink[...] = contract(hidden, grad_all[...].reshape(GROUP * ROW, D), 0, 0).astype(low_type)
    chain.edge_send(*range(4))
    shrink_rest[...] = grad_shrink[pl.ds(units // 2, units // 2), :]
    grad_pre = pre_all[...].reshape(GROUP * ROW, units)
    expand_grads = contract(feed_all[...].reshape(GROUP * ROW, D), grad_pre, 0, 0).astype(low_type)
    grad_expand[...] = expand_grads.reshape(GROUP, rows, units)
    grad_scatter.forward()
    exchange = []
    for step, peer in enumerate(plane):
        exchange.append(
            send(grad_expand.at[peer], expand_own.at[place], expand_sends.at[step], expand_recvs.at[step], peer, layer)
        )
    expand_own[place] = grad_expand[place]
    chain.inward(0)
    grad_bias[...] = jnp.sum(grad_pre.astype(full_type), axis=0, keepdims=True)

    def part_step(step, carry):
        both = pl.ds(2 * step, 2)
        parts = contract(hidden_all[both].reshape(2 * ROW, units), shrink_low[...], 1, 0)
        grad_all[both] = parts.astype(low_type).reshape(2, ROW, D)
        return carry

    lax.fori_loop(0, 2, part_step, 0)
    chain.inward(1)
    lax.fori_loop(2, GROUP // 2, part_step, 0)
    feed_copy = pltpu.make_async_copy(grad_all, feed_parts, local_sems.at[3])
    feed_copy.start()
    chain.inward(2)
    chain.outward(0)
    chain.inward(3)
    chain.outward(1)
    for copy in late_copies:
        copy.wait()
    grad_scatter.settle()
    chain.outward(2)

    def feed_step(step, carry):
        part = block_part(step)
        onehot = slot_onehot(slots[part, :])
        normed, inverse = normalize_rows(resid[part, :])
        grad_in = grad_scatter.total(part)
        slot_grads[3] += slot_sums(onehot, grad_in)
        slot_grads[4] += slot_sums(onehot, grad_in * normed)
        grad = cotangent[part, :].astype(full_type) + normalize_back(
            grad_in * (1.0 + spread_slots(onehot, modulation, 4)), normed, inverse
        )
        grad_resid[part, :] = grad
        slot_grads[2] += slot_sums(onehot, grad * attend_out[part, :])
        grad_attend[part, :] = (spread_slots(onehot, modulation, 2) * grad).astype(low_type)
        return carry

    lax.fori_loop(0, ROW // BLOCK // 2, feed_step, 0)
    chain.outward(3)
    lax.fori_loop(ROW // BLOCK // 2, ROW // BLOCK, feed_step, 0)
    weight_copy.wait()
    grad_mixed[...] = contract(grad_attend[...], output_weight[...].reshape(D, D), 1, 1).astype(low_type)

    def weight_step(step, carry):
        where = pl.ds(pl.multiple_of(step * 384, 128), 384)
        values = contract(mixed[...], grad_attend[:, where], 0, 0).astype(low_type)
        output_weight[:, :, where] = values.reshape(GROUP, rows, 384)
        return carry

    lax.fori_loop(0, 3, weight_step, 0)
    output_copy = pltpu.make_async_copy(output_weight, output_parts, local_sems.at[4])
    output_copy.start()
    feed_copy.wait()
    output_copy.wait()
    feed_gather.finish_sends()
    for copy in exchange:
        copy.wait()
    chain.finish()
    shrink_square[...] = jnp.broadcast_to(square_sum(shrink_sum[...]), shrink_square.shape)


def feed_call(
    lengths, feed_own, expand, bias, modulation, cotangent, attend_out, resid, mixed, shrink, grads, full_weights
):
    units = expand.shape[1]
    rows = full_weights.shape[1]
    shape = jax.ShapeDtypeStruct
    dma = pltpu.SemaphoreType.DMA
    return pl.pallas_call(
        feed_kernel,
        out_shape=(
            shape((GROUP, ROW, D), low_type),
            shape((units // 2, D), low_type),
            shape((units // 2, D), low_type),
            shape((8, LANES), full_type),
            shape((GROUP, rows, units), low_type),
            shape((1, units), full_type),
            shape((ROW, D), full_type),
            shape((ROW, D), low_type),
            shape((ROW, D), low_type),
            shape((GROUP, rows, D), low_type),
            shape((6, 8, D), full_type),
        ),
        in_specs=[pl.BlockSpec(memory_space=pltpu.SMEM)] + [vmem()] * 4 + [anywhere()] * 7,
        out_specs=(anywhere(),) + (vmem(),) * 8 + (anywhere(), vmem()),
        scratch_shapes=[
            pltpu.VMEM((GROUP, ROW, D), low_type),
            pltpu.VMEM((GROUP, ROW, D), low_type),
            pltpu.VMEM((GROUP, ROW, units), low_type),
            pltpu.VMEM((GROUP, ROW, units), low_type),
            pltpu.VMEM((GROUP, ROW, D), low_type),
            pltpu.VMEM((units, D), full_type),
            pltpu.VMEM((units, D), low_type),
            pltpu.VMEM((units, D), low_type),
            pltpu.VMEM((units // 2, D), low_type),
            pltpu.VMEM((GROUP, rows, units), low_type),
            pltpu.VMEM((GROUP, rows, D), low_type),
            pltpu.VMEM((ROW, 1), jnp.int32),
            pltpu.VMEM((ROW, D), low_type),
            pltpu.VMEM((ROW, D), full_type),
            pltpu.VMEM((ROW, D), full_type),
            pltpu.VMEM((ROW, D), low_type),
            dma((9,)),
            dma((9,)),
            dma((9,)),
            dma((7,)),
            dma((7,)),
            dma((4, 8)),
            *scatter_scratch(ROW, ROW // 2, D),
        ],
        compiler_params=pltpu.CompilerParams(
            collective_id=1, has_side_effects=True, vmem_limit_bytes=VMEM_BYTES
        ),
        name="feed_forward",
    )(lengths, feed_own, expand, bias, modulation, cotangent, attend_out, resid, mixed, shrink, grads, full_weights)


def sample_compactor():
    row, column = iota((16, 32), 0), iota((16, 32), 1)
    return (column == (row >> 2) * 8 + (row & 3)).astype(full_type).astype(low_type)


def sample_scatterer():
    row, column = iota((256, 128), 0), iota((256, 128), 1)
    wanted = ((row >> 3) & 7) * 16 + (row >> 6) * 4 + (row & 7)
    return jnp.where(((row & 7) < 4) & (column == wanted), 1.0, 0.0).astype(low_type)


def column_sum(values):
    return jnp.sum(values.astype(full_type), axis=0, keepdims=True)


BIAS_ROWS = 128
COLUMN_GROUPS = ((0, 256), (256, 256), (512, 256), (768, 256), (1024, 128))


def back_kernel(
    lengths,
    tokens,
    cotangent,
    modulation,
    packed,
    attend_in,
    resid,
    grad_resid,
    grad_attend,
    grad_mixed,
    slot_grads_in,
    bias_shrink,
    grad_bias_expand,
    shrink_square,
    active,
    conditions,
    modulate,
    full_weights,
    feed_parts_in,
    output_parts,
    expand_parts,
    shrink_rest,
    block_output,
    token_grads,
    project_sum,
    output_sum,
    expand_sum,
    shrink_sum,
    bias_out,
    modulate_sum,
    condition_grads,
    square_total,
    output_store,
    project_store,
    feed_parts,
    grad_packed,
    slot_grads,
    project_own,
    output_own,
    expand_own,
    project_mid,
    output_mid,
    expand_mid,
    shrink_own,
    shrink_mid,
    bias_own,
    bias_recv,
    bias_layers,
    sample_send,
    sample_recv,
    group_all,
    term_send,
    term_recv,
    term_sum,
    square_send,
    square_recv,
    square_part,
    square_all,
    small_sends,
    small_recvs,
    chain_sems,
    local_sems,
    slots,
    bias_sum,
    bias_flat,
    condition_sum,
    *scratch,
):
    place, layer, *_ = plane_places()
    plane = [lax.rem(place + step, GROUP) for step in range(1, GROUP)]
    column = [lax.rem(layer + step, DEPTH) for step in range(1, DEPTH)]
    rows = output_own.shape[0]
    scale = HEAD_DIM ** (-0.5)

    chunks, start = [], 0
    for step in range(4):
        size = 64 + 16 * (step % 2)
        part = pl.ds(start, size)
        start += size
        chunks.append((shrink_own.at[part], shrink_sum.at[part], shrink_mid.at[part]))
    for step in range(GROUP):
        chunks.append((expand_own.at[step], expand_sum.at[step], expand_mid.at[step]))
    chunks.append((output_own, output_sum, output_mid))
    for first, width in COLUMN_GROUPS:
        part = (slice(None), slice(None), pl.ds(first, width))
        chunks.append((project_own.at[part], project_sum.at[part], project_mid.at[part]))
    chain = Chain(chunks, *(chain_sems.at[step] for step in range(4)))

    waits = []

    def exchange(base, peers, source, target):
        copies = []
        for step, peer in enumerate(peers):
            where = (peer, layer) if peers is plane else (place, peer)
            copies.append(
                send(source(peer), target, small_sends.at[base + step], small_recvs.at[base + step], *where)
            )
        waits.extend(copies)
        return copies

    def arrive(copies):
        for copy in copies:
            copy.wait_recv()

    def load(index, source, target):
        copy = pltpu.make_async_copy(source, target, local_sems.at[index])
        copy.start()
        return copy

    feed_scatter = Scatter(feed_parts, scratch[0:7], ROW, ROW // 2, outgoing=feed_parts_in)
    output_scatter = Scatter(output_store, scratch[7:14], rows, 64, outgoing=output_parts)
    project_scatters = []
    for step, (first, width) in enumerate(COLUMN_GROUPS):
        buffers = (*scratch[14:19], scratch[19].at[step], scratch[20].at[step])
        project_scatters.append(
            Scatter(project_store, buffers, rows, 64, columns=pl.ds(first, width))
        )
    shrink_load = load(12, shrink_rest, shrink_own)
    expand_load = load(0, expand_parts, expand_own)
    feed_loads = [
        load(1 + step, feed_parts_in.at[feed_scatter.places[step]], feed_parts.at[step]) for step in range(4)
    ]
    output_loads = [
        load(5 + step, output_parts.at[feed_scatter.places[step]], output_store.at[step]) for step in range(4)
    ]
    project_loads = [
        load(9 + step, full_weights.at[:, :, pl.ds(step * D, D)], project_store.at[step]) for step in range(3)
    ]

    greet([(peer, layer) for peer in plane] + [(place, peer) for peer in column])

    feed_scatter.start_twin()
    output_scatter.start_twin()
    shrink_load.wait()
    chain.edge_send(*range(4))
    expand_load.wait()
    chain.edge_send(*range(4, 12))
    slot_grads[...] = slot_grads_in[...]
    bias_own[...] = jnp.zeros_like(bias_own)
    grad_packed[...] = jnp.zeros_like(grad_packed)

    slot_row = slot_numbers(lengths, (1, ROW), 1)
    slot_column = slot_numbers(lengths, (ROW, 1), 0)
    slots[...] = slot_column

    def block_parts(step):
        part = block_part(step)
        return part, slot_onehot(slots[part, :])

    same = slot_column == slot_row

    def head_step(head, carry):
        start, inside = head_window(head)
        keep = inside.astype(low_type)
        query = window(packed, 0, start) * keep
        key = window(packed, D, start)
        value = window(packed, 2 * D, start)
        grad = window(grad_mixed, 0, start) * keep
        probs = masked_probs(query, key, same)
        grad_probs = contract(grad, value, 1, 1)
        grad_scores = probs * (grad_probs - jnp.sum(probs * grad_probs, axis=1, keepdims=True))
        grad_scores = grad_scores.astype(low_type)

        def put(base, values):
            where = pl.ds(pl.multiple_of(base + start, 128), 256)
            grad_packed[:, where] = (grad_packed[:, where].astype(full_type) + values).astype(low_type)

        put(0, contract(grad_scores, key * keep, 1, 0) * scale)
        put(D, contract(grad_scores, query, 0, 0) * scale)
        put(2 * D, contract(probs.astype(low_type), grad, 0, 0))
        return carry

    def heads(first, last):
        lax.fori_loop(first, last, head_step, 0, unroll=2)

    def project_group(step):
        first, width = COLUMN_GROUPS[step]
        for kind in range(3):
            where = pl.ds(first, width)
            grads = grad_packed[:, kind * D + first : kind * D + first + width]
            back = contract(grads, project_store[kind, :, :, where].reshape(D, width), 1, 1)
            if step == 0 and kind == 0:
                token_grads[...] = back
            else:
                token_grads[...] += back
            weight = contract(attend_in[...], grads, 0, 0).astype(low_type)
            project_store[kind, :, :, where] = weight.reshape(GROUP, rows, width)
        project_scatters[step].start_twin()

    heads(0, 4)
    for copy in feed_loads:
        copy.wait()
    feed_scatter.start_far()
    feed_scatter.start_near()
    for copy in output_loads:
        copy.wait()
    output_scatter.start_far()
    output_scatter.start_near()
    chain.inward(0)
    for copy in project_loads:
        copy.wait()
    project_group(0)
    chain.inward(1)
    heads(4, 8)
    chain.inward(2)
    chain.outward(0)
    project_scatters[0].start_far()
    project_scatters[0].start_near()
    project_group(1)
    feed_scatter.forward()
    chain.inward(3)
    chain.outward(1)
    heads(8, 12)
    chain.inward(4)
    chain.outward(2)
    project_scatters[1].start_far()
    project_scatters[1].start_near()
    project_group(2)
    chain.inward(5)
    chain.outward(3)
    output_scatter.forward()
    heads(12, 16)
    chain.inward(6)
    chain.outward(4)
    chain.inward(7)
    chain.outward(5)
    project_scatters[2].start_far()
    project_scatters[2].start_near()
    project_group(3)
    project_group(4)
    project_scatters[0].forward()
    chain.inward(8)
    chain.outward(6)

    def attend_step(step, carry):
        part, onehot = block_parts(step)
        normed, inverse = normalize_rows(tokens[part, :].astype(full_type))
        grad_in = token_grads[part, :]
        slot_grads[0] += slot_sums(onehot, grad_in)
        slot_grads[1] += slot_sums(onehot, grad_in * normed)
        token_grads[part, :] = grad_resid[part, :] + normalize_back(
            grad_in * (1.0 + spread_slots(onehot, modulation, 1)), normed, inverse
        )
        return carry

    lax.fori_loop(0, ROW // BLOCK, attend_step, 0)
    for step in (3, 4):
        project_scatters[step].start_far()
        project_scatters[step].start_near()
    chain.inward(9)
    chain.outward(7)
    feed_scatter.settle()

    def put_rows(base, values):
        for step in range(values.shape[1] // LANES):
            bias_own[base + step : base + step + 1, :] = values[:, step * LANES : (step + 1) * LANES]

    def output_step(step, carry):
        part, onehot = block_parts(step)
        feed_out = feed_scatter.total(part) + bias_shrink[...]
        grad = cotangent[part, :].astype(full_type)
        gate = spread_slots(onehot, modulation, 5)
        block_output[part, :] = (resid[part, :] + gate * feed_out).astype(low_type)
        slot_grads[5] += slot_sums(onehot, grad * feed_out)
        return carry + column_sum((gate * grad).astype(low_type))

    feed_bias = lax.fori_loop(0, ROW // BLOCK, output_step, jnp.zeros((1, D), full_type))
    rounded = [slot_grads[step].astype(low_type).astype(full_type) for step in range(6)]
    half = D // 2
    for block in range(DEPTH):
        for step in range(3):
            piece, side = divmod(3 * block + step, 2)
            sample_send[block, :, step * half : (step + 1) * half] = rounded[piece][:, side * half : (side + 1) * half]
    sample_copies = exchange(7, column, lambda peer: sample_send.at[peer], sample_recv.at[layer])
    sample_recv[layer] = sample_send[layer]
    put_rows(0, column_sum(grad_packed[:, 0:D]))
    put_rows(9, column_sum(grad_packed[:, 2 * D : 3 * D]))
    put_rows(18, column_sum(grad_attend[...]))
    put_rows(27, feed_bias)
    for step in range(6):
        put_rows(36 + 9 * step, column_sum(rounded[step]))
    bias_recv[place] = bias_own[pl.ds(pl.multiple_of(place * 16, 16), 16), :]
    bias_copies = exchange(
        10, plane, lambda peer: bias_own.at[pl.ds(pl.multiple_of(peer * 16, 16), 16)], bias_recv.at[place]
    )
    def settle_group(step):
        project_scatters[step].settle()
        first, width = COLUMN_GROUPS[step]
        project_own[:, :, pl.ds(first, width)] = project_scatters[step].total().astype(low_type)
        chain.edge_send(13 + step)

    project_scatters[1].forward()
    chain.inward(10)
    chain.outward(8)
    chain.inward(11)
    chain.outward(9)
    output_scatter.settle()
    output_own[...] = output_scatter.total().astype(low_type)
    chain.edge_send(12)
    chain.outward(10, 11)
    project_scatters[2].forward()
    settle_group(0)
    project_scatters[3].forward()
    project_scatters[4].forward()
    arrive(sample_copies)
    group = contract(sample_compactor(), sample_recv[...].reshape(DEPTH * 8, sample_recv.shape[2]).astype(low_type), 1, 0)
    group_all[place] = group.astype(low_type)
    group_copies = exchange(17, plane, lambda peer: group_all.at[place], group_all.at[place])
    chain.inward(12)
    arrive(bias_copies)
    total = bias_recv[0]
    for step in range(1, GROUP):
        total = total + bias_recv[step]
    bias_layers[layer, 0:16, :] = total
    bias_layers[layer, 16:24, :] = jnp.zeros((8, LANES), full_type)
    for step in range(4):
        bias_layers[layer, 16 + step : 17 + step, :] = grad_bias_expand[:, step * LANES : (step + 1) * LANES]
    bias_layers[layer, 20:21, 0:64] = grad_bias_expand[:, 512:576]
    layer_copies = exchange(24, column, lambda peer: bias_layers.at[layer], bias_layers.at[layer])
    settle_group(1)
    chain.inward(13)
    settle_group(2)
    chain.outward(12)
    settle_group(3)
    settle_group(4)
    chain.inward(14)
    chain.outward(13)
    arrive(group_copies)
    every = group_all[...].reshape(GROUP * 16, group_all.shape[2])
    spread = contract(sample_scatterer(), every, 1, 0).astype(low_type)
    terms = contract(spread, modulate[...].astype(low_type), 1, 1)
    term_send[...] = terms.reshape(term_send.shape)
    term_copies = exchange(27, column, lambda peer: term_send.at[peer], term_recv.at[layer])
    term_recv[layer] = term_send[layer]
    chain.inward(15)
    chain.outward(14)
    modulate_sum[...] = contract(active[...], every, 0, 0)
    chain.inward(16)
    arrive(layer_copies)
    total = (bias_layers[0] + bias_layers[1]) + (bias_layers[2] + bias_layers[3])
    bias_sum[place] = total
    bias_copies = exchange(30, plane, lambda peer: bias_sum.at[place], bias_sum.at[place])
    chain.outward(15)
    chain.inward(17)
    modulate_square = square_sum(modulate_sum[...])
    chain.outward(16, 17)
    arrive(term_copies)
    term_sum[...] = (term_recv[0] + term_recv[1]) + (term_recv[2] + term_recv[3])
    last_copies = exchange(37, plane, lambda peer: term_sum.at[peer], condition_sum.at[place])
    condition_sum[place] = term_sum[place]
    chain.finish()
    trunk = (
        square_sum(project_sum[...])
        + square_sum(output_sum[...])
        + square_sum(expand_sum[...])
        + square_sum(shrink_sum[...])
        + shrink_square[0:1, 0:1]
        + square_sum(bias_sum[place])
    )
    square_send[0] = jnp.broadcast_to(trunk, (8, 128))
    square_send[1] = jnp.broadcast_to(modulate_square, (8, 128))
    square_copies = exchange(44, plane, lambda peer: square_send, square_recv.at[place])
    square_recv[place] = square_send[...]
    arrive(bias_copies)
    arrive(last_copies)
    for step in range(GROUP):
        condition_grads[:, step * rows : (step + 1) * rows] = condition_sum[step, 0:IMG_ROW, :]
    given = conditions[...].astype(full_type)
    sigmoid_part = jax.nn.sigmoid(given)
    condition_grads[...] = condition_grads[...] * (sigmoid_part * (1.0 + given * (1.0 - sigmoid_part)))
    bias_flat[:, 16128:16384] = jnp.zeros((1, 256), full_type)
    for step in range(90):
        row = bias_sum[step // 16, step % 16 : step % 16 + 1, :]
        base = step * LANES if step < 27 else FF + step * LANES
        bias_flat[:, base : base + LANES] = row
    units = grad_bias_expand.shape[1]
    for step in range(GROUP):
        base = 3 * D + step * units
        for piece in range(4):
            bias_flat[:, base + piece * LANES : base + (piece + 1) * LANES] = bias_sum[step, 16 + piece : 17 + piece, :]
        bias_flat[:, base + 512 : base + 576] = bias_sum[step, 20:21, 0:64]
    shard = bias_out.shape[1]
    offset = place * shard
    start = pl.multiple_of(lax.div(offset, LANES) * LANES, LANES)
    extent = 17 * LANES
    piece = jnp.broadcast_to(bias_flat[:, pl.ds(start, extent)], (8, extent))
    piece = pltpu.roll(piece, lax.rem(extent - lax.rem(offset, LANES), extent), 1)
    bias_out[...] = piece[0:1, 0:shard]
    arrive(square_copies)
    both = square_recv[0]
    for step in range(1, GROUP):
        both = both + square_recv[step]
    square_part[...] = both
    square_all[layer] = both
    square_copies = exchange(51, column, lambda peer: square_part, square_all.at[layer])
    arrive(square_copies)
    square_total[...] = both[0] + ((square_all[0, 1] + square_all[1, 1]) + (square_all[2, 1] + square_all[3, 1]))
    for copy in waits:
        copy.wait_send()


def back_call(*operands):
    modulate, expand_parts = operands[16], operands[20]
    rows, columns = modulate.shape
    units = expand_parts.shape[2]
    shape = jax.ShapeDtypeStruct
    dma = pltpu.SemaphoreType.DMA
    return pl.pallas_call(
        back_kernel,
        out_shape=(
            shape((ROW, D), low_type),
            shape((ROW, D), full_type),
            shape((3, rows, D), low_type),
            shape((rows, D), low_type),
            shape((GROUP, rows, units), low_type),
            shape((FF // GROUP // 2, D), low_type),
            shape((1, (10 * D + FF) // GROUP), full_type),
            shape((rows, columns), full_type),
            shape((IMG_ROW, D), full_type),
            shape((8, LANES), full_type),
        ),
        in_specs=[pl.BlockSpec(memory_space=pltpu.SMEM)] + [vmem()] * 16 + [anywhere()] * 5,
        out_specs=(vmem(),) * 10,
        scratch_shapes=[
            pltpu.VMEM((4, rows, D), low_type),
            pltpu.VMEM((3, GROUP, rows, D), low_type),
            pltpu.VMEM((4, ROW, D), low_type),
            pltpu.VMEM((ROW, 3 * D), low_type),
            pltpu.VMEM((6, 8, D), full_type),
            pltpu.VMEM((3, rows, D), low_type),
            pltpu.VMEM((rows, D), low_type),
            pltpu.VMEM((GROUP, rows, units), low_type),
            pltpu.VMEM((3, rows, D), low_type),
            pltpu.VMEM((rows, D), low_type),
            pltpu.VMEM((GROUP, rows, units), low_type),
            pltpu.VMEM((FF // GROUP // 2, D), low_type),
            pltpu.VMEM((FF // GROUP // 2, D), low_type),
            pltpu.VMEM((BIAS_ROWS, LANES), full_type),
            pltpu.VMEM((GROUP, 16, LANES), full_type),
            pltpu.VMEM((DEPTH, 24, LANES), full_type),
            pltpu.VMEM((DEPTH, 8, columns), full_type),
            pltpu.VMEM((DEPTH, 8, columns), full_type),
            pltpu.VMEM((GROUP, 16, columns), low_type),
            pltpu.VMEM((DEPTH, GROUP, 8, rows), full_type),
            pltpu.VMEM((DEPTH, GROUP, 8, rows), full_type),
            pltpu.VMEM((GROUP, 8, rows), full_type),
            pltpu.VMEM((2, 8, LANES), full_type),
            pltpu.VMEM((GROUP, 2, 8, LANES), full_type),
            pltpu.VMEM((2, 8, LANES), full_type),
            pltpu.VMEM((DEPTH, 2, 8, LANES), full_type),
            dma((54,)),
            dma((54,)),
            dma((4, 18)),
            dma((13,)),
            pltpu.VMEM((ROW, 1), jnp.int32),
            pltpu.VMEM((GROUP, 24, LANES), full_type),
            pltpu.VMEM((1, 16384), full_type),
            pltpu.VMEM((GROUP, 8, rows), full_type),
            *scatter_scratch(ROW, ROW // 2, D),
            *scatter_scratch(rows, 64, D),
            *scatter_scratch(rows, 64, D, (len(COLUMN_GROUPS),)),
        ],
        compiler_params=pltpu.CompilerParams(
            collective_id=2, has_side_effects=True, vmem_limit_bytes=VMEM_BYTES
        ),
        name="backward",
    )(*operands)


TILES = 12
DEEP = 3


def update_kernel(
    square_total,
    project_sum,
    output_sum,
    expand_sum,
    shrink_low,
    shrink_high,
    modulate_sum,
    *refs,
):
    states, results, scratch = refs[0:15], refs[15:31], refs[31:]
    norm, results = results[0], results[1:]
    held, fresh, wide_held, wide_fresh, joined, load_sems, store_sems, wide_sems = scratch
    rows = output_sum.shape[0]
    units = expand_sum.shape[2]
    places = []
    whole = slice(None)
    for step in range(3):
        places.append((0, (whole, pl.ds(step * D, D)), D ** (-0.5)))
    places.append((1, (whole, whole), (D // 64) ** (-0.5)))
    for step in range(4):
        places.append((2, (whole, pl.ds(step * D, D)), D ** (-0.5)))
    for step in range(4):
        places.append((3, (pl.ds(step * rows, rows), whole), FF ** (-0.5)))

    def loads(tile):
        array, where, _ = places[tile]
        return [
            pltpu.make_async_copy(
                states[3 * array + kind].at[where], held.at[tile % DEEP, kind], load_sems.at[tile % DEEP, kind]
            )
            for kind in range(3)
        ]

    def stores(tile):
        array, where, _ = places[tile]
        return [
            pltpu.make_async_copy(
                fresh.at[tile % DEEP, kind], results[3 * array + kind].at[where], store_sems.at[tile % DEEP, kind]
            )
            for kind in range(3)
        ]

    wide_loads = [pltpu.make_async_copy(states[12 + kind], wide_held.at[kind], wide_sems.at[kind]) for kind in range(3)]
    wide_stores = [
        pltpu.make_async_copy(wide_fresh.at[kind], results[12 + kind], wide_sems.at[3 + kind]) for kind in range(3)
    ]
    for copy in wide_loads:
        copy.start()
    for tile in range(DEEP):
        for copy in loads(tile):
            copy.start()
    total = jnp.sqrt(square_total[...])
    norm[...] = total
    clip = jnp.minimum(1.0, 1.0 / (total[0:1, 0:1] + 1e-06))

    def update(before, after, grads, rate):
        def step(index, carry):
            part = pl.ds(pl.multiple_of(index * 16, 16), 16)
            grad = grads[part, :].astype(full_type) * clip
            results = adam_update(before[0, part, :], before[1, part, :], before[2, part, :], grad, rate)
            for kind in range(3):
                after[kind, part, :] = results[kind]
            return carry

        lax.fori_loop(0, rows // 16, step, 0)

    for copy in wide_loads:
        copy.wait()
    update(wide_held, wide_fresh, modulate_sum, D ** (-0.5))
    for copy in wide_stores:
        copy.start()
    for tile in range(TILES):
        for copy in loads(tile):
            copy.wait()
        if tile >= DEEP:
            for copy in stores(tile - DEEP):
                copy.wait()
        array, where, rate = places[tile]
        if array == 0:
            grads = project_sum.at[tile]
        elif array == 1:
            grads = output_sum
        elif array == 2:
            index = 2 * (tile - 4)
            joined[:, 0:units] = expand_sum[index].astype(full_type)
            joined[:, units : 2 * units] = expand_sum[index + 1].astype(full_type)
            grads = joined
        else:
            grads = (shrink_low if tile < 10 else shrink_high).at[pl.ds((tile - 8) % 2 * rows, rows)]
        update(held.at[tile % DEEP], fresh.at[tile % DEEP], grads, rate)
        for copy in stores(tile):
            copy.start()
        if tile + DEEP < TILES:
            for copy in loads(tile + DEEP):
                copy.start()
    for tile in range(TILES - DEEP, TILES):
        for copy in stores(tile):
            copy.wait()
    for copy in wide_stores:
        copy.wait()


def update_call(square_total, project_sum, output_sum, expand_sum, shrink_low, shrink_high, modulate_sum, *states):
    rows, columns = modulate_sum.shape
    shape = jax.ShapeDtypeStruct
    dma = pltpu.SemaphoreType.DMA
    results = pl.pallas_call(
        update_kernel,
        out_shape=(shape((8, LANES), full_type), *(shape(state.shape, full_type) for state in states)),
        in_specs=[vmem()] * 7 + [anywhere()] * 15,
        out_specs=(vmem(),) + (anywhere(),) * 15,
        scratch_shapes=[
            pltpu.VMEM((DEEP, 3, rows, D), full_type),
            pltpu.VMEM((DEEP, 3, rows, D), full_type),
            pltpu.VMEM((3, rows, columns), full_type),
            pltpu.VMEM((3, rows, columns), full_type),
            pltpu.VMEM((rows, D), full_type),
            dma((DEEP, 3)),
            dma((DEEP, 3)),
            dma((6,)),
        ],
        compiler_params=pltpu.CompilerParams(vmem_limit_bytes=VMEM_BYTES),
        name="update",
    )(square_total, project_sum, output_sum, expand_sum, shrink_low, shrink_high, modulate_sum, *states)
    return results[0][0, 0], results[1:]


def plane_body(
    tokens,
    conditions,
    image_lengths,
    cotangent,
    project_weight,
    project_moment,
    project_square,
    output_weight,
    output_moment,
    output_square,
    expand_weight,
    expand_moment,
    expand_square,
    shrink_weight,
    shrink_moment,
    shrink_square,
    modulate_weight,
    modulate_moment,
    modulate_square,
    bias_vector,
    bias_moment,
    bias_square,
):
    units = FF // GROUP
    (
        packed,
        attend_in,
        mixed,
        attend_out,
        resid,
        feed_in,
        modulation,
        active,
        bias_expand,
        bias_shrink,
        full_weights,
        own_expand,
        grad_all,
    ) = front_call(
        image_lengths,
        tokens,
        cotangent,
        conditions,
        bias_vector[None, :],
        project_weight,
        output_weight,
        expand_weight,
        modulate_weight,
    )
    (
        feed_parts,
        shrink_low,
        shrink_rest,
        shrink_norm,
        expand_parts,
        grad_bias_expand,
        grad_resid,
        grad_attend,
        grad_mixed,
        output_parts,
        slot_grads,
    ) = feed_call(
        image_lengths,
        feed_in,
        own_expand.reshape(D, units),
        bias_expand,
        modulation,
        cotangent,
        attend_out,
        resid,
        mixed,
        shrink_weight,
        grad_all,
        full_weights,
    )
    (
        block_output,
        token_grads,
        sum_project,
        sum_output,
        sum_expand,
        shrink_high,
        sum_bias,
        sum_modulate,
        condition_grads,
        square_total,
    ) = back_call(
        image_lengths,
        tokens,
        cotangent,
        modulation,
        packed,
        attend_in,
        resid,
        grad_resid,
        grad_attend,
        grad_mixed,
        slot_grads,
        bias_shrink,
        grad_bias_expand,
        shrink_norm,
        active,
        conditions,
        modulate_weight,
        full_weights,
        feed_parts,
        output_parts,
        expand_parts,
        shrink_rest,
    )
    global_norm, updated = update_call(
        square_total,
        sum_project,
        sum_output,
        sum_expand,
        shrink_low,
        shrink_high,
        sum_modulate,
        project_weight,
        project_moment,
        project_square,
        output_weight,
        output_moment,
        output_square,
        expand_weight,
        expand_moment,
        expand_square,
        shrink_weight,
        shrink_moment,
        shrink_square,
        modulate_weight,
        modulate_moment,
        modulate_square,
    )
    clip_factor = jnp.minimum(1.0, 1.0 / (jnp.sqrt(square_total[0, 0]) + 1e-06))
    updated_bias = adam_update(bias_vector, bias_moment, bias_square, sum_bias[0] * clip_factor, 0.3)
    return (block_output, token_grads, condition_grads, global_norm, *updated, *updated_bias)


def generic_body(
    tokens,
    conditions,
    image_lengths,
    cotangent,
    project_weight,
    project_moment,
    project_square,
    output_weight,
    output_moment,
    output_square,
    expand_weight,
    expand_moment,
    expand_square,
    shrink_weight,
    shrink_moment,
    shrink_square,
    modulate_weight,
    modulate_moment,
    modulate_square,
    bias_vector,
    bias_moment,
    bias_square,
):
    low_type = jnp.bfloat16
    group_size = lax.axis_size("mod")
    group_place = lax.axis_index("mod")
    columns = 6 * D // group_size
    full_project, full_output, full_expand, full_shrink, full_modulate, full_bias = (
        lax.all_gather(project_weight.astype(low_type), "dp", axis=0, tiled=True),
        lax.all_gather(output_weight.astype(low_type), "dp", axis=0, tiled=True),
        lax.all_gather(expand_weight.astype(low_type), "dp", axis=0, tiled=True),
        lax.all_gather(shrink_weight.astype(low_type), "dp", axis=0, tiled=True),
        lax.all_gather(modulate_weight.astype(low_type), "dp", axis=0, tiled=True),
        lax.all_gather(bias_vector.astype(low_type), "dp", axis=0, tiled=True),
    )
    bias_full = full_bias.astype(jnp.float32)
    bias_query = bias_full[0:D]
    bias_value = bias_full[D : 2 * D]
    bias_output = bias_full[2 * D : 3 * D]
    bias_expand = bias_full[3 * D : 3 * D + FF]
    bias_shrink = bias_full[3 * D + FF : 4 * D + FF]
    bias_modulate = lax.dynamic_slice_in_dim(bias_full, 4 * D + FF + group_place * columns, columns)
    group_conditions = lax.all_gather(conditions, "mod", axis=0, tiled=True)
    activated = jax.nn.silu(group_conditions.astype(jnp.float32)).astype(low_type)
    group_mod = (contract(activated, full_modulate, 1, 0) + bias_modulate).astype(low_type)
    own_mod = lax.all_to_all(group_mod, "mod", split_axis=0, concat_axis=1, tiled=True)
    slots = jnp.arange(IMG_ROW, dtype=jnp.int32)
    ends = jnp.sum(
        jnp.where(slots[:, None] <= slots[None, :], image_lengths[0][:, None], 0), axis=0, dtype=jnp.int32
    )
    positions = jnp.arange(ROW, dtype=jnp.int32)
    slot_of = jnp.sum(
        (positions[:, None] >= ends[None, :]).astype(jnp.int32), axis=1, dtype=jnp.int32
    )
    slot_match = slot_of[:, None] == jnp.arange(IMG_ROW, dtype=jnp.int32)[None, :]
    same_image = slot_of[:, None] == slot_of[None, :]
    per_token = contract(slot_match.astype(low_type), own_mod, 1, 0)
    shift_attend = per_token[:, 0:D]
    scale_attend = per_token[:, D : 2 * D]
    gate_attend = per_token[:, 2 * D : 3 * D]
    shift_feed = per_token[:, 3 * D : 4 * D]
    scale_feed = per_token[:, 4 * D : 5 * D]
    gate_feed = per_token[:, 5 * D : 6 * D]
    inputs = tokens.astype(jnp.float32)
    normed_attend, inverse_attend = normalize_rows(inputs)
    attend_in = (normed_attend * (1.0 + scale_attend) + shift_attend).astype(low_type)
    projected = contract(attend_in, full_project, 1, 0)
    query = (projected[:, 0:D] + bias_query).astype(low_type)
    keys = projected[:, D : 2 * D].astype(low_type)
    values = (projected[:, 2 * D : 3 * D] + bias_value).astype(low_type)
    head_scale = HEAD_DIM ** (-0.5)

    def split_heads(matrix):
        return matrix.reshape(ROW, HEADS, HEAD_DIM).transpose(1, 0, 2)

    def head_scores(query_head, key_head):
        return jnp.where(same_image, contract(query_head, key_head, 1, 1) * head_scale, -1e30)

    def attend_head(pieces):
        query_head, key_head, value_head = pieces
        scores = head_scores(query_head, key_head)
        row_top = jnp.max(scores, axis=1, keepdims=True)
        exponent = jnp.exp(scores - row_top)
        total = jnp.sum(exponent, axis=1, keepdims=True)
        probs = (exponent / total).astype(low_type)
        return (contract(probs, value_head, 1, 0), (row_top + jnp.log(total))[:, 0])

    heads_query = split_heads(query)
    heads_key = split_heads(keys)
    heads_value = split_heads(values)
    mixed_heads, log_totals = lax.map(attend_head, (heads_query, heads_key, heads_value))
    mixed = merge_heads(mixed_heads).astype(low_type)
    attend_out = contract(mixed, full_output, 1, 0) + bias_output
    resid = inputs + gate_attend * attend_out
    normed_feed, inverse_feed = normalize_rows(resid)
    feed_in = (normed_feed * (1.0 + scale_feed) + shift_feed).astype(low_type)
    hidden_pre = contract(feed_in, full_expand, 1, 0) + bias_expand
    tanh_part = jnp.tanh(
        tanh_scale * (hidden_pre + cubic_term * hidden_pre * hidden_pre * hidden_pre)
    )
    hidden = (0.5 * hidden_pre * (1.0 + tanh_part)).astype(low_type)
    feed_out = contract(hidden, full_shrink, 1, 0) + bias_shrink
    block_output = (resid + gate_feed * feed_out).astype(low_type)
    grad_out = cotangent.astype(jnp.float32)
    grad_gate_feed = grad_out * feed_out
    grad_feed = (gate_feed * grad_out).astype(low_type)
    grad_shrink = contract(hidden, grad_feed, 0, 0)
    grad_hidden = contract(grad_feed, full_shrink, 1, 1)
    slope = 0.5 * (1.0 + tanh_part) + 0.5 * hidden_pre * (
        1.0 - tanh_part * tanh_part
    ) * tanh_scale * (1.0 + 3.0 * cubic_term * hidden_pre * hidden_pre)
    grad_pre = (grad_hidden * slope).astype(low_type)
    grad_expand = contract(feed_in, grad_pre, 0, 0)
    grad_feed_in = contract(grad_pre, full_expand, 1, 1)
    grad_scale_feed = grad_feed_in * normed_feed
    grad_resid = grad_out + normalize_back(
        grad_feed_in * (1.0 + scale_feed), normed_feed, inverse_feed
    )
    grad_gate_attend = grad_resid * attend_out
    grad_attend = (gate_attend * grad_resid).astype(low_type)
    grad_output = contract(mixed, grad_attend, 0, 0)
    grad_mixed = contract(grad_attend, full_output, 1, 1).astype(low_type)

    def attend_back(pieces):
        query_head, key_head, value_head, grad_head, log_total = pieces
        probs = jnp.exp(head_scores(query_head, key_head) - log_total[:, None])
        grad_value = contract(probs.astype(low_type), grad_head, 0, 0)
        grad_probs = contract(grad_head, value_head, 1, 1)
        grad_scores = (
            probs * (grad_probs - jnp.sum(probs * grad_probs, axis=1, keepdims=True))
        ).astype(low_type)
        grad_query = contract(grad_scores, key_head, 1, 0) * head_scale
        grad_key = contract(grad_scores, query_head, 0, 0) * head_scale
        return (grad_query, grad_key, grad_value)

    heads_grad_query, heads_grad_key, heads_grad_value = lax.map(
        attend_back, (heads_query, heads_key, heads_value, split_heads(grad_mixed), log_totals)
    )
    grad_projected = jnp.concatenate(
        [merge_heads(heads_grad_query), merge_heads(heads_grad_key), merge_heads(heads_grad_value)],
        axis=1,
    ).astype(low_type)
    grad_project = contract(attend_in, grad_projected, 0, 0)
    grad_attend_in = contract(grad_projected, full_project, 1, 1)
    grad_scale_attend = grad_attend_in * normed_attend
    token_grads = grad_resid + normalize_back(
        grad_attend_in * (1.0 + scale_attend), normed_attend, inverse_attend
    )
    token_mod_grads = jnp.concatenate(
        [
            grad_attend_in,
            grad_scale_attend,
            grad_gate_attend,
            grad_feed_in,
            grad_scale_feed,
            grad_gate_feed,
        ],
        axis=1,
    )
    sample_grads = contract(slot_match.astype(jnp.float32), token_mod_grads, 0, 0).astype(low_type)
    group_grads = lax.all_to_all(sample_grads, "mod", split_axis=1, concat_axis=0, tiled=True)
    grad_modulate = contract(activated, group_grads, 0, 0)
    grad_bias_modulate = jnp.sum(group_grads, axis=0, dtype=jnp.float32)
    condition_terms = contract(group_grads, full_modulate, 1, 1)
    condition_sum = lax.psum_scatter(
        condition_terms.astype(jnp.bfloat16), "mod", scatter_dimension=0, tiled=True
    ).astype(jnp.float32)
    own_conditions = conditions.astype(jnp.float32)
    sigmoid_part = jax.nn.sigmoid(own_conditions)
    condition_grads = condition_sum * (sigmoid_part * (1.0 + own_conditions * (1.0 - sigmoid_part)))
    modulate_bias_grad = lax.dynamic_update_slice_in_dim(
        jnp.zeros((6 * D,), jnp.float32), grad_bias_modulate, group_place * columns, 0
    )
    grad_bias = jnp.concatenate(
        [
            jnp.sum(grad_projected[:, 0:D], axis=0, dtype=jnp.float32),
            jnp.sum(grad_projected[:, 2 * D : 3 * D], axis=0, dtype=jnp.float32),
            jnp.sum(grad_attend, axis=0, dtype=jnp.float32),
            jnp.sum(grad_pre, axis=0, dtype=jnp.float32),
            jnp.sum(grad_feed, axis=0, dtype=jnp.float32),
            modulate_bias_grad,
        ],
        axis=0,
    )
    summed = (
        lax.psum_scatter(
            grad_project.astype(jnp.bfloat16), "dp", scatter_dimension=0, tiled=True
        ).astype(jnp.float32),
        lax.psum_scatter(
            grad_output.astype(jnp.bfloat16), "dp", scatter_dimension=0, tiled=True
        ).astype(jnp.float32),
        lax.psum_scatter(
            grad_expand.astype(jnp.bfloat16), "dp", scatter_dimension=0, tiled=True
        ).astype(jnp.float32),
        lax.psum_scatter(
            grad_shrink.astype(jnp.bfloat16), "dp", scatter_dimension=0, tiled=True
        ).astype(jnp.float32),
        lax.psum_scatter(
            grad_modulate.astype(jnp.bfloat16), "dp", scatter_dimension=0, tiled=True
        ).astype(jnp.float32),
        lax.psum_scatter(
            grad_bias.astype(jnp.bfloat16), "dp", scatter_dimension=0, tiled=True
        ).astype(jnp.float32),
    )
    sum_project, sum_output, sum_expand, sum_shrink, sum_bias = (
        lax.psum(summed[0].astype(jnp.bfloat16), "mod").astype(jnp.float32),
        lax.psum(summed[1].astype(jnp.bfloat16), "mod").astype(jnp.float32),
        lax.psum(summed[2].astype(jnp.bfloat16), "mod").astype(jnp.float32),
        lax.psum(summed[3].astype(jnp.bfloat16), "mod").astype(jnp.float32),
        lax.psum(summed[5].astype(jnp.bfloat16), "mod").astype(jnp.float32),
    )
    sum_modulate = summed[4]
    trunk_square = (
        jnp.sum(sum_project * sum_project)
        + jnp.sum(sum_output * sum_output)
        + jnp.sum(sum_expand * sum_expand)
        + jnp.sum(sum_shrink * sum_shrink)
        + jnp.sum(sum_bias * sum_bias)
    )
    totals = lax.psum((trunk_square, jnp.sum(sum_modulate * sum_modulate)), ("dp", "mod"))
    global_norm = jnp.sqrt(totals[0] / group_size + totals[1])
    clip_factor = jnp.minimum(1.0, 1.0 / (global_norm + 1e-06))
    next_project, first_project, second_project = adam_update(
        project_weight, project_moment, project_square, sum_project * clip_factor, D ** (-0.5)
    )
    next_output, first_output, second_output = adam_update(
        output_weight, output_moment, output_square, sum_output * clip_factor, (D // 64) ** (-0.5)
    )
    next_expand, first_expand, second_expand = adam_update(
        expand_weight, expand_moment, expand_square, sum_expand * clip_factor, D ** (-0.5)
    )
    next_shrink, first_shrink, second_shrink = adam_update(
        shrink_weight, shrink_moment, shrink_square, sum_shrink * clip_factor, FF ** (-0.5)
    )
    next_modulate, first_modulate, second_modulate = adam_update(
        modulate_weight, modulate_moment, modulate_square, sum_modulate * clip_factor, D ** (-0.5)
    )
    next_biases, first_biases, second_biases = adam_update(
        bias_vector, bias_moment, bias_square, sum_bias * clip_factor, 0.3
    )
    return (
        block_output,
        token_grads,
        condition_grads,
        global_norm,
        next_project,
        first_project,
        second_project,
        next_output,
        first_output,
        second_output,
        next_expand,
        first_expand,
        second_expand,
        next_shrink,
        first_shrink,
        second_shrink,
        next_modulate,
        first_modulate,
        second_modulate,
        next_biases,
        first_biases,
        second_biases,
    )


def solution(mesh):
    return jax.shard_map(
        plane_body if mesh.shape["dp"] == GROUP and mesh.shape["mod"] == DEPTH else generic_body,
        mesh=mesh,
        in_specs=(
            P(("dp", "mod"), None),
            P(("dp", "mod"), None),
            P(("dp", "mod"), None),
            P(("dp", "mod"), None),
            P("dp", None),
            P("dp", None),
            P("dp", None),
            P("dp", None),
            P("dp", None),
            P("dp", None),
            P("dp", None),
            P("dp", None),
            P("dp", None),
            P("dp", None),
            P("dp", None),
            P("dp", None),
            P("dp", "mod"),
            P("dp", "mod"),
            P("dp", "mod"),
            P("dp"),
            P("dp"),
            P("dp"),
        ),
        out_specs=(
            P(("dp", "mod"), None),
            P(("dp", "mod"), None),
            P(("dp", "mod"), None),
            P(),
            P("dp", None),
            P("dp", None),
            P("dp", None),
            P("dp", None),
            P("dp", None),
            P("dp", None),
            P("dp", None),
            P("dp", None),
            P("dp", None),
            P("dp", None),
            P("dp", None),
            P("dp", None),
            P("dp", "mod"),
            P("dp", "mod"),
            P("dp", "mod"),
            P("dp"),
            P("dp"),
            P("dp"),
        ),
        check_vma=False,
    )
```

```python
import functools

import jax
import jax.numpy as jnp
from jax import lax
from jax.experimental import pallas as pl
from jax.experimental.pallas import tpu as pltpu
from jax.sharding import PartitionSpec as P

D = 1152
HEADS = 16
HEAD_DIM = 72
FF = 4608
ROW = 256
STEP = 10
IMG_ROW = 4


beta_first = 0.9
beta_second = 0.999
weight_decay = 0.01
adam_epsilon = 1e-08
tanh_scale = 0.7978845608028654
cubic_term = 0.044715


def contract(left, right, left_axis, right_axis):
    return lax.dot_general(
        left, right, (((left_axis,), (right_axis,)), ((), ())), preferred_element_type=jnp.float32
    )


def normalize_rows(values):
    center = values - jnp.mean(values, axis=-1, keepdims=True)
    inverse = lax.rsqrt(jnp.mean(center * center, axis=-1, keepdims=True) + 1e-06)
    return (center * inverse, inverse)


def normalize_back(grad_normed, normed, inverse):
    centered = grad_normed - jnp.mean(grad_normed, axis=-1, keepdims=True)
    return (centered - normed * jnp.mean(grad_normed * normed, axis=-1, keepdims=True)) * inverse


def adam_update(weight, moment, square, grad, rate):
    first = beta_first * moment + (1.0 - beta_first) * grad
    second = beta_second * square + (1.0 - beta_second) * grad * grad
    step_size = first / (1.0 - beta_first**STEP)
    divisor = jnp.sqrt(second / (1.0 - beta_second**STEP)) + adam_epsilon
    return (weight - rate * (step_size / divisor + weight_decay * weight), first, second)


def merge_heads(stacked):
    return stacked.transpose(1, 0, 2).reshape(stacked.shape[1], stacked.shape[0] * stacked.shape[2])


MESH = pl.DeviceIdType.MESH
GROUP = 8
DEPTH = 4
VMEM_BYTES = 60 << 20
low_type = jnp.bfloat16
full_type = jnp.float32


def vmem():
    return pl.BlockSpec(memory_space=pltpu.VMEM)


def anywhere():
    return pl.BlockSpec(memory_space=pl.ANY)


def plane_places():
    place = lax.axis_index("dp")
    layer = lax.axis_index("mod")
    twin = place + 1 - 2 * lax.rem(place, 2)
    side = 2 - 4 * lax.rem(lax.div(place, 2), 2)
    across = place + side
    along = place + 4 - 8 * lax.div(place, 4)
    corner = along + side
    return place, layer, twin, across, along, corner


def twin_of(place):
    return place + 1 - 2 * lax.rem(place, 2)


def send(source, target, send_sem, recv_sem, place, layer):
    copy = pltpu.make_async_remote_copy(
        src_ref=source,
        dst_ref=target,
        send_sem=send_sem,
        recv_sem=recv_sem,
        device_id=(place, layer),
        device_id_type=MESH,
    )
    copy.start()
    return copy


def greet(peers):
    barrier = pltpu.get_barrier_semaphore()
    for peer in peers:
        pl.semaphore_signal(barrier, inc=1, device_id=peer, device_id_type=MESH)
    pl.semaphore_wait(barrier, len(peers))


class Gather:
    def __init__(self, own, slots, sends, recvs, base, rows, cut):
        self.own, self.slots, self.sends, self.recvs = own, slots, sends, recvs
        self.whole = pl.ds(base, rows)
        self.first, self.second = pl.ds(base, cut), pl.ds(base + cut, rows - cut)
        self.place, self.layer, self.twin, self.across, self.along, self.corner = plane_places()
        self.copies = {}

    def push(self, index, slot, part, peer, own=False):
        target = self.slots.at[slot, part]
        source = self.own.at[part] if own else target
        self.copies[index] = send(
            source, target, self.sends.at[index], self.recvs.at[index], peer, self.layer
        )

    def start_twin(self):
        self.push(2, self.place, self.whole, self.twin, True)

    def start_links(self):
        self.push(0, self.place, self.whole, self.across, True)
        self.push(1, self.place, self.whole, self.along, True)

    def forward_near(self):
        self.copies[0].wait_recv()
        self.push(3, self.across, self.first, self.along)
        self.push(5, self.across, self.whole, self.twin)
        self.copies[1].wait_recv()
        self.push(4, self.along, self.second, self.across)
        self.push(6, self.along, self.whole, self.twin)

    def forward_far(self):
        self.copies[3].wait_recv()
        self.push(7, self.corner, self.first, self.twin)
        self.copies[4].wait_recv()
        self.push(8, self.corner, self.second, self.twin)

    def arrived(self, *indices):
        for index in indices:
            self.copies[index].wait_recv()

    def finish_sends(self):
        for index in range(9):
            self.copies[index].wait_send()


class Scatter:
    def __init__(self, parts, buffers, rows, cut, outgoing=None, columns=None):
        from_twin, half_across, half_along, whole_across, whole_along, self.sends, self.recvs = buffers
        self.first, self.second, self.rows = pl.ds(0, cut), pl.ds(cut, rows - cut), pl.ds(0, rows)
        self.place, self.layer, self.twin, self.across, self.along, self.corner = plane_places()
        self.places = (self.place, self.across, self.along, self.corner)
        self.slots = self.places if outgoing is None else (0, 1, 2, 3)
        outgoing = parts if outgoing is None else outgoing
        if columns is None:
            self.part = lambda slot, part: parts.at[slot, part]
            self.given = lambda slot: outgoing.at[slot]
            self.twin_part = lambda index, part: from_twin.at[index, part]
            self.half = (half_across, half_along)
            self.whole = (lambda part: whole_across.at[part], lambda part: whole_along.at[part])
        else:
            every = slice(None)
            self.part = lambda slot, part: parts.at[every, slot, part, columns]
            self.given = lambda slot: outgoing.at[every, slot, every, columns]
            self.twin_part = lambda index, part: from_twin.at[index, every, part, columns]
            self.half = (half_across.at[every, every, columns], half_along.at[every, every, columns])
            self.whole = (
                lambda part: whole_across.at[every, part, columns],
                lambda part: whole_along.at[every, part, columns],
            )
        self.copies = {}

    def push(self, index, source, target, peer):
        self.copies[index] = send(
            source, target, self.sends.at[index], self.recvs.at[index], peer, self.layer
        )

    def start_twin(self, *indices):
        for index in indices or (3, 1, 2, 0):
            self.push(index, self.given(twin_of(self.places[index])), self.twin_part(index, self.rows), self.twin)

    def add(self, slot, part, other):
        target = self.part(slot, part)
        target[...] = (target[...].astype(full_type) + other[...].astype(full_type)).astype(low_type)

    def merge_twin(self, index):
        self.copies[index].wait_recv()
        self.add(self.slots[index], self.rows, self.twin_part(index, self.rows))

    def start_near(self):
        _, across, along, _ = self.slots
        self.merge_twin(1)
        self.push(6, self.part(across, self.first), self.whole[0](self.first), self.across)
        self.merge_twin(2)
        self.push(7, self.part(along, self.second), self.whole[1](self.second), self.along)

    def start_far(self):
        corner = self.slots[3]
        self.merge_twin(3)
        self.push(4, self.part(corner, self.first), self.half[0], self.across)
        self.push(5, self.part(corner, self.second), self.half[1], self.along)

    def forward(self):
        _, across, along, _ = self.slots
        self.copies[5].wait_recv()
        self.add(across, self.second, self.half[1])
        self.push(8, self.part(across, self.second), self.whole[0](self.second), self.across)
        self.copies[4].wait_recv()
        self.add(along, self.first, self.half[0])
        self.push(9, self.part(along, self.first), self.whole[1](self.first), self.along)

    def settle(self):
        for index in (0, 6, 8, 7, 9):
            self.copies[index].wait_recv()
        for index in range(10):
            self.copies[index].wait_send()

    def total(self, part=None):
        part = self.rows if part is None else part
        return (
            self.part(self.slots[0], part)[...].astype(full_type)
            + self.twin_part(0, part)[...].astype(full_type)
            + (self.whole[0](part)[...].astype(full_type) + self.whole[1](part)[...].astype(full_type))
        )


def scatter_scratch(rows, cut, columns, copies=()):
    dma = pltpu.SemaphoreType.DMA
    lead = (3,) if copies else ()
    return [
        pltpu.VMEM((4,) + lead + (rows, columns), low_type),
        pltpu.VMEM(lead + (cut, columns), low_type),
        pltpu.VMEM(lead + (rows - cut, columns), low_type),
        pltpu.VMEM(lead + (rows, columns), low_type),
        pltpu.VMEM(lead + (rows, columns), low_type),
        dma(copies + (10,)),
        dma(copies + (10,)),
    ]


def iota(shape, axis):
    return lax.broadcasted_iota(jnp.int32, shape, axis)


def sample_picker():
    row, column = iota((128, 256), 0), iota((128, 256), 1)
    wanted = ((row >> 2) & 3) * 64 + (row >> 4) * 8 + (row & 3)
    return (column == wanted).astype(full_type).astype(low_type)


def slot_spreader():
    row, column = iota((32, 16), 0), iota((32, 16), 1)
    return jnp.where(((row & 7) < 4) & (column == (row >> 3) * 4 + (row & 7)), 1.0, 0.0).astype(low_type)


def head_window(head):
    start = lax.min(lax.div(head * HEAD_DIM, 128) * 128, D - 256)
    start = pl.multiple_of(start, 128)
    lane = iota((1, 256), 1) + start
    inside = (lane >= head * HEAD_DIM) & (lane < (head + 1) * HEAD_DIM)
    return start, inside.astype(full_type)


def window(ref, base, start):
    return ref[:, pl.ds(pl.multiple_of(base + start, 128), 256)]


def masked_probs(query, key, same):
    scores = jnp.where(same, contract(query, key, 1, 1) * HEAD_DIM ** (-0.5), -1e30)
    exponent = jnp.exp(scores - jnp.max(scores, axis=1, keepdims=True))
    return exponent / jnp.sum(exponent, axis=1, keepdims=True)


BLOCK = 64
LANES = 128


def slot_numbers(lengths, shape, axis):
    position = iota(shape, axis)
    slot, end = jnp.zeros(shape, jnp.int32), 0
    for step in range(IMG_ROW):
        end = end + lengths[0, step]
        slot = slot + jnp.where(position >= end, 1, 0)
    return slot


def slot_onehot(slots):
    matched = (slots == iota((slots.shape[0], 8), 1)) & (slots < IMG_ROW)
    return jnp.where(matched, 1.0, 0.0).astype(low_type)


def block_part(step):
    return pl.ds(pl.multiple_of(step * BLOCK, BLOCK), BLOCK)


def spread_slots(onehot, modulation, index):
    return contract(onehot, modulation[index].astype(low_type), 1, 0)


def front_kernel(
    lengths,
    tokens,
    cotangent,
    conditions,
    bias_own,
    project,
    output,
    expand,
    modulate,
    packed,
    attend_in,
    mixed,
    attend_out,
    resid,
    feed_in,
    modulation,
    active_out,
    bias_expand,
    bias_shrink,
    weights_out,
    expand_out,
    grad_all,
    project_load,
    output_load,
    expand_load,
    modulate_load,
    weights_own,
    weights_all,
    expand_own,
    grad_own,
    cond_send,
    cond_plane,
    cond_all,
    part_send,
    twin_recv,
    part_recv,
    mod_send,
    mod_recv,
    bias_recv,
    bias_flat,
    small_sends,
    small_recvs,
    near_sends,
    near_recvs,
    base_sends,
    base_recvs,
    far_sends,
    far_recvs,
    grad_sends,
    grad_recvs,
    local_sems,
):
    place, layer, twin, across, along, corner = plane_places()
    places = (place, across, along, corner)
    plane = [lax.rem(place + step, GROUP) for step in range(1, GROUP)]
    column = [lax.rem(layer + step, DEPTH) for step in range(1, DEPTH)]
    pair = layer + 1 - 2 * lax.rem(layer, 2)
    inner = jnp.where((layer == 0) | (layer == DEPTH - 1), 0, 1)
    rows = weights_own.shape[0]
    third = rows // 3
    shard = bias_own.shape[1]
    columns = modulate_load.shape[1]
    units = expand_own.shape[2]

    def load(index, source, target):
        copy = pltpu.make_async_copy(source, target, local_sems.at[index])
        copy.start()
        return copy

    loads = [
        load(0, project, project_load),
        load(1, modulate, modulate_load),
        load(2, output, output_load),
        load(3, expand, expand_load),
    ]
    peers = [(peer, layer) for peer in plane] + [(place, peer) for peer in column]
    barrier = pltpu.get_barrier_semaphore()
    for peer in peers:
        pl.semaphore_signal(barrier, inc=1, device_id=peer, device_id_type=MESH)
    values = conditions[...].astype(full_type)
    active = (values * jax.nn.sigmoid(values)).astype(low_type).astype(full_type)
    cond_send[...] = jnp.zeros_like(cond_send)
    for step in range(GROUP):
        cond_send[step, 0:IMG_ROW, :] = active[:, step * rows : (step + 1) * rows]
    bias_recv[place] = bias_own[...].astype(low_type).astype(full_type)
    pl.semaphore_wait(barrier, len(peers))

    waits = []

    def exchange(base, peers, source, target):
        copies = []
        for step, peer in enumerate(peers):
            where = (peer, layer) if peers is plane else (place, peer)
            copies.append(
                send(source(peer), target, small_sends.at[base + step], small_recvs.at[base + step], *where)
            )
        waits.extend(copies)
        return copies

    def arrive(copies):
        for copy in copies:
            copy.wait_recv()

    cond_copies = exchange(0, plane, lambda peer: cond_send.at[peer], cond_plane.at[place])
    cond_plane[place] = cond_send[place]
    bias_copies = exchange(7, plane, lambda peer: bias_recv.at[place], bias_recv.at[place])
    loads[0].wait()
    weights_own[:, 0 : 3 * D] = project_load[...].astype(low_type)
    loads[2].wait()
    weights_own[:, 3 * D : 4 * D] = output_load[...].astype(low_type)
    second = pl.multiple_of(third * (1 + inner), 16)
    last = pl.multiple_of(third * (2 - inner), 16)
    near = Gather(weights_own, weights_all, near_sends, near_recvs, second, third, 32)
    base = Gather(weights_own, weights_all, base_sends, base_recvs, 0, third, 16)
    near.start_links()
    near.start_twin()
    base.start_twin()
    whole = pl.ds(last, third)

    def far_copy(index, slot, part, where):
        return send(
            weights_all.at[slot, part],
            weights_all.at[slot, part],
            far_sends.at[index],
            far_recvs.at[index],
            *where,
        )

    far = [
        send(
            weights_own.at[whole], weights_all.at[place, whole], far_sends.at[0], far_recvs.at[0], twin, layer
        )
    ]
    arrive(cond_copies)
    cond_copies = exchange(14, column, lambda peer: cond_plane, cond_all.at[layer])
    cond_all[layer] = cond_plane[...]
    weights_all[place] = weights_own[...]
    loads[1].wait()
    arrive(cond_copies)
    padded = cond_all[...].reshape(DEPTH * GROUP * 8, rows).astype(low_type)
    picked = contract(sample_picker(), padded, 1, 0).astype(low_type)
    active_out[...] = picked
    partial = contract(picked, modulate_load[...].astype(low_type), 1, 0)
    part_send[...] = partial.reshape(part_send.shape)
    twin_copies = []
    for step in (1, 2, 3, 0):
        twin_copies.append(
            send(
                part_send.at[twin_of(places[step])],
                twin_recv.at[step],
                small_sends.at[17 + step],
                small_recvs.at[17 + step],
                twin,
                layer,
            )
        )
    part_copies = []
    for step, copy in zip((1, 2, 3), twin_copies):
        copy.wait_recv()
        part_send[places[step]] = part_send[places[step]] + twin_recv[step]
        part_copies.append(
            send(
                part_send.at[places[step]],
                part_recv.at[step - 1],
                small_sends.at[21 + step],
                small_recvs.at[21 + step],
                places[step],
                layer,
            )
        )
    waits += twin_copies + part_copies
    near.forward_near()
    up = (place, pair)
    far.append(far_copy(1, across, near.whole, up))
    base.start_links()
    arrive(bias_copies)
    for step in range(GROUP):
        bias_flat[:, step * shard : (step + 1) * shard] = bias_recv[step]
    start = pl.multiple_of(4 * D + FF + 2 * columns * lax.div(layer, 2), 128)
    both = bias_flat[:, pl.ds(start, 2 * columns)]
    bias_modulate = jnp.where(lax.rem(layer, 2) == 0, both[:, 0:columns], both[:, columns : 2 * columns])
    start = pl.multiple_of(3 * D + 2 * units * lax.div(place, 2), 128)
    both = bias_flat[:, pl.ds(start, 2 * units)]
    bias_expand[...] = jnp.where(lax.rem(place, 2) == 0, both[:, 0:units], both[:, units : 2 * units])
    bias_shrink[...] = bias_flat[:, 3 * D + FF : 4 * D + FF]
    arrive(twin_copies[3:] + part_copies)
    total = (part_send[place] + twin_recv[0]) + ((part_recv[0] + part_recv[1]) + part_recv[2]) + bias_modulate
    spread = contract(slot_spreader(), total.astype(low_type), 1, 0)
    mod_send[...] = spread.reshape(mod_send.shape)
    mod_copies = exchange(25, column, lambda peer: mod_send.at[peer], mod_recv.at[layer])
    mod_recv[layer] = mod_send[layer]

    far.append(far_copy(2, along, near.whole, up))
    near.forward_far()
    far.append(far_copy(3, corner, near.whole, up))
    loads[3].wait()
    for step in range(GROUP):
        expand_own[step] = expand_load[:, step * units : (step + 1) * units].astype(low_type)
    base.forward_near()

    def expand_copy(index, source, target, where):
        copy = send(source, target, small_sends.at[28 + index], small_recvs.at[28 + index], *where)
        waits.append(copy)
        return copy

    sources = [slot + (twin_of(slot) - slot) * inner for slot in (across, along, corner)]
    expand_copies = [
        expand_copy(step, expand_own.at[slot], expand_out.at[place], (slot, layer)) for step, slot in enumerate(sources)
    ]
    expand_copies.append(expand_copy(3, expand_own.at[twin], expand_out.at[place], (twin, layer)))
    arrive(mod_copies)
    half = D // 2
    for block in range(DEPTH):
        for step in range(3):
            piece, side = divmod(3 * block + step, 2)
            modulation[piece, :, side * half : (side + 1) * half] = mod_recv[block, :, step * half : (step + 1) * half]
    slot_row = slot_numbers(lengths, (1, ROW), 1)
    slot_column = slot_numbers(lengths, (ROW, 1), 0)
    onehot = slot_onehot(slot_column)

    def first_step(step):
        part = pl.ds(step * BLOCK, BLOCK)
        picked = onehot[step * BLOCK : (step + 1) * BLOCK]
        normed, _ = normalize_rows(tokens[part, :].astype(full_type))
        attend_in[part, :] = (
            normed * (1.0 + spread_slots(picked, modulation, 1)) + spread_slots(picked, modulation, 0)
        ).astype(low_type)
        grad_own[part, :] = (spread_slots(picked, modulation, 5) * cotangent[part, :].astype(full_type)).astype(low_type)

    for step in range(ROW // BLOCK):
        first_step(step)
    base.forward_far()
    grad_gather = Gather(grad_own, grad_all, grad_sends, grad_recvs, 0, ROW, ROW // 2)
    grad_gather.start_links()
    grad_gather.start_twin()
    keeps = [
        load(4, grad_own, grad_all.at[place]),
        load(5, expand_own.at[place], expand_out.at[place]),
    ]
    for index, slot in ((1, across), (2, along), (3, corner)):
        far[index].wait_recv()
        far.append(far_copy(3 + index, slot, whole, (twin, layer)))
    near.arrived(2, 5, 6, 7, 8)
    base.arrived(2, 5, 6, 7, 8)
    for index in (0, 4, 5, 6):
        far[index].wait_recv()
    for step, slot in enumerate(sources):
        expand_copies[step].wait_recv()
        expand_copies.append(expand_copy(4 + step, expand_out.at[slot], expand_out.at[slot], up))
    keeps.append(load(6, weights_all, weights_out))

    mixed[...] = jnp.zeros_like(mixed)

    def query_step(step, carry):
        where = pl.ds(pl.multiple_of(step * 384, 128), 384)
        values = contract(attend_in[...], weights_all[:, :, where].reshape(D, 384), 1, 0)
        packed[:, where] = values.astype(low_type)
        return carry

    def biased_step(step, base, carry):
        where = pl.ds(pl.multiple_of(base + step * 384, 128), 384)
        shift = bias_flat[:, pl.ds(pl.multiple_of(lax.div(base, 2) + step * 384, 128), 384)]
        values = contract(attend_in[...], weights_all[:, :, where].reshape(D, 384), 1, 0)
        packed[:, where] = (values + shift).astype(low_type)
        return carry

    lax.fori_loop(0, 3, lambda step, carry: biased_step(step, 0, carry), 0)
    lax.fori_loop(3, 6, query_step, 0)
    lax.fori_loop(0, 3, lambda step, carry: biased_step(step, 2 * D, carry), 0)
    same = slot_column == slot_row

    def head_step(head, carry):
        start, inside = head_window(head)
        keep = inside.astype(low_type)
        probs = masked_probs(window(packed, 0, start) * keep, window(packed, D, start), same)
        out = contract(probs.astype(low_type), window(packed, 2 * D, start) * keep, 1, 0)
        where = pl.ds(start, 256)
        mixed[:, where] = (mixed[:, where].astype(full_type) + out).astype(low_type)
        return carry

    lax.fori_loop(0, 8, head_step, 0, unroll=2)
    grad_gather.forward_near()
    lax.fori_loop(8, HEADS, head_step, 0, unroll=2)

    def out_step(step, carry):
        where = pl.ds(pl.multiple_of(step * 384, 128), 384)
        source = pl.ds(pl.multiple_of(3 * D + step * 384, 128), 384)
        shift = bias_flat[:, pl.ds(pl.multiple_of(2 * D + step * 384, 128), 384)]
        attend_out[:, where] = contract(mixed[...], weights_all[:, :, source].reshape(D, 384), 1, 0) + shift
        return carry

    lax.fori_loop(0, 3, out_step, 0)
    for step in range(ROW // BLOCK):
        part = pl.ds(step * BLOCK, BLOCK)
        picked = onehot[step * BLOCK : (step + 1) * BLOCK]
        joined = tokens[part, :].astype(full_type) + spread_slots(picked, modulation, 2) * attend_out[part, :]
        resid[part, :] = joined
        normed, _ = normalize_rows(joined)
        feed_in[part, :] = (
            normed * (1.0 + spread_slots(picked, modulation, 4)) + spread_slots(picked, modulation, 3)
        ).astype(low_type)
    grad_gather.forward_far()
    grad_gather.arrived(2, 5, 6, 7, 8)
    arrive(expand_copies[3:])
    for gather in (near, base, grad_gather):
        gather.finish_sends()
    for copy in far + waits:
        copy.wait_send()
    for copy in keeps:
        copy.wait()


def front_call(lengths, tokens, cotangent, conditions, bias_own, project, output, expand, modulate):
    rows, columns = modulate.shape
    units = expand.shape[1] // GROUP
    shard = bias_own.shape[1]
    shape = jax.ShapeDtypeStruct
    dma = pltpu.SemaphoreType.DMA
    return pl.pallas_call(
        front_kernel,
        out_shape=(
            shape((ROW, 3 * D), low_type),
            shape((ROW, D), low_type),
            shape((ROW, D), low_type),
            shape((ROW, D), full_type),
            shape((ROW, D), full_type),
            shape((ROW, D), low_type),
            shape((6, 8, D), full_type),
            shape((GROUP * 16, rows), low_type),
            shape((1, units), full_type),
            shape((1, D), full_type),
            shape((GROUP, rows, 4 * D), low_type),
            shape((GROUP, rows, units), low_type),
            shape((GROUP, ROW, D), low_type),
        ),
        in_specs=[pl.BlockSpec(memory_space=pltpu.SMEM)] + [vmem()] * 4 + [anywhere()] * 4,
        out_specs=(vmem(),) * 10 + (anywhere(),) * 3,
        scratch_shapes=[
            pltpu.VMEM(project.shape, full_type),
            pltpu.VMEM(output.shape, full_type),
            pltpu.VMEM(expand.shape, full_type),
            pltpu.VMEM(modulate.shape, full_type),
            pltpu.VMEM((rows, 4 * D), low_type),
            pltpu.VMEM((GROUP, rows, 4 * D), low_type),
            pltpu.VMEM((GROUP, rows, units), low_type),
            pltpu.VMEM((ROW, D), low_type),
            pltpu.VMEM((GROUP, 8, rows), full_type),
            pltpu.VMEM((GROUP, 8, rows), full_type),
            pltpu.VMEM((DEPTH, GROUP, 8, rows), full_type),
            pltpu.VMEM((GROUP, 16, columns), full_type),
            pltpu.VMEM((4, 16, columns), full_type),
            pltpu.VMEM((3, 16, columns), full_type),
            pltpu.VMEM((DEPTH, 8, columns), full_type),
            pltpu.VMEM((DEPTH, 8, columns), full_type),
            pltpu.VMEM((GROUP, 1, shard), full_type),
            pltpu.VMEM((1, GROUP * shard), full_type),
            dma((35,)),
            dma((35,)),
            dma((9,)),
            dma((9,)),
            dma((9,)),
            dma((9,)),
            dma((7,)),
            dma((7,)),
            dma((9,)),
            dma((9,)),
            dma((7,)),
        ],
        compiler_params=pltpu.CompilerParams(
            collective_id=0, has_side_effects=True, vmem_limit_bytes=VMEM_BYTES
        ),
        name="forward",
    )(lengths, tokens, cotangent, conditions, bias_own, project, output, expand, modulate)


def square_sum(values):
    values = values.astype(full_type)
    squares = values * values
    while squares.ndim > 2:
        squares = jnp.sum(squares, axis=0)
    return jnp.sum(jnp.sum(squares, axis=0, keepdims=True), axis=1, keepdims=True)


class Chain:
    def __init__(self, chunks, pair_sends, pair_recvs, mid_sends, mid_recvs):
        self.chunks = chunks
        self.place, self.layer = lax.axis_index("dp"), lax.axis_index("mod")
        self.pair = self.layer + 1 - 2 * lax.rem(self.layer, 2)
        self.edge = (self.layer == 0) | (self.layer == DEPTH - 1)
        self.middle = jnp.logical_not(self.edge)
        self.sems = (pair_sends, pair_recvs, mid_sends, mid_recvs)

    def pair_copy(self, index, source):
        return pltpu.make_async_remote_copy(
            src_ref=source,
            dst_ref=self.chunks[index][1],
            send_sem=self.sems[0].at[index],
            recv_sem=self.sems[1].at[index],
            device_id=(self.place, self.pair),
            device_id_type=MESH,
        )

    def middle_copy(self, index):
        return pltpu.make_async_remote_copy(
            src_ref=self.chunks[index][0],
            dst_ref=self.chunks[index][2],
            send_sem=self.sems[2].at[index],
            recv_sem=self.sems[3].at[index],
            device_id=(self.place, DEPTH - 1 - self.layer),
            device_id_type=MESH,
        )

    def edge_send(self, *indices):
        @pl.when(self.edge)
        def _():
            for index in indices:
                self.pair_copy(index, self.chunks[index][0]).start()

    def inward(self, *indices):
        @pl.when(self.middle)
        def _():
            for index in indices:
                given, result, _ = self.chunks[index]
                self.pair_copy(index, result).wait_recv()
                given[...] = (given[...].astype(full_type) + result[...].astype(full_type)).astype(low_type)
                self.middle_copy(index).start()

    def outward(self, *indices):
        @pl.when(self.middle)
        def _():
            for index in indices:
                given, result, other = self.chunks[index]
                self.middle_copy(index).wait()
                result[...] = (given[...].astype(full_type) + other[...].astype(full_type)).astype(low_type)
                self.pair_copy(index, result).start()

    def finish(self):
        @pl.when(self.edge)
        def _():
            for index in range(len(self.chunks)):
                self.pair_copy(index, self.chunks[index][0]).wait()

        @pl.when(self.middle)
        def _():
            for index in range(len(self.chunks)):
                self.pair_copy(index, self.chunks[index][1]).wait_send()


def slot_sums(onehot, values):
    high = values.astype(low_type)
    rest = (values - high.astype(full_type)).astype(low_type)
    return contract(onehot, high, 0, 0) + contract(onehot, rest, 0, 0)


def feed_kernel(
    lengths,
    feed_own,
    expand,
    bias,
    modulation,
    cotangent_in,
    attend_out_in,
    resid_in,
    mixed_in,
    shrink,
    grads,
    full_weights,
    feed_parts,
    shrink_sum,
    shrink_rest,
    shrink_square,
    expand_own,
    grad_bias,
    grad_resid,
    grad_attend,
    grad_mixed,
    output_parts,
    slot_grads,
    feed_all,
    grad_all,
    hidden_all,
    pre_all,
    grad_parts,
    shrink_full,
    shrink_low,
    grad_shrink,
    shrink_mid,
    grad_expand,
    output_weight,
    slots,
    cotangent,
    attend_out,
    resid,
    mixed,
    local_sems,
    feed_sends,
    feed_recvs,
    expand_sends,
    expand_recvs,
    chain_sems,
    *scratch,
):
    grad_scatter = Scatter(grad_parts, scratch, ROW, ROW // 2)
    place, layer, twin, across, along, corner = plane_places()
    plane = [lax.rem(place + step, GROUP) for step in range(1, GROUP)]
    column = [lax.rem(layer + step, DEPTH) for step in range(1, DEPTH)]
    rows = output_parts.shape[1]
    units = hidden_all.shape[2]
    feed_gather = Gather(feed_own, feed_all, feed_sends, feed_recvs, 0, ROW, ROW // 2)
    chunks, start = [], 0
    for step in range(4):
        size = 64 + 16 * (step % 2)
        part = pl.ds(start, size)
        start += size
        chunks.append((grad_shrink.at[part], shrink_sum.at[part], shrink_mid.at[part]))
    chain = Chain(chunks, *(chain_sems.at[step] for step in range(4)))
    shrink_copy = pltpu.make_async_copy(shrink, shrink_full, local_sems.at[0])
    grad_copy = pltpu.make_async_copy(grads, grad_all, local_sems.at[1])
    weight_copy = pltpu.make_async_copy(full_weights.at[:, :, pl.ds(3 * D, D)], output_weight, local_sems.at[2])
    shrink_copy.start()
    grad_copy.start()
    weight_copy.start()
    late_copies = [
        pltpu.make_async_copy(given, held, local_sems.at[5 + step])
        for step, (given, held) in enumerate(
            ((cotangent_in, cotangent), (attend_out_in, attend_out), (resid_in, resid), (mixed_in, mixed))
        )
    ]
    for copy in late_copies:
        copy.start()
    greet([(peer, layer) for peer in plane] + [(place, peer) for peer in column])
    feed_gather.start_links()
    feed_gather.start_twin()
    feed_all[place] = feed_own[...]
    shrink_copy.wait()
    shrink_low[...] = shrink_full[...].astype(low_type)
    slots[...] = slot_numbers(lengths, (ROW, 1), 0)
    slot_grads[...] = jnp.zeros_like(slot_grads)
    grad_copy.wait()

    def through(slot):
        both = pl.ds(2 * lax.div(slot, 2), 2)
        pre = contract(feed_all[both].reshape(2 * ROW, D), expand[...], 1, 0) + bias[...]
        tanh_part = jnp.tanh(tanh_scale * (pre + cubic_term * pre * pre * pre))
        hidden = (0.5 * pre * (1.0 + tanh_part)).astype(low_type)
        slope = 0.5 * (1.0 + tanh_part) + 0.5 * pre * (1.0 - tanh_part * tanh_part) * tanh_scale * (
            1.0 + 3.0 * cubic_term * pre * pre
        )
        hidden_all[both] = hidden.reshape(2, ROW, units)
        grad_hidden = contract(grad_all[both].reshape(2 * ROW, D), shrink_low[...], 1, 1)
        grad_pre = (grad_hidden * slope).astype(low_type)
        pre_all[both] = grad_pre.reshape(2, ROW, units)
        grad_parts[both] = contract(grad_pre, expand[...], 1, 1).astype(low_type).reshape(2, ROW, D)

    feed_gather.arrived(2)
    through(place)
    feed_gather.forward_near()
    feed_gather.arrived(5)
    through(across)
    grad_scatter.start_twin(1)
    feed_gather.arrived(6)
    through(along)
    grad_scatter.start_twin(2)
    feed_gather.forward_far()
    grad_scatter.start_near()
    feed_gather.arrived(7, 8)
    through(corner)
    grad_scatter.start_twin(3, 0)
    grad_scatter.start_far()

    hidden = hidden_all[...].reshape(GROUP * ROW, units)
    grad_shrink[...] = contract(hidden, grad_all[...].reshape(GROUP * ROW, D), 0, 0).astype(low_type)
    chain.edge_send(*range(4))
    shrink_rest[...] = grad_shrink[pl.ds(units // 2, units // 2), :]
    grad_pre = pre_all[...].reshape(GROUP * ROW, units)
    expand_grads = contract(feed_all[...].reshape(GROUP * ROW, D), grad_pre, 0, 0).astype(low_type)
    grad_expand[...] = expand_grads.reshape(GROUP, rows, units)
    grad_scatter.forward()
    exchange = []
    for step, peer in enumerate(plane):
        exchange.append(
            send(grad_expand.at[peer], expand_own.at[place], expand_sends.at[step], expand_recvs.at[step], peer, layer)
        )
    expand_own[place] = grad_expand[place]
    chain.inward(0)
    grad_bias[...] = jnp.sum(grad_pre.astype(full_type), axis=0, keepdims=True)

    def part_step(step, carry):
        both = pl.ds(2 * step, 2)
        parts = contract(hidden_all[both].reshape(2 * ROW, units), shrink_low[...], 1, 0)
        grad_all[both] = parts.astype(low_type).reshape(2, ROW, D)
        return carry

    lax.fori_loop(0, 2, part_step, 0)
    chain.inward(1)
    lax.fori_loop(2, GROUP // 2, part_step, 0)
    feed_copy = pltpu.make_async_copy(grad_all, feed_parts, local_sems.at[3])
    feed_copy.start()
    chain.inward(2)
    chain.outward(0)
    chain.inward(3)
    chain.outward(1)
    for copy in late_copies:
        copy.wait()
    grad_scatter.settle()
    chain.outward(2)

    def feed_step(step, carry):
        part = block_part(step)
        onehot = slot_onehot(slots[part, :])
        normed, inverse = normalize_rows(resid[part, :])
        grad_in = grad_scatter.total(part)
        slot_grads[3] += slot_sums(onehot, grad_in)
        slot_grads[4] += slot_sums(onehot, grad_in * normed)
        grad = cotangent[part, :].astype(full_type) + normalize_back(
            grad_in * (1.0 + spread_slots(onehot, modulation, 4)), normed, inverse
        )
        grad_resid[part, :] = grad
        slot_grads[2] += slot_sums(onehot, grad * attend_out[part, :])
        grad_attend[part, :] = (spread_slots(onehot, modulation, 2) * grad).astype(low_type)
        return carry

    lax.fori_loop(0, ROW // BLOCK // 2, feed_step, 0)
    chain.outward(3)
    lax.fori_loop(ROW // BLOCK // 2, ROW // BLOCK, feed_step, 0)
    weight_copy.wait()
    grad_mixed[...] = contract(grad_attend[...], output_weight[...].reshape(D, D), 1, 1).astype(low_type)

    def weight_step(step, carry):
        where = pl.ds(pl.multiple_of(step * 384, 128), 384)
        values = contract(mixed[...], grad_attend[:, where], 0, 0).astype(low_type)
        output_weight[:, :, where] = values.reshape(GROUP, rows, 384)
        return carry

    lax.fori_loop(0, 3, weight_step, 0)
    output_copy = pltpu.make_async_copy(output_weight, output_parts, local_sems.at[4])
    output_copy.start()
    feed_copy.wait()
    output_copy.wait()
    feed_gather.finish_sends()
    for copy in exchange:
        copy.wait()
    chain.finish()
    shrink_square[...] = jnp.broadcast_to(square_sum(shrink_sum[...]), shrink_square.shape)


def feed_call(
    lengths, feed_own, expand, bias, modulation, cotangent, attend_out, resid, mixed, shrink, grads, full_weights
):
    units = expand.shape[1]
    rows = full_weights.shape[1]
    shape = jax.ShapeDtypeStruct
    dma = pltpu.SemaphoreType.DMA
    return pl.pallas_call(
        feed_kernel,
        out_shape=(
            shape((GROUP, ROW, D), low_type),
            shape((units // 2, D), low_type),
            shape((units // 2, D), low_type),
            shape((8, LANES), full_type),
            shape((GROUP, rows, units), low_type),
            shape((1, units), full_type),
            shape((ROW, D), full_type),
            shape((ROW, D), low_type),
            shape((ROW, D), low_type),
            shape((GROUP, rows, D), low_type),
            shape((6, 8, D), full_type),
        ),
        in_specs=[pl.BlockSpec(memory_space=pltpu.SMEM)] + [vmem()] * 4 + [anywhere()] * 7,
        out_specs=(anywhere(),) + (vmem(),) * 8 + (anywhere(), vmem()),
        scratch_shapes=[
            pltpu.VMEM((GROUP, ROW, D), low_type),
            pltpu.VMEM((GROUP, ROW, D), low_type),
            pltpu.VMEM((GROUP, ROW, units), low_type),
            pltpu.VMEM((GROUP, ROW, units), low_type),
            pltpu.VMEM((GROUP, ROW, D), low_type),
            pltpu.VMEM((units, D), full_type),
            pltpu.VMEM((units, D), low_type),
            pltpu.VMEM((units, D), low_type),
            pltpu.VMEM((units // 2, D), low_type),
            pltpu.VMEM((GROUP, rows, units), low_type),
            pltpu.VMEM((GROUP, rows, D), low_type),
            pltpu.VMEM((ROW, 1), jnp.int32),
            pltpu.VMEM((ROW, D), low_type),
            pltpu.VMEM((ROW, D), full_type),
            pltpu.VMEM((ROW, D), full_type),
            pltpu.VMEM((ROW, D), low_type),
            dma((9,)),
            dma((9,)),
            dma((9,)),
            dma((7,)),
            dma((7,)),
            dma((4, 8)),
            *scatter_scratch(ROW, ROW // 2, D),
        ],
        compiler_params=pltpu.CompilerParams(
            collective_id=1, has_side_effects=True, vmem_limit_bytes=VMEM_BYTES
        ),
        name="feed_forward",
    )(lengths, feed_own, expand, bias, modulation, cotangent, attend_out, resid, mixed, shrink, grads, full_weights)


def sample_compactor():
    row, column = iota((16, 32), 0), iota((16, 32), 1)
    return (column == (row >> 2) * 8 + (row & 3)).astype(full_type).astype(low_type)


def sample_scatterer():
    row, column = iota((256, 128), 0), iota((256, 128), 1)
    wanted = ((row >> 3) & 7) * 16 + (row >> 6) * 4 + (row & 7)
    return jnp.where(((row & 7) < 4) & (column == wanted), 1.0, 0.0).astype(low_type)


def column_sum(values):
    return jnp.sum(values.astype(full_type), axis=0, keepdims=True)


BIAS_ROWS = 128
COLUMN_GROUPS = ((0, 512), (512, 256), (768, 384))
CHAIN_COLUMNS = ((0, 256), (256, 256), (512, 256), (768, 256), (1024, 128))
GROUP_CHUNKS = ((13, 14), (15,), (16, 17))


def back_kernel(
    lengths,
    tokens_in,
    cotangent_in,
    modulation,
    packed,
    attend_given,
    resid_in,
    grad_resid_in,
    grad_attend,
    grad_mixed,
    slot_grads_in,
    bias_shrink,
    grad_bias_expand,
    shrink_square,
    active,
    conditions,
    modulate,
    full_weights,
    feed_parts_in,
    output_parts,
    expand_parts,
    shrink_rest,
    block_output,
    token_grads,
    project_sum,
    output_sum,
    expand_sum,
    shrink_sum,
    bias_out,
    modulate_sum,
    condition_grads,
    square_total,
    output_store,
    project_store,
    feed_parts,
    grad_packed,
    slot_grads,
    project_own,
    output_own,
    expand_own,
    project_mid,
    output_mid,
    expand_mid,
    shrink_own,
    shrink_mid,
    bias_own,
    bias_recv,
    bias_layers,
    sample_send,
    sample_recv,
    group_all,
    term_send,
    term_recv,
    term_sum,
    square_send,
    square_recv,
    square_part,
    square_all,
    small_sends,
    small_recvs,
    chain_sems,
    local_sems,
    slots,
    bias_sum,
    bias_flat,
    condition_sum,
    tokens,
    cotangent,
    attend_in,
    resid,
    grad_resid,
    *scratch,
):
    place, layer, *_ = plane_places()
    plane = [lax.rem(place + step, GROUP) for step in range(1, GROUP)]
    column = [lax.rem(layer + step, DEPTH) for step in range(1, DEPTH)]
    rows = output_own.shape[0]
    scale = HEAD_DIM ** (-0.5)

    chunks, start = [], 0
    for step in range(4):
        size = 64 + 16 * (step % 2)
        part = pl.ds(start, size)
        start += size
        chunks.append((shrink_own.at[part], shrink_sum.at[part], shrink_mid.at[part]))
    for step in range(GROUP):
        chunks.append((expand_own.at[step], expand_sum.at[step], expand_mid.at[step]))
    chunks.append((output_own, output_sum, output_mid))
    for first, width in CHAIN_COLUMNS:
        part = (slice(None), slice(None), pl.ds(first, width))
        chunks.append((project_own.at[part], project_sum.at[part], project_mid.at[part]))
    chain = Chain(chunks, *(chain_sems.at[step] for step in range(4)))

    waits = []

    def exchange(base, peers, source, target):
        copies = []
        for step, peer in enumerate(peers):
            where = (peer, layer) if peers is plane else (place, peer)
            copies.append(
                send(source(peer), target, small_sends.at[base + step], small_recvs.at[base + step], *where)
            )
        waits.extend(copies)
        return copies

    def arrive(copies):
        for copy in copies:
            copy.wait_recv()

    def load(index, source, target):
        copy = pltpu.make_async_copy(source, target, local_sems.at[index])
        copy.start()
        return copy

    feed_scatter = Scatter(feed_parts, scratch[0:7], ROW, ROW // 2, outgoing=feed_parts_in)
    output_scatter = Scatter(output_store, scratch[7:14], rows, 64, outgoing=output_parts)
    project_scatters = []
    for step, (first, width) in enumerate(COLUMN_GROUPS):
        buffers = (*scratch[14:19], scratch[19].at[step], scratch[20].at[step])
        project_scatters.append(
            Scatter(project_store, buffers, rows, 64, columns=pl.ds(first, width))
        )
    shrink_load = load(12, shrink_rest, shrink_own)
    expand_load = load(0, expand_parts, expand_own)
    feed_loads = [
        load(1 + step, feed_parts_in.at[feed_scatter.places[step]], feed_parts.at[step]) for step in range(4)
    ]
    output_loads = [
        load(5 + step, output_parts.at[feed_scatter.places[step]], output_store.at[step]) for step in range(4)
    ]
    late_loads = [
        load(13 + step, given, held)
        for step, (given, held) in enumerate(
            (
                (attend_given, attend_in),
                (tokens_in, tokens),
                (grad_resid_in, grad_resid),
                (cotangent_in, cotangent),
                (resid_in, resid),
            )
        )
    ]
    project_loads = [
        load(9 + step, full_weights.at[:, :, pl.ds(step * D, D)], project_store.at[step]) for step in range(3)
    ]

    greet([(peer, layer) for peer in plane] + [(place, peer) for peer in column])

    feed_scatter.start_twin()
    output_scatter.start_twin()
    shrink_load.wait()
    chain.edge_send(*range(4))
    expand_load.wait()
    chain.edge_send(*range(4, 12))
    slot_grads[...] = slot_grads_in[...]
    bias_own[...] = jnp.zeros_like(bias_own)
    grad_packed[...] = jnp.zeros_like(grad_packed)

    slot_row = slot_numbers(lengths, (1, ROW), 1)
    slot_column = slot_numbers(lengths, (ROW, 1), 0)
    slots[...] = slot_column

    def block_parts(step):
        part = block_part(step)
        return part, slot_onehot(slots[part, :])

    same = slot_column == slot_row

    def head_step(head, carry):
        start, inside = head_window(head)
        keep = inside.astype(low_type)
        query = window(packed, 0, start) * keep
        key = window(packed, D, start)
        value = window(packed, 2 * D, start)
        grad = window(grad_mixed, 0, start) * keep
        probs = masked_probs(query, key, same)
        grad_probs = contract(grad, value, 1, 1)
        grad_scores = probs * (grad_probs - jnp.sum(probs * grad_probs, axis=1, keepdims=True))
        grad_scores = grad_scores.astype(low_type)

        def put(base, values):
            where = pl.ds(pl.multiple_of(base + start, 128), 256)
            grad_packed[:, where] = (grad_packed[:, where].astype(full_type) + values).astype(low_type)

        put(0, contract(grad_scores, key * keep, 1, 0) * scale)
        put(D, contract(grad_scores, query, 0, 0) * scale)
        put(2 * D, contract(probs.astype(low_type), grad, 0, 0))
        return carry

    def heads(first, last):
        lax.fori_loop(first, last, head_step, 0, unroll=2)

    def project_group(step):
        first, width = COLUMN_GROUPS[step]
        for kind in range(3):
            where = pl.ds(first, width)
            grads = grad_packed[:, kind * D + first : kind * D + first + width]
            back = contract(grads, project_store[kind, :, :, where].reshape(D, width), 1, 1)
            if step == 0 and kind == 0:
                token_grads[...] = back
            else:
                token_grads[...] += back
            weight = contract(attend_in[...], grads, 0, 0).astype(low_type)
            project_store[kind, :, :, where] = weight.reshape(GROUP, rows, width)
        project_scatters[step].start_twin()

    heads(0, 4)
    for copy in feed_loads:
        copy.wait()
    feed_scatter.start_far()
    feed_scatter.start_near()
    for copy in output_loads:
        copy.wait()
    output_scatter.start_far()
    output_scatter.start_near()
    chain.inward(0)
    chain.inward(1)
    heads(4, 8)
    chain.inward(2)
    chain.outward(0)
    for copy in project_loads + late_loads:
        copy.wait()
    project_group(0)
    feed_scatter.forward()
    chain.inward(3)
    chain.outward(1)
    heads(8, 12)
    chain.inward(4)
    chain.outward(2)
    project_scatters[0].start_far()
    project_scatters[0].start_near()
    project_group(1)
    chain.inward(5)
    chain.outward(3)
    output_scatter.forward()
    heads(12, 16)
    chain.inward(6)
    chain.outward(4)
    chain.inward(7)
    chain.outward(5)
    project_scatters[1].start_far()
    project_scatters[1].start_near()
    project_group(2)
    project_scatters[0].forward()
    chain.inward(8)
    chain.outward(6)

    def attend_step(step, carry):
        part, onehot = block_parts(step)
        normed, inverse = normalize_rows(tokens[part, :].astype(full_type))
        grad_in = token_grads[part, :]
        slot_grads[0] += slot_sums(onehot, grad_in)
        slot_grads[1] += slot_sums(onehot, grad_in * normed)
        token_grads[part, :] = grad_resid[part, :] + normalize_back(
            grad_in * (1.0 + spread_slots(onehot, modulation, 1)), normed, inverse
        )
        return carry

    lax.fori_loop(0, ROW // BLOCK, attend_step, 0)
    project_scatters[2].start_far()
    project_scatters[2].start_near()
    chain.inward(9)
    chain.outward(7)
    feed_scatter.settle()

    def put_rows(base, values):
        for step in range(values.shape[1] // LANES):
            bias_own[base + step : base + step + 1, :] = values[:, step * LANES : (step + 1) * LANES]

    def output_step(step, carry):
        part, onehot = block_parts(step)
        feed_out = feed_scatter.total(part) + bias_shrink[...]
        grad = cotangent[part, :].astype(full_type)
        gate = spread_slots(onehot, modulation, 5)
        block_output[part, :] = (resid[part, :] + gate * feed_out).astype(low_type)
        slot_grads[5] += slot_sums(onehot, grad * feed_out)
        return carry + column_sum((gate * grad).astype(low_type))

    feed_bias = lax.fori_loop(0, ROW // BLOCK, output_step, jnp.zeros((1, D), full_type))
    rounded = [slot_grads[step].astype(low_type).astype(full_type) for step in range(6)]
    half = D // 2
    for block in range(DEPTH):
        for step in range(3):
            piece, side = divmod(3 * block + step, 2)
            sample_send[block, :, step * half : (step + 1) * half] = rounded[piece][:, side * half : (side + 1) * half]
    sample_copies = exchange(7, column, lambda peer: sample_send.at[peer], sample_recv.at[layer])
    sample_recv[layer] = sample_send[layer]
    put_rows(0, column_sum(grad_packed[:, 0:D]))
    put_rows(9, column_sum(grad_packed[:, 2 * D : 3 * D]))
    put_rows(18, column_sum(grad_attend[...]))
    put_rows(27, feed_bias)
    for step in range(6):
        put_rows(36 + 9 * step, column_sum(rounded[step]))
    bias_recv[place] = bias_own[pl.ds(pl.multiple_of(place * 16, 16), 16), :]
    bias_copies = exchange(
        10, plane, lambda peer: bias_own.at[pl.ds(pl.multiple_of(peer * 16, 16), 16)], bias_recv.at[place]
    )
    def settle_group(step):
        project_scatters[step].settle()
        first, width = COLUMN_GROUPS[step]
        project_own[:, :, pl.ds(first, width)] = project_scatters[step].total().astype(low_type)
        chain.edge_send(*GROUP_CHUNKS[step])

    project_scatters[1].forward()
    chain.inward(10)
    chain.outward(8)
    chain.inward(11)
    chain.outward(9)
    output_scatter.settle()
    output_own[...] = output_scatter.total().astype(low_type)
    chain.edge_send(12)
    chain.outward(10, 11)
    project_scatters[2].forward()
    settle_group(0)
    arrive(sample_copies)
    group = contract(sample_compactor(), sample_recv[...].reshape(DEPTH * 8, sample_recv.shape[2]).astype(low_type), 1, 0)
    group_all[place] = group.astype(low_type)
    group_copies = exchange(17, plane, lambda peer: group_all.at[place], group_all.at[place])
    chain.inward(12)
    arrive(bias_copies)
    total = bias_recv[0]
    for step in range(1, GROUP):
        total = total + bias_recv[step]
    bias_layers[layer, 0:16, :] = total
    bias_layers[layer, 16:24, :] = jnp.zeros((8, LANES), full_type)
    for step in range(4):
        bias_layers[layer, 16 + step : 17 + step, :] = grad_bias_expand[:, step * LANES : (step + 1) * LANES]
    bias_layers[layer, 20:21, 0:64] = grad_bias_expand[:, 512:576]
    layer_copies = exchange(24, column, lambda peer: bias_layers.at[layer], bias_layers.at[layer])
    settle_group(1)
    chain.inward(13)
    chain.outward(12)
    settle_group(2)
    chain.inward(14)
    chain.outward(13)
    arrive(group_copies)
    every = group_all[...].reshape(GROUP * 16, group_all.shape[2])
    spread = contract(sample_scatterer(), every, 1, 0).astype(low_type)
    terms = contract(spread, modulate[...].astype(low_type), 1, 1)
    term_send[...] = terms.reshape(term_send.shape)
    term_copies = exchange(27, column, lambda peer: term_send.at[peer], term_recv.at[layer])
    term_recv[layer] = term_send[layer]
    chain.inward(15)
    chain.outward(14)
    modulate_sum[...] = contract(active[...], every, 0, 0)
    chain.inward(16)
    arrive(layer_copies)
    total = (bias_layers[0] + bias_layers[1]) + (bias_layers[2] + bias_layers[3])
    bias_sum[place] = total
    bias_copies = exchange(30, plane, lambda peer: bias_sum.at[place], bias_sum.at[place])
    chain.outward(15)
    chain.inward(17)
    square_part[...] = jnp.broadcast_to(square_sum(modulate_sum[...]), (8, LANES))
    square_all[layer] = square_part[...]
    square_copies = exchange(51, column, lambda peer: square_part, square_all.at[layer])
    chain.outward(16, 17)
    arrive(term_copies)
    term_sum[...] = (term_recv[0] + term_recv[1]) + (term_recv[2] + term_recv[3])
    last_copies = exchange(37, plane, lambda peer: term_sum.at[peer], condition_sum.at[place])
    condition_sum[place] = term_sum[place]
    arrive(bias_copies)
    arrive(last_copies)
    for step in range(GROUP):
        condition_grads[:, step * rows : (step + 1) * rows] = condition_sum[step, 0:IMG_ROW, :]
    given = conditions[...].astype(full_type)
    sigmoid_part = jax.nn.sigmoid(given)
    condition_grads[...] = condition_grads[...] * (sigmoid_part * (1.0 + given * (1.0 - sigmoid_part)))
    bias_flat[:, 16128:16384] = jnp.zeros((1, 256), full_type)
    for step in range(90):
        row = bias_sum[step // 16, step % 16 : step % 16 + 1, :]
        base = step * LANES if step < 27 else FF + step * LANES
        bias_flat[:, base : base + LANES] = row
    units = grad_bias_expand.shape[1]
    for step in range(GROUP):
        base = 3 * D + step * units
        for piece in range(4):
            bias_flat[:, base + piece * LANES : base + (piece + 1) * LANES] = bias_sum[step, 16 + piece : 17 + piece, :]
        bias_flat[:, base + 512 : base + 576] = bias_sum[step, 20:21, 0:64]
    shard = bias_out.shape[1]
    offset = place * shard
    start = pl.multiple_of(lax.div(offset, LANES) * LANES, LANES)
    extent = 17 * LANES
    piece = jnp.broadcast_to(bias_flat[:, pl.ds(start, extent)], (8, extent))
    piece = pltpu.roll(piece, lax.rem(extent - lax.rem(offset, LANES), extent), 1)
    bias_out[...] = piece[0:1, 0:shard]
    arrive(square_copies)
    modulate_square = (square_all[0] + square_all[1]) + (square_all[2] + square_all[3])
    chain.finish()
    trunk = (
        square_sum(project_sum[...])
        + square_sum(output_sum[...])
        + square_sum(expand_sum[...])
        + square_sum(shrink_sum[...])
        + shrink_square[0:1, 0:1]
        + square_sum(bias_sum[place])
    )
    square_send[...] = jnp.broadcast_to(trunk, (8, LANES)) + modulate_square
    square_copies = exchange(44, plane, lambda peer: square_send, square_recv.at[place])
    square_recv[place] = square_send[...]
    arrive(square_copies)
    both = square_recv[0]
    for step in range(1, GROUP):
        both = both + square_recv[step]
    square_total[...] = both
    bias_out[...] = bias_out[...] * jnp.minimum(1.0, 1.0 / (jnp.sqrt(both[0:1, 0:1]) + 1e-06))
    for copy in waits:
        copy.wait_send()


def back_call(*operands):
    modulate, expand_parts = operands[16], operands[20]
    rows, columns = modulate.shape
    units = expand_parts.shape[2]
    shape = jax.ShapeDtypeStruct
    dma = pltpu.SemaphoreType.DMA
    return pl.pallas_call(
        back_kernel,
        out_shape=(
            shape((ROW, D), low_type),
            shape((ROW, D), full_type),
            shape((3, rows, D), low_type),
            shape((rows, D), low_type),
            shape((GROUP, rows, units), low_type),
            shape((FF // GROUP // 2, D), low_type),
            shape((1, (10 * D + FF) // GROUP), full_type),
            shape((rows, columns), full_type),
            shape((IMG_ROW, D), full_type),
            shape((8, LANES), full_type),
        ),
        in_specs=[pl.BlockSpec(memory_space=pltpu.SMEM)]
        + [anywhere()] * 2
        + [vmem()] * 2
        + [anywhere()] * 3
        + [vmem()] * 9
        + [anywhere()] * 5,
        out_specs=(vmem(),) * 10,
        scratch_shapes=[
            pltpu.VMEM((4, rows, D), low_type),
            pltpu.VMEM((3, GROUP, rows, D), low_type),
            pltpu.VMEM((4, ROW, D), low_type),
            pltpu.VMEM((ROW, 3 * D), low_type),
            pltpu.VMEM((6, 8, D), full_type),
            pltpu.VMEM((3, rows, D), low_type),
            pltpu.VMEM((rows, D), low_type),
            pltpu.VMEM((GROUP, rows, units), low_type),
            pltpu.VMEM((3, rows, D), low_type),
            pltpu.VMEM((rows, D), low_type),
            pltpu.VMEM((GROUP, rows, units), low_type),
            pltpu.VMEM((FF // GROUP // 2, D), low_type),
            pltpu.VMEM((FF // GROUP // 2, D), low_type),
            pltpu.VMEM((BIAS_ROWS, LANES), full_type),
            pltpu.VMEM((GROUP, 16, LANES), full_type),
            pltpu.VMEM((DEPTH, 24, LANES), full_type),
            pltpu.VMEM((DEPTH, 8, columns), full_type),
            pltpu.VMEM((DEPTH, 8, columns), full_type),
            pltpu.VMEM((GROUP, 16, columns), low_type),
            pltpu.VMEM((DEPTH, GROUP, 8, rows), full_type),
            pltpu.VMEM((DEPTH, GROUP, 8, rows), full_type),
            pltpu.VMEM((GROUP, 8, rows), full_type),
            pltpu.VMEM((8, LANES), full_type),
            pltpu.VMEM((GROUP, 8, LANES), full_type),
            pltpu.VMEM((8, LANES), full_type),
            pltpu.VMEM((DEPTH, 8, LANES), full_type),
            dma((54,)),
            dma((54,)),
            dma((4, 18)),
            dma((18,)),
            pltpu.VMEM((ROW, 1), jnp.int32),
            pltpu.VMEM((GROUP, 24, LANES), full_type),
            pltpu.VMEM((1, 16384), full_type),
            pltpu.VMEM((GROUP, 8, rows), full_type),
            pltpu.VMEM((ROW, D), low_type),
            pltpu.VMEM((ROW, D), low_type),
            pltpu.VMEM((ROW, D), low_type),
            pltpu.VMEM((ROW, D), full_type),
            pltpu.VMEM((ROW, D), full_type),
            *scatter_scratch(ROW, ROW // 2, D),
            *scatter_scratch(rows, 64, D),
            *scatter_scratch(rows, 64, D, (len(COLUMN_GROUPS),)),
        ],
        compiler_params=pltpu.CompilerParams(
            collective_id=2, has_side_effects=True, vmem_limit_bytes=VMEM_BYTES
        ),
        name="backward",
    )(*operands)


TILES = 12
DEEP = 3


def update_kernel(
    square_total,
    project_sum,
    output_sum,
    expand_sum,
    shrink_low,
    shrink_high,
    modulate_sum,
    *refs,
):
    states, results, scratch = refs[0:15], refs[15:31], refs[31:]
    norm, results = results[0], results[1:]
    held, fresh, wide_held, wide_fresh, joined, load_sems, store_sems, wide_sems = scratch
    rows = output_sum.shape[0]
    units = expand_sum.shape[2]
    places = []
    whole = slice(None)
    for step in range(3):
        places.append((0, (whole, pl.ds(step * D, D)), D ** (-0.5)))
    places.append((1, (whole, whole), (D // 64) ** (-0.5)))
    for step in range(4):
        places.append((2, (whole, pl.ds(step * D, D)), D ** (-0.5)))
    for step in range(4):
        places.append((3, (pl.ds(step * rows, rows), whole), FF ** (-0.5)))

    def loads(tile):
        array, where, _ = places[tile]
        return [
            pltpu.make_async_copy(
                states[3 * array + kind].at[where], held.at[tile % DEEP, kind], load_sems.at[tile % DEEP, kind]
            )
            for kind in range(3)
        ]

    def stores(tile):
        array, where, _ = places[tile]
        return [
            pltpu.make_async_copy(
                fresh.at[tile % DEEP, kind], results[3 * array + kind].at[where], store_sems.at[tile % DEEP, kind]
            )
            for kind in range(3)
        ]

    wide_loads = [pltpu.make_async_copy(states[12 + kind], wide_held.at[kind], wide_sems.at[kind]) for kind in range(3)]
    wide_stores = [
        pltpu.make_async_copy(wide_fresh.at[kind], results[12 + kind], wide_sems.at[3 + kind]) for kind in range(3)
    ]
    for copy in wide_loads:
        copy.start()
    for tile in range(DEEP):
        for copy in loads(tile):
            copy.start()
    total = jnp.sqrt(square_total[...])
    norm[...] = total
    clip = jnp.minimum(1.0, 1.0 / (total[0:1, 0:1] + 1e-06))

    def update(before, after, grads, rate):
        def step(index, carry):
            part = pl.ds(pl.multiple_of(index * 16, 16), 16)
            grad = grads[part, :].astype(full_type) * clip
            results = adam_update(before[0, part, :], before[1, part, :], before[2, part, :], grad, rate)
            for kind in range(3):
                after[kind, part, :] = results[kind]
            return carry

        lax.fori_loop(0, rows // 16, step, 0)

    for copy in wide_loads:
        copy.wait()
    update(wide_held, wide_fresh, modulate_sum, D ** (-0.5))
    for copy in wide_stores:
        copy.start()
    for tile in range(TILES):
        for copy in loads(tile):
            copy.wait()
        if tile >= DEEP:
            for copy in stores(tile - DEEP):
                copy.wait()
        array, where, rate = places[tile]
        if array == 0:
            grads = project_sum.at[tile]
        elif array == 1:
            grads = output_sum
        elif array == 2:
            index = 2 * (tile - 4)
            joined[:, 0:units] = expand_sum[index].astype(full_type)
            joined[:, units : 2 * units] = expand_sum[index + 1].astype(full_type)
            grads = joined
        else:
            grads = (shrink_low if tile < 10 else shrink_high).at[pl.ds((tile - 8) % 2 * rows, rows)]
        update(held.at[tile % DEEP], fresh.at[tile % DEEP], grads, rate)
        for copy in stores(tile):
            copy.start()
        if tile + DEEP < TILES:
            for copy in loads(tile + DEEP):
                copy.start()
    for tile in range(TILES - DEEP, TILES):
        for copy in stores(tile):
            copy.wait()
    for copy in wide_stores:
        copy.wait()


def update_call(square_total, project_sum, output_sum, expand_sum, shrink_low, shrink_high, modulate_sum, *states):
    rows, columns = modulate_sum.shape
    shape = jax.ShapeDtypeStruct
    dma = pltpu.SemaphoreType.DMA
    results = pl.pallas_call(
        update_kernel,
        out_shape=(shape((8, LANES), full_type), *(shape(state.shape, full_type) for state in states)),
        in_specs=[vmem()] * 7 + [anywhere()] * 15,
        out_specs=(vmem(),) + (anywhere(),) * 15,
        scratch_shapes=[
            pltpu.VMEM((DEEP, 3, rows, D), full_type),
            pltpu.VMEM((DEEP, 3, rows, D), full_type),
            pltpu.VMEM((3, rows, columns), full_type),
            pltpu.VMEM((3, rows, columns), full_type),
            pltpu.VMEM((rows, D), full_type),
            dma((DEEP, 3)),
            dma((DEEP, 3)),
            dma((6,)),
        ],
        compiler_params=pltpu.CompilerParams(vmem_limit_bytes=VMEM_BYTES),
        name="update",
    )(square_total, project_sum, output_sum, expand_sum, shrink_low, shrink_high, modulate_sum, *states)
    return results[0][0, 0], results[1:]


def plane_body(
    tokens,
    conditions,
    image_lengths,
    cotangent,
    project_weight,
    project_moment,
    project_square,
    output_weight,
    output_moment,
    output_square,
    expand_weight,
    expand_moment,
    expand_square,
    shrink_weight,
    shrink_moment,
    shrink_square,
    modulate_weight,
    modulate_moment,
    modulate_square,
    bias_vector,
    bias_moment,
    bias_square,
):
    units = FF // GROUP
    (
        packed,
        attend_in,
        mixed,
        attend_out,
        resid,
        feed_in,
        modulation,
        active,
        bias_expand,
        bias_shrink,
        full_weights,
        own_expand,
        grad_all,
    ) = front_call(
        image_lengths,
        tokens,
        cotangent,
        conditions,
        bias_vector[None, :],
        project_weight,
        output_weight,
        expand_weight,
        modulate_weight,
    )
    (
        feed_parts,
        shrink_low,
        shrink_rest,
        shrink_norm,
        expand_parts,
        grad_bias_expand,
        grad_resid,
        grad_attend,
        grad_mixed,
        output_parts,
        slot_grads,
    ) = feed_call(
        image_lengths,
        feed_in,
        own_expand.reshape(D, units),
        bias_expand,
        modulation,
        cotangent,
        attend_out,
        resid,
        mixed,
        shrink_weight,
        grad_all,
        full_weights,
    )
    (
        block_output,
        token_grads,
        sum_project,
        sum_output,
        sum_expand,
        shrink_high,
        sum_bias,
        sum_modulate,
        condition_grads,
        square_total,
    ) = back_call(
        image_lengths,
        tokens,
        cotangent,
        modulation,
        packed,
        attend_in,
        resid,
        grad_resid,
        grad_attend,
        grad_mixed,
        slot_grads,
        bias_shrink,
        grad_bias_expand,
        shrink_norm,
        active,
        conditions,
        modulate_weight,
        full_weights,
        feed_parts,
        output_parts,
        expand_parts,
        shrink_rest,
    )
    global_norm, updated = update_call(
        square_total,
        sum_project,
        sum_output,
        sum_expand,
        shrink_low,
        shrink_high,
        sum_modulate,
        project_weight,
        project_moment,
        project_square,
        output_weight,
        output_moment,
        output_square,
        expand_weight,
        expand_moment,
        expand_square,
        shrink_weight,
        shrink_moment,
        shrink_square,
        modulate_weight,
        modulate_moment,
        modulate_square,
    )
    updated_bias = adam_update(bias_vector, bias_moment, bias_square, sum_bias[0], 0.3)
    return (block_output, token_grads, condition_grads, global_norm, *updated, *updated_bias)


def generic_body(
    tokens,
    conditions,
    image_lengths,
    cotangent,
    project_weight,
    project_moment,
    project_square,
    output_weight,
    output_moment,
    output_square,
    expand_weight,
    expand_moment,
    expand_square,
    shrink_weight,
    shrink_moment,
    shrink_square,
    modulate_weight,
    modulate_moment,
    modulate_square,
    bias_vector,
    bias_moment,
    bias_square,
):
    low_type = jnp.bfloat16
    group_size = lax.axis_size("mod")
    group_place = lax.axis_index("mod")
    columns = 6 * D // group_size
    full_project, full_output, full_expand, full_shrink, full_modulate, full_bias = (
        lax.all_gather(project_weight.astype(low_type), "dp", axis=0, tiled=True),
        lax.all_gather(output_weight.astype(low_type), "dp", axis=0, tiled=True),
        lax.all_gather(expand_weight.astype(low_type), "dp", axis=0, tiled=True),
        lax.all_gather(shrink_weight.astype(low_type), "dp", axis=0, tiled=True),
        lax.all_gather(modulate_weight.astype(low_type), "dp", axis=0, tiled=True),
        lax.all_gather(bias_vector.astype(low_type), "dp", axis=0, tiled=True),
    )
    bias_full = full_bias.astype(jnp.float32)
    bias_query = bias_full[0:D]
    bias_value = bias_full[D : 2 * D]
    bias_output = bias_full[2 * D : 3 * D]
    bias_expand = bias_full[3 * D : 3 * D + FF]
    bias_shrink = bias_full[3 * D + FF : 4 * D + FF]
    bias_modulate = lax.dynamic_slice_in_dim(bias_full, 4 * D + FF + group_place * columns, columns)
    group_conditions = lax.all_gather(conditions, "mod", axis=0, tiled=True)
    activated = jax.nn.silu(group_conditions.astype(jnp.float32)).astype(low_type)
    group_mod = (contract(activated, full_modulate, 1, 0) + bias_modulate).astype(low_type)
    own_mod = lax.all_to_all(group_mod, "mod", split_axis=0, concat_axis=1, tiled=True)
    slots = jnp.arange(IMG_ROW, dtype=jnp.int32)
    ends = jnp.sum(
        jnp.where(slots[:, None] <= slots[None, :], image_lengths[0][:, None], 0), axis=0, dtype=jnp.int32
    )
    positions = jnp.arange(ROW, dtype=jnp.int32)
    slot_of = jnp.sum(
        (positions[:, None] >= ends[None, :]).astype(jnp.int32), axis=1, dtype=jnp.int32
    )
    slot_match = slot_of[:, None] == jnp.arange(IMG_ROW, dtype=jnp.int32)[None, :]
    same_image = slot_of[:, None] == slot_of[None, :]
    per_token = contract(slot_match.astype(low_type), own_mod, 1, 0)
    shift_attend = per_token[:, 0:D]
    scale_attend = per_token[:, D : 2 * D]
    gate_attend = per_token[:, 2 * D : 3 * D]
    shift_feed = per_token[:, 3 * D : 4 * D]
    scale_feed = per_token[:, 4 * D : 5 * D]
    gate_feed = per_token[:, 5 * D : 6 * D]
    inputs = tokens.astype(jnp.float32)
    normed_attend, inverse_attend = normalize_rows(inputs)
    attend_in = (normed_attend * (1.0 + scale_attend) + shift_attend).astype(low_type)
    projected = contract(attend_in, full_project, 1, 0)
    query = (projected[:, 0:D] + bias_query).astype(low_type)
    keys = projected[:, D : 2 * D].astype(low_type)
    values = (projected[:, 2 * D : 3 * D] + bias_value).astype(low_type)
    head_scale = HEAD_DIM ** (-0.5)

    def split_heads(matrix):
        return matrix.reshape(ROW, HEADS, HEAD_DIM).transpose(1, 0, 2)

    def head_scores(query_head, key_head):
        return jnp.where(same_image, contract(query_head, key_head, 1, 1) * head_scale, -1e30)

    def attend_head(pieces):
        query_head, key_head, value_head = pieces
        scores = head_scores(query_head, key_head)
        row_top = jnp.max(scores, axis=1, keepdims=True)
        exponent = jnp.exp(scores - row_top)
        total = jnp.sum(exponent, axis=1, keepdims=True)
        probs = (exponent / total).astype(low_type)
        return (contract(probs, value_head, 1, 0), (row_top + jnp.log(total))[:, 0])

    heads_query = split_heads(query)
    heads_key = split_heads(keys)
    heads_value = split_heads(values)
    mixed_heads, log_totals = lax.map(attend_head, (heads_query, heads_key, heads_value))
    mixed = merge_heads(mixed_heads).astype(low_type)
    attend_out = contract(mixed, full_output, 1, 0) + bias_output
    resid = inputs + gate_attend * attend_out
    normed_feed, inverse_feed = normalize_rows(resid)
    feed_in = (normed_feed * (1.0 + scale_feed) + shift_feed).astype(low_type)
    hidden_pre = contract(feed_in, full_expand, 1, 0) + bias_expand
    tanh_part = jnp.tanh(
        tanh_scale * (hidden_pre + cubic_term * hidden_pre * hidden_pre * hidden_pre)
    )
    hidden = (0.5 * hidden_pre * (1.0 + tanh_part)).astype(low_type)
    feed_out = contract(hidden, full_shrink, 1, 0) + bias_shrink
    block_output = (resid + gate_feed * feed_out).astype(low_type)
    grad_out = cotangent.astype(jnp.float32)
    grad_gate_feed = grad_out * feed_out
    grad_feed = (gate_feed * grad_out).astype(low_type)
    grad_shrink = contract(hidden, grad_feed, 0, 0)
    grad_hidden = contract(grad_feed, full_shrink, 1, 1)
    slope = 0.5 * (1.0 + tanh_part) + 0.5 * hidden_pre * (
        1.0 - tanh_part * tanh_part
    ) * tanh_scale * (1.0 + 3.0 * cubic_term * hidden_pre * hidden_pre)
    grad_pre = (grad_hidden * slope).astype(low_type)
    grad_expand = contract(feed_in, grad_pre, 0, 0)
    grad_feed_in = contract(grad_pre, full_expand, 1, 1)
    grad_scale_feed = grad_feed_in * normed_feed
    grad_resid = grad_out + normalize_back(
        grad_feed_in * (1.0 + scale_feed), normed_feed, inverse_feed
    )
    grad_gate_attend = grad_resid * attend_out
    grad_attend = (gate_attend * grad_resid).astype(low_type)
    grad_output = contract(mixed, grad_attend, 0, 0)
    grad_mixed = contract(grad_attend, full_output, 1, 1).astype(low_type)

    def attend_back(pieces):
        query_head, key_head, value_head, grad_head, log_total = pieces
        probs = jnp.exp(head_scores(query_head, key_head) - log_total[:, None])
        grad_value = contract(probs.astype(low_type), grad_head, 0, 0)
        grad_probs = contract(grad_head, value_head, 1, 1)
        grad_scores = (
            probs * (grad_probs - jnp.sum(probs * grad_probs, axis=1, keepdims=True))
        ).astype(low_type)
        grad_query = contract(grad_scores, key_head, 1, 0) * head_scale
        grad_key = contract(grad_scores, query_head, 0, 0) * head_scale
        return (grad_query, grad_key, grad_value)

    heads_grad_query, heads_grad_key, heads_grad_value = lax.map(
        attend_back, (heads_query, heads_key, heads_value, split_heads(grad_mixed), log_totals)
    )
    grad_projected = jnp.concatenate(
        [merge_heads(heads_grad_query), merge_heads(heads_grad_key), merge_heads(heads_grad_value)],
        axis=1,
    ).astype(low_type)
    grad_project = contract(attend_in, grad_projected, 0, 0)
    grad_attend_in = contract(grad_projected, full_project, 1, 1)
    grad_scale_attend = grad_attend_in * normed_attend
    token_grads = grad_resid + normalize_back(
        grad_attend_in * (1.0 + scale_attend), normed_attend, inverse_attend
    )
    token_mod_grads = jnp.concatenate(
        [
            grad_attend_in,
            grad_scale_attend,
            grad_gate_attend,
            grad_feed_in,
            grad_scale_feed,
            grad_gate_feed,
        ],
        axis=1,
    )
    sample_grads = contract(slot_match.astype(jnp.float32), token_mod_grads, 0, 0).astype(low_type)
    group_grads = lax.all_to_all(sample_grads, "mod", split_axis=1, concat_axis=0, tiled=True)
    grad_modulate = contract(activated, group_grads, 0, 0)
    grad_bias_modulate = jnp.sum(group_grads, axis=0, dtype=jnp.float32)
    condition_terms = contract(group_grads, full_modulate, 1, 1)
    condition_sum = lax.psum_scatter(
        condition_terms.astype(jnp.bfloat16), "mod", scatter_dimension=0, tiled=True
    ).astype(jnp.float32)
    own_conditions = conditions.astype(jnp.float32)
    sigmoid_part = jax.nn.sigmoid(own_conditions)
    condition_grads = condition_sum * (sigmoid_part * (1.0 + own_conditions * (1.0 - sigmoid_part)))
    modulate_bias_grad = lax.dynamic_update_slice_in_dim(
        jnp.zeros((6 * D,), jnp.float32), grad_bias_modulate, group_place * columns, 0
    )
    grad_bias = jnp.concatenate(
        [
            jnp.sum(grad_projected[:, 0:D], axis=0, dtype=jnp.float32),
            jnp.sum(grad_projected[:, 2 * D : 3 * D], axis=0, dtype=jnp.float32),
            jnp.sum(grad_attend, axis=0, dtype=jnp.float32),
            jnp.sum(grad_pre, axis=0, dtype=jnp.float32),
            jnp.sum(grad_feed, axis=0, dtype=jnp.float32),
            modulate_bias_grad,
        ],
        axis=0,
    )
    summed = (
        lax.psum_scatter(
            grad_project.astype(jnp.bfloat16), "dp", scatter_dimension=0, tiled=True
        ).astype(jnp.float32),
        lax.psum_scatter(
            grad_output.astype(jnp.bfloat16), "dp", scatter_dimension=0, tiled=True
        ).astype(jnp.float32),
        lax.psum_scatter(
            grad_expand.astype(jnp.bfloat16), "dp", scatter_dimension=0, tiled=True
        ).astype(jnp.float32),
        lax.psum_scatter(
            grad_shrink.astype(jnp.bfloat16), "dp", scatter_dimension=0, tiled=True
        ).astype(jnp.float32),
        lax.psum_scatter(
            grad_modulate.astype(jnp.bfloat16), "dp", scatter_dimension=0, tiled=True
        ).astype(jnp.float32),
        lax.psum_scatter(
            grad_bias.astype(jnp.bfloat16), "dp", scatter_dimension=0, tiled=True
        ).astype(jnp.float32),
    )
    sum_project, sum_output, sum_expand, sum_shrink, sum_bias = (
        lax.psum(summed[0].astype(jnp.bfloat16), "mod").astype(jnp.float32),
        lax.psum(summed[1].astype(jnp.bfloat16), "mod").astype(jnp.float32),
        lax.psum(summed[2].astype(jnp.bfloat16), "mod").astype(jnp.float32),
        lax.psum(summed[3].astype(jnp.bfloat16), "mod").astype(jnp.float32),
        lax.psum(summed[5].astype(jnp.bfloat16), "mod").astype(jnp.float32),
    )
    sum_modulate = summed[4]
    trunk_square = (
        jnp.sum(sum_project * sum_project)
        + jnp.sum(sum_output * sum_output)
        + jnp.sum(sum_expand * sum_expand)
        + jnp.sum(sum_shrink * sum_shrink)
        + jnp.sum(sum_bias * sum_bias)
    )
    totals = lax.psum((trunk_square, jnp.sum(sum_modulate * sum_modulate)), ("dp", "mod"))
    global_norm = jnp.sqrt(totals[0] / group_size + totals[1])
    clip_factor = jnp.minimum(1.0, 1.0 / (global_norm + 1e-06))
    next_project, first_project, second_project = adam_update(
        project_weight, project_moment, project_square, sum_project * clip_factor, D ** (-0.5)
    )
    next_output, first_output, second_output = adam_update(
        output_weight, output_moment, output_square, sum_output * clip_factor, (D // 64) ** (-0.5)
    )
    next_expand, first_expand, second_expand = adam_update(
        expand_weight, expand_moment, expand_square, sum_expand * clip_factor, D ** (-0.5)
    )
    next_shrink, first_shrink, second_shrink = adam_update(
        shrink_weight, shrink_moment, shrink_square, sum_shrink * clip_factor, FF ** (-0.5)
    )
    next_modulate, first_modulate, second_modulate = adam_update(
        modulate_weight, modulate_moment, modulate_square, sum_modulate * clip_factor, D ** (-0.5)
    )
    next_biases, first_biases, second_biases = adam_update(
        bias_vector, bias_moment, bias_square, sum_bias * clip_factor, 0.3
    )
    return (
        block_output,
        token_grads,
        condition_grads,
        global_norm,
        next_project,
        first_project,
        second_project,
        next_output,
        first_output,
        second_output,
        next_expand,
        first_expand,
        second_expand,
        next_shrink,
        first_shrink,
        second_shrink,
        next_modulate,
        first_modulate,
        second_modulate,
        next_biases,
        first_biases,
        second_biases,
    )


def solution(mesh):
    return jax.shard_map(
        plane_body if mesh.shape["dp"] == GROUP and mesh.shape["mod"] == DEPTH else generic_body,
        mesh=mesh,
        in_specs=(
            P(("dp", "mod"), None),
            P(("dp", "mod"), None),
            P(("dp", "mod"), None),
            P(("dp", "mod"), None),
            P("dp", None),
            P("dp", None),
            P("dp", None),
            P("dp", None),
            P("dp", None),
            P("dp", None),
            P("dp", None),
            P("dp", None),
            P("dp", None),
            P("dp", None),
            P("dp", None),
            P("dp", None),
            P("dp", "mod"),
            P("dp", "mod"),
            P("dp", "mod"),
            P("dp"),
            P("dp"),
            P("dp"),
        ),
        out_specs=(
            P(("dp", "mod"), None),
            P(("dp", "mod"), None),
            P(("dp", "mod"), None),
            P(),
            P("dp", None),
            P("dp", None),
            P("dp", None),
            P("dp", None),
            P("dp", None),
            P("dp", None),
            P("dp", None),
            P("dp", None),
            P("dp", None),
            P("dp", None),
            P("dp", None),
            P("dp", None),
            P("dp", "mod"),
            P("dp", "mod"),
            P("dp", "mod"),
            P("dp"),
            P("dp"),
            P("dp"),
        ),
        check_vma=False,
    )
```

```python
import functools

import jax
import jax.numpy as jnp
from jax import lax
from jax.experimental import pallas as pl
from jax.experimental.pallas import tpu as pltpu
from jax.sharding import PartitionSpec as P

D = 1152
HEADS = 16
HEAD_DIM = 72
FF = 4608
ROW = 256
STEP = 10
IMG_ROW = 4


beta_first = 0.9
beta_second = 0.999
weight_decay = 0.01
adam_epsilon = 1e-08
tanh_scale = 0.7978845608028654
cubic_term = 0.044715


def contract(left, right, left_axis, right_axis):
    return lax.dot_general(
        left, right, (((left_axis,), (right_axis,)), ((), ())), preferred_element_type=jnp.float32
    )


def normalize_rows(values):
    center = values - jnp.mean(values, axis=-1, keepdims=True)
    inverse = lax.rsqrt(jnp.mean(center * center, axis=-1, keepdims=True) + 1e-06)
    return (center * inverse, inverse)


def normalize_back(grad_normed, normed, inverse):
    centered = grad_normed - jnp.mean(grad_normed, axis=-1, keepdims=True)
    return (centered - normed * jnp.mean(grad_normed * normed, axis=-1, keepdims=True)) * inverse


def adam_update(weight, moment, square, grad, rate):
    first = beta_first * moment + (1.0 - beta_first) * grad
    second = beta_second * square + (1.0 - beta_second) * grad * grad
    step_size = first / (1.0 - beta_first**STEP)
    divisor = jnp.sqrt(second / (1.0 - beta_second**STEP)) + adam_epsilon
    return (weight - rate * (step_size / divisor + weight_decay * weight), first, second)


def merge_heads(stacked):
    return stacked.transpose(1, 0, 2).reshape(stacked.shape[1], stacked.shape[0] * stacked.shape[2])


MESH = pl.DeviceIdType.MESH
GROUP = 8
DEPTH = 4
VMEM_BYTES = 60 << 20
low_type = jnp.bfloat16
full_type = jnp.float32


def vmem():
    return pl.BlockSpec(memory_space=pltpu.VMEM)


def anywhere():
    return pl.BlockSpec(memory_space=pl.ANY)


def plane_places():
    place = lax.axis_index("dp")
    layer = lax.axis_index("mod")
    twin = place + 1 - 2 * lax.rem(place, 2)
    side = 2 - 4 * lax.rem(lax.div(place, 2), 2)
    across = place + side
    along = place + 4 - 8 * lax.div(place, 4)
    corner = along + side
    return place, layer, twin, across, along, corner


def twin_of(place):
    return place + 1 - 2 * lax.rem(place, 2)


def send(source, target, send_sem, recv_sem, place, layer):
    copy = pltpu.make_async_remote_copy(
        src_ref=source,
        dst_ref=target,
        send_sem=send_sem,
        recv_sem=recv_sem,
        device_id=(place, layer),
        device_id_type=MESH,
    )
    copy.start()
    return copy


def greet(peers):
    barrier = pltpu.get_barrier_semaphore()
    for peer in peers:
        pl.semaphore_signal(barrier, inc=1, device_id=peer, device_id_type=MESH)
    pl.semaphore_wait(barrier, len(peers))


class Gather:
    def __init__(self, own, slots, sends, recvs, base, rows, cut):
        self.own, self.slots, self.sends, self.recvs = own, slots, sends, recvs
        self.whole = pl.ds(base, rows)
        self.first, self.second = pl.ds(base, cut), pl.ds(base + cut, rows - cut)
        self.place, self.layer, self.twin, self.across, self.along, self.corner = plane_places()
        self.copies = {}

    def push(self, index, slot, part, peer, own=False):
        target = self.slots.at[slot, part]
        source = self.own.at[part] if own else target
        self.copies[index] = send(
            source, target, self.sends.at[index], self.recvs.at[index], peer, self.layer
        )

    def start_twin(self):
        self.push(2, self.place, self.whole, self.twin, True)

    def start_links(self):
        self.push(0, self.place, self.whole, self.across, True)
        self.push(1, self.place, self.whole, self.along, True)

    def forward_near(self):
        self.copies[0].wait_recv()
        self.push(3, self.across, self.first, self.along)
        self.push(5, self.across, self.whole, self.twin)
        self.copies[1].wait_recv()
        self.push(4, self.along, self.second, self.across)
        self.push(6, self.along, self.whole, self.twin)

    def forward_far(self):
        self.copies[3].wait_recv()
        self.push(7, self.corner, self.first, self.twin)
        self.copies[4].wait_recv()
        self.push(8, self.corner, self.second, self.twin)

    def arrived(self, *indices):
        for index in indices:
            self.copies[index].wait_recv()

    def finish_sends(self):
        for index in range(9):
            self.copies[index].wait_send()


class Scatter:
    def __init__(self, parts, buffers, rows, cut, outgoing=None, columns=None):
        from_twin, half_across, half_along, whole_across, whole_along, self.sends, self.recvs = buffers
        self.first, self.second, self.rows = pl.ds(0, cut), pl.ds(cut, rows - cut), pl.ds(0, rows)
        self.place, self.layer, self.twin, self.across, self.along, self.corner = plane_places()
        self.places = (self.place, self.across, self.along, self.corner)
        self.slots = self.places if outgoing is None else (0, 1, 2, 3)
        outgoing = parts if outgoing is None else outgoing
        if columns is None:
            self.part = lambda slot, part: parts.at[slot, part]
            self.given = lambda slot: outgoing.at[slot]
            self.twin_part = lambda index, part: from_twin.at[index, part]
            self.half = (half_across, half_along)
            self.whole = (lambda part: whole_across.at[part], lambda part: whole_along.at[part])
        else:
            every = slice(None)
            self.part = lambda slot, part: parts.at[every, slot, part, columns]
            self.given = lambda slot: outgoing.at[every, slot, every, columns]
            self.twin_part = lambda index, part: from_twin.at[index, every, part, columns]
            self.half = (half_across.at[every, every, columns], half_along.at[every, every, columns])
            self.whole = (
                lambda part: whole_across.at[every, part, columns],
                lambda part: whole_along.at[every, part, columns],
            )
        self.copies = {}

    def push(self, index, source, target, peer):
        self.copies[index] = send(
            source, target, self.sends.at[index], self.recvs.at[index], peer, self.layer
        )

    def start_twin(self, *indices):
        for index in indices or (3, 1, 2, 0):
            self.push(index, self.given(twin_of(self.places[index])), self.twin_part(index, self.rows), self.twin)

    def add(self, slot, part, other):
        target = self.part(slot, part)
        target[...] = (target[...].astype(full_type) + other[...].astype(full_type)).astype(low_type)

    def merge_twin(self, index):
        self.copies[index].wait_recv()
        self.add(self.slots[index], self.rows, self.twin_part(index, self.rows))

    def start_near(self):
        _, across, along, _ = self.slots
        self.merge_twin(1)
        self.push(6, self.part(across, self.first), self.whole[0](self.first), self.across)
        self.merge_twin(2)
        self.push(7, self.part(along, self.second), self.whole[1](self.second), self.along)

    def start_far(self):
        corner = self.slots[3]
        self.merge_twin(3)
        self.push(4, self.part(corner, self.first), self.half[0], self.across)
        self.push(5, self.part(corner, self.second), self.half[1], self.along)

    def forward(self):
        _, across, along, _ = self.slots
        self.copies[5].wait_recv()
        self.add(across, self.second, self.half[1])
        self.push(8, self.part(across, self.second), self.whole[0](self.second), self.across)
        self.copies[4].wait_recv()
        self.add(along, self.first, self.half[0])
        self.push(9, self.part(along, self.first), self.whole[1](self.first), self.along)

    def settle(self):
        for index in (0, 6, 8, 7, 9):
            self.copies[index].wait_recv()
        for index in range(10):
            self.copies[index].wait_send()

    def total(self, part=None):
        part = self.rows if part is None else part
        return (
            self.part(self.slots[0], part)[...].astype(full_type)
            + self.twin_part(0, part)[...].astype(full_type)
            + (self.whole[0](part)[...].astype(full_type) + self.whole[1](part)[...].astype(full_type))
        )


def scatter_scratch(rows, cut, columns, copies=()):
    dma = pltpu.SemaphoreType.DMA
    lead = (3,) if copies else ()
    return [
        pltpu.VMEM((4,) + lead + (rows, columns), low_type),
        pltpu.VMEM(lead + (cut, columns), low_type),
        pltpu.VMEM(lead + (rows - cut, columns), low_type),
        pltpu.VMEM(lead + (rows, columns), low_type),
        pltpu.VMEM(lead + (rows, columns), low_type),
        dma(copies + (10,)),
        dma(copies + (10,)),
    ]


def iota(shape, axis):
    return lax.broadcasted_iota(jnp.int32, shape, axis)


def sample_picker():
    row, column = iota((128, 256), 0), iota((128, 256), 1)
    wanted = ((row >> 2) & 3) * 64 + (row >> 4) * 8 + (row & 3)
    return (column == wanted).astype(full_type).astype(low_type)


def slot_spreader():
    row, column = iota((32, 16), 0), iota((32, 16), 1)
    return jnp.where(((row & 7) < 4) & (column == (row >> 3) * 4 + (row & 7)), 1.0, 0.0).astype(low_type)


def head_window(head):
    start = lax.min(lax.div(head * HEAD_DIM, 128) * 128, D - 256)
    start = pl.multiple_of(start, 128)
    lane = iota((1, 256), 1) + start
    inside = (lane >= head * HEAD_DIM) & (lane < (head + 1) * HEAD_DIM)
    return start, inside.astype(full_type)


def window(ref, base, start):
    return ref[:, pl.ds(pl.multiple_of(base + start, 128), 256)]


def masked_probs(query, key, same):
    scores = jnp.where(same, contract(query, key, 1, 1) * HEAD_DIM ** (-0.5), -1e30)
    exponent = jnp.exp(scores - jnp.max(scores, axis=1, keepdims=True))
    return exponent / jnp.sum(exponent, axis=1, keepdims=True)


BLOCK = 64
LANES = 128


def slot_numbers(lengths, shape, axis):
    position = iota(shape, axis)
    slot, end = jnp.zeros(shape, jnp.int32), 0
    for step in range(IMG_ROW):
        end = end + lengths[0, step]
        slot = slot + jnp.where(position >= end, 1, 0)
    return slot


def slot_onehot(slots):
    matched = (slots == iota((slots.shape[0], 8), 1)) & (slots < IMG_ROW)
    return jnp.where(matched, 1.0, 0.0).astype(low_type)


def block_part(step):
    return pl.ds(pl.multiple_of(step * BLOCK, BLOCK), BLOCK)


def spread_slots(onehot, modulation, index):
    return contract(onehot, modulation[index].astype(low_type), 1, 0)


def front_kernel(
    lengths,
    tokens,
    cotangent,
    conditions,
    bias_own,
    project,
    output,
    expand,
    modulate,
    packed_out,
    attend_in_out,
    mixed,
    attend_out,
    resid,
    feed_in,
    modulation,
    active_out,
    bias_expand,
    bias_shrink,
    weights_out,
    expand_out,
    grad_all,
    project_load,
    output_load,
    expand_load,
    modulate_load,
    weights_own,
    weights_all,
    expand_own,
    grad_own,
    cond_send,
    cond_plane,
    cond_all,
    part_send,
    twin_recv,
    part_recv,
    mod_send,
    mod_recv,
    bias_recv,
    bias_flat,
    small_sends,
    small_recvs,
    near_sends,
    near_recvs,
    base_sends,
    base_recvs,
    far_sends,
    far_recvs,
    grad_sends,
    grad_recvs,
    local_sems,
    packed,
    attend_in,
):
    place, layer, twin, across, along, corner = plane_places()
    places = (place, across, along, corner)
    plane = [lax.rem(place + step, GROUP) for step in range(1, GROUP)]
    column = [lax.rem(layer + step, DEPTH) for step in range(1, DEPTH)]
    pair = layer + 1 - 2 * lax.rem(layer, 2)
    inner = jnp.where((layer == 0) | (layer == DEPTH - 1), 0, 1)
    rows = weights_own.shape[0]
    third = rows // 3
    shard = bias_own.shape[1]
    columns = modulate_load.shape[1]
    units = expand_own.shape[2]

    def load(index, source, target):
        copy = pltpu.make_async_copy(source, target, local_sems.at[index])
        copy.start()
        return copy

    loads = [
        load(0, project, project_load),
        load(1, modulate, modulate_load),
        load(2, output, output_load),
        load(3, expand, expand_load),
    ]
    peers = [(peer, layer) for peer in plane] + [(place, peer) for peer in column]
    barrier = pltpu.get_barrier_semaphore()
    for peer in peers:
        pl.semaphore_signal(barrier, inc=1, device_id=peer, device_id_type=MESH)
    values = conditions[...].astype(full_type)
    active = (values * jax.nn.sigmoid(values)).astype(low_type).astype(full_type)
    cond_send[...] = jnp.zeros_like(cond_send)
    for step in range(GROUP):
        cond_send[step, 0:IMG_ROW, :] = active[:, step * rows : (step + 1) * rows]
    bias_recv[place] = bias_own[...].astype(low_type).astype(full_type)
    pl.semaphore_wait(barrier, len(peers))

    waits = []

    def exchange(base, peers, source, target):
        copies = []
        for step, peer in enumerate(peers):
            where = (peer, layer) if peers is plane else (place, peer)
            copies.append(
                send(source(peer), target, small_sends.at[base + step], small_recvs.at[base + step], *where)
            )
        waits.extend(copies)
        return copies

    def arrive(copies):
        for copy in copies:
            copy.wait_recv()

    cond_copies = exchange(0, plane, lambda peer: cond_send.at[peer], cond_plane.at[place])
    cond_plane[place] = cond_send[place]
    bias_copies = exchange(7, plane, lambda peer: bias_recv.at[place], bias_recv.at[place])
    loads[0].wait()
    weights_own[:, 0 : 3 * D] = project_load[...].astype(low_type)
    loads[2].wait()
    weights_own[:, 3 * D : 4 * D] = output_load[...].astype(low_type)
    second = pl.multiple_of(third * (1 + inner), 16)
    last = pl.multiple_of(third * (2 - inner), 16)
    near = Gather(weights_own, weights_all, near_sends, near_recvs, second, third, 32)
    base = Gather(weights_own, weights_all, base_sends, base_recvs, 0, third, 16)
    near.start_links()
    near.start_twin()
    base.start_twin()
    whole = pl.ds(last, third)

    def far_copy(index, slot, part, where):
        return send(
            weights_all.at[slot, part],
            weights_all.at[slot, part],
            far_sends.at[index],
            far_recvs.at[index],
            *where,
        )

    far = [
        send(
            weights_own.at[whole], weights_all.at[place, whole], far_sends.at[0], far_recvs.at[0], twin, layer
        )
    ]
    arrive(cond_copies)
    cond_copies = exchange(14, column, lambda peer: cond_plane, cond_all.at[layer])
    cond_all[layer] = cond_plane[...]
    weights_all[place] = weights_own[...]
    loads[1].wait()
    arrive(cond_copies)
    padded = cond_all[...].reshape(DEPTH * GROUP * 8, rows).astype(low_type)
    picked = contract(sample_picker(), padded, 1, 0).astype(low_type)
    active_out[...] = picked
    partial = contract(picked, modulate_load[...].astype(low_type), 1, 0)
    part_send[...] = partial.reshape(part_send.shape)
    twin_copies = []
    for step in (1, 2, 3, 0):
        twin_copies.append(
            send(
                part_send.at[twin_of(places[step])],
                twin_recv.at[step],
                small_sends.at[17 + step],
                small_recvs.at[17 + step],
                twin,
                layer,
            )
        )
    part_copies = []
    for step, copy in zip((1, 2, 3), twin_copies):
        copy.wait_recv()
        part_send[places[step]] = part_send[places[step]] + twin_recv[step]
        part_copies.append(
            send(
                part_send.at[places[step]],
                part_recv.at[step - 1],
                small_sends.at[21 + step],
                small_recvs.at[21 + step],
                places[step],
                layer,
            )
        )
    waits += twin_copies + part_copies
    near.forward_near()
    up = (place, pair)
    far.append(far_copy(1, across, near.whole, up))
    base.start_links()
    arrive(bias_copies)
    for step in range(GROUP):
        bias_flat[:, step * shard : (step + 1) * shard] = bias_recv[step]
    start = pl.multiple_of(4 * D + FF + 2 * columns * lax.div(layer, 2), 128)
    both = bias_flat[:, pl.ds(start, 2 * columns)]
    bias_modulate = jnp.where(lax.rem(layer, 2) == 0, both[:, 0:columns], both[:, columns : 2 * columns])
    start = pl.multiple_of(3 * D + 2 * units * lax.div(place, 2), 128)
    both = bias_flat[:, pl.ds(start, 2 * units)]
    bias_expand[...] = jnp.where(lax.rem(place, 2) == 0, both[:, 0:units], both[:, units : 2 * units])
    bias_shrink[...] = bias_flat[:, 3 * D + FF : 4 * D + FF]
    arrive(twin_copies[3:] + part_copies)
    total = (part_send[place] + twin_recv[0]) + ((part_recv[0] + part_recv[1]) + part_recv[2]) + bias_modulate
    spread = contract(slot_spreader(), total.astype(low_type), 1, 0)
    mod_send[...] = spread.reshape(mod_send.shape)
    mod_copies = exchange(25, column, lambda peer: mod_send.at[peer], mod_recv.at[layer])
    mod_recv[layer] = mod_send[layer]

    far.append(far_copy(2, along, near.whole, up))
    near.forward_far()
    far.append(far_copy(3, corner, near.whole, up))
    loads[3].wait()
    for step in range(GROUP):
        expand_own[step] = expand_load[:, step * units : (step + 1) * units].astype(low_type)
    base.forward_near()

    def expand_copy(index, source, target, where):
        copy = send(source, target, small_sends.at[28 + index], small_recvs.at[28 + index], *where)
        waits.append(copy)
        return copy

    sources = [slot + (twin_of(slot) - slot) * inner for slot in (across, along, corner)]
    expand_copies = [
        expand_copy(step, expand_own.at[slot], expand_out.at[place], (slot, layer)) for step, slot in enumerate(sources)
    ]
    expand_copies.append(expand_copy(3, expand_own.at[twin], expand_out.at[place], (twin, layer)))
    arrive(mod_copies)
    half = D // 2
    for block in range(DEPTH):
        for step in range(3):
            piece, side = divmod(3 * block + step, 2)
            modulation[piece, :, side * half : (side + 1) * half] = mod_recv[block, :, step * half : (step + 1) * half]
    slot_row = slot_numbers(lengths, (1, ROW), 1)
    slot_column = slot_numbers(lengths, (ROW, 1), 0)
    onehot = slot_onehot(slot_column)

    def first_step(step):
        part = pl.ds(step * BLOCK, BLOCK)
        picked = onehot[step * BLOCK : (step + 1) * BLOCK]
        normed, _ = normalize_rows(tokens[part, :].astype(full_type))
        attend_in[part, :] = (
            normed * (1.0 + spread_slots(picked, modulation, 1)) + spread_slots(picked, modulation, 0)
        ).astype(low_type)
        grad_own[part, :] = (spread_slots(picked, modulation, 5) * cotangent[part, :].astype(full_type)).astype(low_type)

    for step in range(ROW // BLOCK):
        first_step(step)
    base.forward_far()
    grad_gather = Gather(grad_own, grad_all, grad_sends, grad_recvs, 0, ROW, ROW // 2)
    grad_gather.start_links()
    grad_gather.start_twin()
    keeps = [
        load(4, grad_own, grad_all.at[place]),
        load(5, expand_own.at[place], expand_out.at[place]),
    ]
    for index, slot in ((1, across), (2, along), (3, corner)):
        far[index].wait_recv()
        far.append(far_copy(3 + index, slot, whole, (twin, layer)))
    near.arrived(2, 5, 6, 7, 8)
    base.arrived(2, 5, 6, 7, 8)
    for index in (0, 4, 5, 6):
        far[index].wait_recv()
    for step, slot in enumerate(sources):
        expand_copies[step].wait_recv()
        expand_copies.append(expand_copy(4 + step, expand_out.at[slot], expand_out.at[slot], up))
    keeps.append(load(6, weights_all, weights_out))

    mixed[...] = jnp.zeros_like(mixed)

    def query_step(step, carry):
        where = pl.ds(pl.multiple_of(step * 384, 128), 384)
        values = contract(attend_in[...], weights_all[:, :, where].reshape(D, 384), 1, 0)
        packed[:, where] = values.astype(low_type)
        return carry

    def biased_step(step, base, carry):
        where = pl.ds(pl.multiple_of(base + step * 384, 128), 384)
        shift = bias_flat[:, pl.ds(pl.multiple_of(lax.div(base, 2) + step * 384, 128), 384)]
        values = contract(attend_in[...], weights_all[:, :, where].reshape(D, 384), 1, 0)
        packed[:, where] = (values + shift).astype(low_type)
        return carry

    lax.fori_loop(0, 3, lambda step, carry: biased_step(step, 0, carry), 0)
    lax.fori_loop(3, 6, query_step, 0)
    lax.fori_loop(0, 3, lambda step, carry: biased_step(step, 2 * D, carry), 0)
    keeps.append(load(7, packed, packed_out))
    keeps.append(load(8, attend_in, attend_in_out))
    same = slot_column == slot_row

    def head_step(head, carry):
        start, inside = head_window(head)
        keep = inside.astype(low_type)
        probs = masked_probs(window(packed, 0, start) * keep, window(packed, D, start), same)
        out = contract(probs.astype(low_type), window(packed, 2 * D, start) * keep, 1, 0)
        where = pl.ds(start, 256)
        mixed[:, where] = (mixed[:, where].astype(full_type) + out).astype(low_type)
        return carry

    lax.fori_loop(0, 8, head_step, 0, unroll=4)
    grad_gather.forward_near()
    lax.fori_loop(8, HEADS, head_step, 0, unroll=4)

    def out_step(step, carry):
        where = pl.ds(pl.multiple_of(step * 384, 128), 384)
        source = pl.ds(pl.multiple_of(3 * D + step * 384, 128), 384)
        shift = bias_flat[:, pl.ds(pl.multiple_of(2 * D + step * 384, 128), 384)]
        attend_out[:, where] = contract(mixed[...], weights_all[:, :, source].reshape(D, 384), 1, 0) + shift
        return carry

    lax.fori_loop(0, 3, out_step, 0)
    for step in range(ROW // BLOCK):
        part = pl.ds(step * BLOCK, BLOCK)
        picked = onehot[step * BLOCK : (step + 1) * BLOCK]
        joined = tokens[part, :].astype(full_type) + spread_slots(picked, modulation, 2) * attend_out[part, :]
        resid[part, :] = joined
        normed, _ = normalize_rows(joined)
        feed_in[part, :] = (
            normed * (1.0 + spread_slots(picked, modulation, 4)) + spread_slots(picked, modulation, 3)
        ).astype(low_type)
    grad_gather.forward_far()
    grad_gather.arrived(2, 5, 6, 7, 8)
    arrive(expand_copies[3:])
    for gather in (near, base, grad_gather):
        gather.finish_sends()
    for copy in far + waits:
        copy.wait_send()
    for copy in keeps:
        copy.wait()


def front_call(lengths, tokens, cotangent, conditions, bias_own, project, output, expand, modulate):
    rows, columns = modulate.shape
    units = expand.shape[1] // GROUP
    shard = bias_own.shape[1]
    shape = jax.ShapeDtypeStruct
    dma = pltpu.SemaphoreType.DMA
    return pl.pallas_call(
        front_kernel,
        out_shape=(
            shape((ROW, 3 * D), low_type),
            shape((ROW, D), low_type),
            shape((ROW, D), low_type),
            shape((ROW, D), full_type),
            shape((ROW, D), full_type),
            shape((ROW, D), low_type),
            shape((6, 8, D), full_type),
            shape((GROUP * 16, rows), low_type),
            shape((1, units), full_type),
            shape((1, D), full_type),
            shape((GROUP, rows, 4 * D), low_type),
            shape((GROUP, rows, units), low_type),
            shape((GROUP, ROW, D), low_type),
        ),
        in_specs=[pl.BlockSpec(memory_space=pltpu.SMEM)] + [vmem()] * 4 + [anywhere()] * 4,
        out_specs=(anywhere(),) * 2 + (vmem(),) * 8 + (anywhere(),) * 3,
        scratch_shapes=[
            pltpu.VMEM(project.shape, full_type),
            pltpu.VMEM(output.shape, full_type),
            pltpu.VMEM(expand.shape, full_type),
            pltpu.VMEM(modulate.shape, full_type),
            pltpu.VMEM((rows, 4 * D), low_type),
            pltpu.VMEM((GROUP, rows, 4 * D), low_type),
            pltpu.VMEM((GROUP, rows, units), low_type),
            pltpu.VMEM((ROW, D), low_type),
            pltpu.VMEM((GROUP, 8, rows), full_type),
            pltpu.VMEM((GROUP, 8, rows), full_type),
            pltpu.VMEM((DEPTH, GROUP, 8, rows), full_type),
            pltpu.VMEM((GROUP, 16, columns), full_type),
            pltpu.VMEM((4, 16, columns), full_type),
            pltpu.VMEM((3, 16, columns), full_type),
            pltpu.VMEM((DEPTH, 8, columns), full_type),
            pltpu.VMEM((DEPTH, 8, columns), full_type),
            pltpu.VMEM((GROUP, 1, shard), full_type),
            pltpu.VMEM((1, GROUP * shard), full_type),
            dma((35,)),
            dma((35,)),
            dma((9,)),
            dma((9,)),
            dma((9,)),
            dma((9,)),
            dma((7,)),
            dma((7,)),
            dma((9,)),
            dma((9,)),
            dma((9,)),
            pltpu.VMEM((ROW, 3 * D), low_type),
            pltpu.VMEM((ROW, D), low_type),
        ],
        compiler_params=pltpu.CompilerParams(
            collective_id=0, has_side_effects=True, vmem_limit_bytes=VMEM_BYTES
        ),
        name="forward",
    )(lengths, tokens, cotangent, conditions, bias_own, project, output, expand, modulate)


def square_sum(values):
    values = values.astype(full_type)
    squares = values * values
    while squares.ndim > 2:
        squares = jnp.sum(squares, axis=0)
    return jnp.sum(jnp.sum(squares, axis=0, keepdims=True), axis=1, keepdims=True)


class Chain:
    def __init__(self, chunks, pair_sends, pair_recvs, mid_sends, mid_recvs):
        self.chunks = chunks
        self.place, self.layer = lax.axis_index("dp"), lax.axis_index("mod")
        self.pair = self.layer + 1 - 2 * lax.rem(self.layer, 2)
        self.edge = (self.layer == 0) | (self.layer == DEPTH - 1)
        self.middle = jnp.logical_not(self.edge)
        self.sems = (pair_sends, pair_recvs, mid_sends, mid_recvs)

    def pair_copy(self, index, source):
        return pltpu.make_async_remote_copy(
            src_ref=source,
            dst_ref=self.chunks[index][1],
            send_sem=self.sems[0].at[index],
            recv_sem=self.sems[1].at[index],
            device_id=(self.place, self.pair),
            device_id_type=MESH,
        )

    def middle_copy(self, index):
        return pltpu.make_async_remote_copy(
            src_ref=self.chunks[index][0],
            dst_ref=self.chunks[index][2],
            send_sem=self.sems[2].at[index],
            recv_sem=self.sems[3].at[index],
            device_id=(self.place, DEPTH - 1 - self.layer),
            device_id_type=MESH,
        )

    def edge_send(self, *indices):
        @pl.when(self.edge)
        def _():
            for index in indices:
                self.pair_copy(index, self.chunks[index][0]).start()

    def inward(self, *indices):
        @pl.when(self.middle)
        def _():
            for index in indices:
                given, result, _ = self.chunks[index]
                self.pair_copy(index, result).wait_recv()
                given[...] = (given[...].astype(full_type) + result[...].astype(full_type)).astype(low_type)
                self.middle_copy(index).start()

    def outward(self, *indices):
        @pl.when(self.middle)
        def _():
            for index in indices:
                given, result, other = self.chunks[index]
                self.middle_copy(index).wait()
                result[...] = (given[...].astype(full_type) + other[...].astype(full_type)).astype(low_type)
                self.pair_copy(index, result).start()

    def finish(self):
        @pl.when(self.edge)
        def _():
            for index in range(len(self.chunks)):
                self.pair_copy(index, self.chunks[index][0]).wait()

        @pl.when(self.middle)
        def _():
            for index in range(len(self.chunks)):
                self.pair_copy(index, self.chunks[index][1]).wait_send()


def slot_sums(onehot, values):
    high = values.astype(low_type)
    rest = (values - high.astype(full_type)).astype(low_type)
    return contract(onehot, high, 0, 0) + contract(onehot, rest, 0, 0)


def feed_kernel(
    lengths,
    feed_own,
    expand,
    bias,
    modulation,
    cotangent_in,
    attend_out_in,
    resid_in,
    mixed_in,
    shrink,
    grads,
    full_weights,
    feed_parts,
    shrink_sum,
    shrink_rest,
    shrink_square,
    expand_own,
    grad_bias,
    grad_resid,
    grad_attend,
    grad_mixed,
    output_parts,
    slot_grads,
    feed_all,
    grad_all,
    hidden_all,
    pre_all,
    grad_parts,
    shrink_full,
    shrink_low,
    grad_shrink,
    shrink_mid,
    grad_expand,
    output_weight,
    slots,
    cotangent,
    attend_out,
    resid,
    mixed,
    local_sems,
    feed_sends,
    feed_recvs,
    expand_sends,
    expand_recvs,
    chain_sems,
    *scratch,
):
    grad_scatter = Scatter(grad_parts, scratch, ROW, ROW // 2)
    place, layer, twin, across, along, corner = plane_places()
    plane = [lax.rem(place + step, GROUP) for step in range(1, GROUP)]
    column = [lax.rem(layer + step, DEPTH) for step in range(1, DEPTH)]
    rows = output_parts.shape[1]
    units = hidden_all.shape[2]
    feed_gather = Gather(feed_own, feed_all, feed_sends, feed_recvs, 0, ROW, ROW // 2)
    chunks, start = [], 0
    for step in range(4):
        size = 64 + 16 * (step % 2)
        part = pl.ds(start, size)
        start += size
        chunks.append((grad_shrink.at[part], shrink_sum.at[part], shrink_mid.at[part]))
    chain = Chain(chunks, *(chain_sems.at[step] for step in range(4)))
    shrink_copy = pltpu.make_async_copy(shrink, shrink_full, local_sems.at[0])
    grad_copy = pltpu.make_async_copy(grads, grad_all, local_sems.at[1])
    weight_copy = pltpu.make_async_copy(full_weights.at[:, :, pl.ds(3 * D, D)], output_weight, local_sems.at[2])
    shrink_copy.start()
    grad_copy.start()
    weight_copy.start()
    late_copies = [
        pltpu.make_async_copy(given, held, local_sems.at[5 + step])
        for step, (given, held) in enumerate(
            ((cotangent_in, cotangent), (attend_out_in, attend_out), (resid_in, resid), (mixed_in, mixed))
        )
    ]
    for copy in late_copies:
        copy.start()
    greet([(peer, layer) for peer in plane] + [(place, peer) for peer in column])
    feed_gather.start_links()
    feed_gather.start_twin()
    feed_all[place] = feed_own[...]
    shrink_copy.wait()
    shrink_low[...] = shrink_full[...].astype(low_type)
    slots[...] = slot_numbers(lengths, (ROW, 1), 0)
    slot_grads[...] = jnp.zeros_like(slot_grads)
    grad_copy.wait()

    def through(slot):
        both = pl.ds(2 * lax.div(slot, 2), 2)
        pre = contract(feed_all[both].reshape(2 * ROW, D), expand[...], 1, 0) + bias[...]
        tanh_part = jnp.tanh(tanh_scale * (pre + cubic_term * pre * pre * pre))
        hidden = (0.5 * pre * (1.0 + tanh_part)).astype(low_type)
        slope = 0.5 * (1.0 + tanh_part) + 0.5 * pre * (1.0 - tanh_part * tanh_part) * tanh_scale * (
            1.0 + 3.0 * cubic_term * pre * pre
        )
        hidden_all[both] = hidden.reshape(2, ROW, units)
        grad_hidden = contract(grad_all[both].reshape(2 * ROW, D), shrink_low[...], 1, 1)
        grad_pre = (grad_hidden * slope).astype(low_type)
        pre_all[both] = grad_pre.reshape(2, ROW, units)
        grad_parts[both] = contract(grad_pre, expand[...], 1, 1).astype(low_type).reshape(2, ROW, D)

    feed_gather.arrived(2)
    through(place)
    feed_gather.forward_near()
    feed_gather.arrived(5)
    through(across)
    grad_scatter.start_twin(1)
    feed_gather.arrived(6)
    through(along)
    grad_scatter.start_twin(2)
    feed_gather.forward_far()
    grad_scatter.start_near()
    feed_gather.arrived(7, 8)
    through(corner)
    grad_scatter.start_twin(3, 0)
    grad_scatter.start_far()

    hidden = hidden_all[...].reshape(GROUP * ROW, units)
    grad_shrink[...] = contract(hidden, grad_all[...].reshape(GROUP * ROW, D), 0, 0).astype(low_type)
    chain.edge_send(*range(4))
    shrink_rest[...] = grad_shrink[pl.ds(units // 2, units // 2), :]
    grad_pre = pre_all[...].reshape(GROUP * ROW, units)
    expand_grads = contract(feed_all[...].reshape(GROUP * ROW, D), grad_pre, 0, 0).astype(low_type)
    grad_expand[...] = expand_grads.reshape(GROUP, rows, units)
    grad_scatter.forward()
    exchange = []
    for step, peer in enumerate(plane):
        exchange.append(
            send(grad_expand.at[peer], expand_own.at[place], expand_sends.at[step], expand_recvs.at[step], peer, layer)
        )
    expand_own[place] = grad_expand[place]
    chain.inward(0)
    grad_bias[...] = jnp.sum(grad_pre.astype(full_type), axis=0, keepdims=True)

    def part_step(step, carry):
        both = pl.ds(2 * step, 2)
        parts = contract(hidden_all[both].reshape(2 * ROW, units), shrink_low[...], 1, 0)
        grad_all[both] = parts.astype(low_type).reshape(2, ROW, D)
        return carry

    lax.fori_loop(0, 2, part_step, 0)
    chain.inward(1)
    lax.fori_loop(2, GROUP // 2, part_step, 0)
    feed_copy = pltpu.make_async_copy(grad_all, feed_parts, local_sems.at[3])
    feed_copy.start()
    chain.inward(2)
    chain.outward(0)
    chain.inward(3)
    chain.outward(1)
    for copy in late_copies:
        copy.wait()
    grad_scatter.settle()
    chain.outward(2)

    def feed_step(step, carry):
        part = block_part(step)
        onehot = slot_onehot(slots[part, :])
        normed, inverse = normalize_rows(resid[part, :])
        grad_in = grad_scatter.total(part)
        slot_grads[3] += slot_sums(onehot, grad_in)
        slot_grads[4] += slot_sums(onehot, grad_in * normed)
        grad = cotangent[part, :].astype(full_type) + normalize_back(
            grad_in * (1.0 + spread_slots(onehot, modulation, 4)), normed, inverse
        )
        grad_resid[part, :] = grad
        slot_grads[2] += slot_sums(onehot, grad * attend_out[part, :])
        grad_attend[part, :] = (spread_slots(onehot, modulation, 2) * grad).astype(low_type)
        return carry

    lax.fori_loop(0, ROW // BLOCK // 2, feed_step, 0)
    chain.outward(3)
    lax.fori_loop(ROW // BLOCK // 2, ROW // BLOCK, feed_step, 0)
    weight_copy.wait()
    grad_mixed[...] = contract(grad_attend[...], output_weight[...].reshape(D, D), 1, 1).astype(low_type)

    def weight_step(step, carry):
        where = pl.ds(pl.multiple_of(step * 384, 128), 384)
        values = contract(mixed[...], grad_attend[:, where], 0, 0).astype(low_type)
        output_weight[:, :, where] = values.reshape(GROUP, rows, 384)
        return carry

    lax.fori_loop(0, 3, weight_step, 0)
    output_copy = pltpu.make_async_copy(output_weight, output_parts, local_sems.at[4])
    output_copy.start()
    feed_copy.wait()
    output_copy.wait()
    feed_gather.finish_sends()
    for copy in exchange:
        copy.wait()
    chain.finish()
    shrink_square[...] = jnp.broadcast_to(square_sum(shrink_sum[...]), shrink_square.shape)


def feed_call(
    lengths, feed_own, expand, bias, modulation, cotangent, attend_out, resid, mixed, shrink, grads, full_weights
):
    units = expand.shape[1]
    rows = full_weights.shape[1]
    shape = jax.ShapeDtypeStruct
    dma = pltpu.SemaphoreType.DMA
    return pl.pallas_call(
        feed_kernel,
        out_shape=(
            shape((GROUP, ROW, D), low_type),
            shape((units // 2, D), low_type),
            shape((units // 2, D), low_type),
            shape((8, LANES), full_type),
            shape((GROUP, rows, units), low_type),
            shape((1, units), full_type),
            shape((ROW, D), full_type),
            shape((ROW, D), low_type),
            shape((ROW, D), low_type),
            shape((GROUP, rows, D), low_type),
            shape((6, 8, D), full_type),
        ),
        in_specs=[pl.BlockSpec(memory_space=pltpu.SMEM)] + [vmem()] * 4 + [anywhere()] * 7,
        out_specs=(anywhere(),) + (vmem(),) * 8 + (anywhere(), vmem()),
        scratch_shapes=[
            pltpu.VMEM((GROUP, ROW, D), low_type),
            pltpu.VMEM((GROUP, ROW, D), low_type),
            pltpu.VMEM((GROUP, ROW, units), low_type),
            pltpu.VMEM((GROUP, ROW, units), low_type),
            pltpu.VMEM((GROUP, ROW, D), low_type),
            pltpu.VMEM((units, D), full_type),
            pltpu.VMEM((units, D), low_type),
            pltpu.VMEM((units, D), low_type),
            pltpu.VMEM((units // 2, D), low_type),
            pltpu.VMEM((GROUP, rows, units), low_type),
            pltpu.VMEM((GROUP, rows, D), low_type),
            pltpu.VMEM((ROW, 1), jnp.int32),
            pltpu.VMEM((ROW, D), low_type),
            pltpu.VMEM((ROW, D), full_type),
            pltpu.VMEM((ROW, D), full_type),
            pltpu.VMEM((ROW, D), low_type),
            dma((9,)),
            dma((9,)),
            dma((9,)),
            dma((7,)),
            dma((7,)),
            dma((4, 8)),
            *scatter_scratch(ROW, ROW // 2, D),
        ],
        compiler_params=pltpu.CompilerParams(
            collective_id=1, has_side_effects=True, vmem_limit_bytes=VMEM_BYTES
        ),
        name="feed_forward",
    )(lengths, feed_own, expand, bias, modulation, cotangent, attend_out, resid, mixed, shrink, grads, full_weights)


def sample_compactor():
    row, column = iota((16, 32), 0), iota((16, 32), 1)
    return (column == (row >> 2) * 8 + (row & 3)).astype(full_type).astype(low_type)


def sample_scatterer():
    row, column = iota((256, 128), 0), iota((256, 128), 1)
    wanted = ((row >> 3) & 7) * 16 + (row >> 6) * 4 + (row & 7)
    return jnp.where(((row & 7) < 4) & (column == wanted), 1.0, 0.0).astype(low_type)


def column_sum(values):
    return jnp.sum(values.astype(full_type), axis=0, keepdims=True)


BIAS_ROWS = 128
COLUMN_GROUPS = ((0, 512), (512, 256), (768, 384))
CHAIN_COLUMNS = ((0, 256), (256, 256), (512, 256), (768, 256), (1024, 128))
GROUP_CHUNKS = ((13, 14), (15,), (16, 17))


def back_kernel(
    lengths,
    tokens_in,
    cotangent_in,
    modulation,
    packed,
    attend_given,
    resid_in,
    grad_resid_in,
    grad_attend,
    grad_mixed,
    slot_grads_in,
    bias_shrink,
    grad_bias_expand,
    shrink_square,
    active,
    conditions,
    modulate,
    full_weights,
    feed_parts_in,
    output_parts,
    expand_parts,
    shrink_rest,
    block_output,
    token_grads,
    project_sum,
    output_sum,
    expand_sum,
    shrink_sum,
    bias_out,
    modulate_sum,
    condition_grads,
    square_total,
    output_store,
    project_store,
    feed_parts,
    grad_packed,
    slot_grads,
    project_own,
    output_own,
    expand_own,
    project_mid,
    output_mid,
    expand_mid,
    shrink_own,
    shrink_mid,
    bias_own,
    bias_recv,
    bias_layers,
    sample_send,
    sample_recv,
    group_all,
    term_send,
    term_recv,
    term_sum,
    square_send,
    square_recv,
    square_part,
    square_all,
    small_sends,
    small_recvs,
    chain_sems,
    local_sems,
    slots,
    bias_sum,
    bias_flat,
    condition_sum,
    tokens,
    cotangent,
    attend_in,
    resid,
    grad_resid,
    *scratch,
):
    place, layer, *_ = plane_places()
    plane = [lax.rem(place + step, GROUP) for step in range(1, GROUP)]
    column = [lax.rem(layer + step, DEPTH) for step in range(1, DEPTH)]
    rows = output_own.shape[0]
    scale = HEAD_DIM ** (-0.5)

    chunks, start = [], 0
    for step in range(4):
        size = 64 + 16 * (step % 2)
        part = pl.ds(start, size)
        start += size
        chunks.append((shrink_own.at[part], shrink_sum.at[part], shrink_mid.at[part]))
    for step in range(GROUP):
        chunks.append((expand_own.at[step], expand_sum.at[step], expand_mid.at[step]))
    chunks.append((output_own, output_sum, output_mid))
    for first, width in CHAIN_COLUMNS:
        part = (slice(None), slice(None), pl.ds(first, width))
        chunks.append((project_own.at[part], project_sum.at[part], project_mid.at[part]))
    chain = Chain(chunks, *(chain_sems.at[step] for step in range(4)))

    waits = []

    def exchange(base, peers, source, target):
        copies = []
        for step, peer in enumerate(peers):
            where = (peer, layer) if peers is plane else (place, peer)
            copies.append(
                send(source(peer), target, small_sends.at[base + step], small_recvs.at[base + step], *where)
            )
        waits.extend(copies)
        return copies

    def arrive(copies):
        for copy in copies:
            copy.wait_recv()

    def load(index, source, target):
        copy = pltpu.make_async_copy(source, target, local_sems.at[index])
        copy.start()
        return copy

    feed_scatter = Scatter(feed_parts, scratch[0:7], ROW, ROW // 2, outgoing=feed_parts_in)
    output_scatter = Scatter(output_store, scratch[7:14], rows, 64, outgoing=output_parts)
    project_scatters = []
    for step, (first, width) in enumerate(COLUMN_GROUPS):
        buffers = (*scratch[14:19], scratch[19].at[step], scratch[20].at[step])
        project_scatters.append(
            Scatter(project_store, buffers, rows, 64, columns=pl.ds(first, width))
        )
    shrink_load = load(12, shrink_rest, shrink_own)
    expand_load = load(0, expand_parts, expand_own)
    feed_loads = [
        load(1 + step, feed_parts_in.at[feed_scatter.places[step]], feed_parts.at[step]) for step in range(4)
    ]
    output_loads = [
        load(5 + step, output_parts.at[feed_scatter.places[step]], output_store.at[step]) for step in range(4)
    ]
    late_loads = [
        load(13 + step, given, held)
        for step, (given, held) in enumerate(
            (
                (attend_given, attend_in),
                (tokens_in, tokens),
                (grad_resid_in, grad_resid),
                (cotangent_in, cotangent),
                (resid_in, resid),
            )
        )
    ]
    project_loads = [
        load(9 + step, full_weights.at[:, :, pl.ds(step * D, D)], project_store.at[step]) for step in range(3)
    ]

    greet([(peer, layer) for peer in plane] + [(place, peer) for peer in column])

    feed_scatter.start_twin()
    output_scatter.start_twin()
    shrink_load.wait()
    chain.edge_send(*range(4))
    expand_load.wait()
    chain.edge_send(*range(4, 12))
    slot_grads[...] = slot_grads_in[...]
    bias_own[...] = jnp.zeros_like(bias_own)
    grad_packed[...] = jnp.zeros_like(grad_packed)

    slot_row = slot_numbers(lengths, (1, ROW), 1)
    slot_column = slot_numbers(lengths, (ROW, 1), 0)
    slots[...] = slot_column

    def block_parts(step):
        part = block_part(step)
        return part, slot_onehot(slots[part, :])

    same = slot_column == slot_row

    def head_step(head, carry):
        start, inside = head_window(head)
        keep = inside.astype(low_type)
        query = window(packed, 0, start) * keep
        key = window(packed, D, start)
        value = window(packed, 2 * D, start)
        grad = window(grad_mixed, 0, start) * keep
        probs = masked_probs(query, key, same)
        grad_probs = contract(grad, value, 1, 1)
        grad_scores = probs * (grad_probs - jnp.sum(probs * grad_probs, axis=1, keepdims=True))
        grad_scores = grad_scores.astype(low_type)

        def put(base, values):
            where = pl.ds(pl.multiple_of(base + start, 128), 256)
            grad_packed[:, where] = (grad_packed[:, where].astype(full_type) + values).astype(low_type)

        put(0, contract(grad_scores, key * keep, 1, 0) * scale)
        put(D, contract(grad_scores, query, 0, 0) * scale)
        put(2 * D, contract(probs.astype(low_type), grad, 0, 0))
        return carry

    def heads(first, last):
        lax.fori_loop(first, last, head_step, 0, unroll=4)

    def project_group(step):
        first, width = COLUMN_GROUPS[step]
        for kind in range(3):
            where = pl.ds(first, width)
            grads = grad_packed[:, kind * D + first : kind * D + first + width]
            back = contract(grads, project_store[kind, :, :, where].reshape(D, width), 1, 1)
            if step == 0 and kind == 0:
                token_grads[...] = back
            else:
                token_grads[...] += back
            weight = contract(attend_in[...], grads, 0, 0).astype(low_type)
            project_store[kind, :, :, where] = weight.reshape(GROUP, rows, width)
        project_scatters[step].start_twin()

    heads(0, 4)
    for copy in feed_loads:
        copy.wait()
    feed_scatter.start_far()
    feed_scatter.start_near()
    for copy in output_loads:
        copy.wait()
    output_scatter.start_far()
    output_scatter.start_near()
    chain.inward(0)
    chain.inward(1)
    heads(4, 8)
    chain.inward(2)
    chain.outward(0)
    for copy in project_loads + late_loads:
        copy.wait()
    project_group(0)
    feed_scatter.forward()
    chain.inward(3)
    chain.outward(1)
    heads(8, 12)
    chain.inward(4)
    chain.outward(2)
    project_scatters[0].start_far()
    project_scatters[0].start_near()
    project_group(1)
    chain.inward(5)
    chain.outward(3)
    output_scatter.forward()
    heads(12, 16)
    chain.inward(6)
    chain.outward(4)
    chain.inward(7)
    chain.outward(5)
    project_scatters[1].start_far()
    project_scatters[1].start_near()
    project_group(2)
    project_scatters[0].forward()
    chain.inward(8)
    chain.outward(6)

    def attend_step(step, carry):
        part, onehot = block_parts(step)
        normed, inverse = normalize_rows(tokens[part, :].astype(full_type))
        grad_in = token_grads[part, :]
        slot_grads[0] += slot_sums(onehot, grad_in)
        slot_grads[1] += slot_sums(onehot, grad_in * normed)
        token_grads[part, :] = grad_resid[part, :] + normalize_back(
            grad_in * (1.0 + spread_slots(onehot, modulation, 1)), normed, inverse
        )
        return carry

    lax.fori_loop(0, ROW // BLOCK, attend_step, 0)
    project_scatters[2].start_far()
    project_scatters[2].start_near()
    chain.inward(9)
    chain.outward(7)
    feed_scatter.settle()

    def put_rows(base, values):
        for step in range(values.shape[1] // LANES):
            bias_own[base + step : base + step + 1, :] = values[:, step * LANES : (step + 1) * LANES]

    def output_step(step, carry):
        part, onehot = block_parts(step)
        feed_out = feed_scatter.total(part) + bias_shrink[...]
        grad = cotangent[part, :].astype(full_type)
        gate = spread_slots(onehot, modulation, 5)
        block_output[part, :] = (resid[part, :] + gate * feed_out).astype(low_type)
        slot_grads[5] += slot_sums(onehot, grad * feed_out)
        return carry + column_sum((gate * grad).astype(low_type))

    feed_bias = lax.fori_loop(0, ROW // BLOCK, output_step, jnp.zeros((1, D), full_type))
    rounded = [slot_grads[step].astype(low_type).astype(full_type) for step in range(6)]
    half = D // 2
    for block in range(DEPTH):
        for step in range(3):
            piece, side = divmod(3 * block + step, 2)
            sample_send[block, :, step * half : (step + 1) * half] = rounded[piece][:, side * half : (side + 1) * half]
    sample_copies = exchange(7, column, lambda peer: sample_send.at[peer], sample_recv.at[layer])
    sample_recv[layer] = sample_send[layer]
    put_rows(0, column_sum(grad_packed[:, 0:D]))
    put_rows(9, column_sum(grad_packed[:, 2 * D : 3 * D]))
    put_rows(18, column_sum(grad_attend[...]))
    put_rows(27, feed_bias)
    for step in range(6):
        put_rows(36 + 9 * step, column_sum(rounded[step]))
    bias_recv[place] = bias_own[pl.ds(pl.multiple_of(place * 16, 16), 16), :]
    bias_copies = exchange(
        10, plane, lambda peer: bias_own.at[pl.ds(pl.multiple_of(peer * 16, 16), 16)], bias_recv.at[place]
    )
    def settle_group(step):
        project_scatters[step].settle()
        first, width = COLUMN_GROUPS[step]
        project_own[:, :, pl.ds(first, width)] = project_scatters[step].total().astype(low_type)
        chain.edge_send(*GROUP_CHUNKS[step])

    project_scatters[1].forward()
    chain.inward(10)
    chain.outward(8)
    chain.inward(11)
    chain.outward(9)
    output_scatter.settle()
    output_own[...] = output_scatter.total().astype(low_type)
    chain.edge_send(12)
    chain.outward(10, 11)
    project_scatters[2].forward()
    settle_group(0)
    arrive(sample_copies)
    group = contract(sample_compactor(), sample_recv[...].reshape(DEPTH * 8, sample_recv.shape[2]).astype(low_type), 1, 0)
    group_all[place] = group.astype(low_type)
    group_copies = exchange(17, plane, lambda peer: group_all.at[place], group_all.at[place])
    chain.inward(12)
    arrive(bias_copies)
    total = bias_recv[0]
    for step in range(1, GROUP):
        total = total + bias_recv[step]
    bias_layers[layer, 0:16, :] = total
    bias_layers[layer, 16:24, :] = jnp.zeros((8, LANES), full_type)
    for step in range(4):
        bias_layers[layer, 16 + step : 17 + step, :] = grad_bias_expand[:, step * LANES : (step + 1) * LANES]
    bias_layers[layer, 20:21, 0:64] = grad_bias_expand[:, 512:576]
    layer_copies = exchange(24, column, lambda peer: bias_layers.at[layer], bias_layers.at[layer])
    settle_group(1)
    chain.inward(13)
    chain.outward(12)
    settle_group(2)
    chain.inward(14)
    chain.outward(13)
    arrive(group_copies)
    every = group_all[...].reshape(GROUP * 16, group_all.shape[2])
    spread = contract(sample_scatterer(), every, 1, 0).astype(low_type)
    terms = contract(spread, modulate[...].astype(low_type), 1, 1)
    term_send[...] = terms.reshape(term_send.shape)
    term_copies = exchange(27, column, lambda peer: term_send.at[peer], term_recv.at[layer])
    term_recv[layer] = term_send[layer]
    chain.inward(15)
    chain.outward(14)
    modulate_sum[...] = contract(active[...], every, 0, 0)
    chain.inward(16)
    arrive(layer_copies)
    total = (bias_layers[0] + bias_layers[1]) + (bias_layers[2] + bias_layers[3])
    bias_sum[place] = total
    bias_copies = exchange(30, plane, lambda peer: bias_sum.at[place], bias_sum.at[place])
    chain.outward(15)
    chain.inward(17)
    square_part[...] = jnp.broadcast_to(square_sum(modulate_sum[...]), (8, LANES))
    square_all[layer] = square_part[...]
    square_copies = exchange(51, column, lambda peer: square_part, square_all.at[layer])
    chain.outward(16, 17)
    arrive(term_copies)
    term_sum[...] = (term_recv[0] + term_recv[1]) + (term_recv[2] + term_recv[3])
    last_copies = exchange(37, plane, lambda peer: term_sum.at[peer], condition_sum.at[place])
    condition_sum[place] = term_sum[place]
    arrive(bias_copies)
    arrive(last_copies)
    for step in range(GROUP):
        condition_grads[:, step * rows : (step + 1) * rows] = condition_sum[step, 0:IMG_ROW, :]
    given = conditions[...].astype(full_type)
    sigmoid_part = jax.nn.sigmoid(given)
    condition_grads[...] = condition_grads[...] * (sigmoid_part * (1.0 + given * (1.0 - sigmoid_part)))
    bias_flat[:, 16128:16384] = jnp.zeros((1, 256), full_type)
    for step in range(90):
        row = bias_sum[step // 16, step % 16 : step % 16 + 1, :]
        base = step * LANES if step < 27 else FF + step * LANES
        bias_flat[:, base : base + LANES] = row
    units = grad_bias_expand.shape[1]
    for step in range(GROUP):
        base = 3 * D + step * units
        for piece in range(4):
            bias_flat[:, base + piece * LANES : base + (piece + 1) * LANES] = bias_sum[step, 16 + piece : 17 + piece, :]
        bias_flat[:, base + 512 : base + 576] = bias_sum[step, 20:21, 0:64]
    shard = bias_out.shape[1]
    offset = place * shard
    start = pl.multiple_of(lax.div(offset, LANES) * LANES, LANES)
    extent = 17 * LANES
    piece = jnp.broadcast_to(bias_flat[:, pl.ds(start, extent)], (8, extent))
    piece = pltpu.roll(piece, lax.rem(extent - lax.rem(offset, LANES), extent), 1)
    bias_out[...] = piece[0:1, 0:shard]
    arrive(square_copies)
    modulate_square = (square_all[0] + square_all[1]) + (square_all[2] + square_all[3])
    chain.finish()
    trunk = (
        square_sum(project_sum[...])
        + square_sum(output_sum[...])
        + square_sum(expand_sum[...])
        + square_sum(shrink_sum[...])
        + shrink_square[0:1, 0:1]
        + square_sum(bias_sum[place])
    )
    square_send[...] = jnp.broadcast_to(trunk, (8, LANES)) + modulate_square
    square_copies = exchange(44, plane, lambda peer: square_send, square_recv.at[place])
    square_recv[place] = square_send[...]
    arrive(square_copies)
    both = square_recv[0]
    for step in range(1, GROUP):
        both = both + square_recv[step]
    square_total[...] = both
    bias_out[...] = bias_out[...] * jnp.minimum(1.0, 1.0 / (jnp.sqrt(both[0:1, 0:1]) + 1e-06))
    for copy in waits:
        copy.wait_send()


def back_call(*operands):
    modulate, expand_parts = operands[16], operands[20]
    rows, columns = modulate.shape
    units = expand_parts.shape[2]
    shape = jax.ShapeDtypeStruct
    dma = pltpu.SemaphoreType.DMA
    return pl.pallas_call(
        back_kernel,
        out_shape=(
            shape((ROW, D), low_type),
            shape((ROW, D), full_type),
            shape((3, rows, D), low_type),
            shape((rows, D), low_type),
            shape((GROUP, rows, units), low_type),
            shape((FF // GROUP // 2, D), low_type),
            shape((1, (10 * D + FF) // GROUP), full_type),
            shape((rows, columns), full_type),
            shape((IMG_ROW, D), full_type),
            shape((8, LANES), full_type),
        ),
        in_specs=[pl.BlockSpec(memory_space=pltpu.SMEM)]
        + [anywhere()] * 2
        + [vmem()] * 2
        + [anywhere()] * 3
        + [vmem()] * 9
        + [anywhere()] * 5,
        out_specs=(vmem(),) * 10,
        scratch_shapes=[
            pltpu.VMEM((4, rows, D), low_type),
            pltpu.VMEM((3, GROUP, rows, D), low_type),
            pltpu.VMEM((4, ROW, D), low_type),
            pltpu.VMEM((ROW, 3 * D), low_type),
            pltpu.VMEM((6, 8, D), full_type),
            pltpu.VMEM((3, rows, D), low_type),
            pltpu.VMEM((rows, D), low_type),
            pltpu.VMEM((GROUP, rows, units), low_type),
            pltpu.VMEM((3, rows, D), low_type),
            pltpu.VMEM((rows, D), low_type),
            pltpu.VMEM((GROUP, rows, units), low_type),
            pltpu.VMEM((FF // GROUP // 2, D), low_type),
            pltpu.VMEM((FF // GROUP // 2, D), low_type),
            pltpu.VMEM((BIAS_ROWS, LANES), full_type),
            pltpu.VMEM((GROUP, 16, LANES), full_type),
            pltpu.VMEM((DEPTH, 24, LANES), full_type),
            pltpu.VMEM((DEPTH, 8, columns), full_type),
            pltpu.VMEM((DEPTH, 8, columns), full_type),
            pltpu.VMEM((GROUP, 16, columns), low_type),
            pltpu.VMEM((DEPTH, GROUP, 8, rows), full_type),
            pltpu.VMEM((DEPTH, GROUP, 8, rows), full_type),
            pltpu.VMEM((GROUP, 8, rows), full_type),
            pltpu.VMEM((8, LANES), full_type),
            pltpu.VMEM((GROUP, 8, LANES), full_type),
            pltpu.VMEM((8, LANES), full_type),
            pltpu.VMEM((DEPTH, 8, LANES), full_type),
            dma((54,)),
            dma((54,)),
            dma((4, 18)),
            dma((18,)),
            pltpu.VMEM((ROW, 1), jnp.int32),
            pltpu.VMEM((GROUP, 24, LANES), full_type),
            pltpu.VMEM((1, 16384), full_type),
            pltpu.VMEM((GROUP, 8, rows), full_type),
            pltpu.VMEM((ROW, D), low_type),
            pltpu.VMEM((ROW, D), low_type),
            pltpu.VMEM((ROW, D), low_type),
            pltpu.VMEM((ROW, D), full_type),
            pltpu.VMEM((ROW, D), full_type),
            *scatter_scratch(ROW, ROW // 2, D),
            *scatter_scratch(rows, 64, D),
            *scatter_scratch(rows, 64, D, (len(COLUMN_GROUPS),)),
        ],
        compiler_params=pltpu.CompilerParams(
            collective_id=2, has_side_effects=True, vmem_limit_bytes=VMEM_BYTES
        ),
        name="backward",
    )(*operands)


TILES = 12
DEEP = 3


def update_kernel(
    square_total,
    project_sum,
    output_sum,
    expand_sum,
    shrink_low,
    shrink_high,
    modulate_sum,
    *refs,
):
    states, results, scratch = refs[0:15], refs[15:31], refs[31:]
    norm, results = results[0], results[1:]
    held, fresh, wide_held, wide_fresh, joined, load_sems, store_sems, wide_sems = scratch
    rows = output_sum.shape[0]
    units = expand_sum.shape[2]
    places = []
    whole = slice(None)
    for step in range(3):
        places.append((0, (whole, pl.ds(step * D, D)), D ** (-0.5)))
    places.append((1, (whole, whole), (D // 64) ** (-0.5)))
    for step in range(4):
        places.append((2, (whole, pl.ds(step * D, D)), D ** (-0.5)))
    for step in range(4):
        places.append((3, (pl.ds(step * rows, rows), whole), FF ** (-0.5)))

    def loads(tile):
        array, where, _ = places[tile]
        return [
            pltpu.make_async_copy(
                states[3 * array + kind].at[where], held.at[tile % DEEP, kind], load_sems.at[tile % DEEP, kind]
            )
            for kind in range(3)
        ]

    def stores(tile):
        array, where, _ = places[tile]
        return [
            pltpu.make_async_copy(
                fresh.at[tile % DEEP, kind], results[3 * array + kind].at[where], store_sems.at[tile % DEEP, kind]
            )
            for kind in range(3)
        ]

    wide_loads = [pltpu.make_async_copy(states[12 + kind], wide_held.at[kind], wide_sems.at[kind]) for kind in range(3)]
    wide_stores = [
        pltpu.make_async_copy(wide_fresh.at[kind], results[12 + kind], wide_sems.at[3 + kind]) for kind in range(3)
    ]
    for copy in wide_loads:
        copy.start()
    for tile in range(DEEP):
        for copy in loads(tile):
            copy.start()
    total = jnp.sqrt(square_total[...])
    norm[...] = total
    clip = jnp.minimum(1.0, 1.0 / (total[0:1, 0:1] + 1e-06))

    def update(before, after, grads, rate):
        def step(index, carry):
            part = pl.ds(pl.multiple_of(index * 16, 16), 16)
            grad = grads[part, :].astype(full_type) * clip
            results = adam_update(before[0, part, :], before[1, part, :], before[2, part, :], grad, rate)
            for kind in range(3):
                after[kind, part, :] = results[kind]
            return carry

        lax.fori_loop(0, rows // 16, step, 0)

    for copy in wide_loads:
        copy.wait()
    update(wide_held, wide_fresh, modulate_sum, D ** (-0.5))
    for copy in wide_stores:
        copy.start()
    for tile in range(TILES):
        for copy in loads(tile):
            copy.wait()
        if tile >= DEEP:
            for copy in stores(tile - DEEP):
                copy.wait()
        array, where, rate = places[tile]
        if array == 0:
            grads = project_sum.at[tile]
        elif array == 1:
            grads = output_sum
        elif array == 2:
            index = 2 * (tile - 4)
            joined[:, 0:units] = expand_sum[index].astype(full_type)
            joined[:, units : 2 * units] = expand_sum[index + 1].astype(full_type)
            grads = joined
        else:
            grads = (shrink_low if tile < 10 else shrink_high).at[pl.ds((tile - 8) % 2 * rows, rows)]
        update(held.at[tile % DEEP], fresh.at[tile % DEEP], grads, rate)
        for copy in stores(tile):
            copy.start()
        if tile + DEEP < TILES:
            for copy in loads(tile + DEEP):
                copy.start()
    for tile in range(TILES - DEEP, TILES):
        for copy in stores(tile):
            copy.wait()
    for copy in wide_stores:
        copy.wait()


def update_call(square_total, project_sum, output_sum, expand_sum, shrink_low, shrink_high, modulate_sum, *states):
    rows, columns = modulate_sum.shape
    shape = jax.ShapeDtypeStruct
    dma = pltpu.SemaphoreType.DMA
    results = pl.pallas_call(
        update_kernel,
        out_shape=(shape((8, LANES), full_type), *(shape(state.shape, full_type) for state in states)),
        in_specs=[vmem()] * 7 + [anywhere()] * 15,
        out_specs=(vmem(),) + (anywhere(),) * 15,
        scratch_shapes=[
            pltpu.VMEM((DEEP, 3, rows, D), full_type),
            pltpu.VMEM((DEEP, 3, rows, D), full_type),
            pltpu.VMEM((3, rows, columns), full_type),
            pltpu.VMEM((3, rows, columns), full_type),
            pltpu.VMEM((rows, D), full_type),
            dma((DEEP, 3)),
            dma((DEEP, 3)),
            dma((6,)),
        ],
        compiler_params=pltpu.CompilerParams(vmem_limit_bytes=VMEM_BYTES),
        name="update",
    )(square_total, project_sum, output_sum, expand_sum, shrink_low, shrink_high, modulate_sum, *states)
    return results[0][0, 0], results[1:]


def plane_body(
    tokens,
    conditions,
    image_lengths,
    cotangent,
    project_weight,
    project_moment,
    project_square,
    output_weight,
    output_moment,
    output_square,
    expand_weight,
    expand_moment,
    expand_square,
    shrink_weight,
    shrink_moment,
    shrink_square,
    modulate_weight,
    modulate_moment,
    modulate_square,
    bias_vector,
    bias_moment,
    bias_square,
):
    units = FF // GROUP
    (
        packed,
        attend_in,
        mixed,
        attend_out,
        resid,
        feed_in,
        modulation,
        active,
        bias_expand,
        bias_shrink,
        full_weights,
        own_expand,
        grad_all,
    ) = front_call(
        image_lengths,
        tokens,
        cotangent,
        conditions,
        bias_vector[None, :],
        project_weight,
        output_weight,
        expand_weight,
        modulate_weight,
    )
    (
        feed_parts,
        shrink_low,
        shrink_rest,
        shrink_norm,
        expand_parts,
        grad_bias_expand,
        grad_resid,
        grad_attend,
        grad_mixed,
        output_parts,
        slot_grads,
    ) = feed_call(
        image_lengths,
        feed_in,
        own_expand.reshape(D, units),
        bias_expand,
        modulation,
        cotangent,
        attend_out,
        resid,
        mixed,
        shrink_weight,
        grad_all,
        full_weights,
    )
    (
        block_output,
        token_grads,
        sum_project,
        sum_output,
        sum_expand,
        shrink_high,
        sum_bias,
        sum_modulate,
        condition_grads,
        square_total,
    ) = back_call(
        image_lengths,
        tokens,
        cotangent,
        modulation,
        packed,
        attend_in,
        resid,
        grad_resid,
        grad_attend,
        grad_mixed,
        slot_grads,
        bias_shrink,
        grad_bias_expand,
        shrink_norm,
        active,
        conditions,
        modulate_weight,
        full_weights,
        feed_parts,
        output_parts,
        expand_parts,
        shrink_rest,
    )
    global_norm, updated = update_call(
        square_total,
        sum_project,
        sum_output,
        sum_expand,
        shrink_low,
        shrink_high,
        sum_modulate,
        project_weight,
        project_moment,
        project_square,
        output_weight,
        output_moment,
        output_square,
        expand_weight,
        expand_moment,
        expand_square,
        shrink_weight,
        shrink_moment,
        shrink_square,
        modulate_weight,
        modulate_moment,
        modulate_square,
    )
    updated_bias = adam_update(bias_vector, bias_moment, bias_square, sum_bias[0], 0.3)
    return (block_output, token_grads, condition_grads, global_norm, *updated, *updated_bias)


def generic_body(
    tokens,
    conditions,
    image_lengths,
    cotangent,
    project_weight,
    project_moment,
    project_square,
    output_weight,
    output_moment,
    output_square,
    expand_weight,
    expand_moment,
    expand_square,
    shrink_weight,
    shrink_moment,
    shrink_square,
    modulate_weight,
    modulate_moment,
    modulate_square,
    bias_vector,
    bias_moment,
    bias_square,
):
    low_type = jnp.bfloat16
    group_size = lax.axis_size("mod")
    group_place = lax.axis_index("mod")
    columns = 6 * D // group_size
    full_project, full_output, full_expand, full_shrink, full_modulate, full_bias = (
        lax.all_gather(project_weight.astype(low_type), "dp", axis=0, tiled=True),
        lax.all_gather(output_weight.astype(low_type), "dp", axis=0, tiled=True),
        lax.all_gather(expand_weight.astype(low_type), "dp", axis=0, tiled=True),
        lax.all_gather(shrink_weight.astype(low_type), "dp", axis=0, tiled=True),
        lax.all_gather(modulate_weight.astype(low_type), "dp", axis=0, tiled=True),
        lax.all_gather(bias_vector.astype(low_type), "dp", axis=0, tiled=True),
    )
    bias_full = full_bias.astype(jnp.float32)
    bias_query = bias_full[0:D]
    bias_value = bias_full[D : 2 * D]
    bias_output = bias_full[2 * D : 3 * D]
    bias_expand = bias_full[3 * D : 3 * D + FF]
    bias_shrink = bias_full[3 * D + FF : 4 * D + FF]
    bias_modulate = lax.dynamic_slice_in_dim(bias_full, 4 * D + FF + group_place * columns, columns)
    group_conditions = lax.all_gather(conditions, "mod", axis=0, tiled=True)
    activated = jax.nn.silu(group_conditions.astype(jnp.float32)).astype(low_type)
    group_mod = (contract(activated, full_modulate, 1, 0) + bias_modulate).astype(low_type)
    own_mod = lax.all_to_all(group_mod, "mod", split_axis=0, concat_axis=1, tiled=True)
    slots = jnp.arange(IMG_ROW, dtype=jnp.int32)
    ends = jnp.sum(
        jnp.where(slots[:, None] <= slots[None, :], image_lengths[0][:, None], 0), axis=0, dtype=jnp.int32
    )
    positions = jnp.arange(ROW, dtype=jnp.int32)
    slot_of = jnp.sum(
        (positions[:, None] >= ends[None, :]).astype(jnp.int32), axis=1, dtype=jnp.int32
    )
    slot_match = slot_of[:, None] == jnp.arange(IMG_ROW, dtype=jnp.int32)[None, :]
    same_image = slot_of[:, None] == slot_of[None, :]
    per_token = contract(slot_match.astype(low_type), own_mod, 1, 0)
    shift_attend = per_token[:, 0:D]
    scale_attend = per_token[:, D : 2 * D]
    gate_attend = per_token[:, 2 * D : 3 * D]
    shift_feed = per_token[:, 3 * D : 4 * D]
    scale_feed = per_token[:, 4 * D : 5 * D]
    gate_feed = per_token[:, 5 * D : 6 * D]
    inputs = tokens.astype(jnp.float32)
    normed_attend, inverse_attend = normalize_rows(inputs)
    attend_in = (normed_attend * (1.0 + scale_attend) + shift_attend).astype(low_type)
    projected = contract(attend_in, full_project, 1, 0)
    query = (projected[:, 0:D] + bias_query).astype(low_type)
    keys = projected[:, D : 2 * D].astype(low_type)
    values = (projected[:, 2 * D : 3 * D] + bias_value).astype(low_type)
    head_scale = HEAD_DIM ** (-0.5)

    def split_heads(matrix):
        return matrix.reshape(ROW, HEADS, HEAD_DIM).transpose(1, 0, 2)

    def head_scores(query_head, key_head):
        return jnp.where(same_image, contract(query_head, key_head, 1, 1) * head_scale, -1e30)

    def attend_head(pieces):
        query_head, key_head, value_head = pieces
        scores = head_scores(query_head, key_head)
        row_top = jnp.max(scores, axis=1, keepdims=True)
        exponent = jnp.exp(scores - row_top)
        total = jnp.sum(exponent, axis=1, keepdims=True)
        probs = (exponent / total).astype(low_type)
        return (contract(probs, value_head, 1, 0), (row_top + jnp.log(total))[:, 0])

    heads_query = split_heads(query)
    heads_key = split_heads(keys)
    heads_value = split_heads(values)
    mixed_heads, log_totals = lax.map(attend_head, (heads_query, heads_key, heads_value))
    mixed = merge_heads(mixed_heads).astype(low_type)
    attend_out = contract(mixed, full_output, 1, 0) + bias_output
    resid = inputs + gate_attend * attend_out
    normed_feed, inverse_feed = normalize_rows(resid)
    feed_in = (normed_feed * (1.0 + scale_feed) + shift_feed).astype(low_type)
    hidden_pre = contract(feed_in, full_expand, 1, 0) + bias_expand
    tanh_part = jnp.tanh(
        tanh_scale * (hidden_pre + cubic_term * hidden_pre * hidden_pre * hidden_pre)
    )
    hidden = (0.5 * hidden_pre * (1.0 + tanh_part)).astype(low_type)
    feed_out = contract(hidden, full_shrink, 1, 0) + bias_shrink
    block_output = (resid + gate_feed * feed_out).astype(low_type)
    grad_out = cotangent.astype(jnp.float32)
    grad_gate_feed = grad_out * feed_out
    grad_feed = (gate_feed * grad_out).astype(low_type)
    grad_shrink = contract(hidden, grad_feed, 0, 0)
    grad_hidden = contract(grad_feed, full_shrink, 1, 1)
    slope = 0.5 * (1.0 + tanh_part) + 0.5 * hidden_pre * (
        1.0 - tanh_part * tanh_part
    ) * tanh_scale * (1.0 + 3.0 * cubic_term * hidden_pre * hidden_pre)
    grad_pre = (grad_hidden * slope).astype(low_type)
    grad_expand = contract(feed_in, grad_pre, 0, 0)
    grad_feed_in = contract(grad_pre, full_expand, 1, 1)
    grad_scale_feed = grad_feed_in * normed_feed
    grad_resid = grad_out + normalize_back(
        grad_feed_in * (1.0 + scale_feed), normed_feed, inverse_feed
    )
    grad_gate_attend = grad_resid * attend_out
    grad_attend = (gate_attend * grad_resid).astype(low_type)
    grad_output = contract(mixed, grad_attend, 0, 0)
    grad_mixed = contract(grad_attend, full_output, 1, 1).astype(low_type)

    def attend_back(pieces):
        query_head, key_head, value_head, grad_head, log_total = pieces
        probs = jnp.exp(head_scores(query_head, key_head) - log_total[:, None])
        grad_value = contract(probs.astype(low_type), grad_head, 0, 0)
        grad_probs = contract(grad_head, value_head, 1, 1)
        grad_scores = (
            probs * (grad_probs - jnp.sum(probs * grad_probs, axis=1, keepdims=True))
        ).astype(low_type)
        grad_query = contract(grad_scores, key_head, 1, 0) * head_scale
        grad_key = contract(grad_scores, query_head, 0, 0) * head_scale
        return (grad_query, grad_key, grad_value)

    heads_grad_query, heads_grad_key, heads_grad_value = lax.map(
        attend_back, (heads_query, heads_key, heads_value, split_heads(grad_mixed), log_totals)
    )
    grad_projected = jnp.concatenate(
        [merge_heads(heads_grad_query), merge_heads(heads_grad_key), merge_heads(heads_grad_value)],
        axis=1,
    ).astype(low_type)
    grad_project = contract(attend_in, grad_projected, 0, 0)
    grad_attend_in = contract(grad_projected, full_project, 1, 1)
    grad_scale_attend = grad_attend_in * normed_attend
    token_grads = grad_resid + normalize_back(
        grad_attend_in * (1.0 + scale_attend), normed_attend, inverse_attend
    )
    token_mod_grads = jnp.concatenate(
        [
            grad_attend_in,
            grad_scale_attend,
            grad_gate_attend,
            grad_feed_in,
            grad_scale_feed,
            grad_gate_feed,
        ],
        axis=1,
    )
    sample_grads = contract(slot_match.astype(jnp.float32), token_mod_grads, 0, 0).astype(low_type)
    group_grads = lax.all_to_all(sample_grads, "mod", split_axis=1, concat_axis=0, tiled=True)
    grad_modulate = contract(activated, group_grads, 0, 0)
    grad_bias_modulate = jnp.sum(group_grads, axis=0, dtype=jnp.float32)
    condition_terms = contract(group_grads, full_modulate, 1, 1)
    condition_sum = lax.psum_scatter(
        condition_terms.astype(jnp.bfloat16), "mod", scatter_dimension=0, tiled=True
    ).astype(jnp.float32)
    own_conditions = conditions.astype(jnp.float32)
    sigmoid_part = jax.nn.sigmoid(own_conditions)
    condition_grads = condition_sum * (sigmoid_part * (1.0 + own_conditions * (1.0 - sigmoid_part)))
    modulate_bias_grad = lax.dynamic_update_slice_in_dim(
        jnp.zeros((6 * D,), jnp.float32), grad_bias_modulate, group_place * columns, 0
    )
    grad_bias = jnp.concatenate(
        [
            jnp.sum(grad_projected[:, 0:D], axis=0, dtype=jnp.float32),
            jnp.sum(grad_projected[:, 2 * D : 3 * D], axis=0, dtype=jnp.float32),
            jnp.sum(grad_attend, axis=0, dtype=jnp.float32),
            jnp.sum(grad_pre, axis=0, dtype=jnp.float32),
            jnp.sum(grad_feed, axis=0, dtype=jnp.float32),
            modulate_bias_grad,
        ],
        axis=0,
    )
    summed = (
        lax.psum_scatter(
            grad_project.astype(jnp.bfloat16), "dp", scatter_dimension=0, tiled=True
        ).astype(jnp.float32),
        lax.psum_scatter(
            grad_output.astype(jnp.bfloat16), "dp", scatter_dimension=0, tiled=True
        ).astype(jnp.float32),
        lax.psum_scatter(
            grad_expand.astype(jnp.bfloat16), "dp", scatter_dimension=0, tiled=True
        ).astype(jnp.float32),
        lax.psum_scatter(
            grad_shrink.astype(jnp.bfloat16), "dp", scatter_dimension=0, tiled=True
        ).astype(jnp.float32),
        lax.psum_scatter(
            grad_modulate.astype(jnp.bfloat16), "dp", scatter_dimension=0, tiled=True
        ).astype(jnp.float32),
        lax.psum_scatter(
            grad_bias.astype(jnp.bfloat16), "dp", scatter_dimension=0, tiled=True
        ).astype(jnp.float32),
    )
    sum_project, sum_output, sum_expand, sum_shrink, sum_bias = (
        lax.psum(summed[0].astype(jnp.bfloat16), "mod").astype(jnp.float32),
        lax.psum(summed[1].astype(jnp.bfloat16), "mod").astype(jnp.float32),
        lax.psum(summed[2].astype(jnp.bfloat16), "mod").astype(jnp.float32),
        lax.psum(summed[3].astype(jnp.bfloat16), "mod").astype(jnp.float32),
        lax.psum(summed[5].astype(jnp.bfloat16), "mod").astype(jnp.float32),
    )
    sum_modulate = summed[4]
    trunk_square = (
        jnp.sum(sum_project * sum_project)
        + jnp.sum(sum_output * sum_output)
        + jnp.sum(sum_expand * sum_expand)
        + jnp.sum(sum_shrink * sum_shrink)
        + jnp.sum(sum_bias * sum_bias)
    )
    totals = lax.psum((trunk_square, jnp.sum(sum_modulate * sum_modulate)), ("dp", "mod"))
    global_norm = jnp.sqrt(totals[0] / group_size + totals[1])
    clip_factor = jnp.minimum(1.0, 1.0 / (global_norm + 1e-06))
    next_project, first_project, second_project = adam_update(
        project_weight, project_moment, project_square, sum_project * clip_factor, D ** (-0.5)
    )
    next_output, first_output, second_output = adam_update(
        output_weight, output_moment, output_square, sum_output * clip_factor, (D // 64) ** (-0.5)
    )
    next_expand, first_expand, second_expand = adam_update(
        expand_weight, expand_moment, expand_square, sum_expand * clip_factor, D ** (-0.5)
    )
    next_shrink, first_shrink, second_shrink = adam_update(
        shrink_weight, shrink_moment, shrink_square, sum_shrink * clip_factor, FF ** (-0.5)
    )
    next_modulate, first_modulate, second_modulate = adam_update(
        modulate_weight, modulate_moment, modulate_square, sum_modulate * clip_factor, D ** (-0.5)
    )
    next_biases, first_biases, second_biases = adam_update(
        bias_vector, bias_moment, bias_square, sum_bias * clip_factor, 0.3
    )
    return (
        block_output,
        token_grads,
        condition_grads,
        global_norm,
        next_project,
        first_project,
        second_project,
        next_output,
        first_output,
        second_output,
        next_expand,
        first_expand,
        second_expand,
        next_shrink,
        first_shrink,
        second_shrink,
        next_modulate,
        first_modulate,
        second_modulate,
        next_biases,
        first_biases,
        second_biases,
    )


def solution(mesh):
    return jax.shard_map(
        plane_body if mesh.shape["dp"] == GROUP and mesh.shape["mod"] == DEPTH else generic_body,
        mesh=mesh,
        in_specs=(
            P(("dp", "mod"), None),
            P(("dp", "mod"), None),
            P(("dp", "mod"), None),
            P(("dp", "mod"), None),
            P("dp", None),
            P("dp", None),
            P("dp", None),
            P("dp", None),
            P("dp", None),
            P("dp", None),
            P("dp", None),
            P("dp", None),
            P("dp", None),
            P("dp", None),
            P("dp", None),
            P("dp", None),
            P("dp", "mod"),
            P("dp", "mod"),
            P("dp", "mod"),
            P("dp"),
            P("dp"),
            P("dp"),
        ),
        out_specs=(
            P(("dp", "mod"), None),
            P(("dp", "mod"), None),
            P(("dp", "mod"), None),
            P(),
            P("dp", None),
            P("dp", None),
            P("dp", None),
            P("dp", None),
            P("dp", None),
            P("dp", None),
            P("dp", None),
            P("dp", None),
            P("dp", None),
            P("dp", None),
            P("dp", None),
            P("dp", None),
            P("dp", "mod"),
            P("dp", "mod"),
            P("dp", "mod"),
            P("dp"),
            P("dp"),
            P("dp"),
        ),
        check_vma=False,
    )
```
